32 devices in a mesh: rep: 4 (over y, x), shard: 8 (over z, core).
Axes of the slice: x: 2, y: 2, z: 4, core: 2. Of those that a mesh axis runs over, the one named last changes fastest.
Arguments:
- block_in: bfloat16 [16384, 768], P(('rep', 'shard')), may hold values from -6 to 6
- earlier: bfloat16 [4, 16384, 768], P(None, ('rep', 'shard')), may hold values from -6 to 6
- cotangent: float32 [16384, 768], P(('rep', 'shard')), may hold values from -6 to 6
- qkv_weight: float32 [768, 2304], P('shard'), may hold values from -0.21875 to 0.21875
- out_weight: float32 [768, 768], P('shard'), may hold values from -6 to 6
- in_weight: float32 [768, 3072], P('shard'), may hold values from -0.21875 to 0.21875
- down_weight: float32 [3072, 768], P('shard'), may hold values from -0.109375 to 0.109375
- qk_bias: float32 [1536], P('shard'), may hold values from -3 to 3
- value_bias: float32 [768], P('shard'), may hold values from -3 to 3
- out_bias: float32 [768], P('shard'), may hold values from -3 to 3
- in_bias: float32 [3072], P('shard'), may hold values from -3 to 3
- down_bias: float32 [768], P('shard'), may hold values from -3 to 3
- gain_one: float32 [768], P('shard'), may hold values from 0.5 to 1.5
- shift_one: float32 [768], P('shard'), may hold values from -3 to 3
- gain_two: float32 [768], P('shard'), may hold values from 0.5 to 1.5
- shift_two: float32 [768], P('shard'), may hold values from -3 to 3
- depth_weights: float32 [5], replicated, may hold values from 0.3 to 1.2
Outputs:
- layer_out: float32 [16384, 768], P(('rep', 'shard'))
- grad_block_in: float32 [16384, 768], P(('rep', 'shard'))
- grad_earlier: float32 [4, 16384, 768], P(None, ('rep', 'shard'))
- grad_qkv_weight: float32 [768, 2304], P('shard')
- grad_out_weight: float32 [768, 768], P('shard')
- grad_in_weight: float32 [768, 3072], P('shard')
- grad_down_weight: float32 [3072, 768], P('shard')
- grad_qk_bias: float32 [1536], P('shard')
- grad_value_bias: float32 [768], P('shard')
- grad_out_bias: float32 [768], P('shard')
- grad_in_bias: float32 [3072], P('shard')
- grad_down_bias: float32 [768], P('shard')
- grad_gain_one: float32 [768], P('shard')
- grad_shift_one: float32 [768], P('shard')
- grad_gain_two: float32 [768], P('shard')
- grad_shift_two: float32 [768], P('shard')
- grad_depth: float32 [5], replicated
The draws below stay inside these ranges and needn't reach their ends.
All inputs are finite; a program needn't handle non-finite values.
Results may differ from the reference program's by a relative error of at most 0.035.
Values may be sent and summed in bfloat16 or wider, within the bound.
No kernel may reach another device: no remote copies, remote signals or barrier semaphores. Data moves between devices by JAX's collectives and lax.ppermute only.
A program may use at most 192 MiB of HBM per device.

```python
import jax
import jax.numpy as jnp
from jax import lax

D = 768
HEAD_DIM = 64
FF = 3072
BLOCK = 256
SEQ_LEN = 4096
TOKENS = 16384
N_REP = 4


def steps_of(key, dims, pieces, low, top_value):
    level = 1.0
    for dim, shards_of in pieces:
        steps = jax.random.uniform(jax.random.fold_in(jax.random.fold_in(key, 6), dim), (shards_of,), jnp.float32, low / len(pieces), top_value / len(pieces))
        level = level * jnp.repeat(jnp.exp(steps), dims[dim] // shards_of).reshape((-1,) + (1,) * (len(dims) - 1 - dim))
    return level


def bell_draw(key, shape, scale, reach, shards=(), held_as=jnp.bfloat16):
    level = steps_of(key, shape, shards, -0.22, 0.18) if shards else 1.0
    array = jax.random.normal(key, shape, jnp.float32) * scale * level
    return jnp.minimum(jnp.maximum(array, -reach), reach).astype(held_as)


def setup_inputs(seed: int = 0) -> dict:
    streams_of = jax.random.split(jax.random.key(seed), 18)
    block_in = bell_draw(streams_of[0], (TOKENS, D), 1.0, 6.0, ((0, 32),))
    earlier = bell_draw(streams_of[1], (4, TOKENS, D), 1.0, 6.0, ((1, 32),))
    cotangent = bell_draw(streams_of[2], (TOKENS, D), 1.0, 6.0, ((0, 32),), jnp.float32)
    qkv_weight = bell_draw(streams_of[3], (D, 3 * D), D ** -0.5, 0.21875, ((0, 8),), jnp.float32)
    out_weight = bell_draw(streams_of[4], (D, D), (max(1, 4 * D // SEQ_LEN)) ** -0.5, 6.0, ((0, 8),), jnp.float32)
    in_weight = bell_draw(streams_of[5], (D, FF), D ** -0.5, 0.21875, ((0, 8),), jnp.float32)
    down_weight = bell_draw(streams_of[6], (FF, D), FF ** -0.5, 0.109375, ((0, 8),), jnp.float32)
    qk_bias = bell_draw(streams_of[7], (2 * D,), 0.3, 3.0, ((0, 8),), jnp.float32)
    value_bias = bell_draw(streams_of[8], (D,), 0.3, 3.0, ((0, 8),), jnp.float32)
    out_bias = bell_draw(streams_of[9], (D,), 0.3, 3.0, ((0, 8),), jnp.float32)
    in_bias = bell_draw(streams_of[10], (FF,), 0.3, 3.0, ((0, 8),), jnp.float32)
    down_bias = bell_draw(streams_of[11], (D,), 0.3, 3.0, ((0, 8),), jnp.float32)
    gain_one = jnp.clip(1.0 + 0.1 * jax.random.normal(streams_of[12], (D,), jnp.float32), 0.5, 1.5)
    shift_one = bell_draw(streams_of[13], (D,), 0.3, 3.0, ((0, 8),), jnp.float32)
    gain_two = jnp.clip(1.0 + 0.1 * jax.random.normal(streams_of[14], (D,), jnp.float32), 0.5, 1.5)
    shift_two = bell_draw(streams_of[15], (D,), 0.3, 3.0, ((0, 8),), jnp.float32)
    depth_weights = jnp.clip(jax.random.uniform(streams_of[16], (5,), jnp.float32, 0.3, 1.2), 0.3, 1.2)
    return {"block_in": block_in, "earlier": earlier, "cotangent": cotangent, "qkv_weight": qkv_weight, "out_weight": out_weight, "in_weight": in_weight, "down_weight": down_weight, "qk_bias": qk_bias, "value_bias": value_bias, "out_bias": out_bias, "in_bias": in_bias, "down_bias": down_bias, "gain_one": gain_one, "shift_one": shift_one, "gain_two": gain_two, "shift_two": shift_two, "depth_weights": depth_weights}


NEG = -1e+30
EPSILON = 1e-05
HIGH = lax.Precision.HIGHEST

@jax.custom_vjp
def low(v):
    return lax.optimization_barrier(v.astype(jnp.bfloat16)).astype(jnp.float32)

@jax.custom_vjp
def low_back(v):
    return v

def low_keep(v):
    return (low(v), None)

def low_pass(kept, grad):
    return (grad,)

def back_keep(v):
    return (v, None)

def back_low(kept, grad):
    return (low(grad),)
low.defvjp(low_keep, low_pass)
low_back.defvjp(back_keep, back_low)

def layer_norm(inputs, gain, shift):
    center = inputs - lax.optimization_barrier(jnp.mean(inputs, axis=-1, keepdims=True))
    spread = lax.optimization_barrier(jnp.mean(center * center, axis=-1, keepdims=True))
    return center * lax.rsqrt(spread + EPSILON) * gain + shift

def rotate(inputs, positions):
    row_count = inputs.shape[0]
    split = inputs.reshape(row_count, -1, HEAD_DIM)
    half_dim = HEAD_DIM // 2
    freqs = 10000.0 ** (-jnp.arange(half_dim, dtype=jnp.float32) / half_dim)
    angles = positions.astype(jnp.float32)[:, None] * freqs[None, :]
    cosine = jnp.cos(angles)[:, None, :]
    sine = jnp.sin(angles)[:, None, :]
    former = split[..., :half_dim]
    latter = split[..., half_dim:]
    turned = jnp.concatenate([former * cosine - latter * sine, former * sine + latter * cosine], axis=-1)
    return turned.reshape(row_count, -1)

def attention(queries, key_rows, values):
    length = queries.shape[0]
    head_count = queries.shape[1] // HEAD_DIM
    window = min(512, length)
    block_total = length // window
    key_heads = key_rows.reshape(length, head_count, HEAD_DIM)
    value_heads = values.reshape(length, head_count, HEAD_DIM)
    key_block = jnp.arange(length).astype(jnp.int32) // BLOCK
    score_scale = HEAD_DIM ** (-0.5)

    @jax.checkpoint
    def one_block(element):
        query_block, anchor = element
        scores = low_back(jnp.einsum('qhd,khd->hqk', query_block, key_heads, precision=HIGH) * score_scale)
        query_pos = (anchor + jnp.arange(window).astype(jnp.int32)) // BLOCK
        allowed = key_block[None, :] <= query_pos[:, None]
        scores = jnp.where(allowed[None], scores, NEG)
        highest = lax.optimization_barrier(jnp.max(scores, axis=-1, keepdims=True))
        weights = jnp.exp(scores - highest)
        weights = low(weights / lax.optimization_barrier(jnp.sum(weights, axis=-1, keepdims=True)))
        return jnp.einsum('hqk,khd->qhd', weights, value_heads, precision=HIGH)
    anchors = (jnp.arange(block_total) * window).astype(jnp.int32)
    mixed = lax.map(one_block, (queries.reshape(block_total, window, head_count, HEAD_DIM), anchors))
    return mixed.reshape(length, head_count * HEAD_DIM)

def forward(params, depth, inputs, stack):
    w_qkv, w_out, w_in, w_down, b_qk, b_value, b_out, b_in, b_down, g_one, s_one, g_two, s_two = [low(master) for master in params]
    length, model_width = inputs.shape
    positions = jnp.arange(length).astype(jnp.int32)
    normed = layer_norm(inputs, g_one, s_one)
    b_joint = jnp.concatenate([b_qk, b_value])
    projected = low_back(jnp.dot(low(normed), w_qkv, precision=HIGH) + b_joint)
    queries = low(rotate(projected[:, :model_width], positions))
    key_rows = low(rotate(projected[:, model_width:2 * model_width], positions))
    values = low(projected[:, 2 * model_width:])
    mixed = low_back(low(attention(queries, key_rows, values)))
    branch = low_back(jnp.dot(mixed, w_out, precision=HIGH) + b_out)
    middle = inputs + branch
    normed_two = layer_norm(middle, g_two, s_two)
    hidden = low_back(jnp.dot(low(normed_two), w_in, precision=HIGH) + b_in)
    active = low(jax.nn.gelu(hidden, approximate=True))
    branch_two = low_back(jnp.dot(active, w_down, precision=HIGH) + b_down)
    result = middle + branch_two
    combined = depth[4] * result
    for level in range(4):
        combined = combined + depth[level] * stack[level]
    return combined

def reference(block_in, earlier, cotangent, qkv_weight, out_weight, in_weight, down_weight, qk_bias, value_bias, out_bias, in_bias, down_bias, gain_one, shift_one, gain_two, shift_two, depth_weights):
    params = (qkv_weight, out_weight, in_weight, down_weight, qk_bias, value_bias, out_bias, in_bias, down_bias, gain_one, shift_one, gain_two, shift_two)
    sequences = block_in.astype(jnp.float32).reshape(N_REP, SEQ_LEN, D)
    stacks = jnp.transpose(earlier.astype(jnp.float32).reshape(4, N_REP, SEQ_LEN, D), (1, 0, 2, 3))
    cotangents = cotangent.astype(jnp.float32).reshape(N_REP, SEQ_LEN, D)

    def per_sequence(running, element):
        inputs, stack, seq_cot = element
        output, backward = jax.vjp(forward, params, depth_weights, inputs, stack)
        grad_params, grad_dep, grad_inputs, grad_stack = backward(seq_cot)
        param_sums, depth_sum = running
        param_sums = tuple((total_one + part_one for total_one, part_one in zip(param_sums, grad_params)))
        return ((param_sums, depth_sum + grad_dep), (output, grad_inputs, grad_stack))
    start = (tuple((jnp.zeros_like(master) for master in params)), jnp.zeros_like(depth_weights))
    (param_sums, depth_sum), (outputs, grad_inputs, grad_stacks) = lax.scan(per_sequence, start, (sequences, stacks, cotangents))
    layer_out = outputs.reshape(TOKENS, D)
    grad_block_in = grad_inputs.reshape(TOKENS, D)
    grad_earlier = jnp.transpose(grad_stacks, (1, 0, 2, 3)).reshape(4, TOKENS, D)
    return (layer_out, grad_block_in, grad_earlier, param_sums[0], param_sums[1], param_sums[2], param_sums[3], param_sums[4], param_sums[5], param_sums[6], param_sums[7], param_sums[8], param_sums[9], param_sums[10], param_sums[11], param_sums[12], depth_sum)
```

```python
from functools import partial
import math

import jax
import jax.numpy as jnp
from jax import lax
from jax.experimental import pallas as pl
from jax.experimental.pallas import tpu as pltpu
from jax.sharding import PartitionSpec as P

HEAD_DIM = 64
BLOCK = 256


NEG = -1e30
EPSILON = 1e-05


def layer_norm(inputs, gain, shift):
    center = inputs - jnp.mean(inputs, axis=-1, keepdims=True)
    spread = jnp.mean(center * center, axis=-1, keepdims=True)
    return center * lax.rsqrt(spread + EPSILON) * gain + shift


def rotate(inputs, positions):
    row_count = inputs.shape[0]
    split = inputs.reshape(row_count, -1, HEAD_DIM)
    half_dim = HEAD_DIM // 2
    freqs = 10000.0 ** (-jnp.arange(half_dim, dtype=jnp.float32) / half_dim)
    angles = positions.astype(jnp.float32)[:, None] * freqs[None, :]
    cosine = jnp.cos(angles)[:, None, :]
    sine = jnp.sin(angles)[:, None, :]
    former = split[..., :half_dim]
    latter = split[..., half_dim:]
    turned = jnp.concatenate(
        [former * cosine - latter * sine, former * sine + latter * cosine], axis=-1
    )
    return turned.reshape(row_count, -1)


def generic_device(
    block_in,
    earlier,
    cotangent,
    qkv_weight,
    out_weight,
    in_weight,
    down_weight,
    qk_bias,
    value_bias,
    out_bias,
    in_bias,
    down_bias,
    gain_one,
    shift_one,
    gain_two,
    shift_two,
    depth_weights,
):
    bf16 = jnp.bfloat16
    f32 = jnp.float32
    w_qkv, w_out, w_in, w_down, b_qk, b_value, b_out, b_in, b_down, g_one, s_one, g_two, s_two = (
        lax.all_gather(qkv_weight.astype(bf16), "shard", axis=0, tiled=True),
        lax.all_gather(out_weight.astype(bf16), "shard", axis=0, tiled=True),
        lax.all_gather(in_weight.astype(bf16), "shard", axis=0, tiled=True),
        lax.all_gather(down_weight.astype(bf16), "shard", axis=0, tiled=True),
        lax.all_gather(qk_bias.astype(bf16), "shard", axis=0, tiled=True),
        lax.all_gather(value_bias.astype(bf16), "shard", axis=0, tiled=True),
        lax.all_gather(out_bias.astype(bf16), "shard", axis=0, tiled=True),
        lax.all_gather(in_bias.astype(bf16), "shard", axis=0, tiled=True),
        lax.all_gather(down_bias.astype(bf16), "shard", axis=0, tiled=True),
        lax.all_gather(gain_one.astype(bf16), "shard", axis=0, tiled=True),
        lax.all_gather(shift_one.astype(bf16), "shard", axis=0, tiled=True),
        lax.all_gather(gain_two.astype(bf16), "shard", axis=0, tiled=True),
        lax.all_gather(shift_two.astype(bf16), "shard", axis=0, tiled=True),
    )
    row_count, model_width = block_in.shape
    head_count = model_width // HEAD_DIM
    groups = lax.axis_size("shard")
    length = row_count * groups
    window = min(512, length)
    member = lax.axis_index("shard")
    first_row = member * row_count
    last_end = first_row + row_count
    positions = first_row + jnp.arange(row_count, dtype=jnp.int32)
    query_block = positions // BLOCK
    score_scale = HEAD_DIM ** (-0.5)
    needed = (last_end + window - 1) // window
    inputs = block_in.astype(f32)
    normed, norm_back = jax.vjp(layer_norm, inputs, g_one.astype(f32), s_one.astype(f32))
    normed_low = normed.astype(bf16)
    joint_bias = jnp.concatenate([b_qk.astype(f32), b_value.astype(f32)])
    projected = jnp.dot(normed_low, w_qkv, preferred_element_type=f32) + joint_bias
    queries = rotate(projected[:, :model_width], positions).astype(bf16)
    key_rows = rotate(projected[:, model_width : 2 * model_width], positions).astype(bf16)
    values = projected[:, 2 * model_width :].astype(bf16)
    query_heads = queries.reshape(row_count, head_count, HEAD_DIM)

    def masked_scores(key_piece, key_start):
        piece_rows = key_piece.shape[0]
        key_heads = key_piece.reshape(piece_rows, head_count, HEAD_DIM)
        scores = (
            jnp.einsum("qhd,khd->hqk", query_heads, key_heads, preferred_element_type=f32)
            * score_scale
        )
        key_block = (key_start + jnp.arange(piece_rows, dtype=jnp.int32)) // BLOCK
        allowed = key_block[None, :] <= query_block[:, None]
        return (scores, allowed)

    def absorb(running, key_piece, value_piece, key_start):
        highest, denominator, summed = running
        scores, allowed = masked_scores(key_piece, key_start)
        scores = jnp.where(allowed[None], scores, NEG)
        new_high = jnp.maximum(highest, jnp.max(scores, axis=-1))
        rescale = jnp.exp(highest - new_high)
        weights = jnp.where(allowed[None], jnp.exp(scores - new_high[..., None]), 0.0)
        value_heads = value_piece.reshape(-1, head_count, HEAD_DIM)
        summed = summed * rescale[..., None] + jnp.einsum(
            "hqk,khd->hqd", weights.astype(bf16), value_heads, preferred_element_type=f32
        )
        return (new_high, denominator * rescale + jnp.sum(weights, axis=-1), summed)

    start_state = (
        jnp.full((head_count, row_count), NEG, f32),
        jnp.zeros((head_count, row_count), f32),
        jnp.zeros((head_count, row_count, HEAD_DIM), f32),
    )
    key_piece = lax.all_gather(key_rows, "shard", axis=0, tiled=True)
    value_piece = lax.all_gather(values, "shard", axis=0, tiled=True)
    piece_rows = key_piece.shape[0]
    sub_rows = math.gcd(piece_rows, window)
    usable = jnp.clip((last_end + sub_rows - 1) // sub_rows, 0, piece_rows // sub_rows)

    def advance(block_step, state_inner):
        offset = block_step * sub_rows
        return absorb(
            state_inner,
            lax.dynamic_slice_in_dim(key_piece, offset, sub_rows, 0),
            lax.dynamic_slice_in_dim(value_piece, offset, sub_rows, 0),
            offset,
        )

    highest, denominator, summed = lax.fori_loop(0, usable, advance, start_state)
    attended = summed / denominator[..., None]
    log_norm = highest + jnp.log(denominator)
    mixed = jnp.transpose(attended, (1, 0, 2)).reshape(row_count, model_width).astype(bf16)
    branch = jnp.dot(mixed, w_out, preferred_element_type=f32) + b_out.astype(f32)
    middle = inputs + branch
    normed_two, norm_two_back = jax.vjp(layer_norm, middle, g_two.astype(f32), s_two.astype(f32))
    normed_two_low = normed_two.astype(bf16)
    hidden = jnp.dot(normed_two_low, w_in, preferred_element_type=f32) + b_in.astype(f32)
    active_full, gelu_back = jax.vjp(partial(jax.nn.gelu, approximate=True), hidden)
    active = active_full.astype(bf16)
    result = middle + jnp.dot(active, w_down, preferred_element_type=f32) + b_down.astype(f32)
    stacked = earlier.astype(f32)
    layer_out = depth_weights[4] * result
    for level in range(4):
        layer_out = layer_out + depth_weights[level] * stacked[level]
    grad_earlier = depth_weights[:4][:, None, None] * cotangent[None]
    local_depth = jnp.concatenate(
        [jnp.sum(stacked * cotangent[None], axis=(1, 2)), jnp.sum(result * cotangent)[None]]
    )
    grad_depth = lax.psum(local_depth, ("rep", "shard"))
    grad_result = depth_weights[4] * cotangent
    down_grad = grad_result.astype(bf16)
    grad_down_w = jnp.einsum("tf,td->fd", active, down_grad, preferred_element_type=f32)
    grad_down_b = jnp.sum(down_grad.astype(f32), axis=0)
    grad_active = jnp.einsum("td,fd->tf", down_grad, w_down, preferred_element_type=f32)
    grad_hidden = gelu_back(grad_active)[0].astype(bf16)
    grad_in_w = jnp.einsum("td,tf->df", normed_two_low, grad_hidden, preferred_element_type=f32)
    grad_in_b = jnp.sum(grad_hidden.astype(f32), axis=0)
    grad_normed_two = jnp.einsum("tf,df->td", grad_hidden, w_in, preferred_element_type=f32)
    grad_mid_norm, grad_gain_two, grad_shift_two = norm_two_back(grad_normed_two)
    grad_middle = grad_result + grad_mid_norm
    branch_grad = grad_middle.astype(bf16)
    grad_out_w = jnp.einsum("td,te->de", mixed, branch_grad, preferred_element_type=f32)
    grad_out_b = jnp.sum(branch_grad.astype(f32), axis=0)
    grad_mixed = jnp.einsum("te,de->td", branch_grad, w_out, preferred_element_type=f32).astype(
        bf16
    )
    key_all, value_all = (
        lax.all_gather(key_rows, "shard", axis=0, tiled=True),
        lax.all_gather(values, "shard", axis=0, tiled=True),
    )
    grad_heads = grad_mixed.reshape(row_count, head_count, HEAD_DIM)
    delta = jnp.einsum("qhd,hqd->hq", grad_heads.astype(f32), attended)

    def score_grads(key_piece, value_piece, offset, piece_rows):
        scores, allowed = masked_scores(key_piece, offset)
        probs = jnp.where(allowed[None], jnp.exp(scores - log_norm[..., None]), 0.0)
        value_heads = value_piece.reshape(piece_rows, head_count, HEAD_DIM)
        grad_probs = jnp.einsum("qhd,khd->hqk", grad_heads, value_heads, preferred_element_type=f32)
        grad_scores = (probs * (grad_probs - delta[..., None])).astype(bf16)
        return (probs, grad_scores)

    def retrace(block_step, running):
        grad_query, grad_keys, grad_values = running
        offset = block_step * window
        key_piece = lax.dynamic_slice_in_dim(key_all, offset, window, 0)
        value_piece = lax.dynamic_slice_in_dim(value_all, offset, window, 0)
        probs, grad_scores = score_grads(key_piece, value_piece, offset, window)
        key_heads = key_piece.reshape(window, head_count, HEAD_DIM)
        grad_query = grad_query + jnp.einsum(
            "hqk,khd->qhd", grad_scores, key_heads, preferred_element_type=f32
        )
        piece_keys = (
            jnp.einsum("hqk,qhd->khd", grad_scores, query_heads, preferred_element_type=f32)
            * score_scale
        )
        piece_values = jnp.einsum(
            "hqk,qhd->khd", probs.astype(bf16), grad_heads, preferred_element_type=f32
        )
        grad_keys = lax.dynamic_update_slice_in_dim(
            grad_keys, piece_keys.reshape(window, model_width), offset, 0
        )
        grad_values = lax.dynamic_update_slice_in_dim(
            grad_values, piece_values.reshape(window, model_width), offset, 0
        )
        return (grad_query, grad_keys, grad_values)

    start_back = (
        jnp.zeros((row_count, head_count, HEAD_DIM), f32),
        jnp.zeros((length, model_width), f32),
        jnp.zeros((length, model_width), f32),
    )
    grad_query, grad_keys, grad_values = lax.fori_loop(0, needed, retrace, start_back)
    own_keys, own_values = (
        lax.psum_scatter(
            grad_keys.astype(jnp.bfloat16), "shard", scatter_dimension=0, tiled=True
        ).astype(jnp.float32),
        lax.psum_scatter(
            grad_values.astype(jnp.bfloat16), "shard", scatter_dimension=0, tiled=True
        ).astype(jnp.float32),
    )
    grad_q_turned = rotate(grad_query.reshape(row_count, model_width) * score_scale, -positions)
    grad_k_turned = rotate(own_keys, -positions)
    grad_joint = jnp.concatenate([grad_q_turned, grad_k_turned, own_values], axis=1).astype(bf16)
    grad_qkv_w = jnp.einsum("td,tf->df", normed_low, grad_joint, preferred_element_type=f32)
    joint_sums = jnp.sum(grad_joint.astype(f32), axis=0)
    grad_qk_b = joint_sums[: 2 * model_width]
    grad_value_b = joint_sums[2 * model_width :]
    grad_normed = jnp.einsum("tf,df->td", grad_joint, w_qkv, preferred_element_type=f32)
    grad_in_norm, grad_gain_one, grad_shift_one = norm_back(grad_normed)
    grad_block = grad_middle + grad_in_norm
    (
        own_qkv_w,
        own_out_w,
        own_in_w,
        own_down_w,
        own_qk_b,
        own_value_b,
        own_out_b,
        own_in_b,
        own_down_b,
        own_gain_one,
        own_shift_one,
        own_gain_two,
        own_shift_two,
    ) = (
        lax.psum_scatter(
            grad_qkv_w.astype(jnp.bfloat16), "shard", scatter_dimension=0, tiled=True
        ).astype(jnp.float32),
        lax.psum_scatter(
            grad_out_w.astype(jnp.bfloat16), "shard", scatter_dimension=0, tiled=True
        ).astype(jnp.float32),
        lax.psum_scatter(
            grad_in_w.astype(jnp.bfloat16), "shard", scatter_dimension=0, tiled=True
        ).astype(jnp.float32),
        lax.psum_scatter(
            grad_down_w.astype(jnp.bfloat16), "shard", scatter_dimension=0, tiled=True
        ).astype(jnp.float32),
        lax.psum_scatter(
            grad_qk_b.astype(jnp.bfloat16), "shard", scatter_dimension=0, tiled=True
        ).astype(jnp.float32),
        lax.psum_scatter(
            grad_value_b.astype(jnp.bfloat16), "shard", scatter_dimension=0, tiled=True
        ).astype(jnp.float32),
        lax.psum_scatter(
            grad_out_b.astype(jnp.bfloat16), "shard", scatter_dimension=0, tiled=True
        ).astype(jnp.float32),
        lax.psum_scatter(
            grad_in_b.astype(jnp.bfloat16), "shard", scatter_dimension=0, tiled=True
        ).astype(jnp.float32),
        lax.psum_scatter(
            grad_down_b.astype(jnp.bfloat16), "shard", scatter_dimension=0, tiled=True
        ).astype(jnp.float32),
        lax.psum_scatter(
            grad_gain_one.astype(jnp.bfloat16), "shard", scatter_dimension=0, tiled=True
        ).astype(jnp.float32),
        lax.psum_scatter(
            grad_shift_one.astype(jnp.bfloat16), "shard", scatter_dimension=0, tiled=True
        ).astype(jnp.float32),
        lax.psum_scatter(
            grad_gain_two.astype(jnp.bfloat16), "shard", scatter_dimension=0, tiled=True
        ).astype(jnp.float32),
        lax.psum_scatter(
            grad_shift_two.astype(jnp.bfloat16), "shard", scatter_dimension=0, tiled=True
        ).astype(jnp.float32),
    )
    (
        sum_qkv_w,
        sum_out_w,
        sum_in_w,
        sum_down_w,
        sum_qk_b,
        sum_value_b,
        sum_out_b,
        sum_in_b,
        sum_down_b,
        sum_gain_one,
        sum_shift_one,
        sum_gain_two,
        sum_shift_two,
    ) = (
        lax.psum(own_qkv_w.astype(jnp.bfloat16), "rep").astype(jnp.float32),
        lax.psum(own_out_w.astype(jnp.bfloat16), "rep").astype(jnp.float32),
        lax.psum(own_in_w.astype(jnp.bfloat16), "rep").astype(jnp.float32),
        lax.psum(own_down_w.astype(jnp.bfloat16), "rep").astype(jnp.float32),
        lax.psum(own_qk_b.astype(jnp.bfloat16), "rep").astype(jnp.float32),
        lax.psum(own_value_b.astype(jnp.bfloat16), "rep").astype(jnp.float32),
        lax.psum(own_out_b.astype(jnp.bfloat16), "rep").astype(jnp.float32),
        lax.psum(own_in_b.astype(jnp.bfloat16), "rep").astype(jnp.float32),
        lax.psum(own_down_b.astype(jnp.bfloat16), "rep").astype(jnp.float32),
        lax.psum(own_gain_one.astype(jnp.bfloat16), "rep").astype(jnp.float32),
        lax.psum(own_shift_one.astype(jnp.bfloat16), "rep").astype(jnp.float32),
        lax.psum(own_gain_two.astype(jnp.bfloat16), "rep").astype(jnp.float32),
        lax.psum(own_shift_two.astype(jnp.bfloat16), "rep").astype(jnp.float32),
    )
    return (
        layer_out,
        grad_block,
        grad_earlier,
        sum_qkv_w,
        sum_out_w,
        sum_in_w,
        sum_down_w,
        sum_qk_b,
        sum_value_b,
        sum_out_b,
        sum_in_b,
        sum_down_b,
        sum_gain_one,
        sum_shift_one,
        sum_gain_two,
        sum_shift_two,
        grad_depth,
    )


F32 = jnp.float32
BF16 = jnp.bfloat16
CHUNK = 2 * BLOCK
VMEM_LIMIT = 56 * 1024 * 1024


def contract(left, right, left_dim, right_dim):
    return lax.dot_general(
        left, right, (((left_dim,), (right_dim,)), ((), ())), preferred_element_type=F32
    )


def qkv_kernel(
    x_ref, weight_ref, bias_ref, gain_ref, shift_ref, cos_ref, sin_ref,
    normed_ref, qt_ref, kt_ref, vt_ref, k_ref, v_ref,
):
    x = x_ref[...].astype(F32)
    center = x - jnp.mean(x, axis=-1, keepdims=True)
    spread = jnp.mean(center * center, axis=-1, keepdims=True)
    normed = center * lax.rsqrt(spread + EPSILON) * gain_ref[...] + shift_ref[...]
    low = normed.astype(BF16)
    normed_ref[...] = low
    width = qt_ref.shape[0]
    half = HEAD_DIM // 2
    joint = contract(weight_ref[...], low, 1, 1) + bias_ref[...]
    cosine = cos_ref[...]
    sine = sin_ref[...]
    for head in range(width // HEAD_DIM):
        base = head * HEAD_DIM
        for part in range(2):
            start = part * width + base
            former = joint[start : start + half]
            latter = joint[start + half : start + HEAD_DIM]
            turned = jnp.concatenate(
                [former * cosine - latter * sine, former * sine + latter * cosine], axis=0
            )
            if part == 0:
                qt_ref[base : base + HEAD_DIM, :] = (turned * HEAD_DIM ** (-0.5)).astype(BF16)
            else:
                kt_ref[base : base + HEAD_DIM, :] = turned.astype(BF16)
                k_ref[head] = jnp.transpose(turned).astype(BF16)
        start = 2 * width + base
        value = joint[start : start + HEAD_DIM]
        vt_ref[base : base + HEAD_DIM, :] = value.astype(BF16)
        v_ref[head] = jnp.transpose(value).astype(BF16)


def project(tokens, weight_t, bias, gain, shift, cosine, sine):
    length, model_width = tokens.shape
    columns = weight_t.shape[0]
    width = columns // 3
    heads = width // HEAD_DIM
    half = HEAD_DIM // 2
    tile = CHUNK
    fixed = lambda i: (0, 0)
    across = lambda i: (0, i)
    return pl.pallas_call(
        qkv_kernel,
        name="project",
        grid=(length // tile,),
        in_specs=[
            pl.BlockSpec((tile, model_width), lambda i: (i, 0)),
            pl.BlockSpec((columns, model_width), fixed),
            pl.BlockSpec((columns, 1), fixed),
            pl.BlockSpec((1, model_width), fixed),
            pl.BlockSpec((1, model_width), fixed),
            pl.BlockSpec((half, tile), across),
            pl.BlockSpec((half, tile), across),
        ],
        out_specs=[
            pl.BlockSpec((tile, model_width), lambda i: (i, 0)),
            pl.BlockSpec((width, tile), across),
            pl.BlockSpec((width, tile), across),
            pl.BlockSpec((width, tile), across),
            pl.BlockSpec((heads, tile, HEAD_DIM), lambda i: (0, i, 0)),
            pl.BlockSpec((heads, tile, HEAD_DIM), lambda i: (0, i, 0)),
        ],
        out_shape=[
            jax.ShapeDtypeStruct((length, model_width), BF16),
            jax.ShapeDtypeStruct((width, length), BF16),
            jax.ShapeDtypeStruct((width, length), BF16),
            jax.ShapeDtypeStruct((width, length), BF16),
            jax.ShapeDtypeStruct((heads, length, HEAD_DIM), BF16),
            jax.ShapeDtypeStruct((heads, length, HEAD_DIM), BF16),
        ],
        compiler_params=pltpu.CompilerParams(vmem_limit_bytes=VMEM_LIMIT),
    )(tokens, weight_t, bias, gain, shift, cosine, sine)


def last_mask(odd):
    row = lax.broadcasted_iota(jnp.int32, (CHUNK, BLOCK), 0)
    return row < BLOCK * (1 + odd)


def attend_kernel(core_ref, qt_ref, k_ref, vt_ref, low_ref, full_ref, stat_ref):
    pair = pl.program_id(0)
    odd = core_ref[0] ^ (pair & 1)
    width = qt_ref.shape[0]
    heads = width // HEAD_DIM
    queries = [qt_ref[h * HEAD_DIM : (h + 1) * HEAD_DIM, :] for h in range(heads)]

    def absorb(step, state, masked):
        offset = pl.multiple_of(step * CHUNK, CHUNK)
        fresh = []
        for h in range(heads):
            highest, total, summed = state[h]
            scores = contract(k_ref[h, pl.ds(offset, CHUNK), :], queries[h], 1, 0)
            if masked:
                scores = jnp.where(last_mask(odd), scores, NEG)
            new_high = jnp.maximum(highest, jnp.max(scores, axis=0, keepdims=True))
            rescale = jnp.exp(highest - new_high)
            weights = jnp.exp(scores - new_high)
            total = total * rescale + jnp.sum(weights, axis=0, keepdims=True)
            values = vt_ref[h * HEAD_DIM : (h + 1) * HEAD_DIM, pl.ds(offset, CHUNK)]
            summed = summed * rescale + contract(values, weights.astype(BF16), 1, 0)
            fresh.append((new_high, total, summed))
        return fresh

    state = [
        (
            jnp.full((1, BLOCK), NEG, F32),
            jnp.zeros((1, BLOCK), F32),
            jnp.zeros((HEAD_DIM, BLOCK), F32),
        )
        for _ in range(heads)
    ]
    state = lax.fori_loop(0, pair, lambda i, s: absorb(i, s, False), state)
    state = absorb(pair, state, True)
    for h in range(heads):
        highest, total, summed = state[h]
        attended = summed / total
        full_ref[0, h * HEAD_DIM : (h + 1) * HEAD_DIM, :] = attended
        low_ref[0, h * HEAD_DIM : (h + 1) * HEAD_DIM, :] = attended.astype(BF16)
        stat_ref[0, h : h + 1, :] = highest + jnp.log(total)


def attend(core, qt, k, vt):
    width, length = qt.shape
    pairs = length // CHUNK
    own = lambda j, core: (0, 2 * j + (core[0] ^ (j & 1)))
    slot = lambda j, core: (j, 0, 0)
    return pl.pallas_call(
        attend_kernel,
        name="attend",
        grid_spec=pltpu.PrefetchScalarGridSpec(
            num_scalar_prefetch=1,
            grid=(pairs,),
            in_specs=[
                pl.BlockSpec((width, BLOCK), own),
                pl.BlockSpec(k.shape, lambda j, core: (0, 0, 0)),
                pl.BlockSpec(vt.shape, lambda j, core: (0, 0)),
            ],
            out_specs=[
                pl.BlockSpec((1, width, BLOCK), slot),
                pl.BlockSpec((1, width, BLOCK), slot),
                pl.BlockSpec((1, 8, BLOCK), slot),
            ],
        ),
        out_shape=[
            jax.ShapeDtypeStruct((pairs, width, BLOCK), BF16),
            jax.ShapeDtypeStruct((pairs, width, BLOCK), F32),
            jax.ShapeDtypeStruct((pairs, 8, BLOCK), F32),
        ],
        compiler_params=pltpu.CompilerParams(vmem_limit_bytes=VMEM_LIMIT),
    )(core, qt, k, vt)


def retrace_kernel(
    core_ref, qt_ref, grad_ref, full_ref, stat_ref, cos_ref, sin_ref, k_ref, v_ref, kt_ref,
    joint_ref, dk_ref, dv_ref,
):
    step_id = pl.program_id(0)
    pair = pl.num_programs(0) - 1 - step_id
    odd = core_ref[0] ^ (pair & 1)
    width = qt_ref.shape[0]
    heads = width // HEAD_DIM
    half = HEAD_DIM // 2

    @pl.when(step_id == 0)
    def _():
        dk_ref[...] = jnp.zeros_like(dk_ref)
        dv_ref[...] = jnp.zeros_like(dv_ref)

    queries, grads, deltas, norms = [], [], [], []
    for h in range(heads):
        rows = slice(h * HEAD_DIM, (h + 1) * HEAD_DIM)
        queries.append(qt_ref[rows, :])
        grad = grad_ref[0, rows, :]
        grads.append(grad)
        deltas.append(jnp.sum(grad.astype(F32) * full_ref[0, rows, :], axis=0, keepdims=True))
        norms.append(stat_ref[0, h : h + 1, :])

    def absorb(step, state, masked):
        offset = pl.multiple_of(step * CHUNK, CHUNK)
        keys = pl.ds(offset, CHUNK)
        fresh = []
        for h in range(heads):
            scores = contract(k_ref[h, keys, :], queries[h], 1, 0)
            probs = jnp.exp(scores - norms[h])
            if masked:
                probs = jnp.where(last_mask(odd), probs, 0.0)
            grad_probs = contract(v_ref[h, keys, :], grads[h], 1, 0)
            grad_scores = (probs * (grad_probs - deltas[h])).astype(BF16)
            dv_ref[h, keys, :] += contract(probs.astype(BF16), grads[h], 1, 1)
            dk_ref[h, keys, :] += contract(grad_scores, queries[h], 1, 1)
            turned = kt_ref[h * HEAD_DIM : (h + 1) * HEAD_DIM, keys]
            fresh.append(state[h] + contract(turned, grad_scores, 1, 0))
        return fresh

    state = [jnp.zeros((HEAD_DIM, BLOCK), F32) for _ in range(heads)]
    state = lax.fori_loop(0, pair, lambda i, s: absorb(i, s, False), state)
    state = absorb(pair, state, True)
    offset = pl.multiple_of(pair * CHUNK, CHUNK)
    cosine = cos_ref[...]
    sine = sin_ref[...]
    for h in range(heads):
        base = h * HEAD_DIM
        doubled = jnp.concatenate([state[h], state[h]], axis=1) * HEAD_DIM ** (-0.5)
        column = lax.broadcasted_iota(jnp.int32, doubled.shape, 1) // BLOCK
        doubled = jnp.where(column == odd, doubled, 0.0)
        key_grad = jnp.transpose(dk_ref[h, pl.ds(offset, CHUNK), :])
        for part, value in ((0, doubled), (1, key_grad)):
            former = value[:half]
            latter = value[half:]
            turned = jnp.concatenate(
                [former * cosine + latter * sine, latter * cosine - former * sine], axis=0
            )
            start = part * width + base
            joint_ref[start : start + HEAD_DIM, :] = turned.astype(BF16)
        start = 2 * width + base
        joint_ref[start : start + HEAD_DIM, :] = jnp.transpose(
            dv_ref[h, pl.ds(offset, CHUNK), :]
        ).astype(BF16)


def retrace(core, qt, grads, full, stats, cosine, sine, k, v, kt):
    width, length = qt.shape
    heads = width // HEAD_DIM
    half = HEAD_DIM // 2
    pairs = length // CHUNK
    back = lambda j: pairs - 1 - j
    own = lambda j, core: (0, 2 * back(j) + (core[0] ^ (back(j) & 1)))
    slot = lambda j, core: (back(j), 0, 0)
    across = lambda j, core: (0, back(j))
    return pl.pallas_call(
        retrace_kernel,
        name="retrace",
        grid_spec=pltpu.PrefetchScalarGridSpec(
            num_scalar_prefetch=1,
            grid=(pairs,),
            in_specs=[
                pl.BlockSpec((width, BLOCK), own),
                pl.BlockSpec((1, width, BLOCK), slot),
                pl.BlockSpec((1, width, BLOCK), slot),
                pl.BlockSpec((1, 8, BLOCK), slot),
                pl.BlockSpec((half, CHUNK), across),
                pl.BlockSpec((half, CHUNK), across),
                pl.BlockSpec(k.shape, lambda j, core: (0, 0, 0)),
                pl.BlockSpec(v.shape, lambda j, core: (0, 0, 0)),
                pl.BlockSpec(kt.shape, lambda j, core: (0, 0)),
            ],
            out_specs=pl.BlockSpec((3 * width, CHUNK), across),
            scratch_shapes=[
                pltpu.VMEM((heads, length, HEAD_DIM), F32),
                pltpu.VMEM((heads, length, HEAD_DIM), F32),
            ],
        ),
        out_shape=jax.ShapeDtypeStruct((3 * width, length), BF16),
        compiler_params=pltpu.CompilerParams(vmem_limit_bytes=VMEM_LIMIT),
    )(core, qt, grads, full, stats, cosine, sine, k, v, kt)


def head_split_device(
    block_in,
    earlier,
    cotangent,
    qkv_weight,
    out_weight,
    in_weight,
    down_weight,
    qk_bias,
    value_bias,
    out_bias,
    in_bias,
    down_bias,
    gain_one,
    shift_one,
    gain_two,
    shift_two,
    depth_weights,
):
    row_count, model_width = block_in.shape
    hidden_width = in_weight.shape[1]
    groups = lax.axis_size("shard")
    owners = groups // 2
    width = model_width // owners
    part = model_width // groups
    length = row_count * groups
    half = HEAD_DIM // 2
    member = lax.axis_index("shard")
    owner = member // 2
    core = member % 2

    tokens = lax.all_gather(block_in, "shard", axis=0, tiled=True)
    pieces = qkv_weight.astype(BF16).reshape(part, 3, owners, width)
    pieces = jnp.transpose(pieces, (2, 0, 1, 3)).reshape(owners, part, 3 * width)
    early = jnp.concatenate([qk_bias, value_bias, gain_one, shift_one]).astype(BF16)
    early = jnp.pad(early, (0, 3 * width - early.shape[0]))
    early = jnp.broadcast_to(early, (owners, 1, 3 * width))
    packet = jnp.concatenate([pieces, early], axis=1)
    packet = jnp.broadcast_to(packet[:, None], (owners, 2) + packet.shape[1:])
    packet = packet.reshape(groups, part + 1, 3 * width)
    packet = lax.all_to_all(packet, "shard", 0, 0)
    w_own = packet[:, :part].reshape(model_width, 3 * width)
    early = packet[:, part].astype(F32)
    b_qk = early[:, : 2 * part].reshape(2 * model_width)
    b_value = early[:, 2 * part : 3 * part].reshape(model_width)
    g_one = early[:, 3 * part : 4 * part].reshape(1, model_width)
    s_one = early[:, 4 * part : 5 * part].reshape(1, model_width)
    b_joint = jnp.concatenate([b_qk, b_value]).reshape(3, owners, width)
    b_own = lax.dynamic_index_in_dim(b_joint, owner, 1, keepdims=False).reshape(3 * width, 1)

    freqs = 10000.0 ** (-jnp.arange(half, dtype=F32) / half)
    angles = freqs[:, None] * jnp.arange(length, dtype=jnp.int32).astype(F32)[None, :]
    cosine = jnp.cos(angles)
    sine = jnp.sin(angles)
    core_index = core.astype(jnp.int32).reshape(1)

    normed_all, qt, kt, vt, k, v = project(
        tokens, jnp.transpose(w_own), b_own, g_one, s_one, cosine, sine
    )
    mixed_own, attended, stats = attend(core_index, qt, k, vt)

    late = jnp.concatenate([out_bias, in_bias, down_bias, gain_two, shift_two]).astype(BF16)
    late = late.reshape(-1, model_width)
    late_rows = late.shape[0]
    gathered = lax.all_gather(
        jnp.concatenate([out_weight.astype(BF16), late], axis=0), "shard", axis=0
    )
    w_out = gathered[:, :part].reshape(model_width, model_width)
    late = gathered[:, part:].reshape(groups, late_rows * model_width).astype(F32)
    hidden_part = hidden_width // groups
    b_out = late[:, :part].reshape(model_width)
    b_in = late[:, part : part + hidden_part].reshape(hidden_width)
    b_down = late[:, part + hidden_part : 2 * part + hidden_part].reshape(model_width)
    g_two = late[:, 2 * part + hidden_part : 3 * part + hidden_part].reshape(model_width)
    s_two = late[:, 3 * part + hidden_part :].reshape(model_width)
    w_in = lax.all_gather(in_weight.astype(BF16), "shard", axis=0, tiled=True)
    w_down = lax.all_gather(down_weight.astype(BF16), "shard", axis=0, tiled=True)

    mixed_two = lax.all_to_all(mixed_own, "shard", 0, 0).reshape(owners, 2, width, BLOCK)
    first = lax.dynamic_index_in_dim(mixed_two, core, 1, keepdims=False)
    second = lax.dynamic_index_in_dim(mixed_two, 1 - core, 1, keepdims=False)
    mixed_t = jnp.concatenate(
        [first.reshape(model_width, BLOCK), second.reshape(model_width, BLOCK)], axis=1
    )

    inputs = block_in.astype(F32)
    branch = contract(mixed_t, w_out, 0, 0) + b_out
    middle = inputs + branch
    normed_two, norm_two_back = jax.vjp(layer_norm, middle, g_two, s_two)
    normed_two_low = normed_two.astype(BF16)
    hidden = contract(normed_two_low, w_in, 1, 0) + b_in
    active_full, gelu_back = jax.vjp(partial(jax.nn.gelu, approximate=True), hidden)
    active = active_full.astype(BF16)
    result = middle + contract(active, w_down, 1, 0) + b_down
    stacked = earlier.astype(F32)
    layer_out = depth_weights[4] * result
    for level in range(4):
        layer_out = layer_out + depth_weights[level] * stacked[level]
    grad_earlier = depth_weights[:4][:, None, None] * cotangent[None]
    local_depth = jnp.concatenate(
        [jnp.sum(stacked * cotangent[None], axis=(1, 2)), jnp.sum(result * cotangent)[None]]
    )
    grad_result = depth_weights[4] * cotangent
    down_grad = grad_result.astype(BF16)
    grad_down_w = contract(active, down_grad, 0, 0)
    grad_down_b = jnp.sum(down_grad.astype(F32), axis=0)
    grad_active = contract(down_grad, w_down, 1, 1)
    grad_hidden = gelu_back(grad_active)[0].astype(BF16)
    grad_in_w = contract(normed_two_low, grad_hidden, 0, 0)
    grad_in_b = jnp.sum(grad_hidden.astype(F32), axis=0)
    grad_normed_two = contract(grad_hidden, w_in, 1, 1)
    grad_mid_norm, grad_gain_two, grad_shift_two = norm_two_back(grad_normed_two)
    grad_middle = grad_result + grad_mid_norm
    branch_grad = grad_middle.astype(BF16)
    grad_out_w = contract(mixed_t, branch_grad, 1, 0)
    grad_out_b = jnp.sum(branch_grad.astype(F32), axis=0)
    grad_mixed_t = contract(w_out, branch_grad, 1, 1).astype(BF16)

    grad_mixed_t = grad_mixed_t.reshape(owners, width, 2, BLOCK)
    first = lax.dynamic_index_in_dim(grad_mixed_t, core, 2, keepdims=False)
    second = lax.dynamic_index_in_dim(grad_mixed_t, 1 - core, 2, keepdims=False)
    grad_own = jnp.stack([first, second], axis=1).reshape(groups, width, BLOCK)
    grad_own = lax.all_to_all(grad_own, "shard", 0, 0)

    joint_t = retrace(core_index, qt, grad_own, attended, stats, cosine, sine, k, v, kt)
    grad_normed = contract(joint_t, w_own, 0, 1).astype(BF16)
    grad_normed = lax.psum_scatter(
        grad_normed, "shard", scatter_dimension=0, tiled=True
    ).astype(F32)
    grad_qkv = contract(normed_all, joint_t, 0, 1).astype(BF16).reshape(groups, part, 3 * width)
    grad_qkv = lax.all_to_all(grad_qkv, "shard", 0, 0).astype(F32)
    grad_qkv = jnp.sum(grad_qkv.reshape(owners, 2, part, 3, width), axis=1)
    grad_qkv = jnp.transpose(grad_qkv, (1, 2, 0, 3)).reshape(part, 3 * model_width)
    joint_sums = jnp.sum(joint_t.astype(F32), axis=1).reshape(3, width)

    _, norm_back = jax.vjp(layer_norm, inputs, g_one[0], s_one[0])
    grad_in_norm, grad_gain_one, grad_shift_one = norm_back(grad_normed)
    grad_block = grad_middle + grad_in_norm

    spread_sums = lax.dynamic_update_slice(
        jnp.zeros((3, model_width), F32), joint_sums, (0, owner * width)
    ).reshape(3 * model_width)
    sizes = (2 * part, part, part, hidden_part, part, part, part, part, part)
    small = jnp.concatenate(
        [
            spread_sums,
            grad_out_b,
            grad_in_b,
            grad_down_b,
            grad_gain_one,
            grad_shift_one,
            grad_gain_two,
            grad_shift_two,
            local_depth,
        ]
    )
    small = lax.psum(small, ("rep", "shard"))
    small_outs = []
    start = 0
    for size in sizes:
        small_outs.append(lax.dynamic_slice_in_dim(small, start + member * size, size, 0))
        start += size * groups
    grad_depth = small[start:]

    sums = [
        lax.psum_scatter(grad.astype(BF16), "shard", scatter_dimension=0, tiled=True)
        for grad in (grad_out_w, grad_in_w, grad_down_w)
    ]
    sums = [
        lax.psum(grad, "rep").astype(F32) for grad in [grad_qkv.astype(BF16)] + sums
    ]
    return (layer_out, grad_block, grad_earlier, *sums, *small_outs, grad_depth)


def per_device(*args):
    block_in = args[0]
    row_count, model_width = block_in.shape
    groups = lax.axis_size("shard")
    head_count = model_width // HEAD_DIM
    late_size = (4 * model_width + args[5].shape[1]) // groups
    if (
        groups % 2 == 0
        and row_count == CHUNK
        and head_count % (groups // 2) == 0
        and head_count // (groups // 2) <= 8
        and late_size % model_width == 0
    ):
        return head_split_device(*args)
    return generic_device(*args)


def solution(mesh):
    placed = (
        P(("rep", "shard"), None),
        P(None, ("rep", "shard"), None),
        P(("rep", "shard"), None),
        P("shard", None),
        P("shard", None),
        P("shard", None),
        P("shard", None),
        P("shard"),
        P("shard"),
        P("shard"),
        P("shard"),
        P("shard"),
        P("shard"),
        P("shard"),
        P("shard"),
        P("shard"),
        P(),
    )
    return jax.shard_map(
        per_device,
        mesh=mesh,
        in_specs=placed,
        out_specs=(
            P(("rep", "shard"), None),
            P(("rep", "shard"), None),
            P(None, ("rep", "shard"), None),
            P("shard", None),
            P("shard", None),
            P("shard", None),
            P("shard", None),
            P("shard"),
            P("shard"),
            P("shard"),
            P("shard"),
            P("shard"),
            P("shard"),
            P("shard"),
            P("shard"),
            P("shard"),
            P(),
        ),
        check_vma=False,
    )
```

```python
from functools import partial
import math

import jax
import jax.numpy as jnp
from jax import lax
from jax.experimental import pallas as pl
from jax.experimental.pallas import tpu as pltpu
from jax.sharding import PartitionSpec as P

HEAD_DIM = 64
BLOCK = 256


NEG = -1e30
EPSILON = 1e-05


def layer_norm(inputs, gain, shift):
    center = inputs - jnp.mean(inputs, axis=-1, keepdims=True)
    spread = jnp.mean(center * center, axis=-1, keepdims=True)
    return center * lax.rsqrt(spread + EPSILON) * gain + shift


def rotate(inputs, positions):
    row_count = inputs.shape[0]
    split = inputs.reshape(row_count, -1, HEAD_DIM)
    half_dim = HEAD_DIM // 2
    freqs = 10000.0 ** (-jnp.arange(half_dim, dtype=jnp.float32) / half_dim)
    angles = positions.astype(jnp.float32)[:, None] * freqs[None, :]
    cosine = jnp.cos(angles)[:, None, :]
    sine = jnp.sin(angles)[:, None, :]
    former = split[..., :half_dim]
    latter = split[..., half_dim:]
    turned = jnp.concatenate(
        [former * cosine - latter * sine, former * sine + latter * cosine], axis=-1
    )
    return turned.reshape(row_count, -1)


def generic_device(
    block_in,
    earlier,
    cotangent,
    qkv_weight,
    out_weight,
    in_weight,
    down_weight,
    qk_bias,
    value_bias,
    out_bias,
    in_bias,
    down_bias,
    gain_one,
    shift_one,
    gain_two,
    shift_two,
    depth_weights,
):
    bf16 = jnp.bfloat16
    f32 = jnp.float32
    w_qkv, w_out, w_in, w_down, b_qk, b_value, b_out, b_in, b_down, g_one, s_one, g_two, s_two = (
        lax.all_gather(qkv_weight.astype(bf16), "shard", axis=0, tiled=True),
        lax.all_gather(out_weight.astype(bf16), "shard", axis=0, tiled=True),
        lax.all_gather(in_weight.astype(bf16), "shard", axis=0, tiled=True),
        lax.all_gather(down_weight.astype(bf16), "shard", axis=0, tiled=True),
        lax.all_gather(qk_bias.astype(bf16), "shard", axis=0, tiled=True),
        lax.all_gather(value_bias.astype(bf16), "shard", axis=0, tiled=True),
        lax.all_gather(out_bias.astype(bf16), "shard", axis=0, tiled=True),
        lax.all_gather(in_bias.astype(bf16), "shard", axis=0, tiled=True),
        lax.all_gather(down_bias.astype(bf16), "shard", axis=0, tiled=True),
        lax.all_gather(gain_one.astype(bf16), "shard", axis=0, tiled=True),
        lax.all_gather(shift_one.astype(bf16), "shard", axis=0, tiled=True),
        lax.all_gather(gain_two.astype(bf16), "shard", axis=0, tiled=True),
        lax.all_gather(shift_two.astype(bf16), "shard", axis=0, tiled=True),
    )
    row_count, model_width = block_in.shape
    head_count = model_width // HEAD_DIM
    groups = lax.axis_size("shard")
    length = row_count * groups
    window = min(512, length)
    member = lax.axis_index("shard")
    first_row = member * row_count
    last_end = first_row + row_count
    positions = first_row + jnp.arange(row_count, dtype=jnp.int32)
    query_block = positions // BLOCK
    score_scale = HEAD_DIM ** (-0.5)
    needed = (last_end + window - 1) // window
    inputs = block_in.astype(f32)
    normed, norm_back = jax.vjp(layer_norm, inputs, g_one.astype(f32), s_one.astype(f32))
    normed_low = normed.astype(bf16)
    joint_bias = jnp.concatenate([b_qk.astype(f32), b_value.astype(f32)])
    projected = jnp.dot(normed_low, w_qkv, preferred_element_type=f32) + joint_bias
    queries = rotate(projected[:, :model_width], positions).astype(bf16)
    key_rows = rotate(projected[:, model_width : 2 * model_width], positions).astype(bf16)
    values = projected[:, 2 * model_width :].astype(bf16)
    query_heads = queries.reshape(row_count, head_count, HEAD_DIM)

    def masked_scores(key_piece, key_start):
        piece_rows = key_piece.shape[0]
        key_heads = key_piece.reshape(piece_rows, head_count, HEAD_DIM)
        scores = (
            jnp.einsum("qhd,khd->hqk", query_heads, key_heads, preferred_element_type=f32)
            * score_scale
        )
        key_block = (key_start + jnp.arange(piece_rows, dtype=jnp.int32)) // BLOCK
        allowed = key_block[None, :] <= query_block[:, None]
        return (scores, allowed)

    def absorb(running, key_piece, value_piece, key_start):
        highest, denominator, summed = running
        scores, allowed = masked_scores(key_piece, key_start)
        scores = jnp.where(allowed[None], scores, NEG)
        new_high = jnp.maximum(highest, jnp.max(scores, axis=-1))
        rescale = jnp.exp(highest - new_high)
        weights = jnp.where(allowed[None], jnp.exp(scores - new_high[..., None]), 0.0)
        value_heads = value_piece.reshape(-1, head_count, HEAD_DIM)
        summed = summed * rescale[..., None] + jnp.einsum(
            "hqk,khd->hqd", weights.astype(bf16), value_heads, preferred_element_type=f32
        )
        return (new_high, denominator * rescale + jnp.sum(weights, axis=-1), summed)

    start_state = (
        jnp.full((head_count, row_count), NEG, f32),
        jnp.zeros((head_count, row_count), f32),
        jnp.zeros((head_count, row_count, HEAD_DIM), f32),
    )
    key_piece = lax.all_gather(key_rows, "shard", axis=0, tiled=True)
    value_piece = lax.all_gather(values, "shard", axis=0, tiled=True)
    piece_rows = key_piece.shape[0]
    sub_rows = math.gcd(piece_rows, window)
    usable = jnp.clip((last_end + sub_rows - 1) // sub_rows, 0, piece_rows // sub_rows)

    def advance(block_step, state_inner):
        offset = block_step * sub_rows
        return absorb(
            state_inner,
            lax.dynamic_slice_in_dim(key_piece, offset, sub_rows, 0),
            lax.dynamic_slice_in_dim(value_piece, offset, sub_rows, 0),
            offset,
        )

    highest, denominator, summed = lax.fori_loop(0, usable, advance, start_state)
    attended = summed / denominator[..., None]
    log_norm = highest + jnp.log(denominator)
    mixed = jnp.transpose(attended, (1, 0, 2)).reshape(row_count, model_width).astype(bf16)
    branch = jnp.dot(mixed, w_out, preferred_element_type=f32) + b_out.astype(f32)
    middle = inputs + branch
    normed_two, norm_two_back = jax.vjp(layer_norm, middle, g_two.astype(f32), s_two.astype(f32))
    normed_two_low = normed_two.astype(bf16)
    hidden = jnp.dot(normed_two_low, w_in, preferred_element_type=f32) + b_in.astype(f32)
    active_full, gelu_back = jax.vjp(partial(jax.nn.gelu, approximate=True), hidden)
    active = active_full.astype(bf16)
    result = middle + jnp.dot(active, w_down, preferred_element_type=f32) + b_down.astype(f32)
    stacked = earlier.astype(f32)
    layer_out = depth_weights[4] * result
    for level in range(4):
        layer_out = layer_out + depth_weights[level] * stacked[level]
    grad_earlier = depth_weights[:4][:, None, None] * cotangent[None]
    local_depth = jnp.concatenate(
        [jnp.sum(stacked * cotangent[None], axis=(1, 2)), jnp.sum(result * cotangent)[None]]
    )
    grad_depth = lax.psum(local_depth, ("rep", "shard"))
    grad_result = depth_weights[4] * cotangent
    down_grad = grad_result.astype(bf16)
    grad_down_w = jnp.einsum("tf,td->fd", active, down_grad, preferred_element_type=f32)
    grad_down_b = jnp.sum(down_grad.astype(f32), axis=0)
    grad_active = jnp.einsum("td,fd->tf", down_grad, w_down, preferred_element_type=f32)
    grad_hidden = gelu_back(grad_active)[0].astype(bf16)
    grad_in_w = jnp.einsum("td,tf->df", normed_two_low, grad_hidden, preferred_element_type=f32)
    grad_in_b = jnp.sum(grad_hidden.astype(f32), axis=0)
    grad_normed_two = jnp.einsum("tf,df->td", grad_hidden, w_in, preferred_element_type=f32)
    grad_mid_norm, grad_gain_two, grad_shift_two = norm_two_back(grad_normed_two)
    grad_middle = grad_result + grad_mid_norm
    branch_grad = grad_middle.astype(bf16)
    grad_out_w = jnp.einsum("td,te->de", mixed, branch_grad, preferred_element_type=f32)
    grad_out_b = jnp.sum(branch_grad.astype(f32), axis=0)
    grad_mixed = jnp.einsum("te,de->td", branch_grad, w_out, preferred_element_type=f32).astype(
        bf16
    )
    key_all, value_all = (
        lax.all_gather(key_rows, "shard", axis=0, tiled=True),
        lax.all_gather(values, "shard", axis=0, tiled=True),
    )
    grad_heads = grad_mixed.reshape(row_count, head_count, HEAD_DIM)
    delta = jnp.einsum("qhd,hqd->hq", grad_heads.astype(f32), attended)

    def score_grads(key_piece, value_piece, offset, piece_rows):
        scores, allowed = masked_scores(key_piece, offset)
        probs = jnp.where(allowed[None], jnp.exp(scores - log_norm[..., None]), 0.0)
        value_heads = value_piece.reshape(piece_rows, head_count, HEAD_DIM)
        grad_probs = jnp.einsum("qhd,khd->hqk", grad_heads, value_heads, preferred_element_type=f32)
        grad_scores = (probs * (grad_probs - delta[..., None])).astype(bf16)
        return (probs, grad_scores)

    def retrace(block_step, running):
        grad_query, grad_keys, grad_values = running
        offset = block_step * window
        key_piece = lax.dynamic_slice_in_dim(key_all, offset, window, 0)
        value_piece = lax.dynamic_slice_in_dim(value_all, offset, window, 0)
        probs, grad_scores = score_grads(key_piece, value_piece, offset, window)
        key_heads = key_piece.reshape(window, head_count, HEAD_DIM)
        grad_query = grad_query + jnp.einsum(
            "hqk,khd->qhd", grad_scores, key_heads, preferred_element_type=f32
        )
        piece_keys = (
            jnp.einsum("hqk,qhd->khd", grad_scores, query_heads, preferred_element_type=f32)
            * score_scale
        )
        piece_values = jnp.einsum(
            "hqk,qhd->khd", probs.astype(bf16), grad_heads, preferred_element_type=f32
        )
        grad_keys = lax.dynamic_update_slice_in_dim(
            grad_keys, piece_keys.reshape(window, model_width), offset, 0
        )
        grad_values = lax.dynamic_update_slice_in_dim(
            grad_values, piece_values.reshape(window, model_width), offset, 0
        )
        return (grad_query, grad_keys, grad_values)

    start_back = (
        jnp.zeros((row_count, head_count, HEAD_DIM), f32),
        jnp.zeros((length, model_width), f32),
        jnp.zeros((length, model_width), f32),
    )
    grad_query, grad_keys, grad_values = lax.fori_loop(0, needed, retrace, start_back)
    own_keys, own_values = (
        lax.psum_scatter(
            grad_keys.astype(jnp.bfloat16), "shard", scatter_dimension=0, tiled=True
        ).astype(jnp.float32),
        lax.psum_scatter(
            grad_values.astype(jnp.bfloat16), "shard", scatter_dimension=0, tiled=True
        ).astype(jnp.float32),
    )
    grad_q_turned = rotate(grad_query.reshape(row_count, model_width) * score_scale, -positions)
    grad_k_turned = rotate(own_keys, -positions)
    grad_joint = jnp.concatenate([grad_q_turned, grad_k_turned, own_values], axis=1).astype(bf16)
    grad_qkv_w = jnp.einsum("td,tf->df", normed_low, grad_joint, preferred_element_type=f32)
    joint_sums = jnp.sum(grad_joint.astype(f32), axis=0)
    grad_qk_b = joint_sums[: 2 * model_width]
    grad_value_b = joint_sums[2 * model_width :]
    grad_normed = jnp.einsum("tf,df->td", grad_joint, w_qkv, preferred_element_type=f32)
    grad_in_norm, grad_gain_one, grad_shift_one = norm_back(grad_normed)
    grad_block = grad_middle + grad_in_norm
    (
        own_qkv_w,
        own_out_w,
        own_in_w,
        own_down_w,
        own_qk_b,
        own_value_b,
        own_out_b,
        own_in_b,
        own_down_b,
        own_gain_one,
        own_shift_one,
        own_gain_two,
        own_shift_two,
    ) = (
        lax.psum_scatter(
            grad_qkv_w.astype(jnp.bfloat16), "shard", scatter_dimension=0, tiled=True
        ).astype(jnp.float32),
        lax.psum_scatter(
            grad_out_w.astype(jnp.bfloat16), "shard", scatter_dimension=0, tiled=True
        ).astype(jnp.float32),
        lax.psum_scatter(
            grad_in_w.astype(jnp.bfloat16), "shard", scatter_dimension=0, tiled=True
        ).astype(jnp.float32),
        lax.psum_scatter(
            grad_down_w.astype(jnp.bfloat16), "shard", scatter_dimension=0, tiled=True
        ).astype(jnp.float32),
        lax.psum_scatter(
            grad_qk_b.astype(jnp.bfloat16), "shard", scatter_dimension=0, tiled=True
        ).astype(jnp.float32),
        lax.psum_scatter(
            grad_value_b.astype(jnp.bfloat16), "shard", scatter_dimension=0, tiled=True
        ).astype(jnp.float32),
        lax.psum_scatter(
            grad_out_b.astype(jnp.bfloat16), "shard", scatter_dimension=0, tiled=True
        ).astype(jnp.float32),
        lax.psum_scatter(
            grad_in_b.astype(jnp.bfloat16), "shard", scatter_dimension=0, tiled=True
        ).astype(jnp.float32),
        lax.psum_scatter(
            grad_down_b.astype(jnp.bfloat16), "shard", scatter_dimension=0, tiled=True
        ).astype(jnp.float32),
        lax.psum_scatter(
            grad_gain_one.astype(jnp.bfloat16), "shard", scatter_dimension=0, tiled=True
        ).astype(jnp.float32),
        lax.psum_scatter(
            grad_shift_one.astype(jnp.bfloat16), "shard", scatter_dimension=0, tiled=True
        ).astype(jnp.float32),
        lax.psum_scatter(
            grad_gain_two.astype(jnp.bfloat16), "shard", scatter_dimension=0, tiled=True
        ).astype(jnp.float32),
        lax.psum_scatter(
            grad_shift_two.astype(jnp.bfloat16), "shard", scatter_dimension=0, tiled=True
        ).astype(jnp.float32),
    )
    (
        sum_qkv_w,
        sum_out_w,
        sum_in_w,
        sum_down_w,
        sum_qk_b,
        sum_value_b,
        sum_out_b,
        sum_in_b,
        sum_down_b,
        sum_gain_one,
        sum_shift_one,
        sum_gain_two,
        sum_shift_two,
    ) = (
        lax.psum(own_qkv_w.astype(jnp.bfloat16), "rep").astype(jnp.float32),
        lax.psum(own_out_w.astype(jnp.bfloat16), "rep").astype(jnp.float32),
        lax.psum(own_in_w.astype(jnp.bfloat16), "rep").astype(jnp.float32),
        lax.psum(own_down_w.astype(jnp.bfloat16), "rep").astype(jnp.float32),
        lax.psum(own_qk_b.astype(jnp.bfloat16), "rep").astype(jnp.float32),
        lax.psum(own_value_b.astype(jnp.bfloat16), "rep").astype(jnp.float32),
        lax.psum(own_out_b.astype(jnp.bfloat16), "rep").astype(jnp.float32),
        lax.psum(own_in_b.astype(jnp.bfloat16), "rep").astype(jnp.float32),
        lax.psum(own_down_b.astype(jnp.bfloat16), "rep").astype(jnp.float32),
        lax.psum(own_gain_one.astype(jnp.bfloat16), "rep").astype(jnp.float32),
        lax.psum(own_shift_one.astype(jnp.bfloat16), "rep").astype(jnp.float32),
        lax.psum(own_gain_two.astype(jnp.bfloat16), "rep").astype(jnp.float32),
        lax.psum(own_shift_two.astype(jnp.bfloat16), "rep").astype(jnp.float32),
    )
    return (
        layer_out,
        grad_block,
        grad_earlier,
        sum_qkv_w,
        sum_out_w,
        sum_in_w,
        sum_down_w,
        sum_qk_b,
        sum_value_b,
        sum_out_b,
        sum_in_b,
        sum_down_b,
        sum_gain_one,
        sum_shift_one,
        sum_gain_two,
        sum_shift_two,
        grad_depth,
    )


F32 = jnp.float32
BF16 = jnp.bfloat16
CHUNK = 2 * BLOCK
VMEM_LIMIT = 56 * 1024 * 1024


def cost(flops, moved, exps=0):
    return pl.CostEstimate(flops=flops, bytes_accessed=moved, transcendentals=exps)


def contract(left, right, left_dim, right_dim):
    return lax.dot_general(
        left, right, (((left_dim,), (right_dim,)), ((), ())), preferred_element_type=F32
    )


def qkv_kernel(
    x_ref, weight_ref, bias_ref, gain_ref, shift_ref, cos_ref, sin_ref,
    plain_ref, qt_ref, kt_ref, vt_ref, k_ref, v_ref,
):
    x = x_ref[...].astype(F32)
    center = x - jnp.mean(x, axis=-1, keepdims=True)
    spread = jnp.mean(center * center, axis=-1, keepdims=True)
    plain = center * lax.rsqrt(spread + EPSILON)
    plain_ref[...] = plain.astype(BF16)
    low = (plain * gain_ref[...] + shift_ref[...]).astype(BF16)
    width = qt_ref.shape[0]
    half = HEAD_DIM // 2
    joint = contract(weight_ref[...], low, 1, 1) + bias_ref[...]
    cosine = cos_ref[...]
    sine = sin_ref[...]
    for head in range(width // HEAD_DIM):
        base = head * HEAD_DIM
        for part in range(2):
            start = part * width + base
            former = joint[start : start + half]
            latter = joint[start + half : start + HEAD_DIM]
            turned = jnp.concatenate(
                [former * cosine - latter * sine, former * sine + latter * cosine], axis=0
            )
            if part == 0:
                qt_ref[base : base + HEAD_DIM, :] = (turned * HEAD_DIM ** (-0.5)).astype(BF16)
            else:
                kt_ref[base : base + HEAD_DIM, :] = turned.astype(BF16)
                k_ref[head] = jnp.transpose(turned).astype(BF16)
        start = 2 * width + base
        value = joint[start : start + HEAD_DIM]
        vt_ref[base : base + HEAD_DIM, :] = value.astype(BF16)
        v_ref[head] = jnp.transpose(value).astype(BF16)


def project(tokens, weight_t, bias, gain, shift, cosine, sine):
    length, model_width = tokens.shape
    columns = weight_t.shape[0]
    width = columns // 3
    heads = width // HEAD_DIM
    half = HEAD_DIM // 2
    tile = CHUNK
    fixed = lambda i: (0, 0)
    across = lambda i: (0, i)
    return pl.pallas_call(
        qkv_kernel,
        name="project",
        cost_estimate=cost(2 * length * model_width * columns, 12 * length * model_width),
        grid=(length // tile,),
        in_specs=[
            pl.BlockSpec((tile, model_width), lambda i: (i, 0)),
            pl.BlockSpec((columns, model_width), fixed),
            pl.BlockSpec((columns, 1), fixed),
            pl.BlockSpec((1, model_width), fixed),
            pl.BlockSpec((1, model_width), fixed),
            pl.BlockSpec((half, tile), across),
            pl.BlockSpec((half, tile), across),
        ],
        out_specs=[
            pl.BlockSpec((tile, model_width), lambda i: (i, 0)),
            pl.BlockSpec((width, tile), across),
            pl.BlockSpec((width, tile), across),
            pl.BlockSpec((width, tile), across),
            pl.BlockSpec((heads, tile, HEAD_DIM), lambda i: (0, i, 0)),
            pl.BlockSpec((heads, tile, HEAD_DIM), lambda i: (0, i, 0)),
        ],
        out_shape=[
            jax.ShapeDtypeStruct((length, model_width), BF16),
            jax.ShapeDtypeStruct((width, length), BF16),
            jax.ShapeDtypeStruct((width, length), BF16),
            jax.ShapeDtypeStruct((width, length), BF16),
            jax.ShapeDtypeStruct((heads, length, HEAD_DIM), BF16),
            jax.ShapeDtypeStruct((heads, length, HEAD_DIM), BF16),
        ],
        compiler_params=pltpu.CompilerParams(vmem_limit_bytes=VMEM_LIMIT),
    )(tokens, weight_t, bias, gain, shift, cosine, sine)


def average_kernel(weights_ref, earlier_ref, cotangent_ref, grad_ref, mix_ref, sums_ref):
    @pl.when(pl.program_id(0) == 0)
    def _():
        sums_ref[...] = jnp.zeros_like(sums_ref)

    cotangent = cotangent_ref[...]
    rows, columns = cotangent.shape
    mix = jnp.zeros_like(cotangent)
    for level in range(earlier_ref.shape[0]):
        value = earlier_ref[level].astype(F32)
        weight = weights_ref[level]
        mix = mix + weight * value
        grad_ref[level] = weight * cotangent
        sums_ref[level] += jnp.sum((value * cotangent).reshape(rows // 8, 8, columns), axis=0)
    mix_ref[...] = mix


def average(depth_weights, earlier, cotangent):
    levels, row_count, model_width = earlier.shape
    tile = row_count // 4
    return pl.pallas_call(
        average_kernel,
        name="average",
        cost_estimate=cost(6 * earlier.size, 6 * earlier.size + 8 * cotangent.size),
        grid_spec=pltpu.PrefetchScalarGridSpec(
            num_scalar_prefetch=1,
            grid=(4,),
            in_specs=[
                pl.BlockSpec((levels, tile, model_width), lambda i, w: (0, i, 0)),
                pl.BlockSpec((tile, model_width), lambda i, w: (i, 0)),
            ],
            out_specs=[
                pl.BlockSpec((levels, tile, model_width), lambda i, w: (0, i, 0)),
                pl.BlockSpec((tile, model_width), lambda i, w: (i, 0)),
                pl.BlockSpec((levels, 8, model_width), lambda i, w: (0, 0, 0)),
            ],
        ),
        out_shape=[
            jax.ShapeDtypeStruct(earlier.shape, F32),
            jax.ShapeDtypeStruct(cotangent.shape, F32),
            jax.ShapeDtypeStruct((levels, 8, model_width), F32),
        ],
        compiler_params=pltpu.CompilerParams(vmem_limit_bytes=VMEM_LIMIT),
    )(depth_weights, earlier, cotangent)


def last_mask(odd):
    row = lax.broadcasted_iota(jnp.int32, (CHUNK, BLOCK), 0)
    return row < BLOCK * (1 + odd)


def attend_kernel(first, core_ref, qt_ref, k_ref, vt_ref, low_ref, full_ref, stat_ref):
    pair = first + pl.program_id(0)
    odd = core_ref[0] ^ (pair & 1)
    width = qt_ref.shape[0]
    heads = width // HEAD_DIM
    queries = [qt_ref[h * HEAD_DIM : (h + 1) * HEAD_DIM, :] for h in range(heads)]

    def absorb(step, state, masked):
        offset = pl.multiple_of(step * CHUNK, CHUNK)
        fresh = []
        for h in range(heads):
            highest, total, summed = state[h]
            scores = contract(k_ref[h, pl.ds(offset, CHUNK), :], queries[h], 1, 0)
            if masked:
                scores = jnp.where(last_mask(odd), scores, NEG)
            new_high = jnp.maximum(highest, jnp.max(scores, axis=0, keepdims=True))
            rescale = jnp.exp(highest - new_high)
            weights = jnp.exp(scores - new_high)
            total = total * rescale + jnp.sum(weights, axis=0, keepdims=True)
            values = vt_ref[h * HEAD_DIM : (h + 1) * HEAD_DIM, pl.ds(offset, CHUNK)]
            summed = summed * rescale + contract(values, weights.astype(BF16), 1, 0)
            fresh.append((new_high, total, summed))
        return fresh

    state = [
        (
            jnp.full((1, BLOCK), NEG, F32),
            jnp.zeros((1, BLOCK), F32),
            jnp.zeros((HEAD_DIM, BLOCK), F32),
        )
        for _ in range(heads)
    ]
    state = lax.fori_loop(0, pair, lambda i, s: absorb(i, s, False), state)
    state = absorb(pair, state, True)
    for h in range(heads):
        highest, total, summed = state[h]
        attended = summed / total
        full_ref[0, h * HEAD_DIM : (h + 1) * HEAD_DIM, :] = attended
        low_ref[0, h * HEAD_DIM : (h + 1) * HEAD_DIM, :] = attended.astype(BF16)
        stat_ref[0, h : h + 1, :] = highest + jnp.log(total)


def attend(core, qt, k, vt, first, pairs):
    width = qt.shape[0]
    own = lambda j, core: (0, 2 * (first + j) + (core[0] ^ ((first + j) & 1)))
    slot = lambda j, core: (j, 0, 0)
    return pl.pallas_call(
        partial(attend_kernel, first),
        name="attend",
        cost_estimate=cost(
            2 * 2 * BLOCK * BLOCK * BLOCK * 2 * sum(range(first + 1, first + pairs + 1)) * (width // HEAD_DIM),
            4 * k.size + 8 * pairs * width * BLOCK,
            CHUNK * BLOCK * sum(range(first + 1, first + pairs + 1)) * (width // HEAD_DIM),
        ),
        grid_spec=pltpu.PrefetchScalarGridSpec(
            num_scalar_prefetch=1,
            grid=(pairs,),
            in_specs=[
                pl.BlockSpec((width, BLOCK), own),
                pl.BlockSpec(k.shape, lambda j, core: (0, 0, 0)),
                pl.BlockSpec(vt.shape, lambda j, core: (0, 0)),
            ],
            out_specs=[
                pl.BlockSpec((1, width, BLOCK), slot),
                pl.BlockSpec((1, width, BLOCK), slot),
                pl.BlockSpec((1, 8, BLOCK), slot),
            ],
        ),
        out_shape=[
            jax.ShapeDtypeStruct((pairs, width, BLOCK), BF16),
            jax.ShapeDtypeStruct((pairs, width, BLOCK), F32),
            jax.ShapeDtypeStruct((pairs, 8, BLOCK), F32),
        ],
        compiler_params=pltpu.CompilerParams(vmem_limit_bytes=VMEM_LIMIT),
    )(core, qt, k, vt)


def retrace_kernel(
    core_ref, qt_ref, grad_ref, full_ref, stat_ref, cos_ref, sin_ref, k_ref, v_ref, kt_ref,
    joint_ref, dk_ref, dv_ref,
):
    step_id = pl.program_id(0)
    pair = pl.num_programs(0) - 1 - step_id
    odd = core_ref[0] ^ (pair & 1)
    width = qt_ref.shape[0]
    heads = width // HEAD_DIM
    half = HEAD_DIM // 2

    @pl.when(step_id == 0)
    def _():
        dk_ref[...] = jnp.zeros_like(dk_ref)
        dv_ref[...] = jnp.zeros_like(dv_ref)

    queries, grads, deltas, norms = [], [], [], []
    for h in range(heads):
        rows = slice(h * HEAD_DIM, (h + 1) * HEAD_DIM)
        queries.append(qt_ref[rows, :])
        grad = grad_ref[0, rows, :]
        grads.append(grad)
        deltas.append(jnp.sum(grad.astype(F32) * full_ref[0, rows, :], axis=0, keepdims=True))
        norms.append(stat_ref[0, h : h + 1, :])

    def absorb(step, state, masked):
        offset = pl.multiple_of(step * CHUNK, CHUNK)
        keys = pl.ds(offset, CHUNK)
        fresh = []
        for h in range(heads):
            scores = contract(k_ref[h, keys, :], queries[h], 1, 0)
            probs = jnp.exp(scores - norms[h])
            if masked:
                probs = jnp.where(last_mask(odd), probs, 0.0)
            grad_probs = contract(v_ref[h, keys, :], grads[h], 1, 0)
            grad_scores = (probs * (grad_probs - deltas[h])).astype(BF16)
            dv_ref[h, keys, :] += contract(probs.astype(BF16), grads[h], 1, 1)
            dk_ref[h, keys, :] += contract(grad_scores, queries[h], 1, 1)
            turned = kt_ref[h * HEAD_DIM : (h + 1) * HEAD_DIM, keys]
            fresh.append(state[h] + contract(turned, grad_scores, 1, 0))
        return fresh

    state = [jnp.zeros((HEAD_DIM, BLOCK), F32) for _ in range(heads)]
    state = lax.fori_loop(0, pair, lambda i, s: absorb(i, s, False), state)
    state = absorb(pair, state, True)
    offset = pl.multiple_of(pair * CHUNK, CHUNK)
    cosine = cos_ref[...]
    sine = sin_ref[...]
    column = lax.broadcasted_iota(jnp.int32, (HEAD_DIM, CHUNK), 1) // BLOCK

    for h in range(heads):
        base = h * HEAD_DIM
        doubled = jnp.concatenate([state[h], state[h]], axis=1) * HEAD_DIM ** (-0.5)
        doubled = jnp.where(column == odd, doubled, 0.0)
        key_grad = jnp.transpose(dk_ref[h, pl.ds(offset, CHUNK), :])
        for part, value in ((0, doubled), (1, key_grad)):
            former = value[:half]
            latter = value[half:]
            turned = jnp.concatenate(
                [former * cosine + latter * sine, latter * cosine - former * sine], axis=0
            )
            start = part * width + base
            joint_ref[start : start + HEAD_DIM, :] = turned.astype(BF16)
        start = 2 * width + base
        joint_ref[start : start + HEAD_DIM, :] = jnp.transpose(
            dv_ref[h, pl.ds(offset, CHUNK), :]
        ).astype(BF16)


def retrace(core, qt, grads, full, stats, cosine, sine, k, v, kt):
    width, length = qt.shape
    heads = width // HEAD_DIM
    half = HEAD_DIM // 2
    pairs = length // CHUNK
    back = lambda j: pairs - 1 - j
    own = lambda j, core: (0, 2 * back(j) + (core[0] ^ (back(j) & 1)))
    slot = lambda j, core: (back(j), 0, 0)
    across = lambda j, core: (0, back(j))
    return pl.pallas_call(
        retrace_kernel,
        name="retrace",
        cost_estimate=cost(
            5 * 2 * BLOCK * BLOCK * BLOCK * 2 * sum(range(1, pairs + 1)) * heads,
            6 * k.size + 16 * pairs * width * BLOCK,
            CHUNK * BLOCK * sum(range(1, pairs + 1)) * heads,
        ),
        grid_spec=pltpu.PrefetchScalarGridSpec(
            num_scalar_prefetch=1,
            grid=(pairs,),
            in_specs=[
                pl.BlockSpec((width, BLOCK), own),
                pl.BlockSpec((1, width, BLOCK), slot),
                pl.BlockSpec((1, width, BLOCK), slot),
                pl.BlockSpec((1, 8, BLOCK), slot),
                pl.BlockSpec((half, CHUNK), across),
                pl.BlockSpec((half, CHUNK), across),
                pl.BlockSpec(k.shape, lambda j, core: (0, 0, 0)),
                pl.BlockSpec(v.shape, lambda j, core: (0, 0, 0)),
                pl.BlockSpec(kt.shape, lambda j, core: (0, 0)),
            ],
            out_specs=pl.BlockSpec((3 * width, CHUNK), across),
            scratch_shapes=[
                pltpu.VMEM((heads, length, HEAD_DIM), F32),
                pltpu.VMEM((heads, length, HEAD_DIM), F32),
            ],
        ),
        out_shape=jax.ShapeDtypeStruct((3 * width, length), BF16),
        compiler_params=pltpu.CompilerParams(vmem_limit_bytes=VMEM_LIMIT),
    )(core, qt, grads, full, stats, cosine, sine, k, v, kt)


def after(values, *earlier_values):
    values = tuple(values)
    return lax.optimization_barrier(values + tuple(earlier_values))[: len(values)]


def assemble_kernel(place_ref, *refs):
    down_ref, out_ref = refs[-2:]
    rep = place_ref[1]
    reps = (len(refs) - 2) // 2
    rows = out_ref.shape[1]
    for side in range(2):
        @pl.when(pl.program_id(0) == side)
        def _():
            for k in range(reps):
                piece = refs[side * reps + k]
                target = rep ^ k

                @pl.when(target < reps - 1)
                def _():
                    down_ref[0, pl.ds(pl.multiple_of(target * rows, rows), rows), :] = piece[0]

                @pl.when(target == reps - 1)
                def _():
                    out_ref[0] = piece[0]


def assemble(place, mine, twin):
    owners, rows, columns = mine[0].shape
    reps = len(mine)

    def held(side):
        def index(which, z, place):
            moving = (place[0] // 2 - z) % owners
            fixed = (place[0] // 2 - (owners - 1) * (1 - side)) % owners
            return (jnp.where(which == side, moving, fixed), 0, 0)

        return pl.BlockSpec((1, rows, columns), index)

    target = lambda which, z, place: (2 * z + (which ^ (place[0] % 2)), 0, 0)
    return pl.pallas_call(
        assemble_kernel,
        name="assemble",
        cost_estimate=cost(0, 4 * 2 * reps * owners * rows * columns),
        grid_spec=pltpu.PrefetchScalarGridSpec(
            num_scalar_prefetch=1,
            grid=(2, owners),
            in_specs=[held(0)] * reps + [held(1)] * reps,
            out_specs=[
                pl.BlockSpec((1, (reps - 1) * rows, columns), target),
                pl.BlockSpec((1, rows, columns), target),
            ],
        ),
        out_shape=[
            jax.ShapeDtypeStruct((2 * owners, (reps - 1) * rows, columns), BF16),
            jax.ShapeDtypeStruct((2 * owners, rows, columns), BF16),
        ],
        compiler_params=pltpu.CompilerParams(vmem_limit_bytes=VMEM_LIMIT),
    )(place, *mine, *twin)


def swap_core(value):
    groups = lax.axis_size("shard")
    return lax.ppermute(value, "shard", [(i, i ^ 1) for i in range(groups)])


def shift_owner(value, distance):
    groups = lax.axis_size("shard")
    step = 2 * distance
    return lax.ppermute(value, "shard", [(i, (i + step) % groups) for i in range(groups)])


def cross_rep(value, mask):
    return lax.ppermute(value, "rep", [(i, i ^ mask) for i in range(lax.axis_size("rep"))])


def pick(stacked, index, axis=0):
    return lax.dynamic_index_in_dim(stacked, index, axis, keepdims=False)


def add_low(*values):
    total = values[0].astype(F32)
    for value in values[1:]:
        total = total + value.astype(F32)
    return total.astype(BF16)


def fold_core(partial_sums, core):
    halves = partial_sums.reshape((-1, 2) + partial_sums.shape[1:])
    received = swap_core(pick(halves, 1 - core, 1))
    return add_low(pick(halves, core, 1), received)


def rep_parts(value):
    reps = lax.axis_size("rep")
    owners, rows, columns = value.shape
    return value.reshape(owners, reps, rows // reps, columns)


def send_rep(value):
    rep = lax.axis_index("rep")
    parts = rep_parts(value)
    return [cross_rep(pick(parts, rep ^ k, 1), k) for k in range(1, lax.axis_size("rep"))]


def join_rep(value, received):
    return add_low(pick(rep_parts(value), lax.axis_index("rep"), 1), *received)


def fold_rep(value):
    return join_rep(value, send_rep(value))


def spread_rep(value):
    reps = lax.axis_size("rep")
    rep = lax.axis_index("rep")
    pieces = jnp.stack([value] + [cross_rep(value, k) for k in range(1, reps)])
    return jnp.concatenate([pick(pieces, rep ^ k) for k in range(reps)], axis=0)


def exchange_owner(value, owner):
    owners = value.shape[0]
    received = [pick(value, owner)]
    for k in range(1, owners):
        received.append(shift_owner(pick(value, (owner + k) % owners), k))
    return received


def reduce_columns(partial_sums, owner, core):
    folded = fold_rep(fold_core(partial_sums, core))
    received = jnp.stack(exchange_owner(folded, owner))
    owners = received.shape[0]
    ordered = [pick(received, (owner - k) % owners) for k in range(owners)]
    columns = folded.shape[-1]
    whole = spread_rep(jnp.concatenate(ordered, axis=1))
    return whole.reshape(-1, owners, columns).astype(F32)


def reduce_small(value):
    for mask in range(2):
        value = value + cross_rep(value, 1 << mask)
    groups = lax.axis_size("shard")
    mask = 1
    while mask < groups:
        value = value + lax.ppermute(value, "shard", [(i, i ^ mask) for i in range(groups)])
        mask *= 2
    return value


def head_split_device(
    block_in,
    earlier,
    cotangent,
    qkv_weight,
    out_weight,
    in_weight,
    down_weight,
    qk_bias,
    value_bias,
    out_bias,
    in_bias,
    down_bias,
    gain_one,
    shift_one,
    gain_two,
    shift_two,
    depth_weights,
):
    row_count, model_width = block_in.shape
    hidden_width = in_weight.shape[1]
    groups = lax.axis_size("shard")
    owners = groups // 2
    width = model_width // owners
    part = model_width // groups
    length = row_count * groups
    half = HEAD_DIM // 2
    member = lax.axis_index("shard")
    owner = member // 2
    core = member % 2

    pieces = qkv_weight.astype(BF16).reshape(part, 3, owners, width)
    pieces = jnp.transpose(pieces, (2, 0, 1, 3)).reshape(owners, part, 3 * width)
    early = jnp.concatenate([qk_bias, value_bias, gain_one, shift_one]).astype(BF16)
    early = jnp.pad(early, (0, 8 * 3 * width - early.shape[0])).reshape(8, 3 * width)
    early = jnp.broadcast_to(early, (owners, 8, 3 * width))
    packets = exchange_owner(jnp.concatenate([pieces, early], axis=1), owner)
    packet = jnp.stack(packets)
    other_packet = swap_core(packet)

    tokens = lax.all_gather(block_in, "shard", axis=0, tiled=True)
    grad_earlier, mix, depth_sums = average(depth_weights, earlier, cotangent)

    by_core = jnp.stack([packet, other_packet])
    packet = jnp.stack(
        [
            lax.dynamic_slice(
                by_core,
                (core ^ (d % 2), (owner - d // 2) % owners, 0, 0),
                (1, 1, part + 8, 3 * width),
            )[0, 0]
            for d in range(groups)
        ]
    )
    w_own = packet[:, :part].reshape(model_width, 3 * width)
    early = packet[:, part].astype(F32)
    b_qk = early[:, : 2 * part].reshape(2 * model_width)
    b_value = early[:, 2 * part : 3 * part].reshape(model_width)
    g_one = early[:, 3 * part : 4 * part].reshape(1, model_width)
    s_one = early[:, 4 * part : 5 * part].reshape(1, model_width)
    b_joint = jnp.concatenate([b_qk, b_value]).reshape(3, owners, width)
    b_own = lax.dynamic_index_in_dim(b_joint, owner, 1, keepdims=False).reshape(3 * width, 1)
    w_turned = jnp.transpose(w_own)

    freqs = 10000.0 ** (-jnp.arange(half, dtype=F32) / half)
    angles = freqs[:, None] * jnp.arange(length, dtype=jnp.int32).astype(F32)[None, :]
    cosine = jnp.cos(angles)
    sine = jnp.sin(angles)
    core_index = core.astype(jnp.int32).reshape(1)

    late = jnp.concatenate([out_bias, in_bias, down_bias, gain_two, shift_two]).astype(BF16)
    late = late.reshape(-1, model_width)
    hidden_part = hidden_width // groups
    share = hidden_part // 3
    last = jnp.concatenate([out_weight.astype(BF16), late], axis=0)
    last = jnp.pad(last, ((0, share - last.shape[0]), (0, 0)))
    rep = lax.axis_index("rep")
    tail_packet = lax.dynamic_slice_in_dim(
        jnp.concatenate([down_weight.astype(BF16), last], axis=0), rep * share, share, 0
    )
    tokens, w_turned, b_own, cosine, sine, mix, tail_packet, in_packet = after(
        (tokens, w_turned, b_own, cosine, sine, mix, tail_packet, in_weight.astype(BF16)),
        grad_earlier,
        depth_sums,
    )
    w_in = lax.all_gather(in_packet, "shard", axis=0, tiled=True)
    tail_parts = [tail_packet] + [shift_owner(tail_packet, k) for k in range(1, owners)]
    states = project(tokens, w_turned, b_own, g_one, s_one, cosine, sine)
    plain_all, qt, kt, vt, k, v, *tail_parts = lax.optimization_barrier(
        (*states, *tail_parts)
    )
    tail_stack = jnp.stack(tail_parts)
    qt, tail_stack = lax.optimization_barrier((qt, tail_stack))
    tail_mine = [tail_stack] + [cross_rep(tail_stack, m) for m in range(1, 4)]
    mixed_own, attended, stats = attend(core_index, qt, k, vt, 0, groups)
    mixed_own, attended, stats, *tail_mine = lax.optimization_barrier(
        (mixed_own, attended, stats, *tail_mine)
    )
    mixed_two = lax.all_to_all(mixed_own, "shard", 0, 0).reshape(owners, 2, width, BLOCK)
    tail_other = [swap_core(value) for value in tail_mine]
    w_down, last = assemble(
        jnp.stack([member, rep]).astype(jnp.int32), tail_mine, tail_other
    )
    w_down = w_down.reshape(hidden_width, model_width)
    w_out = last[:, :part].reshape(model_width, model_width)
    late = last[:, part : part + late.shape[0]].reshape(groups, -1).astype(F32)
    b_out = late[:, :part].reshape(model_width)
    b_in = late[:, part : part + hidden_part].reshape(hidden_width)
    b_down = late[:, part + hidden_part : 2 * part + hidden_part].reshape(model_width)
    g_two = late[:, 2 * part + hidden_part : 3 * part + hidden_part].reshape(model_width)
    s_two = late[:, 3 * part + hidden_part :].reshape(model_width)

    first = lax.dynamic_index_in_dim(mixed_two, core, 1, keepdims=False)
    second = lax.dynamic_index_in_dim(mixed_two, 1 - core, 1, keepdims=False)
    mixed_t = jnp.concatenate(
        [first.reshape(model_width, BLOCK), second.reshape(model_width, BLOCK)], axis=1
    )

    inputs = block_in.astype(F32)
    branch = contract(mixed_t, w_out, 0, 0) + b_out
    middle = inputs + branch
    normed_two, norm_two_back = jax.vjp(layer_norm, middle, g_two, s_two)
    normed_two_low = normed_two.astype(BF16)
    hidden = contract(normed_two_low, w_in, 1, 0) + b_in
    active_full, gelu_back = jax.vjp(partial(jax.nn.gelu, approximate=True), hidden)
    active = active_full.astype(BF16)
    result = middle + contract(active, w_down, 1, 0) + b_down
    layer_out = depth_weights[4] * result + mix
    local_depth = jnp.concatenate(
        [jnp.sum(depth_sums, axis=(1, 2)), jnp.sum(result * cotangent)[None]]
    )
    grad_result = depth_weights[4] * cotangent
    down_grad = grad_result.astype(BF16)
    grad_down_w = contract(active, down_grad, 0, 0)
    grad_down_b = jnp.sum(down_grad.astype(F32), axis=0)
    grad_active = contract(down_grad, w_down, 1, 1)
    grad_hidden = gelu_back(grad_active)[0].astype(BF16)
    grad_in_w = contract(normed_two_low, grad_hidden, 0, 0)
    grad_in_b = jnp.sum(grad_hidden.astype(F32), axis=0)
    grad_normed_two = contract(grad_hidden, w_in, 1, 1)
    grad_mid_norm, grad_gain_two, grad_shift_two = norm_two_back(grad_normed_two)
    grad_middle = grad_result + grad_mid_norm
    branch_grad = grad_middle.astype(BF16)
    grad_out_w = contract(mixed_t, branch_grad, 1, 0)
    grad_out_b = jnp.sum(branch_grad.astype(F32), axis=0)
    grad_mixed_t = contract(w_out, branch_grad, 1, 1).astype(BF16)

    grad_mixed_t = grad_mixed_t.reshape(owners, width, 2, BLOCK)
    first = lax.dynamic_index_in_dim(grad_mixed_t, core, 2, keepdims=False)
    second = lax.dynamic_index_in_dim(grad_mixed_t, 1 - core, 2, keepdims=False)
    grad_own = jnp.stack([first, second], axis=1).reshape(groups, width, BLOCK)
    grad_own = lax.all_to_all(grad_own, "shard", 0, 0)

    pair_sums = jnp.concatenate(
        [
            grad_in_w.astype(BF16).reshape(groups, part, hidden_width),
            grad_out_w.astype(BF16).reshape(groups, part, model_width),
        ],
        axis=2,
    )
    folded = fold_core(pair_sums, core)
    grad_own, folded, down_sums = lax.optimization_barrier(
        (grad_own, folded, grad_down_w.astype(BF16))
    )
    sent = send_rep(folded)
    down_sums = lax.psum_scatter(down_sums, "shard", scatter_dimension=0, tiled=True)
    joint_t = retrace(core_index, qt, grad_own, attended, stats, cosine, sine, k, v, kt)
    joint_t, folded, *sent = lax.optimization_barrier((joint_t, folded, *sent))
    grad_normed = contract(joint_t, w_own, 0, 1).astype(BF16)
    joint_t, folded, plain_all, down_sums, *sent = after(
        (joint_t, folded, plain_all, down_sums, *sent), grad_normed
    )
    grad_normed = lax.psum_scatter(
        grad_normed, "shard", scatter_dimension=0, tiled=True
    )
    folded = join_rep(folded, sent)
    sum_pair = spread_rep(add_low(*exchange_owner(folded, owner))).astype(F32)
    sum_in = sum_pair[:, :hidden_width]
    sum_out = sum_pair[:, hidden_width:]
    sum_down = spread_rep(fold_rep(down_sums[None])[0]).astype(F32)

    product = contract(plain_all, joint_t, 0, 1)
    joint_sums = jnp.sum(joint_t.astype(F32), axis=1)
    w_wide = w_own.astype(F32)
    grad_gain_one = jnp.sum(product * w_wide, axis=1)
    grad_shift_one = jnp.sum(joint_sums[None, :] * w_wide, axis=1)
    grad_qkv = g_one.reshape(-1, 1) * product + s_one.reshape(-1, 1) * joint_sums[None, :]
    grad_qkv = grad_qkv.astype(BF16).reshape(groups, part, 3 * width)
    sum_qkv = reduce_columns(grad_qkv, owner, core).reshape(part, owners, 3, width)
    sum_qkv = jnp.transpose(sum_qkv, (0, 2, 1, 3)).reshape(part, 3 * model_width)

    spread_sums = lax.dynamic_update_slice(
        jnp.zeros((3, model_width), F32), joint_sums.reshape(3, width), (0, owner * width)
    ).reshape(3 * model_width)
    sizes = (2 * part, part, part, hidden_part, part, part, part, part, part)
    small = jnp.concatenate(
        [
            spread_sums,
            grad_out_b,
            grad_in_b,
            grad_down_b,
            grad_gain_one,
            grad_shift_one,
            grad_gain_two,
            grad_shift_two,
            local_depth,
        ]
    )
    small = reduce_small(small)

    grad_normed, sum_qkv, sum_out, sum_in, sum_down, small = lax.optimization_barrier(
        (grad_normed, sum_qkv, sum_out, sum_in, sum_down, small)
    )
    grad_normed = grad_normed.astype(F32)
    center = inputs - jnp.mean(inputs, axis=-1, keepdims=True)
    scale = lax.rsqrt(jnp.mean(center * center, axis=-1, keepdims=True) + EPSILON)
    plain = center * scale
    scaled = grad_normed * g_one
    grad_block = grad_middle + scale * (
        scaled
        - jnp.mean(scaled, axis=-1, keepdims=True)
        - plain * jnp.mean(scaled * plain, axis=-1, keepdims=True)
    )

    small_outs = []
    start = 0
    for size in sizes:
        small_outs.append(lax.dynamic_slice_in_dim(small, start + member * size, size, 0))
        start += size * groups
    grad_depth = small[start:]
    return (
        layer_out,
        grad_block,
        grad_earlier,
        sum_qkv,
        sum_out,
        sum_in,
        sum_down,
        *small_outs,
        grad_depth,
    )


def per_device(*args):
    block_in = args[0]
    row_count, model_width = block_in.shape
    groups = lax.axis_size("shard")
    head_count = model_width // HEAD_DIM
    late_size = (4 * model_width + args[5].shape[1]) // groups
    if (
        groups == 8
        and lax.axis_size("rep") == 4
        and row_count == CHUNK
        and head_count % (groups // 2) == 0
        and head_count // (groups // 2) <= 8
        and late_size % model_width == 0
        and args[5].shape[1] % (3 * groups) == 0
        and model_width // groups + late_size // model_width
        <= args[5].shape[1] // (3 * groups)
    ):
        return head_split_device(*args)
    return generic_device(*args)


def solution(mesh):
    placed = (
        P(("rep", "shard"), None),
        P(None, ("rep", "shard"), None),
        P(("rep", "shard"), None),
        P("shard", None),
        P("shard", None),
        P("shard", None),
        P("shard", None),
        P("shard"),
        P("shard"),
        P("shard"),
        P("shard"),
        P("shard"),
        P("shard"),
        P("shard"),
        P("shard"),
        P("shard"),
        P(),
    )
    return jax.shard_map(
        per_device,
        mesh=mesh,
        in_specs=placed,
        out_specs=(
            P(("rep", "shard"), None),
            P(("rep", "shard"), None),
            P(None, ("rep", "shard"), None),
            P("shard", None),
            P("shard", None),
            P("shard", None),
            P("shard", None),
            P("shard"),
            P("shard"),
            P("shard"),
            P("shard"),
            P("shard"),
            P("shard"),
            P("shard"),
            P("shard"),
            P("shard"),
            P(),
        ),
        check_vma=False,
    )
```

```python
from functools import partial
import math

import jax
import jax.numpy as jnp
from jax import lax
from jax.experimental import pallas as pl
from jax.experimental.pallas import tpu as pltpu
from jax.sharding import PartitionSpec as P

HEAD_DIM = 64
BLOCK = 256


NEG = -1e30
EPSILON = 1e-05


def layer_norm(inputs, gain, shift):
    center = inputs - jnp.mean(inputs, axis=-1, keepdims=True)
    spread = jnp.mean(center * center, axis=-1, keepdims=True)
    return center * lax.rsqrt(spread + EPSILON) * gain + shift


def rotate(inputs, positions):
    row_count = inputs.shape[0]
    split = inputs.reshape(row_count, -1, HEAD_DIM)
    half_dim = HEAD_DIM // 2
    freqs = 10000.0 ** (-jnp.arange(half_dim, dtype=jnp.float32) / half_dim)
    angles = positions.astype(jnp.float32)[:, None] * freqs[None, :]
    cosine = jnp.cos(angles)[:, None, :]
    sine = jnp.sin(angles)[:, None, :]
    former = split[..., :half_dim]
    latter = split[..., half_dim:]
    turned = jnp.concatenate(
        [former * cosine - latter * sine, former * sine + latter * cosine], axis=-1
    )
    return turned.reshape(row_count, -1)


def generic_device(
    block_in,
    earlier,
    cotangent,
    qkv_weight,
    out_weight,
    in_weight,
    down_weight,
    qk_bias,
    value_bias,
    out_bias,
    in_bias,
    down_bias,
    gain_one,
    shift_one,
    gain_two,
    shift_two,
    depth_weights,
):
    bf16 = jnp.bfloat16
    f32 = jnp.float32
    w_qkv, w_out, w_in, w_down, b_qk, b_value, b_out, b_in, b_down, g_one, s_one, g_two, s_two = (
        lax.all_gather(qkv_weight.astype(bf16), "shard", axis=0, tiled=True),
        lax.all_gather(out_weight.astype(bf16), "shard", axis=0, tiled=True),
        lax.all_gather(in_weight.astype(bf16), "shard", axis=0, tiled=True),
        lax.all_gather(down_weight.astype(bf16), "shard", axis=0, tiled=True),
        lax.all_gather(qk_bias.astype(bf16), "shard", axis=0, tiled=True),
        lax.all_gather(value_bias.astype(bf16), "shard", axis=0, tiled=True),
        lax.all_gather(out_bias.astype(bf16), "shard", axis=0, tiled=True),
        lax.all_gather(in_bias.astype(bf16), "shard", axis=0, tiled=True),
        lax.all_gather(down_bias.astype(bf16), "shard", axis=0, tiled=True),
        lax.all_gather(gain_one.astype(bf16), "shard", axis=0, tiled=True),
        lax.all_gather(shift_one.astype(bf16), "shard", axis=0, tiled=True),
        lax.all_gather(gain_two.astype(bf16), "shard", axis=0, tiled=True),
        lax.all_gather(shift_two.astype(bf16), "shard", axis=0, tiled=True),
    )
    row_count, model_width = block_in.shape
    head_count = model_width // HEAD_DIM
    groups = lax.axis_size("shard")
    length = row_count * groups
    window = min(512, length)
    member = lax.axis_index("shard")
    first_row = member * row_count
    last_end = first_row + row_count
    positions = first_row + jnp.arange(row_count, dtype=jnp.int32)
    query_block = positions // BLOCK
    score_scale = HEAD_DIM ** (-0.5)
    needed = (last_end + window - 1) // window
    inputs = block_in.astype(f32)
    normed, norm_back = jax.vjp(layer_norm, inputs, g_one.astype(f32), s_one.astype(f32))
    normed_low = normed.astype(bf16)
    joint_bias = jnp.concatenate([b_qk.astype(f32), b_value.astype(f32)])
    projected = jnp.dot(normed_low, w_qkv, preferred_element_type=f32) + joint_bias
    queries = rotate(projected[:, :model_width], positions).astype(bf16)
    key_rows = rotate(projected[:, model_width : 2 * model_width], positions).astype(bf16)
    values = projected[:, 2 * model_width :].astype(bf16)
    query_heads = queries.reshape(row_count, head_count, HEAD_DIM)

    def masked_scores(key_piece, key_start):
        piece_rows = key_piece.shape[0]
        key_heads = key_piece.reshape(piece_rows, head_count, HEAD_DIM)
        scores = (
            jnp.einsum("qhd,khd->hqk", query_heads, key_heads, preferred_element_type=f32)
            * score_scale
        )
        key_block = (key_start + jnp.arange(piece_rows, dtype=jnp.int32)) // BLOCK
        allowed = key_block[None, :] <= query_block[:, None]
        return (scores, allowed)

    def absorb(running, key_piece, value_piece, key_start):
        highest, denominator, summed = running
        scores, allowed = masked_scores(key_piece, key_start)
        scores = jnp.where(allowed[None], scores, NEG)
        new_high = jnp.maximum(highest, jnp.max(scores, axis=-1))
        rescale = jnp.exp(highest - new_high)
        weights = jnp.where(allowed[None], jnp.exp(scores - new_high[..., None]), 0.0)
        value_heads = value_piece.reshape(-1, head_count, HEAD_DIM)
        summed = summed * rescale[..., None] + jnp.einsum(
            "hqk,khd->hqd", weights.astype(bf16), value_heads, preferred_element_type=f32
        )
        return (new_high, denominator * rescale + jnp.sum(weights, axis=-1), summed)

    start_state = (
        jnp.full((head_count, row_count), NEG, f32),
        jnp.zeros((head_count, row_count), f32),
        jnp.zeros((head_count, row_count, HEAD_DIM), f32),
    )
    key_piece = lax.all_gather(key_rows, "shard", axis=0, tiled=True)
    value_piece = lax.all_gather(values, "shard", axis=0, tiled=True)
    piece_rows = key_piece.shape[0]
    sub_rows = math.gcd(piece_rows, window)
    usable = jnp.clip((last_end + sub_rows - 1) // sub_rows, 0, piece_rows // sub_rows)

    def advance(block_step, state_inner):
        offset = block_step * sub_rows
        return absorb(
            state_inner,
            lax.dynamic_slice_in_dim(key_piece, offset, sub_rows, 0),
            lax.dynamic_slice_in_dim(value_piece, offset, sub_rows, 0),
            offset,
        )

    highest, denominator, summed = lax.fori_loop(0, usable, advance, start_state)
    attended = summed / denominator[..., None]
    log_norm = highest + jnp.log(denominator)
    mixed = jnp.transpose(attended, (1, 0, 2)).reshape(row_count, model_width).astype(bf16)
    branch = jnp.dot(mixed, w_out, preferred_element_type=f32) + b_out.astype(f32)
    middle = inputs + branch
    normed_two, norm_two_back = jax.vjp(layer_norm, middle, g_two.astype(f32), s_two.astype(f32))
    normed_two_low = normed_two.astype(bf16)
    hidden = jnp.dot(normed_two_low, w_in, preferred_element_type=f32) + b_in.astype(f32)
    active_full, gelu_back = jax.vjp(partial(jax.nn.gelu, approximate=True), hidden)
    active = active_full.astype(bf16)
    result = middle + jnp.dot(active, w_down, preferred_element_type=f32) + b_down.astype(f32)
    stacked = earlier.astype(f32)
    layer_out = depth_weights[4] * result
    for level in range(4):
        layer_out = layer_out + depth_weights[level] * stacked[level]
    grad_earlier = depth_weights[:4][:, None, None] * cotangent[None]
    local_depth = jnp.concatenate(
        [jnp.sum(stacked * cotangent[None], axis=(1, 2)), jnp.sum(result * cotangent)[None]]
    )
    grad_depth = lax.psum(local_depth, ("rep", "shard"))
    grad_result = depth_weights[4] * cotangent
    down_grad = grad_result.astype(bf16)
    grad_down_w = jnp.einsum("tf,td->fd", active, down_grad, preferred_element_type=f32)
    grad_down_b = jnp.sum(down_grad.astype(f32), axis=0)
    grad_active = jnp.einsum("td,fd->tf", down_grad, w_down, preferred_element_type=f32)
    grad_hidden = gelu_back(grad_active)[0].astype(bf16)
    grad_in_w = jnp.einsum("td,tf->df", normed_two_low, grad_hidden, preferred_element_type=f32)
    grad_in_b = jnp.sum(grad_hidden.astype(f32), axis=0)
    grad_normed_two = jnp.einsum("tf,df->td", grad_hidden, w_in, preferred_element_type=f32)
    grad_mid_norm, grad_gain_two, grad_shift_two = norm_two_back(grad_normed_two)
    grad_middle = grad_result + grad_mid_norm
    branch_grad = grad_middle.astype(bf16)
    grad_out_w = jnp.einsum("td,te->de", mixed, branch_grad, preferred_element_type=f32)
    grad_out_b = jnp.sum(branch_grad.astype(f32), axis=0)
    grad_mixed = jnp.einsum("te,de->td", branch_grad, w_out, preferred_element_type=f32).astype(
        bf16
    )
    key_all, value_all = (
        lax.all_gather(key_rows, "shard", axis=0, tiled=True),
        lax.all_gather(values, "shard", axis=0, tiled=True),
    )
    grad_heads = grad_mixed.reshape(row_count, head_count, HEAD_DIM)
    delta = jnp.einsum("qhd,hqd->hq", grad_heads.astype(f32), attended)

    def score_grads(key_piece, value_piece, offset, piece_rows):
        scores, allowed = masked_scores(key_piece, offset)
        probs = jnp.where(allowed[None], jnp.exp(scores - log_norm[..., None]), 0.0)
        value_heads = value_piece.reshape(piece_rows, head_count, HEAD_DIM)
        grad_probs = jnp.einsum("qhd,khd->hqk", grad_heads, value_heads, preferred_element_type=f32)
        grad_scores = (probs * (grad_probs - delta[..., None])).astype(bf16)
        return (probs, grad_scores)

    def retrace(block_step, running):
        grad_query, grad_keys, grad_values = running
        offset = block_step * window
        key_piece = lax.dynamic_slice_in_dim(key_all, offset, window, 0)
        value_piece = lax.dynamic_slice_in_dim(value_all, offset, window, 0)
        probs, grad_scores = score_grads(key_piece, value_piece, offset, window)
        key_heads = key_piece.reshape(window, head_count, HEAD_DIM)
        grad_query = grad_query + jnp.einsum(
            "hqk,khd->qhd", grad_scores, key_heads, preferred_element_type=f32
        )
        piece_keys = (
            jnp.einsum("hqk,qhd->khd", grad_scores, query_heads, preferred_element_type=f32)
            * score_scale
        )
        piece_values = jnp.einsum(
            "hqk,qhd->khd", probs.astype(bf16), grad_heads, preferred_element_type=f32
        )
        grad_keys = lax.dynamic_update_slice_in_dim(
            grad_keys, piece_keys.reshape(window, model_width), offset, 0
        )
        grad_values = lax.dynamic_update_slice_in_dim(
            grad_values, piece_values.reshape(window, model_width), offset, 0
        )
        return (grad_query, grad_keys, grad_values)

    start_back = (
        jnp.zeros((row_count, head_count, HEAD_DIM), f32),
        jnp.zeros((length, model_width), f32),
        jnp.zeros((length, model_width), f32),
    )
    grad_query, grad_keys, grad_values = lax.fori_loop(0, needed, retrace, start_back)
    own_keys, own_values = (
        lax.psum_scatter(
            grad_keys.astype(jnp.bfloat16), "shard", scatter_dimension=0, tiled=True
        ).astype(jnp.float32),
        lax.psum_scatter(
            grad_values.astype(jnp.bfloat16), "shard", scatter_dimension=0, tiled=True
        ).astype(jnp.float32),
    )
    grad_q_turned = rotate(grad_query.reshape(row_count, model_width) * score_scale, -positions)
    grad_k_turned = rotate(own_keys, -positions)
    grad_joint = jnp.concatenate([grad_q_turned, grad_k_turned, own_values], axis=1).astype(bf16)
    grad_qkv_w = jnp.einsum("td,tf->df", normed_low, grad_joint, preferred_element_type=f32)
    joint_sums = jnp.sum(grad_joint.astype(f32), axis=0)
    grad_qk_b = joint_sums[: 2 * model_width]
    grad_value_b = joint_sums[2 * model_width :]
    grad_normed = jnp.einsum("tf,df->td", grad_joint, w_qkv, preferred_element_type=f32)
    grad_in_norm, grad_gain_one, grad_shift_one = norm_back(grad_normed)
    grad_block = grad_middle + grad_in_norm
    (
        own_qkv_w,
        own_out_w,
        own_in_w,
        own_down_w,
        own_qk_b,
        own_value_b,
        own_out_b,
        own_in_b,
        own_down_b,
        own_gain_one,
        own_shift_one,
        own_gain_two,
        own_shift_two,
    ) = (
        lax.psum_scatter(
            grad_qkv_w.astype(jnp.bfloat16), "shard", scatter_dimension=0, tiled=True
        ).astype(jnp.float32),
        lax.psum_scatter(
            grad_out_w.astype(jnp.bfloat16), "shard", scatter_dimension=0, tiled=True
        ).astype(jnp.float32),
        lax.psum_scatter(
            grad_in_w.astype(jnp.bfloat16), "shard", scatter_dimension=0, tiled=True
        ).astype(jnp.float32),
        lax.psum_scatter(
            grad_down_w.astype(jnp.bfloat16), "shard", scatter_dimension=0, tiled=True
        ).astype(jnp.float32),
        lax.psum_scatter(
            grad_qk_b.astype(jnp.bfloat16), "shard", scatter_dimension=0, tiled=True
        ).astype(jnp.float32),
        lax.psum_scatter(
            grad_value_b.astype(jnp.bfloat16), "shard", scatter_dimension=0, tiled=True
        ).astype(jnp.float32),
        lax.psum_scatter(
            grad_out_b.astype(jnp.bfloat16), "shard", scatter_dimension=0, tiled=True
        ).astype(jnp.float32),
        lax.psum_scatter(
            grad_in_b.astype(jnp.bfloat16), "shard", scatter_dimension=0, tiled=True
        ).astype(jnp.float32),
        lax.psum_scatter(
            grad_down_b.astype(jnp.bfloat16), "shard", scatter_dimension=0, tiled=True
        ).astype(jnp.float32),
        lax.psum_scatter(
            grad_gain_one.astype(jnp.bfloat16), "shard", scatter_dimension=0, tiled=True
        ).astype(jnp.float32),
        lax.psum_scatter(
            grad_shift_one.astype(jnp.bfloat16), "shard", scatter_dimension=0, tiled=True
        ).astype(jnp.float32),
        lax.psum_scatter(
            grad_gain_two.astype(jnp.bfloat16), "shard", scatter_dimension=0, tiled=True
        ).astype(jnp.float32),
        lax.psum_scatter(
            grad_shift_two.astype(jnp.bfloat16), "shard", scatter_dimension=0, tiled=True
        ).astype(jnp.float32),
    )
    (
        sum_qkv_w,
        sum_out_w,
        sum_in_w,
        sum_down_w,
        sum_qk_b,
        sum_value_b,
        sum_out_b,
        sum_in_b,
        sum_down_b,
        sum_gain_one,
        sum_shift_one,
        sum_gain_two,
        sum_shift_two,
    ) = (
        lax.psum(own_qkv_w.astype(jnp.bfloat16), "rep").astype(jnp.float32),
        lax.psum(own_out_w.astype(jnp.bfloat16), "rep").astype(jnp.float32),
        lax.psum(own_in_w.astype(jnp.bfloat16), "rep").astype(jnp.float32),
        lax.psum(own_down_w.astype(jnp.bfloat16), "rep").astype(jnp.float32),
        lax.psum(own_qk_b.astype(jnp.bfloat16), "rep").astype(jnp.float32),
        lax.psum(own_value_b.astype(jnp.bfloat16), "rep").astype(jnp.float32),
        lax.psum(own_out_b.astype(jnp.bfloat16), "rep").astype(jnp.float32),
        lax.psum(own_in_b.astype(jnp.bfloat16), "rep").astype(jnp.float32),
        lax.psum(own_down_b.astype(jnp.bfloat16), "rep").astype(jnp.float32),
        lax.psum(own_gain_one.astype(jnp.bfloat16), "rep").astype(jnp.float32),
        lax.psum(own_shift_one.astype(jnp.bfloat16), "rep").astype(jnp.float32),
        lax.psum(own_gain_two.astype(jnp.bfloat16), "rep").astype(jnp.float32),
        lax.psum(own_shift_two.astype(jnp.bfloat16), "rep").astype(jnp.float32),
    )
    return (
        layer_out,
        grad_block,
        grad_earlier,
        sum_qkv_w,
        sum_out_w,
        sum_in_w,
        sum_down_w,
        sum_qk_b,
        sum_value_b,
        sum_out_b,
        sum_in_b,
        sum_down_b,
        sum_gain_one,
        sum_shift_one,
        sum_gain_two,
        sum_shift_two,
        grad_depth,
    )


F32 = jnp.float32
BF16 = jnp.bfloat16
CHUNK = 2 * BLOCK
VMEM_LIMIT = 56 * 1024 * 1024


def cost(flops, moved, exps=0):
    return pl.CostEstimate(flops=flops, bytes_accessed=moved, transcendentals=exps)


def contract(left, right, left_dim, right_dim):
    return lax.dot_general(
        left, right, (((left_dim,), (right_dim,)), ((), ())), preferred_element_type=F32
    )


def qkv_kernel(
    x_ref, weight_ref, bias_ref, gain_ref, shift_ref, cos_ref, sin_ref,
    plain_ref, qt_ref, kt_ref, vt_ref, kv_ref,
):
    x = x_ref[...].astype(F32)
    center = x - jnp.mean(x, axis=-1, keepdims=True)
    spread = jnp.mean(center * center, axis=-1, keepdims=True)
    plain = center * lax.rsqrt(spread + EPSILON)
    plain_ref[...] = plain.astype(BF16)
    low = (plain * gain_ref[...] + shift_ref[...]).astype(BF16)
    width = qt_ref.shape[0]
    half = HEAD_DIM // 2
    joint = contract(weight_ref[...], low, 1, 1) + bias_ref[...]
    cosine = cos_ref[...]
    sine = sin_ref[...]
    for head in range(width // HEAD_DIM):
        base = head * HEAD_DIM
        for part in range(2):
            start = part * width + base
            former = joint[start : start + half]
            latter = joint[start + half : start + HEAD_DIM]
            turned = jnp.concatenate(
                [former * cosine - latter * sine, former * sine + latter * cosine], axis=0
            )
            if part == 0:
                qt_ref[base : base + HEAD_DIM, :] = (turned * HEAD_DIM ** (-0.5)).astype(BF16)
            else:
                kt_ref[base : base + HEAD_DIM, :] = turned.astype(BF16)
                key = turned
        start = 2 * width + base
        value = joint[start : start + HEAD_DIM]
        vt_ref[base : base + HEAD_DIM, :] = value.astype(BF16)
        kv_ref[head] = jnp.transpose(jnp.concatenate([key, value], axis=0)).astype(BF16)


def project(tokens, weight_t, bias, gain, shift, cosine, sine):
    length, model_width = tokens.shape
    columns = weight_t.shape[0]
    width = columns // 3
    heads = width // HEAD_DIM
    half = HEAD_DIM // 2
    tile = CHUNK
    fixed = lambda i: (0, 0)
    across = lambda i: (0, i)
    return pl.pallas_call(
        qkv_kernel,
        name="project",
        cost_estimate=cost(2 * length * model_width * columns, 12 * length * model_width),
        grid=(length // tile,),
        in_specs=[
            pl.BlockSpec((tile, model_width), lambda i: (i, 0)),
            pl.BlockSpec((columns, model_width), fixed),
            pl.BlockSpec((columns, 1), fixed),
            pl.BlockSpec((1, model_width), fixed),
            pl.BlockSpec((1, model_width), fixed),
            pl.BlockSpec((half, tile), across),
            pl.BlockSpec((half, tile), across),
        ],
        out_specs=[
            pl.BlockSpec((tile, model_width), lambda i: (i, 0)),
            pl.BlockSpec((width, tile), across),
            pl.BlockSpec((width, tile), across),
            pl.BlockSpec((width, tile), across),
            pl.BlockSpec((heads, tile, 2 * HEAD_DIM), lambda i: (0, i, 0)),
        ],
        out_shape=[
            jax.ShapeDtypeStruct((length, model_width), BF16),
            jax.ShapeDtypeStruct((width, length), BF16),
            jax.ShapeDtypeStruct((width, length), BF16),
            jax.ShapeDtypeStruct((width, length), BF16),
            jax.ShapeDtypeStruct((heads, length, 2 * HEAD_DIM), BF16),
        ],
        compiler_params=pltpu.CompilerParams(vmem_limit_bytes=VMEM_LIMIT),
    )(tokens, weight_t, bias, gain, shift, cosine, sine)


def average_kernel(weights_ref, earlier_ref, cotangent_ref, grad_ref, mix_ref, sums_ref):
    @pl.when(pl.program_id(0) == 0)
    def _():
        sums_ref[...] = jnp.zeros_like(sums_ref)

    cotangent = cotangent_ref[...]
    rows, columns = cotangent.shape
    mix = jnp.zeros_like(cotangent)
    for level in range(earlier_ref.shape[0]):
        value = earlier_ref[level].astype(F32)
        weight = weights_ref[level]
        mix = mix + weight * value
        grad_ref[level] = weight * cotangent
        sums_ref[level] += jnp.sum((value * cotangent).reshape(rows // 8, 8, columns), axis=0)
    mix_ref[...] = mix


def average(depth_weights, earlier, cotangent):
    levels, row_count, model_width = earlier.shape
    tile = row_count // 4
    return pl.pallas_call(
        average_kernel,
        name="average",
        cost_estimate=cost(6 * earlier.size, 6 * earlier.size + 8 * cotangent.size),
        grid_spec=pltpu.PrefetchScalarGridSpec(
            num_scalar_prefetch=1,
            grid=(4,),
            in_specs=[
                pl.BlockSpec((levels, tile, model_width), lambda i, w: (0, i, 0)),
                pl.BlockSpec((tile, model_width), lambda i, w: (i, 0)),
            ],
            out_specs=[
                pl.BlockSpec((levels, tile, model_width), lambda i, w: (0, i, 0)),
                pl.BlockSpec((tile, model_width), lambda i, w: (i, 0)),
                pl.BlockSpec((levels, 8, model_width), lambda i, w: (0, 0, 0)),
            ],
        ),
        out_shape=[
            jax.ShapeDtypeStruct(earlier.shape, F32),
            jax.ShapeDtypeStruct(cotangent.shape, F32),
            jax.ShapeDtypeStruct((levels, 8, model_width), F32),
        ],
        compiler_params=pltpu.CompilerParams(vmem_limit_bytes=VMEM_LIMIT),
    )(depth_weights, earlier, cotangent)


def last_mask(odd, rows):
    row = lax.broadcasted_iota(jnp.int32, (rows, BLOCK), 0)
    return row < rows - BLOCK * (1 - odd)


def over_chunks(pair, absorb, state):
    state = lax.fori_loop(0, pair // 2, lambda i, s: absorb(2 * i, 2 * CHUNK, s, False), state)
    return lax.cond(
        pair % 2 == 0,
        lambda s: absorb(pair, CHUNK, s, True),
        lambda s: absorb(pair - 1, 2 * CHUNK, s, True),
        state,
    )


def attend_kernel(core_ref, qt_ref, kv_ref, vt_ref, low_ref, full_ref, stat_ref, scores_ref):
    pair = pl.program_id(0)
    odd = core_ref[0] ^ (pair & 1)
    heads = qt_ref.shape[0] // HEAD_DIM
    blank = jnp.zeros((HEAD_DIM, BLOCK), BF16)
    queries = [
        jnp.concatenate([qt_ref[h * HEAD_DIM : (h + 1) * HEAD_DIM, :], blank], axis=0)
        for h in range(heads)
    ]
    fold = lambda value: value.reshape(value.shape[0] // 8, 8, BLOCK)

    def score(step, size, state, masked):
        keys = pl.ds(pl.multiple_of(step * CHUNK, CHUNK), size)
        fresh = []
        for h in range(heads):
            scores = contract(kv_ref[h, keys, :], queries[h], 1, 0)
            if masked:
                scores = jnp.where(last_mask(odd, size), scores, NEG)
            scores_ref[h, keys, :] = scores
            fresh.append(jnp.maximum(state[h], jnp.max(fold(scores), axis=0)))
        return fresh

    def mix(step, size, state, masked):
        keys = pl.ds(pl.multiple_of(step * CHUNK, CHUNK), size)
        fresh = []
        for h in range(heads):
            total, summed = state[h]
            weights = jnp.exp(scores_ref[h, keys, :] - highest[h])
            values = vt_ref[h * HEAD_DIM : (h + 1) * HEAD_DIM, keys]
            fresh.append(
                (
                    total + jnp.sum(fold(weights), axis=0),
                    summed + contract(values, weights.astype(BF16), 1, 0),
                )
            )
        return fresh

    state = [jnp.full((8, BLOCK), NEG, F32) for _ in range(heads)]
    state = over_chunks(pair, score, state)
    highest = [jnp.max(value, axis=0, keepdims=True) for value in state]
    state = [
        (jnp.zeros((8, BLOCK), F32), jnp.zeros((HEAD_DIM, BLOCK), F32)) for _ in range(heads)
    ]
    state = over_chunks(pair, mix, state)
    for h in range(heads):
        total, summed = state[h]
        total = jnp.sum(total, axis=0, keepdims=True)
        attended = summed / total
        full_ref[0, h * HEAD_DIM : (h + 1) * HEAD_DIM, :] = attended
        low_ref[0, h * HEAD_DIM : (h + 1) * HEAD_DIM, :] = attended.astype(BF16)
        stat_ref[0, h : h + 1, :] = highest[h] + jnp.log(total)


def attend(core, qt, kv, vt):
    width, length = qt.shape
    pairs = length // CHUNK
    own = lambda j, core: (0, 2 * j + (core[0] ^ (j & 1)))
    slot = lambda j, core: (j, 0, 0)
    return pl.pallas_call(
        attend_kernel,
        name="attend",
        cost_estimate=cost(
            2 * 2 * BLOCK * BLOCK * BLOCK * 2 * sum(range(1, pairs + 1)) * (width // HEAD_DIM),
            4 * kv.size + 8 * pairs * width * BLOCK,
            CHUNK * BLOCK * sum(range(1, pairs + 1)) * (width // HEAD_DIM),
        ),
        grid_spec=pltpu.PrefetchScalarGridSpec(
            num_scalar_prefetch=1,
            grid=(pairs,),
            in_specs=[
                pl.BlockSpec((width, BLOCK), own),
                pl.BlockSpec(kv.shape, lambda j, core: (0, 0, 0)),
                pl.BlockSpec(vt.shape, lambda j, core: (0, 0)),
            ],
            out_specs=[
                pl.BlockSpec((1, width, BLOCK), slot),
                pl.BlockSpec((1, width, BLOCK), slot),
                pl.BlockSpec((1, 8, BLOCK), slot),
            ],
            scratch_shapes=[pltpu.VMEM((width // HEAD_DIM, length, BLOCK), F32)],
        ),
        out_shape=[
            jax.ShapeDtypeStruct((pairs, width, BLOCK), BF16),
            jax.ShapeDtypeStruct((pairs, width, BLOCK), F32),
            jax.ShapeDtypeStruct((pairs, 8, BLOCK), F32),
        ],
        compiler_params=pltpu.CompilerParams(vmem_limit_bytes=VMEM_LIMIT),
    )(core, qt, kv, vt)


def retrace_kernel(
    core_ref, qt_ref, grad_ref, full_ref, stat_ref, cos_ref, sin_ref, kv_ref, kt_ref,
    joint_ref, dkv_ref,
):
    step_id = pl.program_id(0)
    pair = pl.num_programs(0) - 1 - step_id
    odd = core_ref[0] ^ (pair & 1)
    width = qt_ref.shape[0]
    heads = width // HEAD_DIM
    half = HEAD_DIM // 2

    @pl.when(step_id == 0)
    def _():
        dkv_ref[...] = jnp.zeros_like(dkv_ref)

    blank = jnp.zeros((HEAD_DIM, BLOCK), BF16)
    lefts, rights, deltas, norms = [], [], [], []
    for h in range(heads):
        rows = slice(h * HEAD_DIM, (h + 1) * HEAD_DIM)
        query = qt_ref[rows, :]
        grad = grad_ref[0, rows, :]
        lefts.append(
            jnp.concatenate(
                [
                    jnp.concatenate([query, blank], axis=1),
                    jnp.concatenate([blank, grad], axis=1),
                ],
                axis=0,
            )
        )
        rights.append(
            jnp.concatenate(
                [
                    jnp.concatenate([blank, query], axis=1),
                    jnp.concatenate([grad, blank], axis=1),
                ],
                axis=0,
            )
        )
        deltas.append(jnp.sum(grad.astype(F32) * full_ref[0, rows, :], axis=0, keepdims=True))
        norms.append(stat_ref[0, h : h + 1, :])

    def absorb(step, state, masked):
        keys = pl.ds(pl.multiple_of(step * CHUNK, CHUNK), CHUNK)
        fresh = []
        for h in range(heads):
            both = contract(kv_ref[h, keys, :], lefts[h], 1, 0)
            probs = jnp.exp(both[:, :BLOCK] - norms[h])
            if masked:
                probs = jnp.where(last_mask(odd, CHUNK), probs, 0.0)
            grad_scores = (probs * (both[:, BLOCK:] - deltas[h])).astype(BF16)
            joined = jnp.concatenate([probs.astype(BF16), grad_scores], axis=1)
            dkv_ref[h, keys, :] += contract(joined, rights[h], 1, 1)
            turned = kt_ref[h * HEAD_DIM : (h + 1) * HEAD_DIM, keys]
            fresh.append(state[h] + contract(turned, grad_scores, 1, 0))
        return fresh

    state = [jnp.zeros((HEAD_DIM, BLOCK), F32) for _ in range(heads)]
    state = lax.fori_loop(0, pair, lambda i, s: absorb(i, s, False), state)
    state = absorb(pair, state, True)
    offset = pl.multiple_of(pair * CHUNK, CHUNK)
    cosine = cos_ref[...]
    sine = sin_ref[...]
    column = lax.broadcasted_iota(jnp.int32, (HEAD_DIM, CHUNK), 1) // BLOCK

    for h in range(heads):
        base = h * HEAD_DIM
        doubled = jnp.concatenate([state[h], state[h]], axis=1) * HEAD_DIM ** (-0.5)
        doubled = jnp.where(column == odd, doubled, 0.0)
        turned_back = jnp.transpose(dkv_ref[h, pl.ds(offset, CHUNK), :])
        for part, value in ((0, doubled), (1, turned_back[:HEAD_DIM])):
            former = value[:half]
            latter = value[half:]
            turned = jnp.concatenate(
                [former * cosine + latter * sine, latter * cosine - former * sine], axis=0
            )
            start = part * width + base
            joint_ref[start : start + HEAD_DIM, :] = turned.astype(BF16)
        start = 2 * width + base
        joint_ref[start : start + HEAD_DIM, :] = turned_back[HEAD_DIM:].astype(BF16)


def retrace(core, qt, grads, full, stats, cosine, sine, kv, kt):
    width, length = qt.shape
    heads = width // HEAD_DIM
    half = HEAD_DIM // 2
    pairs = length // CHUNK
    back = lambda j: pairs - 1 - j
    own = lambda j, core: (0, 2 * back(j) + (core[0] ^ (back(j) & 1)))
    slot = lambda j, core: (back(j), 0, 0)
    across = lambda j, core: (0, back(j))
    return pl.pallas_call(
        retrace_kernel,
        name="retrace",
        cost_estimate=cost(
            5 * 2 * BLOCK * BLOCK * BLOCK * 2 * sum(range(1, pairs + 1)) * heads,
            3 * kv.size + 16 * pairs * width * BLOCK,
            CHUNK * BLOCK * sum(range(1, pairs + 1)) * heads,
        ),
        grid_spec=pltpu.PrefetchScalarGridSpec(
            num_scalar_prefetch=1,
            grid=(pairs,),
            in_specs=[
                pl.BlockSpec((width, BLOCK), own),
                pl.BlockSpec((1, width, BLOCK), slot),
                pl.BlockSpec((1, width, BLOCK), slot),
                pl.BlockSpec((1, 8, BLOCK), slot),
                pl.BlockSpec((half, CHUNK), across),
                pl.BlockSpec((half, CHUNK), across),
                pl.BlockSpec(kv.shape, lambda j, core: (0, 0, 0)),
                pl.BlockSpec(kt.shape, lambda j, core: (0, 0)),
            ],
            out_specs=pl.BlockSpec((3 * width, CHUNK), across),
            scratch_shapes=[pltpu.VMEM((heads, length, 2 * HEAD_DIM), F32)],
        ),
        out_shape=jax.ShapeDtypeStruct((3 * width, length), BF16),
        compiler_params=pltpu.CompilerParams(vmem_limit_bytes=VMEM_LIMIT),
    )(core, qt, grads, full, stats, cosine, sine, kv, kt)


def after(values, *earlier_values):
    values = tuple(values)
    return lax.optimization_barrier(values + tuple(earlier_values))[: len(values)]


def assemble_kernel(place_ref, *refs):
    down_ref, out_ref, late_ref = refs[-3:]
    rep = place_ref[1]
    reps = (len(refs) - 3) // 2
    part = out_ref.shape[0]
    for side in range(2):
        @pl.when(pl.program_id(0) == side)
        def _():
            for k in range(reps):
                piece = refs[side * reps + k]
                rows = piece.shape[1]
                target = rep ^ k

                @pl.when(target < reps - 1)
                def _():
                    down_ref[pl.ds(pl.multiple_of(target * rows, rows), rows), :] = piece[0]

                @pl.when(target == reps - 1)
                def _():
                    out_ref[...] = piece[0, :part]
                    late_ref[0] = piece[0, part : part + 8]


def assemble(place, mine, twin, part):
    owners, rows, columns = mine[0].shape
    reps = len(mine)
    groups = 2 * owners

    def held(side):
        def index(which, z, place):
            moving = (place[0] // 2 + owners - z) % owners
            fixed = (place[0] // 2 + owners - (owners - 1) * (1 - side)) % owners
            return (jnp.where(which == side, moving, fixed), 0, 0)

        return pl.BlockSpec((1, rows, columns), index)

    device = lambda which, z, place: 2 * z + (which ^ (place[0] % 2))
    target = lambda which, z, place: (device(which, z, place), 0)
    return pl.pallas_call(
        assemble_kernel,
        name="assemble",
        cost_estimate=cost(0, 4 * 2 * reps * owners * rows * columns),
        grid_spec=pltpu.PrefetchScalarGridSpec(
            num_scalar_prefetch=1,
            grid=(2, owners),
            in_specs=[held(0)] * reps + [held(1)] * reps,
            out_specs=[
                pl.BlockSpec(((reps - 1) * rows, columns), target),
                pl.BlockSpec((part, columns), target),
                pl.BlockSpec(
                    (1, 8, columns), lambda which, z, place: (device(which, z, place), 0, 0)
                ),
            ],
        ),
        out_shape=[
            jax.ShapeDtypeStruct((groups * (reps - 1) * rows, columns), BF16),
            jax.ShapeDtypeStruct((groups * part, columns), BF16),
            jax.ShapeDtypeStruct((groups, 8, columns), BF16),
        ],
        compiler_params=pltpu.CompilerParams(vmem_limit_bytes=VMEM_LIMIT),
    )(place, *mine, *twin)


def swap_core(value):
    groups = lax.axis_size("shard")
    return lax.ppermute(value, "shard", [(i, i ^ 1) for i in range(groups)])


def shift_owner(value, distance):
    groups = lax.axis_size("shard")
    step = 2 * distance
    return lax.ppermute(value, "shard", [(i, (i + step) % groups) for i in range(groups)])


def cross_rep(value, mask):
    return lax.ppermute(value, "rep", [(i, i ^ mask) for i in range(lax.axis_size("rep"))])


def pick(stacked, index, axis=0):
    return lax.dynamic_index_in_dim(stacked, index, axis, keepdims=False)


def add_low(*values):
    total = values[0].astype(F32)
    for value in values[1:]:
        total = total + value.astype(F32)
    return total.astype(BF16)


def fold_core(partial_sums, core):
    halves = partial_sums.reshape((-1, 2) + partial_sums.shape[1:])
    received = swap_core(pick(halves, 1 - core, 1))
    return add_low(pick(halves, core, 1), received)


def rep_parts(value):
    reps = lax.axis_size("rep")
    owners, rows, columns = value.shape
    return value.reshape(owners, reps, rows // reps, columns)


def send_rep(value):
    rep = lax.axis_index("rep")
    parts = rep_parts(value)
    return [cross_rep(pick(parts, rep ^ k, 1), k) for k in range(1, lax.axis_size("rep"))]


def pick_parts(value):
    rep = lax.axis_index("rep")
    parts = rep_parts(value)
    return [pick(parts, rep ^ k, 1) for k in range(lax.axis_size("rep"))]


def join_rep(value, received):
    return add_low(pick(rep_parts(value), lax.axis_index("rep"), 1), *received)


def unpack_kernel(rep_ref, *refs):
    in_ref, out_ref, qkv_ref, small_ref, down_ref = refs[-5:]
    pieces = refs[:-5]
    reps = len(pieces) // 3
    hidden_width = in_ref.shape[1]
    model_width = out_ref.shape[1]
    columns = qkv_ref.shape[1] // 3
    owners = down_ref.shape[0] // in_ref.shape[0]
    width = columns // owners
    for k in range(reps):
        pair, joint, down = pieces[k::reps]
        rows = pair.shape[0]
        first = pl.multiple_of((rep_ref[0] ^ k) * rows, 8)
        own = pl.ds(first, rows)
        in_ref[own, :] = pair[:, :hidden_width].astype(F32)
        out_ref[own, :] = pair[:, hidden_width:].astype(F32)
        whole = joint[:, : 3 * columns].astype(F32)
        for part in range(3):
            qkv_ref[own, part * columns : (part + 1) * columns] = jnp.concatenate(
                [
                    whole[:, (3 * z + part) * width : (3 * z + part + 1) * width]
                    for z in range(owners)
                ],
                axis=1,
            )
        small_ref[own, :] = joint[:, 3 * columns :].astype(F32)
        for z in range(owners):
            block = pl.ds(pl.multiple_of(owners * first + z * rows, 8), rows)
            down_ref[block, :] = down[:, z * model_width : (z + 1) * model_width].astype(F32)


def unpack(rep, pair, joint, down, widths):
    hidden_width, model_width, columns = widths
    pieces = [*pair, *joint, *down]
    rows = len(pair) * pair[0].shape[0]
    owners = model_width * 3 // columns
    shapes = [
        (rows, hidden_width),
        (rows, model_width),
        (rows, 3 * model_width),
        (rows, 128),
        (owners * rows, model_width),
    ]
    whole = pl.BlockSpec(memory_space=pltpu.VMEM)
    return pl.pallas_call(
        unpack_kernel,
        name="unpack",
        cost_estimate=cost(0, 6 * sum(a * b for a, b in shapes)),
        in_specs=[pl.BlockSpec(memory_space=pltpu.SMEM)] + [whole] * len(pieces),
        out_specs=[whole] * 5,
        out_shape=[jax.ShapeDtypeStruct(shape, F32) for shape in shapes],
        compiler_params=pltpu.CompilerParams(vmem_limit_bytes=VMEM_LIMIT),
    )(rep, *pieces)


def every_rep(value):
    return [value] + [cross_rep(value, k) for k in range(1, lax.axis_size("rep"))]


def exchange_owner(value, owner):
    owners = value.shape[0]
    received = [pick(value, owner)]
    for k in range(1, owners):
        received.append(shift_owner(pick(value, (owner + k) % owners), k))
    return received


def middle_kernel(
    core_ref, weights_ref, mixed_ref, x_ref, cotangent_ref, w_out_ref, b_out_ref, gain_ref,
    shift_ref, w_in_ref, b_in_ref, grad_ref,
    middle_ref, low_ref, active_ref, hidden_ref, total_ref, branch_ref, send_ref,
    sums_ref, hidden_sums_ref, plain_ref, scale_ref, back_ref,
):
    step = pl.program_id(0)
    core = core_ref[0]
    owners = mixed_ref.shape[0] // 2
    width = mixed_ref.shape[1]

    @pl.when(step == 0)
    def _():
        for half in range(2):
            rows = slice(half * BLOCK, (half + 1) * BLOCK)
            mixed = jnp.concatenate(
                [mixed_ref[2 * z + (core ^ half)] for z in range(owners)], axis=0
            )
            branch = contract(mixed, w_out_ref[...], 0, 0) + b_out_ref[...]
            middle = x_ref[rows, :].astype(F32) + branch
            middle_ref[rows, :] = middle
            center = middle - jnp.mean(middle, axis=-1, keepdims=True)
            scale = lax.rsqrt(jnp.mean(center * center, axis=-1, keepdims=True) + EPSILON)
            plain = center * scale
            scale_ref[rows, :] = jnp.broadcast_to(scale, (BLOCK, scale_ref.shape[1]))
            plain_ref[rows, :] = plain
            low_ref[rows, :] = (plain * gain_ref[...] + shift_ref[...]).astype(BF16)
        back_ref[...] = jnp.zeros_like(back_ref)

    hidden = contract(low_ref[...], w_in_ref[...], 1, 0) + b_in_ref[...]
    square = hidden * hidden
    bend = math.sqrt(2 / math.pi)
    turned = jnp.tanh(hidden * (bend + (bend * 0.044715) * square))
    share = 0.5 + 0.5 * turned
    active_ref[...] = (hidden * share).astype(BF16)
    slope = (0.5 * hidden) * (1.0 - turned * turned) * (bend + (3 * bend * 0.044715) * square)
    grad = (grad_ref[...] * (share + slope)).astype(BF16)
    hidden_ref[...] = grad
    hidden_sums_ref[...] = jnp.sum(grad.astype(F32), axis=0, keepdims=True)
    back_ref[...] += contract(grad, w_in_ref[...], 1, 1)

    @pl.when(step == pl.num_programs(0) - 1)
    def _():
        weight = weights_ref[4]
        sums = [jnp.zeros((1, back_ref.shape[1]), F32)] * 3
        for half in range(2):
            rows = slice(half * BLOCK, (half + 1) * BLOCK)
            back = back_ref[rows, :]
            plain = plain_ref[rows, :]
            scaled = back * gain_ref[...]
            total = weight * cotangent_ref[rows, :] + scale_ref[rows, :1] * (
                scaled
                - jnp.mean(scaled, axis=-1, keepdims=True)
                - plain * jnp.mean(scaled * plain, axis=-1, keepdims=True)
            )
            total_ref[rows, :] = total
            low = total.astype(BF16)
            branch_ref[rows, :] = low
            mixed = contract(w_out_ref[...], low, 1, 1).astype(BF16)
            for z in range(owners):
                send_ref[2 * z + (core ^ half)] = mixed[z * width : (z + 1) * width, :]
            for i, value in enumerate((low.astype(F32), back * plain, back)):
                sums[i] = sums[i] + jnp.sum(value, axis=0, keepdims=True)
        for i in range(3):
            sums_ref[i : i + 1, :] = sums[i]


def middle_part(
    core, depth_weights, mixed, x, cotangent, w_out, b_out, gain, shift, w_in, b_in, grad_active
):
    rows, model_width = x.shape
    hidden_width = w_in.shape[1]
    chunk = CHUNK
    whole = lambda value: pl.BlockSpec(value.shape, lambda j, *_: (0,) * value.ndim)
    across = pl.BlockSpec((rows, chunk), lambda j, *_: (0, j))
    line = pl.BlockSpec((1, chunk), lambda j, *_: (0, j))
    shapes = [
        jax.ShapeDtypeStruct((rows, model_width), F32),
        jax.ShapeDtypeStruct((rows, model_width), BF16),
        jax.ShapeDtypeStruct((rows, hidden_width), BF16),
        jax.ShapeDtypeStruct((rows, hidden_width), BF16),
        jax.ShapeDtypeStruct((rows, model_width), F32),
        jax.ShapeDtypeStruct((rows, model_width), BF16),
        jax.ShapeDtypeStruct(mixed.shape, BF16),
        jax.ShapeDtypeStruct((8, model_width), F32),
        jax.ShapeDtypeStruct((1, hidden_width), F32),
    ]
    out_specs = [whole(shape) for shape in shapes]
    out_specs[2] = out_specs[3] = across
    out_specs[8] = line
    return pl.pallas_call(
        middle_kernel,
        name="middle",
        cost_estimate=cost(
            4 * rows * model_width * (hidden_width + model_width),
            2 * w_in.size + 8 * grad_active.size,
            grad_active.size,
        ),
        grid_spec=pltpu.PrefetchScalarGridSpec(
            num_scalar_prefetch=2,
            grid=(hidden_width // chunk,),
            in_specs=[
                whole(mixed),
                whole(x),
                whole(cotangent),
                whole(w_out),
                whole(b_out),
                whole(gain),
                whole(shift),
                pl.BlockSpec((model_width, chunk), lambda j, *_: (0, j)),
                line,
                across,
            ],
            out_specs=out_specs,
            scratch_shapes=[
                pltpu.VMEM((rows, model_width), F32),
                pltpu.VMEM((rows, 128), F32),
                pltpu.VMEM((rows, model_width), F32),
            ],
        ),
        out_shape=shapes,
        compiler_params=pltpu.CompilerParams(vmem_limit_bytes=VMEM_LIMIT),
    )(
        core, depth_weights, mixed, x, cotangent, w_out, b_out, gain, shift, w_in, b_in,
        grad_active,
    )


def pair_kernel(core_ref, low_ref, hidden_ref, mixed_ref, branch_ref, own_ref, other_ref, full_ref):
    step = pl.program_id(0)
    core = core_ref[0]
    owners, part, _ = own_ref.shape

    @pl.when(step < pl.num_programs(0) - 1)
    def _():
        full_ref[...] = contract(low_ref[...], hidden_ref[...], 0, 0)

    @pl.when(step == pl.num_programs(0) - 1)
    def _():
        for half in range(2):
            mixed = jnp.concatenate(
                [mixed_ref[2 * z + (core ^ half)] for z in range(owners)], axis=0
            )
            product = contract(mixed, branch_ref[half * BLOCK : (half + 1) * BLOCK, :], 1, 0)
            if half == 0:
                full_ref[...] = product
            else:
                full_ref[...] += product

    for z in range(owners):
        for side, ref in ((0, own_ref), (1, other_ref)):
            start = pl.multiple_of((2 * z + (core ^ side)) * part, part)
            ref[z] = full_ref[pl.ds(start, part), :].astype(BF16)


def pair_sums(core, low, hidden, mixed, branch):
    rows, model_width = low.shape
    owners = mixed.shape[0] // 2
    part = model_width // (2 * owners)
    steps = hidden.shape[1] // model_width
    whole = lambda value: pl.BlockSpec(value.shape, lambda j, core: (0,) * value.ndim)
    target = pl.BlockSpec((owners, part, model_width), lambda j, core: (0, 0, j))
    shape = jax.ShapeDtypeStruct((owners, part, (steps + 1) * model_width), BF16)
    return pl.pallas_call(
        pair_kernel,
        name="pair_sums",
        grid_spec=pltpu.PrefetchScalarGridSpec(
            num_scalar_prefetch=1,
            grid=(steps + 1,),
            in_specs=[
                whole(low),
                pl.BlockSpec(
                    (rows, model_width), lambda j, core: (0, jnp.minimum(j, steps - 1))
                ),
                whole(mixed),
                whole(branch),
            ],
            out_specs=[target, target],
            scratch_shapes=[pltpu.VMEM((model_width, model_width), F32)],
        ),
        out_shape=[shape, shape],
        compiler_params=pltpu.CompilerParams(vmem_limit_bytes=VMEM_LIMIT),
    )(core, low, hidden, mixed, branch)


def head_split_device(
    block_in,
    earlier,
    cotangent,
    qkv_weight,
    out_weight,
    in_weight,
    down_weight,
    qk_bias,
    value_bias,
    out_bias,
    in_bias,
    down_bias,
    gain_one,
    shift_one,
    gain_two,
    shift_two,
    depth_weights,
):
    row_count, model_width = block_in.shape
    hidden_width = in_weight.shape[1]
    groups = lax.axis_size("shard")
    owners = groups // 2
    width = model_width // owners
    part = model_width // groups
    length = row_count * groups
    half = HEAD_DIM // 2
    member = lax.axis_index("shard")
    owner = member // 2
    core = member % 2

    pieces = qkv_weight.astype(BF16).reshape(part, 3, owners, width)
    pieces = jnp.transpose(pieces, (2, 0, 1, 3)).reshape(owners, part, 3 * width)
    early = jnp.concatenate([qk_bias, value_bias, gain_one, shift_one]).astype(BF16)
    early = jnp.pad(early, (0, 8 * 3 * width - early.shape[0])).reshape(8, 3 * width)
    early = jnp.broadcast_to(early, (owners, 8, 3 * width))
    packets = exchange_owner(jnp.concatenate([pieces, early], axis=1), owner)
    packet = jnp.stack(packets)
    other_packet = swap_core(packet)

    tokens = lax.all_gather(block_in, "shard", axis=0, tiled=True)
    grad_earlier, mix, depth_sums = average(depth_weights, earlier, cotangent)

    by_core = jnp.stack([packet, other_packet])
    packet = jnp.stack(
        [
            lax.dynamic_slice(
                by_core,
                (core ^ (d % 2), (owner - d // 2) % owners, 0, 0),
                (1, 1, part + 8, 3 * width),
            )[0, 0]
            for d in range(groups)
        ]
    )
    w_own = packet[:, :part].reshape(model_width, 3 * width)
    early = packet[:, part].astype(F32)
    b_qk = early[:, : 2 * part].reshape(2 * model_width)
    b_value = early[:, 2 * part : 3 * part].reshape(model_width)
    g_one = early[:, 3 * part : 4 * part].reshape(1, model_width)
    s_one = early[:, 4 * part : 5 * part].reshape(1, model_width)
    b_joint = jnp.concatenate([b_qk, b_value]).reshape(3, owners, width)
    b_own = lax.dynamic_index_in_dim(b_joint, owner, 1, keepdims=False).reshape(3 * width, 1)
    w_turned = jnp.transpose(w_own)

    freqs = 10000.0 ** (-jnp.arange(half, dtype=F32) / half)
    angles = freqs[:, None] * jnp.arange(length, dtype=jnp.int32).astype(F32)[None, :]
    cosine = jnp.cos(angles)
    sine = jnp.sin(angles)
    core_index = core.astype(jnp.int32).reshape(1)

    late = jnp.concatenate([out_bias, in_bias, down_bias, gain_two, shift_two]).astype(BF16)
    late = late.reshape(-1, model_width)
    hidden_part = hidden_width // groups
    share = hidden_part // 3
    last = jnp.concatenate([out_weight.astype(BF16), late], axis=0)
    last = jnp.pad(last, ((0, share - last.shape[0]), (0, 0)))
    rep = lax.axis_index("rep")
    tail_packet = lax.dynamic_slice_in_dim(
        jnp.concatenate([down_weight.astype(BF16), last], axis=0), rep * share, share, 0
    )
    tokens, w_turned, b_own, cosine, sine, mix, tail_packet, in_packet = after(
        (tokens, w_turned, b_own, cosine, sine, mix, tail_packet, in_weight.astype(BF16)),
        grad_earlier,
        depth_sums,
    )
    tail_parts = [tail_packet] + [shift_owner(tail_packet, k) for k in range(1, owners)]
    states = project(tokens, w_turned, b_own, g_one, s_one, cosine, sine)
    plain_all, qt, kt, vt, kv, *tail_parts = lax.optimization_barrier(
        (*states, *tail_parts)
    )
    tail_stack = jnp.stack(tail_parts)
    qt, tail_stack, in_packet = lax.optimization_barrier((qt, tail_stack, in_packet))
    w_in = lax.all_gather(in_packet, "shard", axis=0, tiled=True)
    tail_mine = [tail_stack] + [cross_rep(tail_stack, m) for m in range(1, 4)]
    mixed_own, attended, stats = attend(core_index, qt, kv, vt)
    mixed_own, attended, stats, *tail_mine = lax.optimization_barrier(
        (mixed_own, attended, stats, *tail_mine)
    )
    mixed_two = lax.all_to_all(mixed_own, "shard", 0, 0)
    tail_other = [swap_core(value) for value in tail_mine]
    w_down, w_out, late = assemble(
        jnp.stack([member, rep]).astype(jnp.int32), tail_mine, tail_other, part
    )
    late = late[:, 0].astype(F32)
    grad_result = depth_weights[4] * cotangent
    down_grad = grad_result.astype(BF16)
    grad_active = contract(down_grad, w_down, 1, 1)
    mixed_two, grad_active = lax.optimization_barrier((mixed_two, grad_active))
    row = lambda first, size: late[:, first : first + size].reshape(1, groups * size)
    b_out = row(0, part)
    b_in = row(part, hidden_part)
    b_down = row(part + hidden_part, part)
    g_two = row(2 * part + hidden_part, part)
    s_two = row(3 * part + hidden_part, part)

    inputs = block_in.astype(F32)
    (
        middle, normed_two_low, active, grad_hidden, grad_middle, branch_grad, grad_own,
        token_sums, grad_in_b,
    ) = middle_part(
        core_index, depth_weights, mixed_two, block_in, cotangent, w_out, b_out, g_two, s_two,
        w_in, b_in, grad_active,
    )
    grad_out_b, grad_gain_two, grad_shift_two = (token_sums[i] for i in range(3))
    grad_in_b = grad_in_b[0]
    grad_own = lax.all_to_all(grad_own, "shard", 0, 0)
    folded, twin = pair_sums(core_index, normed_two_low, grad_hidden, mixed_two, branch_grad)
    folded = add_low(folded, swap_core(twin))
    grad_down_w = contract(active, down_grad, 0, 0)
    grad_down_b = jnp.sum(down_grad.astype(F32), axis=0)
    grad_own, folded, down_sums = lax.optimization_barrier(
        (grad_own, folded, grad_down_w.astype(BF16))
    )
    sent = send_rep(folded)
    down_sums = lax.psum_scatter(down_sums, "shard", scatter_dimension=0, tiled=True)
    joint_t = retrace(core_index, qt, grad_own, attended, stats, cosine, sine, kv, kt)
    joint_t, folded, *sent = lax.optimization_barrier((joint_t, folded, *sent))
    grad_normed = contract(joint_t, w_own, 0, 1).astype(BF16)
    joint_t, folded, plain_all, down_sums, *sent = after(
        (joint_t, folded, plain_all, down_sums, *sent), grad_normed
    )
    grad_normed = lax.psum_scatter(
        grad_normed, "shard", scatter_dimension=0, tiled=True
    )
    folded = join_rep(folded, sent)

    product = contract(plain_all, joint_t, 0, 1)
    joint_sums = jnp.sum(joint_t.astype(F32), axis=1)
    arrived = exchange_owner(folded, owner)
    product, joint_sums, *arrived = lax.optimization_barrier((product, joint_sums, *arrived))
    pair_pieces = every_rep(add_low(*arrived))
    w_wide = w_own.astype(F32)
    grad_gain_one = jnp.sum(product * w_wide, axis=1)
    grad_shift_one = jnp.sum(joint_sums[None, :] * w_wide, axis=1)
    grad_qkv = g_one.reshape(-1, 1) * product + s_one.reshape(-1, 1) * joint_sums[None, :]
    grad_qkv = grad_qkv.astype(BF16).reshape(groups, part, 3 * width)
    spread_sums = lax.dynamic_update_slice(
        jnp.zeros((3, model_width), F32), joint_sums.reshape(3, width), (0, owner * width)
    ).reshape(3 * model_width)
    vectors = (
        spread_sums[: 2 * model_width],
        spread_sums[2 * model_width :],
        grad_out_b,
        grad_in_b,
        grad_down_b,
        grad_gain_one,
        grad_shift_one,
        grad_gain_two,
        grad_shift_two,
    )
    small = jnp.concatenate([vector.reshape(groups, -1) for vector in vectors], axis=1)
    small = jnp.pad(small, ((0, 0), (0, part * 128 - small.shape[1]))).astype(BF16)
    small = jnp.transpose(small.reshape(groups, 128, part), (0, 2, 1))
    mixed_sums = fold_core(jnp.concatenate([grad_qkv, small], axis=2), core)
    down_parts = pick_parts(down_sums[None])
    down_rows = part // 4
    columns = 3 * width + 128
    sums_parts = pick_parts(mixed_sums)
    received = [
        cross_rep(
            jnp.concatenate([sums, down.reshape(owners, down_rows, model_width)], axis=2), k
        )
        for k, (sums, down) in enumerate(zip(sums_parts[1:], down_parts[1:]), 1)
    ]
    (active,) = after((active,), *sums_parts)
    result = middle + contract(active, w_down, 1, 0) + b_down
    layer_out = depth_weights[4] * result + mix
    local_depth = jnp.concatenate(
        [jnp.sum(depth_sums, axis=(1, 2)), jnp.sum(result * cotangent)[None]]
    )
    layer_out, local_depth, *arrived = lax.optimization_barrier(
        (layer_out, local_depth, *received, *pair_pieces)
    )
    received, pair_pieces = arrived[:3], arrived[3:]
    depth = local_depth + swap_core(local_depth)
    depth = depth + cross_rep(depth, 1)
    depth = depth + cross_rep(depth, 2)
    mixed_sums = add_low(sums_parts[0], *[value[:, :, :columns] for value in received])
    down_sums = add_low(
        down_parts[0].reshape(owners, down_rows, model_width),
        *[value[:, :, columns:] for value in received],
    )
    down_pieces = every_rep(jnp.concatenate([down_sums[k] for k in range(owners)], axis=1))
    arrived = exchange_owner(mixed_sums, owner)
    depth = depth + lax.ppermute(depth, "shard", [(i, i ^ 2) for i in range(groups)])
    grad_depth = depth + lax.ppermute(depth, "shard", [(i, i ^ 4) for i in range(groups)])
    grad_depth, *arrived = lax.optimization_barrier((grad_depth, *arrived, *down_pieces))
    arrived, down_pieces = arrived[:owners], arrived[owners:]
    small = add_low(*[value[:, 3 * width :] for value in arrived])
    by_distance = jnp.stack([value[:, : 3 * width] for value in arrived])
    by_owner = [pick(by_distance, (owner - k) % owners) for k in range(owners)]
    sum_in, sum_out, sum_qkv, small, sum_down = unpack(
        lax.axis_index("rep").astype(jnp.int32).reshape(1),
        pair_pieces,
        every_rep(jnp.concatenate([*by_owner, small], axis=1)),
        down_pieces,
        (hidden_width, model_width, 3 * width),
    )
    small = jnp.transpose(small).reshape(-1)
    small_outs = []
    start = 0
    for vector in vectors:
        size = vector.shape[0] // groups
        small_outs.append(small[start : start + size])
        start += size
    finished = (layer_out, sum_qkv, sum_out, sum_in, sum_down, grad_depth, *small_outs)
    grad_normed, layer_out, sum_qkv, sum_out, sum_in, sum_down, grad_depth, *small_outs = (
        lax.optimization_barrier((grad_normed, *finished))
    )
    grad_normed = grad_normed.astype(F32)
    center = inputs - jnp.mean(inputs, axis=-1, keepdims=True)
    scale = lax.rsqrt(jnp.mean(center * center, axis=-1, keepdims=True) + EPSILON)
    plain = center * scale
    scaled = grad_normed * g_one
    grad_block = grad_middle + scale * (
        scaled
        - jnp.mean(scaled, axis=-1, keepdims=True)
        - plain * jnp.mean(scaled * plain, axis=-1, keepdims=True)
    )

    return (
        layer_out,
        grad_block,
        grad_earlier,
        sum_qkv,
        sum_out,
        sum_in,
        sum_down,
        *small_outs,
        grad_depth,
    )


def per_device(*args):
    block_in = args[0]
    row_count, model_width = block_in.shape
    groups = lax.axis_size("shard")
    head_count = model_width // HEAD_DIM
    late_size = (4 * model_width + args[5].shape[1]) // groups
    if (
        groups == 8
        and lax.axis_size("rep") == 4
        and row_count == CHUNK
        and head_count % (groups // 2) == 0
        and head_count // (groups // 2) <= 8
        and late_size % model_width == 0
        and args[5].shape[1] % (3 * groups) == 0
        and model_width // groups + late_size // model_width
        <= args[5].shape[1] // (3 * groups)
    ):
        return head_split_device(*args)
    return generic_device(*args)


def solution(mesh):
    placed = (
        P(("rep", "shard"), None),
        P(None, ("rep", "shard"), None),
        P(("rep", "shard"), None),
        P("shard", None),
        P("shard", None),
        P("shard", None),
        P("shard", None),
        P("shard"),
        P("shard"),
        P("shard"),
        P("shard"),
        P("shard"),
        P("shard"),
        P("shard"),
        P("shard"),
        P("shard"),
        P(),
    )
    return jax.shard_map(
        per_device,
        mesh=mesh,
        in_specs=placed,
        out_specs=(
            P(("rep", "shard"), None),
            P(("rep", "shard"), None),
            P(None, ("rep", "shard"), None),
            P("shard", None),
            P("shard", None),
            P("shard", None),
            P("shard", None),
            P("shard"),
            P("shard"),
            P("shard"),
            P("shard"),
            P("shard"),
            P("shard"),
            P("shard"),
            P("shard"),
            P("shard"),
            P(),
        ),
        check_vma=False,
    )
```

```python
from functools import partial
import math

import jax
import jax.numpy as jnp
from jax import lax
from jax.experimental import pallas as pl
from jax.experimental.pallas import tpu as pltpu
from jax.sharding import PartitionSpec as P

HEAD_DIM = 64
BLOCK = 256


NEG = -1e30
EPSILON = 1e-05


def layer_norm(inputs, gain, shift):
    center = inputs - jnp.mean(inputs, axis=-1, keepdims=True)
    spread = jnp.mean(center * center, axis=-1, keepdims=True)
    return center * lax.rsqrt(spread + EPSILON) * gain + shift


def rotate(inputs, positions):
    row_count = inputs.shape[0]
    split = inputs.reshape(row_count, -1, HEAD_DIM)
    half_dim = HEAD_DIM // 2
    freqs = 10000.0 ** (-jnp.arange(half_dim, dtype=jnp.float32) / half_dim)
    angles = positions.astype(jnp.float32)[:, None] * freqs[None, :]
    cosine = jnp.cos(angles)[:, None, :]
    sine = jnp.sin(angles)[:, None, :]
    former = split[..., :half_dim]
    latter = split[..., half_dim:]
    turned = jnp.concatenate(
        [former * cosine - latter * sine, former * sine + latter * cosine], axis=-1
    )
    return turned.reshape(row_count, -1)


def generic_device(
    block_in,
    earlier,
    cotangent,
    qkv_weight,
    out_weight,
    in_weight,
    down_weight,
    qk_bias,
    value_bias,
    out_bias,
    in_bias,
    down_bias,
    gain_one,
    shift_one,
    gain_two,
    shift_two,
    depth_weights,
):
    bf16 = jnp.bfloat16
    f32 = jnp.float32
    w_qkv, w_out, w_in, w_down, b_qk, b_value, b_out, b_in, b_down, g_one, s_one, g_two, s_two = (
        lax.all_gather(qkv_weight.astype(bf16), "shard", axis=0, tiled=True),
        lax.all_gather(out_weight.astype(bf16), "shard", axis=0, tiled=True),
        lax.all_gather(in_weight.astype(bf16), "shard", axis=0, tiled=True),
        lax.all_gather(down_weight.astype(bf16), "shard", axis=0, tiled=True),
        lax.all_gather(qk_bias.astype(bf16), "shard", axis=0, tiled=True),
        lax.all_gather(value_bias.astype(bf16), "shard", axis=0, tiled=True),
        lax.all_gather(out_bias.astype(bf16), "shard", axis=0, tiled=True),
        lax.all_gather(in_bias.astype(bf16), "shard", axis=0, tiled=True),
        lax.all_gather(down_bias.astype(bf16), "shard", axis=0, tiled=True),
        lax.all_gather(gain_one.astype(bf16), "shard", axis=0, tiled=True),
        lax.all_gather(shift_one.astype(bf16), "shard", axis=0, tiled=True),
        lax.all_gather(gain_two.astype(bf16), "shard", axis=0, tiled=True),
        lax.all_gather(shift_two.astype(bf16), "shard", axis=0, tiled=True),
    )
    row_count, model_width = block_in.shape
    head_count = model_width // HEAD_DIM
    groups = lax.axis_size("shard")
    length = row_count * groups
    window = min(512, length)
    member = lax.axis_index("shard")
    first_row = member * row_count
    last_end = first_row + row_count
    positions = first_row + jnp.arange(row_count, dtype=jnp.int32)
    query_block = positions // BLOCK
    score_scale = HEAD_DIM ** (-0.5)
    needed = (last_end + window - 1) // window
    inputs = block_in.astype(f32)
    normed, norm_back = jax.vjp(layer_norm, inputs, g_one.astype(f32), s_one.astype(f32))
    normed_low = normed.astype(bf16)
    joint_bias = jnp.concatenate([b_qk.astype(f32), b_value.astype(f32)])
    projected = jnp.dot(normed_low, w_qkv, preferred_element_type=f32) + joint_bias
    queries = rotate(projected[:, :model_width], positions).astype(bf16)
    key_rows = rotate(projected[:, model_width : 2 * model_width], positions).astype(bf16)
    values = projected[:, 2 * model_width :].astype(bf16)
    query_heads = queries.reshape(row_count, head_count, HEAD_DIM)

    def masked_scores(key_piece, key_start):
        piece_rows = key_piece.shape[0]
        key_heads = key_piece.reshape(piece_rows, head_count, HEAD_DIM)
        scores = (
            jnp.einsum("qhd,khd->hqk", query_heads, key_heads, preferred_element_type=f32)
            * score_scale
        )
        key_block = (key_start + jnp.arange(piece_rows, dtype=jnp.int32)) // BLOCK
        allowed = key_block[None, :] <= query_block[:, None]
        return (scores, allowed)

    def absorb(running, key_piece, value_piece, key_start):
        highest, denominator, summed = running
        scores, allowed = masked_scores(key_piece, key_start)
        scores = jnp.where(allowed[None], scores, NEG)
        new_high = jnp.maximum(highest, jnp.max(scores, axis=-1))
        rescale = jnp.exp(highest - new_high)
        weights = jnp.where(allowed[None], jnp.exp(scores - new_high[..., None]), 0.0)
        value_heads = value_piece.reshape(-1, head_count, HEAD_DIM)
        summed = summed * rescale[..., None] + jnp.einsum(
            "hqk,khd->hqd", weights.astype(bf16), value_heads, preferred_element_type=f32
        )
        return (new_high, denominator * rescale + jnp.sum(weights, axis=-1), summed)

    start_state = (
        jnp.full((head_count, row_count), NEG, f32),
        jnp.zeros((head_count, row_count), f32),
        jnp.zeros((head_count, row_count, HEAD_DIM), f32),
    )
    key_piece = lax.all_gather(key_rows, "shard", axis=0, tiled=True)
    value_piece = lax.all_gather(values, "shard", axis=0, tiled=True)
    piece_rows = key_piece.shape[0]
    sub_rows = math.gcd(piece_rows, window)
    usable = jnp.clip((last_end + sub_rows - 1) // sub_rows, 0, piece_rows // sub_rows)

    def advance(block_step, state_inner):
        offset = block_step * sub_rows
        return absorb(
            state_inner,
            lax.dynamic_slice_in_dim(key_piece, offset, sub_rows, 0),
            lax.dynamic_slice_in_dim(value_piece, offset, sub_rows, 0),
            offset,
        )

    highest, denominator, summed = lax.fori_loop(0, usable, advance, start_state)
    attended = summed / denominator[..., None]
    log_norm = highest + jnp.log(denominator)
    mixed = jnp.transpose(attended, (1, 0, 2)).reshape(row_count, model_width).astype(bf16)
    branch = jnp.dot(mixed, w_out, preferred_element_type=f32) + b_out.astype(f32)
    middle = inputs + branch
    normed_two, norm_two_back = jax.vjp(layer_norm, middle, g_two.astype(f32), s_two.astype(f32))
    normed_two_low = normed_two.astype(bf16)
    hidden = jnp.dot(normed_two_low, w_in, preferred_element_type=f32) + b_in.astype(f32)
    active_full, gelu_back = jax.vjp(partial(jax.nn.gelu, approximate=True), hidden)
    active = active_full.astype(bf16)
    result = middle + jnp.dot(active, w_down, preferred_element_type=f32) + b_down.astype(f32)
    stacked = earlier.astype(f32)
    layer_out = depth_weights[4] * result
    for level in range(4):
        layer_out = layer_out + depth_weights[level] * stacked[level]
    grad_earlier = depth_weights[:4][:, None, None] * cotangent[None]
    local_depth = jnp.concatenate(
        [jnp.sum(stacked * cotangent[None], axis=(1, 2)), jnp.sum(result * cotangent)[None]]
    )
    grad_depth = lax.psum(local_depth, ("rep", "shard"))
    grad_result = depth_weights[4] * cotangent
    down_grad = grad_result.astype(bf16)
    grad_down_w = jnp.einsum("tf,td->fd", active, down_grad, preferred_element_type=f32)
    grad_down_b = jnp.sum(down_grad.astype(f32), axis=0)
    grad_active = jnp.einsum("td,fd->tf", down_grad, w_down, preferred_element_type=f32)
    grad_hidden = gelu_back(grad_active)[0].astype(bf16)
    grad_in_w = jnp.einsum("td,tf->df", normed_two_low, grad_hidden, preferred_element_type=f32)
    grad_in_b = jnp.sum(grad_hidden.astype(f32), axis=0)
    grad_normed_two = jnp.einsum("tf,df->td", grad_hidden, w_in, preferred_element_type=f32)
    grad_mid_norm, grad_gain_two, grad_shift_two = norm_two_back(grad_normed_two)
    grad_middle = grad_result + grad_mid_norm
    branch_grad = grad_middle.astype(bf16)
    grad_out_w = jnp.einsum("td,te->de", mixed, branch_grad, preferred_element_type=f32)
    grad_out_b = jnp.sum(branch_grad.astype(f32), axis=0)
    grad_mixed = jnp.einsum("te,de->td", branch_grad, w_out, preferred_element_type=f32).astype(
        bf16
    )
    key_all, value_all = (
        lax.all_gather(key_rows, "shard", axis=0, tiled=True),
        lax.all_gather(values, "shard", axis=0, tiled=True),
    )
    grad_heads = grad_mixed.reshape(row_count, head_count, HEAD_DIM)
    delta = jnp.einsum("qhd,hqd->hq", grad_heads.astype(f32), attended)

    def score_grads(key_piece, value_piece, offset, piece_rows):
        scores, allowed = masked_scores(key_piece, offset)
        probs = jnp.where(allowed[None], jnp.exp(scores - log_norm[..., None]), 0.0)
        value_heads = value_piece.reshape(piece_rows, head_count, HEAD_DIM)
        grad_probs = jnp.einsum("qhd,khd->hqk", grad_heads, value_heads, preferred_element_type=f32)
        grad_scores = (probs * (grad_probs - delta[..., None])).astype(bf16)
        return (probs, grad_scores)

    def retrace(block_step, running):
        grad_query, grad_keys, grad_values = running
        offset = block_step * window
        key_piece = lax.dynamic_slice_in_dim(key_all, offset, window, 0)
        value_piece = lax.dynamic_slice_in_dim(value_all, offset, window, 0)
        probs, grad_scores = score_grads(key_piece, value_piece, offset, window)
        key_heads = key_piece.reshape(window, head_count, HEAD_DIM)
        grad_query = grad_query + jnp.einsum(
            "hqk,khd->qhd", grad_scores, key_heads, preferred_element_type=f32
        )
        piece_keys = (
            jnp.einsum("hqk,qhd->khd", grad_scores, query_heads, preferred_element_type=f32)
            * score_scale
        )
        piece_values = jnp.einsum(
            "hqk,qhd->khd", probs.astype(bf16), grad_heads, preferred_element_type=f32
        )
        grad_keys = lax.dynamic_update_slice_in_dim(
            grad_keys, piece_keys.reshape(window, model_width), offset, 0
        )
        grad_values = lax.dynamic_update_slice_in_dim(
            grad_values, piece_values.reshape(window, model_width), offset, 0
        )
        return (grad_query, grad_keys, grad_values)

    start_back = (
        jnp.zeros((row_count, head_count, HEAD_DIM), f32),
        jnp.zeros((length, model_width), f32),
        jnp.zeros((length, model_width), f32),
    )
    grad_query, grad_keys, grad_values = lax.fori_loop(0, needed, retrace, start_back)
    own_keys, own_values = (
        lax.psum_scatter(
            grad_keys.astype(jnp.bfloat16), "shard", scatter_dimension=0, tiled=True
        ).astype(jnp.float32),
        lax.psum_scatter(
            grad_values.astype(jnp.bfloat16), "shard", scatter_dimension=0, tiled=True
        ).astype(jnp.float32),
    )
    grad_q_turned = rotate(grad_query.reshape(row_count, model_width) * score_scale, -positions)
    grad_k_turned = rotate(own_keys, -positions)
    grad_joint = jnp.concatenate([grad_q_turned, grad_k_turned, own_values], axis=1).astype(bf16)
    grad_qkv_w = jnp.einsum("td,tf->df", normed_low, grad_joint, preferred_element_type=f32)
    joint_sums = jnp.sum(grad_joint.astype(f32), axis=0)
    grad_qk_b = joint_sums[: 2 * model_width]
    grad_value_b = joint_sums[2 * model_width :]
    grad_normed = jnp.einsum("tf,df->td", grad_joint, w_qkv, preferred_element_type=f32)
    grad_in_norm, grad_gain_one, grad_shift_one = norm_back(grad_normed)
    grad_block = grad_middle + grad_in_norm
    (
        own_qkv_w,
        own_out_w,
        own_in_w,
        own_down_w,
        own_qk_b,
        own_value_b,
        own_out_b,
        own_in_b,
        own_down_b,
        own_gain_one,
        own_shift_one,
        own_gain_two,
        own_shift_two,
    ) = (
        lax.psum_scatter(
            grad_qkv_w.astype(jnp.bfloat16), "shard", scatter_dimension=0, tiled=True
        ).astype(jnp.float32),
        lax.psum_scatter(
            grad_out_w.astype(jnp.bfloat16), "shard", scatter_dimension=0, tiled=True
        ).astype(jnp.float32),
        lax.psum_scatter(
            grad_in_w.astype(jnp.bfloat16), "shard", scatter_dimension=0, tiled=True
        ).astype(jnp.float32),
        lax.psum_scatter(
            grad_down_w.astype(jnp.bfloat16), "shard", scatter_dimension=0, tiled=True
        ).astype(jnp.float32),
        lax.psum_scatter(
            grad_qk_b.astype(jnp.bfloat16), "shard", scatter_dimension=0, tiled=True
        ).astype(jnp.float32),
        lax.psum_scatter(
            grad_value_b.astype(jnp.bfloat16), "shard", scatter_dimension=0, tiled=True
        ).astype(jnp.float32),
        lax.psum_scatter(
            grad_out_b.astype(jnp.bfloat16), "shard", scatter_dimension=0, tiled=True
        ).astype(jnp.float32),
        lax.psum_scatter(
            grad_in_b.astype(jnp.bfloat16), "shard", scatter_dimension=0, tiled=True
        ).astype(jnp.float32),
        lax.psum_scatter(
            grad_down_b.astype(jnp.bfloat16), "shard", scatter_dimension=0, tiled=True
        ).astype(jnp.float32),
        lax.psum_scatter(
            grad_gain_one.astype(jnp.bfloat16), "shard", scatter_dimension=0, tiled=True
        ).astype(jnp.float32),
        lax.psum_scatter(
            grad_shift_one.astype(jnp.bfloat16), "shard", scatter_dimension=0, tiled=True
        ).astype(jnp.float32),
        lax.psum_scatter(
            grad_gain_two.astype(jnp.bfloat16), "shard", scatter_dimension=0, tiled=True
        ).astype(jnp.float32),
        lax.psum_scatter(
            grad_shift_two.astype(jnp.bfloat16), "shard", scatter_dimension=0, tiled=True
        ).astype(jnp.float32),
    )
    (
        sum_qkv_w,
        sum_out_w,
        sum_in_w,
        sum_down_w,
        sum_qk_b,
        sum_value_b,
        sum_out_b,
        sum_in_b,
        sum_down_b,
        sum_gain_one,
        sum_shift_one,
        sum_gain_two,
        sum_shift_two,
    ) = (
        lax.psum(own_qkv_w.astype(jnp.bfloat16), "rep").astype(jnp.float32),
        lax.psum(own_out_w.astype(jnp.bfloat16), "rep").astype(jnp.float32),
        lax.psum(own_in_w.astype(jnp.bfloat16), "rep").astype(jnp.float32),
        lax.psum(own_down_w.astype(jnp.bfloat16), "rep").astype(jnp.float32),
        lax.psum(own_qk_b.astype(jnp.bfloat16), "rep").astype(jnp.float32),
        lax.psum(own_value_b.astype(jnp.bfloat16), "rep").astype(jnp.float32),
        lax.psum(own_out_b.astype(jnp.bfloat16), "rep").astype(jnp.float32),
        lax.psum(own_in_b.astype(jnp.bfloat16), "rep").astype(jnp.float32),
        lax.psum(own_down_b.astype(jnp.bfloat16), "rep").astype(jnp.float32),
        lax.psum(own_gain_one.astype(jnp.bfloat16), "rep").astype(jnp.float32),
        lax.psum(own_shift_one.astype(jnp.bfloat16), "rep").astype(jnp.float32),
        lax.psum(own_gain_two.astype(jnp.bfloat16), "rep").astype(jnp.float32),
        lax.psum(own_shift_two.astype(jnp.bfloat16), "rep").astype(jnp.float32),
    )
    return (
        layer_out,
        grad_block,
        grad_earlier,
        sum_qkv_w,
        sum_out_w,
        sum_in_w,
        sum_down_w,
        sum_qk_b,
        sum_value_b,
        sum_out_b,
        sum_in_b,
        sum_down_b,
        sum_gain_one,
        sum_shift_one,
        sum_gain_two,
        sum_shift_two,
        grad_depth,
    )


F32 = jnp.float32
BF16 = jnp.bfloat16
CHUNK = 2 * BLOCK
VMEM_LIMIT = 56 * 1024 * 1024


def cost(flops, moved, exps=0):
    return pl.CostEstimate(flops=flops, bytes_accessed=moved, transcendentals=exps)


def contract(left, right, left_dim, right_dim):
    return lax.dot_general(
        left, right, (((left_dim,), (right_dim,)), ((), ())), preferred_element_type=F32
    )


def qkv_kernel(x_ref, weight_ref, bias_ref, gain_ref, shift_ref, cos_ref, sin_ref, *refs):
    plain_ref, qt_ref, kt_ref, vt_ref, kv_ref = refs[-5:]
    x = x_ref[...].astype(F32)
    center = x - jnp.mean(x, axis=-1, keepdims=True)
    spread = jnp.mean(center * center, axis=-1, keepdims=True)
    plain = center * lax.rsqrt(spread + EPSILON)
    plain_ref[...] = plain.astype(BF16)
    low = (plain * gain_ref[...] + shift_ref[...]).astype(BF16)
    width = qt_ref.shape[0]
    half = HEAD_DIM // 2
    joint = contract(weight_ref[...], low, 1, 1) + bias_ref[...]
    cosine = cos_ref[...]
    sine = sin_ref[...]
    for head in range(width // HEAD_DIM):
        base = head * HEAD_DIM
        for part in range(2):
            start = part * width + base
            former = joint[start : start + half]
            latter = joint[start + half : start + HEAD_DIM]
            turned = jnp.concatenate(
                [former * cosine - latter * sine, former * sine + latter * cosine], axis=0
            )
            if part == 0:
                qt_ref[base : base + HEAD_DIM, :] = (turned * HEAD_DIM ** (-0.5)).astype(BF16)
            else:
                kt_ref[base : base + HEAD_DIM, :] = turned.astype(BF16)
                key = turned
        start = 2 * width + base
        value = joint[start : start + HEAD_DIM]
        vt_ref[base : base + HEAD_DIM, :] = value.astype(BF16)
        kv_ref[head] = jnp.transpose(jnp.concatenate([key, value], axis=0)).astype(BF16)


def project(tokens, weight_t, bias, gain, shift, cosine, sine, first, count, held):
    length, model_width = tokens.shape
    columns = weight_t.shape[0]
    width = columns // 3
    heads = width // HEAD_DIM
    half = HEAD_DIM // 2
    tile = CHUNK
    fixed = lambda i: (0, 0)
    down = lambda i: (first + i, 0)
    across = lambda i: (0, first + i)
    inputs = [tokens, weight_t, bias, gain, shift, cosine, sine]
    return pl.pallas_call(
        qkv_kernel,
        name="project",
        cost_estimate=cost(2 * count * tile * model_width * columns, 12 * count * tile * model_width),
        grid=(count,),
        in_specs=[
            pl.BlockSpec((tile, model_width), down),
            pl.BlockSpec((columns, model_width), fixed),
            pl.BlockSpec((columns, 1), fixed),
            pl.BlockSpec((1, model_width), fixed),
            pl.BlockSpec((1, model_width), fixed),
            pl.BlockSpec((half, tile), across),
            pl.BlockSpec((half, tile), across),
        ]
        + [pl.BlockSpec(memory_space=pl.ANY)] * len(held),
        out_specs=[
            pl.BlockSpec((tile, model_width), down),
            pl.BlockSpec((width, tile), across),
            pl.BlockSpec((width, tile), across),
            pl.BlockSpec((width, tile), across),
            pl.BlockSpec((heads, tile, 2 * HEAD_DIM), lambda i: (0, first + i, 0)),
        ],
        out_shape=[
            jax.ShapeDtypeStruct((length, model_width), BF16),
            jax.ShapeDtypeStruct((width, length), BF16),
            jax.ShapeDtypeStruct((width, length), BF16),
            jax.ShapeDtypeStruct((width, length), BF16),
            jax.ShapeDtypeStruct((heads, length, 2 * HEAD_DIM), BF16),
        ],
        input_output_aliases={len(inputs) + i: i for i in range(len(held))},
        compiler_params=pltpu.CompilerParams(vmem_limit_bytes=VMEM_LIMIT),
    )(*inputs, *held)


def average_kernel(weights_ref, earlier_ref, cotangent_ref, grad_ref, mix_ref, sums_ref):
    @pl.when(pl.program_id(0) == 0)
    def _():
        sums_ref[...] = jnp.zeros_like(sums_ref)

    cotangent = cotangent_ref[...]
    rows, columns = cotangent.shape
    mix = jnp.zeros_like(cotangent)
    for level in range(earlier_ref.shape[0]):
        value = earlier_ref[level].astype(F32)
        weight = weights_ref[level]
        mix = mix + weight * value
        grad_ref[level] = weight * cotangent
        sums_ref[level] += jnp.sum((value * cotangent).reshape(rows // 8, 8, columns), axis=0)
    mix_ref[...] = mix


def average(depth_weights, earlier, cotangent):
    levels, row_count, model_width = earlier.shape
    tile = row_count // 4
    return pl.pallas_call(
        average_kernel,
        name="average",
        cost_estimate=cost(6 * earlier.size, 6 * earlier.size + 8 * cotangent.size),
        grid_spec=pltpu.PrefetchScalarGridSpec(
            num_scalar_prefetch=1,
            grid=(4,),
            in_specs=[
                pl.BlockSpec((levels, tile, model_width), lambda i, w: (0, i, 0)),
                pl.BlockSpec((tile, model_width), lambda i, w: (i, 0)),
            ],
            out_specs=[
                pl.BlockSpec((levels, tile, model_width), lambda i, w: (0, i, 0)),
                pl.BlockSpec((tile, model_width), lambda i, w: (i, 0)),
                pl.BlockSpec((levels, 8, model_width), lambda i, w: (0, 0, 0)),
            ],
        ),
        out_shape=[
            jax.ShapeDtypeStruct(earlier.shape, F32),
            jax.ShapeDtypeStruct(cotangent.shape, F32),
            jax.ShapeDtypeStruct((levels, 8, model_width), F32),
        ],
        compiler_params=pltpu.CompilerParams(vmem_limit_bytes=VMEM_LIMIT),
    )(depth_weights, earlier, cotangent)


def last_mask(odd, rows):
    row = lax.broadcasted_iota(jnp.int32, (rows, BLOCK), 0)
    return row < rows - BLOCK * (1 - odd)


def over_chunks(pair, absorb, state):
    state = lax.fori_loop(0, pair // 2, lambda i, s: absorb(2 * i, 2 * CHUNK, s, False), state)
    return lax.cond(
        pair % 2 == 0,
        lambda s: absorb(pair, CHUNK, s, True),
        lambda s: absorb(pair - 1, 2 * CHUNK, s, True),
        state,
    )


def attend_kernel(core_ref, qt_ref, kv_ref, vt_ref, low_ref, full_ref, stat_ref, scores_ref):
    pair = pl.program_id(0)
    odd = core_ref[0] ^ (pair & 1)
    heads = qt_ref.shape[0] // HEAD_DIM
    blank = jnp.zeros((HEAD_DIM, BLOCK), BF16)
    queries = [
        jnp.concatenate([qt_ref[h * HEAD_DIM : (h + 1) * HEAD_DIM, :], blank], axis=0)
        for h in range(heads)
    ]
    fold = lambda value: value.reshape(value.shape[0] // 8, 8, BLOCK)

    def score(step, size, state, masked):
        keys = pl.ds(pl.multiple_of(step * CHUNK, CHUNK), size)
        fresh = []
        for h in range(heads):
            scores = contract(kv_ref[h, keys, :], queries[h], 1, 0)
            if masked:
                scores = jnp.where(last_mask(odd, size), scores, NEG)
            scores_ref[h, keys, :] = scores
            fresh.append(jnp.maximum(state[h], jnp.max(fold(scores), axis=0)))
        return fresh

    def mix(step, size, state, masked):
        keys = pl.ds(pl.multiple_of(step * CHUNK, CHUNK), size)
        fresh = []
        for h in range(heads):
            total, summed = state[h]
            weights = jnp.exp(scores_ref[h, keys, :] - highest[h])
            values = vt_ref[h * HEAD_DIM : (h + 1) * HEAD_DIM, keys]
            fresh.append(
                (
                    total + jnp.sum(fold(weights), axis=0),
                    summed + contract(values, weights.astype(BF16), 1, 0),
                )
            )
        return fresh

    state = [jnp.full((8, BLOCK), NEG, F32) for _ in range(heads)]
    state = over_chunks(pair, score, state)
    highest = [jnp.max(value, axis=0, keepdims=True) for value in state]
    state = [
        (jnp.zeros((8, BLOCK), F32), jnp.zeros((HEAD_DIM, BLOCK), F32)) for _ in range(heads)
    ]
    state = over_chunks(pair, mix, state)
    for h in range(heads):
        total, summed = state[h]
        total = jnp.sum(total, axis=0, keepdims=True)
        attended = summed / total
        full_ref[0, h * HEAD_DIM : (h + 1) * HEAD_DIM, :] = attended
        low_ref[0, h * HEAD_DIM : (h + 1) * HEAD_DIM, :] = attended.astype(BF16)
        stat_ref[0, h : h + 1, :] = highest[h] + jnp.log(total)


def attend(core, qt, kv, vt):
    width, length = qt.shape
    pairs = length // CHUNK
    own = lambda j, core: (0, 2 * j + (core[0] ^ (j & 1)))
    slot = lambda j, core: (j, 0, 0)
    return pl.pallas_call(
        attend_kernel,
        name="attend",
        cost_estimate=cost(
            2 * 2 * BLOCK * BLOCK * BLOCK * 2 * sum(range(1, pairs + 1)) * (width // HEAD_DIM),
            4 * kv.size + 8 * pairs * width * BLOCK,
            CHUNK * BLOCK * sum(range(1, pairs + 1)) * (width // HEAD_DIM),
        ),
        grid_spec=pltpu.PrefetchScalarGridSpec(
            num_scalar_prefetch=1,
            grid=(pairs,),
            in_specs=[
                pl.BlockSpec((width, BLOCK), own),
                pl.BlockSpec(kv.shape, lambda j, core: (0, 0, 0)),
                pl.BlockSpec(vt.shape, lambda j, core: (0, 0)),
            ],
            out_specs=[
                pl.BlockSpec((1, width, BLOCK), slot),
                pl.BlockSpec((1, width, BLOCK), slot),
                pl.BlockSpec((1, 8, BLOCK), slot),
            ],
            scratch_shapes=[pltpu.VMEM((width // HEAD_DIM, length, BLOCK), F32)],
        ),
        out_shape=[
            jax.ShapeDtypeStruct((pairs, width, BLOCK), BF16),
            jax.ShapeDtypeStruct((pairs, width, BLOCK), F32),
            jax.ShapeDtypeStruct((pairs, 8, BLOCK), F32),
        ],
        compiler_params=pltpu.CompilerParams(vmem_limit_bytes=VMEM_LIMIT),
    )(core, qt, kv, vt)


def retrace_kernel(
    core_ref, qt_ref, grad_ref, full_ref, stat_ref, cos_ref, sin_ref, kv_ref, kt_ref,
    weight_ref, joint_ref, normed_ref, dkv_ref,
):
    step_id = pl.program_id(0)
    pair = pl.num_programs(0) - 1 - step_id
    odd = core_ref[0] ^ (pair & 1)
    width = qt_ref.shape[0]
    heads = width // HEAD_DIM
    half = HEAD_DIM // 2

    @pl.when(step_id == 0)
    def _():
        dkv_ref[...] = jnp.zeros_like(dkv_ref)

    blank = jnp.zeros((HEAD_DIM, BLOCK), BF16)
    lefts, rights, deltas, norms = [], [], [], []
    for h in range(heads):
        rows = slice(h * HEAD_DIM, (h + 1) * HEAD_DIM)
        query = qt_ref[rows, :]
        grad = grad_ref[0, rows, :]
        lefts.append(
            jnp.concatenate(
                [
                    jnp.concatenate([query, blank], axis=1),
                    jnp.concatenate([blank, grad], axis=1),
                ],
                axis=0,
            )
        )
        rights.append(
            jnp.concatenate(
                [
                    jnp.concatenate([blank, query], axis=1),
                    jnp.concatenate([grad, blank], axis=1),
                ],
                axis=0,
            )
        )
        deltas.append(jnp.sum(grad.astype(F32) * full_ref[0, rows, :], axis=0, keepdims=True))
        norms.append(stat_ref[0, h : h + 1, :])

    def absorb(step, state, masked):
        keys = pl.ds(pl.multiple_of(step * CHUNK, CHUNK), CHUNK)
        fresh = []
        for h in range(heads):
            both = contract(kv_ref[h, keys, :], lefts[h], 1, 0)
            probs = jnp.exp(both[:, :BLOCK] - norms[h])
            if masked:
                probs = jnp.where(last_mask(odd, CHUNK), probs, 0.0)
            grad_scores = (probs * (both[:, BLOCK:] - deltas[h])).astype(BF16)
            joined = jnp.concatenate([probs.astype(BF16), grad_scores], axis=1)
            dkv_ref[h, keys, :] += contract(joined, rights[h], 1, 1)
            turned = kt_ref[h * HEAD_DIM : (h + 1) * HEAD_DIM, keys]
            fresh.append(state[h] + contract(turned, grad_scores, 1, 0))
        return fresh

    state = [jnp.zeros((HEAD_DIM, BLOCK), F32) for _ in range(heads)]
    state = lax.fori_loop(0, pair, lambda i, s: absorb(i, s, False), state)
    state = absorb(pair, state, True)
    offset = pl.multiple_of(pair * CHUNK, CHUNK)
    cosine = cos_ref[...]
    sine = sin_ref[...]
    column = lax.broadcasted_iota(jnp.int32, (HEAD_DIM, CHUNK), 1) // BLOCK

    for h in range(heads):
        base = h * HEAD_DIM
        doubled = jnp.concatenate([state[h], state[h]], axis=1) * HEAD_DIM ** (-0.5)
        doubled = jnp.where(column == odd, doubled, 0.0)
        turned_back = jnp.transpose(dkv_ref[h, pl.ds(offset, CHUNK), :])
        for part, value in ((0, doubled), (1, turned_back[:HEAD_DIM])):
            former = value[:half]
            latter = value[half:]
            turned = jnp.concatenate(
                [former * cosine + latter * sine, latter * cosine - former * sine], axis=0
            )
            start = part * width + base
            joint_ref[start : start + HEAD_DIM, :] = turned.astype(BF16)
        start = 2 * width + base
        joint_ref[start : start + HEAD_DIM, :] = turned_back[HEAD_DIM:].astype(BF16)
    normed_ref[...] = contract(joint_ref[...], weight_ref[...], 0, 0).astype(BF16)


def retrace(core, qt, grads, full, stats, cosine, sine, kv, kt, weight):
    width, length = qt.shape
    heads = width // HEAD_DIM
    half = HEAD_DIM // 2
    pairs = length // CHUNK
    back = lambda j: pairs - 1 - j
    own = lambda j, core: (0, 2 * back(j) + (core[0] ^ (back(j) & 1)))
    slot = lambda j, core: (back(j), 0, 0)
    across = lambda j, core: (0, back(j))
    return pl.pallas_call(
        retrace_kernel,
        name="retrace",
        cost_estimate=cost(
            5 * 2 * BLOCK * BLOCK * BLOCK * 2 * sum(range(1, pairs + 1)) * heads,
            3 * kv.size + 16 * pairs * width * BLOCK,
            CHUNK * BLOCK * sum(range(1, pairs + 1)) * heads,
        ),
        grid_spec=pltpu.PrefetchScalarGridSpec(
            num_scalar_prefetch=1,
            grid=(pairs,),
            in_specs=[
                pl.BlockSpec((width, BLOCK), own),
                pl.BlockSpec((1, width, BLOCK), slot),
                pl.BlockSpec((1, width, BLOCK), slot),
                pl.BlockSpec((1, 8, BLOCK), slot),
                pl.BlockSpec((half, CHUNK), across),
                pl.BlockSpec((half, CHUNK), across),
                pl.BlockSpec(kv.shape, lambda j, core: (0, 0, 0)),
                pl.BlockSpec(kt.shape, lambda j, core: (0, 0)),
                pl.BlockSpec(weight.shape, lambda j, core: (0, 0)),
            ],
            out_specs=[
                pl.BlockSpec((3 * width, CHUNK), across),
                pl.BlockSpec((CHUNK, weight.shape[1]), lambda j, core: (back(j), 0)),
            ],
            scratch_shapes=[pltpu.VMEM((heads, length, 2 * HEAD_DIM), F32)],
        ),
        out_shape=[
            jax.ShapeDtypeStruct((3 * width, length), BF16),
            jax.ShapeDtypeStruct((length, weight.shape[1]), BF16),
        ],
        compiler_params=pltpu.CompilerParams(vmem_limit_bytes=VMEM_LIMIT),
    )(core, qt, grads, full, stats, cosine, sine, kv, kt, weight)


def after(values, *earlier_values):
    values = tuple(values)
    return lax.optimization_barrier(values + tuple(earlier_values))[: len(values)]


def assemble_kernel(place_ref, *refs):
    down_ref, out_ref = refs[-2:]
    rep = place_ref[1]
    reps = (len(refs) - 2) // 2
    part = out_ref.shape[0]
    for side in range(2):
        @pl.when(pl.program_id(0) == side)
        def _():
            for k in range(reps):
                piece = refs[side * reps + k]
                rows = piece.shape[1]
                target = rep ^ k

                @pl.when(target < reps - 1)
                def _():
                    down_ref[pl.ds(pl.multiple_of(target * rows, rows), rows), :] = piece[0]

                @pl.when(target == reps - 1)
                def _():
                    out_ref[...] = piece[0, :part]


def assemble(place, mine, twin, part):
    owners, rows, columns = mine[0].shape
    reps = len(mine)
    groups = 2 * owners

    def held(side):
        def index(which, z, place):
            moving = (place[0] // 2 + owners - z) % owners
            fixed = (place[0] // 2 + owners - (owners - 1) * (1 - side)) % owners
            return (jnp.where(which == side, moving, fixed), 0, 0)

        return pl.BlockSpec((1, rows, columns), index)

    device = lambda which, z, place: 2 * z + (which ^ (place[0] % 2))
    target = lambda which, z, place: (device(which, z, place), 0)
    return pl.pallas_call(
        assemble_kernel,
        name="assemble",
        grid_spec=pltpu.PrefetchScalarGridSpec(
            num_scalar_prefetch=1,
            grid=(2, owners),
            in_specs=[held(0)] * reps + [held(1)] * reps,
            out_specs=[
                pl.BlockSpec(((reps - 1) * rows, columns), target),
                pl.BlockSpec((part, columns), target),
            ],
        ),
        out_shape=[
            jax.ShapeDtypeStruct((groups * (reps - 1) * rows, columns), BF16),
            jax.ShapeDtypeStruct((groups * part, columns), BF16),
        ],
        compiler_params=pltpu.CompilerParams(vmem_limit_bytes=VMEM_LIMIT),
    )(place, *mine, *twin)


def swap_core(value):
    groups = lax.axis_size("shard")
    return lax.ppermute(value, "shard", [(i, i ^ 1) for i in range(groups)])


def shift_owner(value, distance):
    groups = lax.axis_size("shard")
    step = 2 * distance
    return lax.ppermute(value, "shard", [(i, (i + step) % groups) for i in range(groups)])


def cross_rep(value, mask):
    return lax.ppermute(value, "rep", [(i, i ^ mask) for i in range(lax.axis_size("rep"))])


def pick(stacked, index, axis=0):
    return lax.dynamic_index_in_dim(stacked, index, axis, keepdims=False)


def add_low(*values):
    total = values[0].astype(F32)
    for value in values[1:]:
        total = total + value.astype(F32)
    return total.astype(BF16)


def fold_core(partial_sums, core):
    halves = partial_sums.reshape((-1, 2) + partial_sums.shape[1:])
    received = swap_core(pick(halves, 1 - core, 1))
    return add_low(pick(halves, core, 1), received)


def rep_parts(value):
    reps = lax.axis_size("rep")
    owners, rows, columns = value.shape
    return value.reshape(owners, reps, rows // reps, columns)


def send_rep(value):
    rep = lax.axis_index("rep")
    parts = rep_parts(value)
    return [cross_rep(pick(parts, rep ^ k, 1), k) for k in range(1, lax.axis_size("rep"))]


def pick_parts(value):
    rep = lax.axis_index("rep")
    parts = rep_parts(value)
    return [pick(parts, rep ^ k, 1) for k in range(lax.axis_size("rep"))]


def join_rep(value, received):
    return add_low(pick(rep_parts(value), lax.axis_index("rep"), 1), *received)


def unpack_kernel(rep_ref, *refs):
    reps = 4
    pieces = refs[: 3 * reps]
    in_ref, out_ref, qkv_ref, down_ref = refs[3 * reps : 3 * reps + 4]
    line_refs = refs[3 * reps + 4 :]
    hidden_width = in_ref.shape[1]
    model_width = out_ref.shape[1]
    columns = qkv_ref.shape[1] // 3
    owners = down_ref.shape[0] // in_ref.shape[0]
    width = columns // owners
    for k in range(reps):
        pair, joint, down = pieces[k::reps]
        rows = pair.shape[0]
        first = pl.multiple_of((rep_ref[0] ^ k) * rows, 8)
        own = pl.ds(first, rows)
        in_ref[own, :] = pair[:, :hidden_width].astype(F32)
        out_ref[own, :] = pair[:, hidden_width:].astype(F32)
        whole = joint[:, : 3 * columns].astype(F32)
        for part in range(3):
            qkv_ref[own, part * columns : (part + 1) * columns] = jnp.concatenate(
                [
                    whole[:, (3 * z + part) * width : (3 * z + part + 1) * width]
                    for z in range(owners)
                ],
                axis=1,
            )

        @pl.when(rep_ref[0] == k)
        def _():
            part = line_refs[0].shape[1] // 2
            lines = joint[:, 3 * columns :].astype(F32)
            row = 0
            for line_ref in line_refs:
                count = line_ref.shape[1] // part
                line_ref[...] = jnp.concatenate(
                    [lines[row + i : row + i + 1, :part] for i in range(count)], axis=1
                )
                row += count

        for z in range(owners):
            block = pl.ds(pl.multiple_of(owners * first + z * rows, 8), rows)
            down_ref[block, :] = down[:, z * model_width : (z + 1) * model_width].astype(F32)


def unpack(rep, pair, joint, down, widths, counts):
    hidden_width, model_width, columns = widths
    pieces = [*pair, *joint, *down]
    rows = len(pair) * pair[0].shape[0]
    owners = model_width * 3 // columns
    shapes = [
        (rows, hidden_width),
        (rows, model_width),
        (rows, 3 * model_width),
        (owners * rows, model_width),
    ] + [(1, count * rows) for count in counts]
    whole = pl.BlockSpec(memory_space=pltpu.VMEM)
    return pl.pallas_call(
        unpack_kernel,
        name="unpack",
        in_specs=[pl.BlockSpec(memory_space=pltpu.SMEM)] + [whole] * len(pieces),
        out_specs=[whole] * len(shapes),
        out_shape=[jax.ShapeDtypeStruct(shape, F32) for shape in shapes],
        compiler_params=pltpu.CompilerParams(vmem_limit_bytes=VMEM_LIMIT),
    )(rep, *pieces)


def split_depth(value):
    high = lax.reduce_precision(value, 8, 7)
    return jnp.concatenate([high, value - high]).astype(BF16)


def join_depth(value):
    value = value.astype(F32)
    half = value.shape[0] // 2
    return value[:half] + value[half:]


def add_ordered(values, index_of):
    stacked = jnp.stack(values)
    total = pick(stacked, index_of(0))
    for sender in range(1, len(values)):
        total = total + pick(stacked, index_of(sender))
    return total


def every_rep(value):
    return [value] + [cross_rep(value, k) for k in range(1, lax.axis_size("rep"))]


def exchange_owner(value, owner):
    owners = value.shape[0]
    received = [pick(value, owner)]
    for k in range(1, owners):
        received.append(shift_owner(pick(value, (owner + k) % owners), k))
    return received


def middle_kernel(
    core_ref, weights_ref, mixed_ref, x_ref, cotangent_ref, w_out_ref, b_out_ref, gain_ref,
    shift_ref, w_in_ref, b_in_ref, grad_ref,
    middle_ref, low_ref, active_ref, hidden_ref, total_ref, branch_ref, send_ref,
    sums_ref, hidden_sums_ref, plain_ref, scale_ref, back_ref,
):
    step = pl.program_id(0)
    core = core_ref[0]
    owners = mixed_ref.shape[0] // 2
    width = mixed_ref.shape[1]

    @pl.when(step == 0)
    def _():
        for half in range(2):
            rows = slice(half * BLOCK, (half + 1) * BLOCK)
            mixed = jnp.concatenate(
                [mixed_ref[2 * z + (core ^ half)] for z in range(owners)], axis=0
            )
            branch = contract(mixed, w_out_ref[...], 0, 0) + b_out_ref[...]
            middle = x_ref[rows, :].astype(F32) + branch
            middle_ref[rows, :] = middle
            center = middle - jnp.mean(middle, axis=-1, keepdims=True)
            scale = lax.rsqrt(jnp.mean(center * center, axis=-1, keepdims=True) + EPSILON)
            plain = center * scale
            scale_ref[rows, :] = jnp.broadcast_to(scale, (BLOCK, scale_ref.shape[1]))
            plain_ref[rows, :] = plain
            low_ref[rows, :] = (plain * gain_ref[...] + shift_ref[...]).astype(BF16)
        back_ref[...] = jnp.zeros_like(back_ref)

    hidden = contract(low_ref[...], w_in_ref[...], 1, 0) + b_in_ref[...]
    square = hidden * hidden
    bend = math.sqrt(2 / math.pi)
    turned = jnp.tanh(hidden * (bend + (bend * 0.044715) * square))
    share = 0.5 + 0.5 * turned
    active_ref[...] = (hidden * share).astype(BF16)
    slope = (0.5 * hidden) * (1.0 - turned * turned) * (bend + (3 * bend * 0.044715) * square)
    grad = (grad_ref[...].astype(F32) * (share + slope)).astype(BF16)
    hidden_ref[...] = grad
    hidden_sums_ref[...] = jnp.sum(grad.astype(F32), axis=0, keepdims=True)
    back_ref[...] += contract(grad, w_in_ref[...], 1, 1)

    @pl.when(step == pl.num_programs(0) - 1)
    def _():
        weight = weights_ref[4]
        sums = [jnp.zeros((1, back_ref.shape[1]), F32)] * 3
        for half in range(2):
            rows = slice(half * BLOCK, (half + 1) * BLOCK)
            back = back_ref[rows, :]
            plain = plain_ref[rows, :]
            scaled = back * gain_ref[...]
            total = weight * cotangent_ref[rows, :] + scale_ref[rows, :1] * (
                scaled
                - jnp.mean(scaled, axis=-1, keepdims=True)
                - plain * jnp.mean(scaled * plain, axis=-1, keepdims=True)
            )
            total_ref[rows, :] = total
            low = total.astype(BF16)
            branch_ref[rows, :] = low
            mixed = contract(w_out_ref[...], low, 1, 1).astype(BF16)
            for z in range(owners):
                send_ref[2 * z + (core ^ half)] = mixed[z * width : (z + 1) * width, :]
            for i, value in enumerate((low.astype(F32), back * plain, back)):
                sums[i] = sums[i] + jnp.sum(value, axis=0, keepdims=True)
        for i in range(3):
            sums_ref[i : i + 1, :] = sums[i]


def middle_part(
    core, depth_weights, mixed, x, cotangent, w_out, b_out, gain, shift, w_in, b_in, grad_active
):
    rows, model_width = x.shape
    hidden_width = w_in.shape[1]
    chunk = CHUNK
    whole = lambda value: pl.BlockSpec(value.shape, lambda j, *_: (0,) * value.ndim)
    across = pl.BlockSpec((rows, chunk), lambda j, *_: (0, j))
    line = pl.BlockSpec((1, chunk), lambda j, *_: (0, j))
    shapes = [
        jax.ShapeDtypeStruct((rows, model_width), F32),
        jax.ShapeDtypeStruct((rows, model_width), BF16),
        jax.ShapeDtypeStruct((rows, hidden_width), BF16),
        jax.ShapeDtypeStruct((rows, hidden_width), BF16),
        jax.ShapeDtypeStruct((rows, model_width), F32),
        jax.ShapeDtypeStruct((rows, model_width), BF16),
        jax.ShapeDtypeStruct(mixed.shape, BF16),
        jax.ShapeDtypeStruct((8, model_width), F32),
        jax.ShapeDtypeStruct((1, hidden_width), F32),
    ]
    out_specs = [whole(shape) for shape in shapes]
    out_specs[2] = out_specs[3] = across
    out_specs[8] = line
    return pl.pallas_call(
        middle_kernel,
        name="middle",
        cost_estimate=cost(
            4 * rows * model_width * (hidden_width + model_width),
            2 * w_in.size + 8 * grad_active.size,
            grad_active.size,
        ),
        grid_spec=pltpu.PrefetchScalarGridSpec(
            num_scalar_prefetch=2,
            grid=(hidden_width // chunk,),
            in_specs=[
                whole(mixed),
                whole(x),
                whole(cotangent),
                whole(w_out),
                whole(b_out),
                whole(gain),
                whole(shift),
                pl.BlockSpec((model_width, chunk), lambda j, *_: (0, j)),
                line,
                across,
            ],
            out_specs=out_specs,
            scratch_shapes=[
                pltpu.VMEM((rows, model_width), F32),
                pltpu.VMEM((rows, 128), F32),
                pltpu.VMEM((rows, model_width), F32),
            ],
        ),
        out_shape=shapes,
        compiler_params=pltpu.CompilerParams(vmem_limit_bytes=VMEM_LIMIT),
    )(
        core, depth_weights, mixed, x, cotangent, w_out, b_out, gain, shift, w_in, b_in,
        grad_active,
    )


def weight_kernel(
    core_ref, weights_ref, low_ref, hidden_ref, mixed_ref, branch_ref, active_ref, down_grad_ref,
    w_down_ref, b_down_ref, middle_ref, mix_ref, cotangent_ref,
    own_ref, other_ref, down_ref, layer_ref, depth_ref, full_ref, turned_ref, total_ref,
):
    step = pl.program_id(0)
    core = core_ref[0]
    owners, part, _ = own_ref.shape

    @pl.when(step == 0)
    def _():
        turned_ref[...] = jnp.transpose(low_ref[...].astype(F32)).astype(BF16)
        total_ref[...] = middle_ref[...] + b_down_ref[...]

    @pl.when(step < pl.num_programs(0) - 1)
    def _():
        full_ref[...] = contract(turned_ref[...], hidden_ref[...], 1, 0).astype(BF16)
        total_ref[...] += contract(active_ref[...], w_down_ref[...], 1, 0)
        down_ref[...] = contract(active_ref[...], down_grad_ref[...], 0, 0).astype(BF16)

    @pl.when(step == pl.num_programs(0) - 1)
    def _():
        product = 0.0
        for half in range(2):
            mixed = jnp.concatenate(
                [mixed_ref[2 * z + (core ^ half)] for z in range(owners)], axis=0
            )
            rows = slice(half * BLOCK, (half + 1) * BLOCK)
            product = product + contract(mixed, branch_ref[rows, :], 1, 0)
        full_ref[...] = product.astype(BF16)
        result = total_ref[...]
        layer_ref[...] = weights_ref[4] * result + mix_ref[...]
        depth = (result * cotangent_ref[...]).reshape(-1, 8, result.shape[1])
        depth_ref[...] = jnp.sum(depth, axis=0)

    for z in range(owners):
        for side, ref in ((0, own_ref), (1, other_ref)):
            start = pl.multiple_of((2 * z + (core ^ side)) * part, part)
            ref[z] = full_ref[pl.ds(start, part), :]


def weight_sums(
    core, depth_weights, low, hidden, mixed, branch, active, down_grad, w_down, b_down, middle,
    mix, cotangent,
):
    rows, model_width = low.shape
    owners = mixed.shape[0] // 2
    part = model_width // (2 * owners)
    steps = hidden.shape[1] // model_width
    whole = lambda value: pl.BlockSpec(value.shape, lambda j, *_: (0,) * value.ndim)
    chunk = pl.BlockSpec((rows, model_width), lambda j, *_: (0, jnp.minimum(j, steps - 1)))
    square = pl.BlockSpec(
        (model_width, model_width), lambda j, *_: (jnp.minimum(j, steps - 1), 0)
    )
    target = pl.BlockSpec((owners, part, model_width), lambda j, *_: (0, 0, j))
    shape = jax.ShapeDtypeStruct((owners, part, (steps + 1) * model_width), BF16)
    depth = jax.ShapeDtypeStruct((8, model_width), F32)
    return pl.pallas_call(
        weight_kernel,
        name="weight_sums",
        grid_spec=pltpu.PrefetchScalarGridSpec(
            num_scalar_prefetch=2,
            grid=(steps + 1,),
            in_specs=[
                whole(low), chunk, whole(mixed), whole(branch), chunk, whole(down_grad),
                square, whole(b_down), whole(middle), whole(mix), whole(cotangent),
            ],
            out_specs=[target, target, square, whole(middle), whole(depth)],
            scratch_shapes=[
                pltpu.VMEM((model_width, model_width), BF16),
                pltpu.VMEM((model_width, rows), BF16),
                pltpu.VMEM((rows, model_width), F32),
            ],
        ),
        out_shape=[
            shape,
            shape,
            jax.ShapeDtypeStruct((steps * model_width, model_width), BF16),
            jax.ShapeDtypeStruct(middle.shape, F32),
            depth,
        ],
        compiler_params=pltpu.CompilerParams(vmem_limit_bytes=VMEM_LIMIT),
    )(
        core, depth_weights, low, hidden, mixed, branch, active, down_grad, w_down, b_down,
        middle, mix, cotangent,
    )


def joint_kernel(
    core_ref, plain_ref, joint_ref, weight_ref, gain_ref, shift_ref,
    own_ref, other_ref, sums_ref, lines_ref, product_ref, full_ref,
):
    step = pl.program_id(0)
    core = core_ref[0]
    owners, part, columns = own_ref.shape
    joint = joint_ref[...]
    product = contract(joint, plain_ref[...], 1, 0)
    line = contract(jnp.ones((8, joint.shape[1]), BF16), joint, 1, 1)

    @pl.when(step == 0)
    def _():
        product_ref[...] = product
        lines_ref[...] = line

    @pl.when(step > 0)
    def _():
        product_ref[...] += product
        lines_ref[...] += line

    @pl.when(step == pl.num_programs(0) - 1)
    def _():
        total = product_ref[...]
        sums = jnp.transpose(lines_ref[...])[:, :1]
        weight = weight_ref[...].astype(F32)
        sums_ref[0:1, :] = jnp.sum(total * weight, axis=0, keepdims=True)
        sums_ref[1:2, :] = jnp.sum(sums * weight, axis=0, keepdims=True)
        full_ref[...] = jnp.transpose(gain_ref[...] * total + shift_ref[...] * sums).astype(BF16)
        for z in range(owners):
            for side, ref in ((0, own_ref), (1, other_ref)):
                start = pl.multiple_of((2 * z + (core ^ side)) * part, part)
                ref[z] = full_ref[pl.ds(start, part), :]


def joint_part(core, plain, joint_t, weight_t, gain, shift):
    length, model_width = plain.shape
    columns = joint_t.shape[0]
    owners = length // CHUNK // 2
    part = model_width // (2 * owners)
    whole = lambda value: pl.BlockSpec(value.shape, lambda j, core: (0,) * value.ndim)
    shapes = [
        jax.ShapeDtypeStruct((owners, part, columns), BF16),
        jax.ShapeDtypeStruct((owners, part, columns), BF16),
        jax.ShapeDtypeStruct((8, model_width), F32),
        jax.ShapeDtypeStruct((8, columns), F32),
    ]
    return pl.pallas_call(
        joint_kernel,
        name="joint_part",
        grid_spec=pltpu.PrefetchScalarGridSpec(
            num_scalar_prefetch=1,
            grid=(length // CHUNK,),
            in_specs=[
                pl.BlockSpec((CHUNK, model_width), lambda j, core: (j, 0)),
                pl.BlockSpec((columns, CHUNK), lambda j, core: (0, j)),
                whole(weight_t),
                whole(gain),
                whole(shift),
            ],
            out_specs=[whole(shape) for shape in shapes],
            scratch_shapes=[
                pltpu.VMEM((columns, model_width), F32),
                pltpu.VMEM((model_width, columns), BF16),
            ],
        ),
        out_shape=shapes,
        compiler_params=pltpu.CompilerParams(vmem_limit_bytes=VMEM_LIMIT),
    )(core, plain, joint_t, weight_t, gain, shift)


def head_split_device(
    block_in,
    earlier,
    cotangent,
    qkv_weight,
    out_weight,
    in_weight,
    down_weight,
    qk_bias,
    value_bias,
    out_bias,
    in_bias,
    down_bias,
    gain_one,
    shift_one,
    gain_two,
    shift_two,
    depth_weights,
):
    row_count, model_width = block_in.shape
    hidden_width = in_weight.shape[1]
    groups = lax.axis_size("shard")
    owners = groups // 2
    width = model_width // owners
    part = model_width // groups
    length = row_count * groups
    half = HEAD_DIM // 2
    member = lax.axis_index("shard")
    owner = member // 2
    core = member % 2

    pieces = qkv_weight.astype(BF16).reshape(part, 3, owners, width)
    pieces = jnp.transpose(pieces, (2, 0, 1, 3)).reshape(owners, part, 3 * width)
    vectors = (
        qk_bias, value_bias, gain_one, shift_one,
        out_bias, in_bias, down_bias, gain_two, shift_two,
    )
    late = lax.optimization_barrier(jnp.concatenate(vectors))
    early, late = late[: 5 * part], late[5 * part :]
    half_late = late.shape[0] // 2
    rows = [early, late[:half_late], late[half_late:]]
    rows = jnp.stack([jnp.pad(row, (0, 3 * width - row.shape[0])) for row in rows])
    early = jnp.pad(rows.astype(BF16), ((0, 5), (0, 0)))
    early = jnp.broadcast_to(early, (owners, 8, 3 * width))
    packets = exchange_owner(jnp.concatenate([pieces, early], axis=1), owner)
    packet = jnp.stack(packets)
    other_packet = swap_core(packet)

    tokens = lax.all_gather(block_in, "shard", axis=0, tiled=True)
    grad_earlier, mix, depth_sums = average(depth_weights, earlier, cotangent)

    by_core = jnp.stack([packet, other_packet])
    packet = jnp.stack(
        [
            lax.dynamic_slice(
                by_core,
                (core ^ (d % 2), (owner - d // 2) % owners, 0, 0),
                (1, 1, part + 8, 3 * width),
            )[0, 0]
            for d in range(groups)
        ]
    )
    w_own = packet[:, :part].reshape(model_width, 3 * width)
    early = packet[:, part].astype(F32)
    late = packet[:, part + 1 : part + 3, :half_late].astype(F32).reshape(groups, -1)
    b_qk = early[:, : 2 * part].reshape(2 * model_width)
    b_value = early[:, 2 * part : 3 * part].reshape(model_width)
    g_one = early[:, 3 * part : 4 * part].reshape(1, model_width)
    s_one = early[:, 4 * part : 5 * part].reshape(1, model_width)
    b_joint = jnp.concatenate([b_qk, b_value]).reshape(3, owners, width)
    b_own = lax.dynamic_index_in_dim(b_joint, owner, 1, keepdims=False).reshape(3 * width, 1)
    w_turned = jnp.transpose(w_own)

    freqs = 10000.0 ** (-jnp.arange(half, dtype=F32) / half)
    angles = freqs[:, None] * jnp.arange(length, dtype=jnp.int32).astype(F32)[None, :]
    cosine = jnp.cos(angles)
    sine = jnp.sin(angles)
    core_index = core.astype(jnp.int32).reshape(1)

    hidden_part = hidden_width // groups
    share = hidden_part // 3
    row = lambda first, size: late[:, first : first + size].reshape(1, groups * size)
    b_out = row(0, part)
    b_in = row(part, hidden_part)
    b_down = row(part + hidden_part, part)
    g_two = row(2 * part + hidden_part, part)
    s_two = row(3 * part + hidden_part, part)
    last = jnp.pad(out_weight.astype(BF16), ((0, share - part), (0, 0)))
    rep = lax.axis_index("rep")
    tail_packet = lax.dynamic_slice_in_dim(
        jnp.concatenate([down_weight.astype(BF16), last], axis=0), rep * share, share, 0
    )
    tokens, w_turned, b_own, cosine, sine, mix, tail_packet, in_packet = after(
        (tokens, w_turned, b_own, cosine, sine, mix, tail_packet, in_weight.astype(BF16)),
        grad_earlier,
        depth_sums,
    )
    tail_parts = [tail_packet] + [shift_owner(tail_packet, k) for k in range(1, owners)]
    states = project(tokens, w_turned, b_own, g_one, s_one, cosine, sine, 0, groups, ())
    plain_all, qt, kt, vt, kv, *tail_parts = lax.optimization_barrier((*states, *tail_parts))
    grad_result = depth_weights[4] * cotangent
    down_grad = grad_result.astype(BF16)
    tail_stack = jnp.stack(tail_parts)
    qt, tail_stack, in_packet, down_grad = lax.optimization_barrier(
        (qt, tail_stack, in_packet, down_grad)
    )
    w_in = lax.all_gather(in_packet, "shard", axis=0, tiled=True)
    tail_mine = every_rep(tail_stack)
    mixed_own, attended, stats = attend(core_index, qt, kv, vt)
    stats, *tail_mine = lax.optimization_barrier((stats, *tail_mine))
    mixed_two = lax.all_to_all(mixed_own, "shard", 0, 0)
    tail_other = [swap_core(value) for value in tail_mine]
    w_down, w_out = assemble(
        jnp.stack([member, rep]).astype(jnp.int32), tail_mine, tail_other, part
    )
    grad_active = contract(down_grad, w_down, 1, 1).astype(BF16)
    mixed_two, grad_active = lax.optimization_barrier((mixed_two, grad_active))

    inputs = block_in.astype(F32)
    (
        middle, normed_two_low, active, grad_hidden, grad_middle, branch_grad, grad_own,
        token_sums, grad_in_b,
    ) = middle_part(
        core_index, depth_weights, mixed_two, block_in, cotangent, w_out, b_out, g_two, s_two,
        w_in, b_in, grad_active,
    )
    grad_out_b, grad_gain_two, grad_shift_two = (token_sums[i] for i in range(3))
    grad_in_b = grad_in_b[0]
    grad_own = lax.all_to_all(grad_own, "shard", 0, 0)
    folded, twin, grad_down_w, layer_out, last_depth = weight_sums(
        core_index, depth_weights, normed_two_low, grad_hidden, mixed_two, branch_grad, active,
        down_grad, w_down, b_down, middle, mix, cotangent,
    )
    grad_down_b = jnp.sum(down_grad.astype(F32), axis=0)
    grad_own, folded, twin, grad_down_w, last_depth = lax.optimization_barrier(
        (grad_own, folded, twin, grad_down_w, last_depth)
    )
    depth = jnp.concatenate([depth_sums, last_depth[None]], axis=0).sum(axis=(1, 2))
    twin = swap_core(twin)
    down_sums = lax.psum_scatter(grad_down_w, "shard", scatter_dimension=0, tiled=True)
    joint_t, grad_normed = retrace(
        core_index, qt, grad_own, attended, stats, cosine, sine, kv, kt, w_turned
    )
    joint_t, grad_normed, folded, twin, plain_all, depth = lax.optimization_barrier(
        (joint_t, grad_normed, folded, twin, plain_all, depth)
    )
    grad_normed = lax.psum_scatter(
        grad_normed, "shard", scatter_dimension=0, tiled=True
    )
    folded = add_low(folded, twin)
    sent = send_rep(folded)

    own_sums, other_sums, first_sums, joint_sums = joint_part(
        core_index, plain_all, joint_t, w_turned, g_one, s_one
    )
    own_sums, other_sums, first_sums, joint_sums, *sent = lax.optimization_barrier(
        (own_sums, other_sums, first_sums, joint_sums, *sent)
    )
    folded = join_rep(folded, sent)
    arrived = exchange_owner(folded, owner)
    grad_gain_one, grad_shift_one = first_sums[0], first_sums[1]
    joint_sums = joint_sums[0]

    spread_sums = lax.dynamic_update_slice(
        jnp.zeros((3, model_width), F32), joint_sums.reshape(3, width), (0, owner * width)
    ).reshape(3 * model_width)
    vectors = (
        spread_sums[: 2 * model_width],
        spread_sums[2 * model_width :],
        grad_out_b,
        grad_in_b,
        grad_down_b,
        grad_gain_one,
        grad_shift_one,
        grad_gain_two,
        grad_shift_two,
    )
    counts = [vector.shape[0] // model_width for vector in vectors]
    small = jnp.concatenate(
        [
            vector.reshape(groups, count, part).astype(BF16)
            for vector, count in zip(vectors, counts)
        ],
        axis=1,
    )
    small = jnp.pad(small, ((0, 0), (0, part - small.shape[1]), (0, 128 - part)))
    depth = split_depth(depth)
    mark = (part // 4 - 8, 3 * width)
    marked = jnp.zeros((4, part // 4, 128), BF16).at[:, mark[0], : depth.shape[0]].set(depth)
    small = small + marked.reshape(1, part, 128)
    small = small.reshape(owners, 2, part, 128)
    depth_of = lambda value: join_depth(
        value[mark[0], mark[1] : mark[1] + depth.shape[0]]
    )
    with_depth = lambda value, sums: value.at[
        :, mark[0], mark[1] : mark[1] + depth.shape[0]
    ].set(split_depth(sums))
    received = swap_core(
        jnp.concatenate([other_sums, pick(small, 1 - core, 1)], axis=2)
    )
    mixed_sums = add_low(
        jnp.concatenate([own_sums, pick(small, core, 1)], axis=2), received
    )
    depth_sum = join_depth(depth) + depth_of(received[0])
    down_parts = pick_parts(down_sums[None])
    down_rows = part // 4
    columns = 3 * width + 128
    sums_parts = [with_depth(value, depth_sum) for value in pick_parts(mixed_sums)]
    received = [
        cross_rep(
            jnp.concatenate([sums, down.reshape(owners, down_rows, model_width)], axis=2), k
        )
        for k, (sums, down) in enumerate(zip(sums_parts[1:], down_parts[1:]), 1)
    ]
    arrived = lax.optimization_barrier((*arrived, *received))
    arrived, received = arrived[:owners], arrived[owners:]
    pair_pieces = every_rep(add_low(*arrived))
    mixed_sums = add_low(sums_parts[0], *[value[:, :, :columns] for value in received])
    depth_sum = add_ordered(
        [depth_of(value[0]) for value in (sums_parts[0], *received)], lambda k: rep ^ k
    )
    mixed_sums = with_depth(mixed_sums, depth_sum)
    down_sums = add_low(
        down_parts[0].reshape(owners, down_rows, model_width),
        *[value[:, :, columns:] for value in received],
    )
    down_pieces = every_rep(jnp.concatenate([down_sums[k] for k in range(owners)], axis=1))
    arrived = exchange_owner(mixed_sums, owner)
    grad_normed, *arrived = lax.optimization_barrier(
        (grad_normed, *arrived, *pair_pieces, *down_pieces)
    )
    pair_pieces, down_pieces = arrived[owners : 2 * owners], arrived[2 * owners :]
    arrived = arrived[:owners]
    grad_depth = add_ordered(
        [depth_of(value) for value in arrived], lambda k: (owner - k) % owners
    )
    small = add_low(*[value[:, 3 * width :] for value in arrived])
    by_distance = jnp.stack([value[:, : 3 * width] for value in arrived])
    by_owner = [pick(by_distance, (owner - k) % owners) for k in range(owners)]
    sum_in, sum_out, sum_qkv, sum_down, *small_outs = unpack(
        lax.axis_index("rep").astype(jnp.int32).reshape(1),
        pair_pieces,
        every_rep(jnp.concatenate([*by_owner, small], axis=1)),
        down_pieces,
        (hidden_width, model_width, 3 * width),
        counts,
    )
    small_outs = [value[0] for value in small_outs]
    grad_normed = grad_normed.astype(F32)
    center = inputs - jnp.mean(inputs, axis=-1, keepdims=True)
    scale = lax.rsqrt(jnp.mean(center * center, axis=-1, keepdims=True) + EPSILON)
    plain = center * scale
    scaled = grad_normed * g_one
    grad_block = grad_middle + scale * (
        scaled
        - jnp.mean(scaled, axis=-1, keepdims=True)
        - plain * jnp.mean(scaled * plain, axis=-1, keepdims=True)
    )

    return (
        layer_out,
        grad_block,
        grad_earlier,
        sum_qkv,
        sum_out,
        sum_in,
        sum_down,
        *small_outs,
        grad_depth,
    )


def per_device(*args):
    block_in = args[0]
    row_count, model_width = block_in.shape
    groups = lax.axis_size("shard")
    head_count = model_width // HEAD_DIM
    late_size = (4 * model_width + args[5].shape[1]) // groups
    if (
        groups == 8
        and lax.axis_size("rep") == 4
        and row_count == CHUNK
        and head_count % (groups // 2) == 0
        and head_count // (groups // 2) <= 8
        and late_size <= 12 * model_width // groups
        and args[5].shape[1] % (3 * groups) == 0
        and model_width // groups <= args[5].shape[1] // (3 * groups)
    ):
        return head_split_device(*args)
    return generic_device(*args)


def solution(mesh):
    placed = (
        P(("rep", "shard"), None),
        P(None, ("rep", "shard"), None),
        P(("rep", "shard"), None),
        P("shard", None),
        P("shard", None),
        P("shard", None),
        P("shard", None),
        P("shard"),
        P("shard"),
        P("shard"),
        P("shard"),
        P("shard"),
        P("shard"),
        P("shard"),
        P("shard"),
        P("shard"),
        P(),
    )
    return jax.shard_map(
        per_device,
        mesh=mesh,
        in_specs=placed,
        out_specs=(
            P(("rep", "shard"), None),
            P(("rep", "shard"), None),
            P(None, ("rep", "shard"), None),
            P("shard", None),
            P("shard", None),
            P("shard", None),
            P("shard", None),
            P("shard"),
            P("shard"),
            P("shard"),
            P("shard"),
            P("shard"),
            P("shard"),
            P("shard"),
            P("shard"),
            P("shard"),
            P(),
        ),
        check_vma=False,
    )
```

```python
from functools import partial
import math

import jax
import jax.numpy as jnp
from jax import lax
from jax.experimental import pallas as pl
from jax.experimental.pallas import tpu as pltpu
from jax.sharding import PartitionSpec as P

HEAD_DIM = 64
BLOCK = 256


NEG = -1e30
EPSILON = 1e-05


def layer_norm(inputs, gain, shift):
    center = inputs - jnp.mean(inputs, axis=-1, keepdims=True)
    spread = jnp.mean(center * center, axis=-1, keepdims=True)
    return center * lax.rsqrt(spread + EPSILON) * gain + shift


def rotate(inputs, positions):
    row_count = inputs.shape[0]
    split = inputs.reshape(row_count, -1, HEAD_DIM)
    half_dim = HEAD_DIM // 2
    freqs = 10000.0 ** (-jnp.arange(half_dim, dtype=jnp.float32) / half_dim)
    angles = positions.astype(jnp.float32)[:, None] * freqs[None, :]
    cosine = jnp.cos(angles)[:, None, :]
    sine = jnp.sin(angles)[:, None, :]
    former = split[..., :half_dim]
    latter = split[..., half_dim:]
    turned = jnp.concatenate(
        [former * cosine - latter * sine, former * sine + latter * cosine], axis=-1
    )
    return turned.reshape(row_count, -1)


def generic_device(
    block_in,
    earlier,
    cotangent,
    qkv_weight,
    out_weight,
    in_weight,
    down_weight,
    qk_bias,
    value_bias,
    out_bias,
    in_bias,
    down_bias,
    gain_one,
    shift_one,
    gain_two,
    shift_two,
    depth_weights,
):
    bf16 = jnp.bfloat16
    f32 = jnp.float32
    w_qkv, w_out, w_in, w_down, b_qk, b_value, b_out, b_in, b_down, g_one, s_one, g_two, s_two = (
        lax.all_gather(qkv_weight.astype(bf16), "shard", axis=0, tiled=True),
        lax.all_gather(out_weight.astype(bf16), "shard", axis=0, tiled=True),
        lax.all_gather(in_weight.astype(bf16), "shard", axis=0, tiled=True),
        lax.all_gather(down_weight.astype(bf16), "shard", axis=0, tiled=True),
        lax.all_gather(qk_bias.astype(bf16), "shard", axis=0, tiled=True),
        lax.all_gather(value_bias.astype(bf16), "shard", axis=0, tiled=True),
        lax.all_gather(out_bias.astype(bf16), "shard", axis=0, tiled=True),
        lax.all_gather(in_bias.astype(bf16), "shard", axis=0, tiled=True),
        lax.all_gather(down_bias.astype(bf16), "shard", axis=0, tiled=True),
        lax.all_gather(gain_one.astype(bf16), "shard", axis=0, tiled=True),
        lax.all_gather(shift_one.astype(bf16), "shard", axis=0, tiled=True),
        lax.all_gather(gain_two.astype(bf16), "shard", axis=0, tiled=True),
        lax.all_gather(shift_two.astype(bf16), "shard", axis=0, tiled=True),
    )
    row_count, model_width = block_in.shape
    head_count = model_width // HEAD_DIM
    groups = lax.axis_size("shard")
    length = row_count * groups
    window = min(512, length)
    member = lax.axis_index("shard")
    first_row = member * row_count
    last_end = first_row + row_count
    positions = first_row + jnp.arange(row_count, dtype=jnp.int32)
    query_block = positions // BLOCK
    score_scale = HEAD_DIM ** (-0.5)
    needed = (last_end + window - 1) // window
    inputs = block_in.astype(f32)
    normed, norm_back = jax.vjp(layer_norm, inputs, g_one.astype(f32), s_one.astype(f32))
    normed_low = normed.astype(bf16)
    joint_bias = jnp.concatenate([b_qk.astype(f32), b_value.astype(f32)])
    projected = jnp.dot(normed_low, w_qkv, preferred_element_type=f32) + joint_bias
    queries = rotate(projected[:, :model_width], positions).astype(bf16)
    key_rows = rotate(projected[:, model_width : 2 * model_width], positions).astype(bf16)
    values = projected[:, 2 * model_width :].astype(bf16)
    query_heads = queries.reshape(row_count, head_count, HEAD_DIM)

    def masked_scores(key_piece, key_start):
        piece_rows = key_piece.shape[0]
        key_heads = key_piece.reshape(piece_rows, head_count, HEAD_DIM)
        scores = (
            jnp.einsum("qhd,khd->hqk", query_heads, key_heads, preferred_element_type=f32)
            * score_scale
        )
        key_block = (key_start + jnp.arange(piece_rows, dtype=jnp.int32)) // BLOCK
        allowed = key_block[None, :] <= query_block[:, None]
        return (scores, allowed)

    def absorb(running, key_piece, value_piece, key_start):
        highest, denominator, summed = running
        scores, allowed = masked_scores(key_piece, key_start)
        scores = jnp.where(allowed[None], scores, NEG)
        new_high = jnp.maximum(highest, jnp.max(scores, axis=-1))
        rescale = jnp.exp(highest - new_high)
        weights = jnp.where(allowed[None], jnp.exp(scores - new_high[..., None]), 0.0)
        value_heads = value_piece.reshape(-1, head_count, HEAD_DIM)
        summed = summed * rescale[..., None] + jnp.einsum(
            "hqk,khd->hqd", weights.astype(bf16), value_heads, preferred_element_type=f32
        )
        return (new_high, denominator * rescale + jnp.sum(weights, axis=-1), summed)

    start_state = (
        jnp.full((head_count, row_count), NEG, f32),
        jnp.zeros((head_count, row_count), f32),
        jnp.zeros((head_count, row_count, HEAD_DIM), f32),
    )
    key_piece = lax.all_gather(key_rows, "shard", axis=0, tiled=True)
    value_piece = lax.all_gather(values, "shard", axis=0, tiled=True)
    piece_rows = key_piece.shape[0]
    sub_rows = math.gcd(piece_rows, window)
    usable = jnp.clip((last_end + sub_rows - 1) // sub_rows, 0, piece_rows // sub_rows)

    def advance(block_step, state_inner):
        offset = block_step * sub_rows
        return absorb(
            state_inner,
            lax.dynamic_slice_in_dim(key_piece, offset, sub_rows, 0),
            lax.dynamic_slice_in_dim(value_piece, offset, sub_rows, 0),
            offset,
        )

    highest, denominator, summed = lax.fori_loop(0, usable, advance, start_state)
    attended = summed / denominator[..., None]
    log_norm = highest + jnp.log(denominator)
    mixed = jnp.transpose(attended, (1, 0, 2)).reshape(row_count, model_width).astype(bf16)
    branch = jnp.dot(mixed, w_out, preferred_element_type=f32) + b_out.astype(f32)
    middle = inputs + branch
    normed_two, norm_two_back = jax.vjp(layer_norm, middle, g_two.astype(f32), s_two.astype(f32))
    normed_two_low = normed_two.astype(bf16)
    hidden = jnp.dot(normed_two_low, w_in, preferred_element_type=f32) + b_in.astype(f32)
    active_full, gelu_back = jax.vjp(partial(jax.nn.gelu, approximate=True), hidden)
    active = active_full.astype(bf16)
    result = middle + jnp.dot(active, w_down, preferred_element_type=f32) + b_down.astype(f32)
    stacked = earlier.astype(f32)
    layer_out = depth_weights[4] * result
    for level in range(4):
        layer_out = layer_out + depth_weights[level] * stacked[level]
    grad_earlier = depth_weights[:4][:, None, None] * cotangent[None]
    local_depth = jnp.concatenate(
        [jnp.sum(stacked * cotangent[None], axis=(1, 2)), jnp.sum(result * cotangent)[None]]
    )
    grad_depth = lax.psum(local_depth, ("rep", "shard"))
    grad_result = depth_weights[4] * cotangent
    down_grad = grad_result.astype(bf16)
    grad_down_w = jnp.einsum("tf,td->fd", active, down_grad, preferred_element_type=f32)
    grad_down_b = jnp.sum(down_grad.astype(f32), axis=0)
    grad_active = jnp.einsum("td,fd->tf", down_grad, w_down, preferred_element_type=f32)
    grad_hidden = gelu_back(grad_active)[0].astype(bf16)
    grad_in_w = jnp.einsum("td,tf->df", normed_two_low, grad_hidden, preferred_element_type=f32)
    grad_in_b = jnp.sum(grad_hidden.astype(f32), axis=0)
    grad_normed_two = jnp.einsum("tf,df->td", grad_hidden, w_in, preferred_element_type=f32)
    grad_mid_norm, grad_gain_two, grad_shift_two = norm_two_back(grad_normed_two)
    grad_middle = grad_result + grad_mid_norm
    branch_grad = grad_middle.astype(bf16)
    grad_out_w = jnp.einsum("td,te->de", mixed, branch_grad, preferred_element_type=f32)
    grad_out_b = jnp.sum(branch_grad.astype(f32), axis=0)
    grad_mixed = jnp.einsum("te,de->td", branch_grad, w_out, preferred_element_type=f32).astype(
        bf16
    )
    key_all, value_all = (
        lax.all_gather(key_rows, "shard", axis=0, tiled=True),
        lax.all_gather(values, "shard", axis=0, tiled=True),
    )
    grad_heads = grad_mixed.reshape(row_count, head_count, HEAD_DIM)
    delta = jnp.einsum("qhd,hqd->hq", grad_heads.astype(f32), attended)

    def score_grads(key_piece, value_piece, offset, piece_rows):
        scores, allowed = masked_scores(key_piece, offset)
        probs = jnp.where(allowed[None], jnp.exp(scores - log_norm[..., None]), 0.0)
        value_heads = value_piece.reshape(piece_rows, head_count, HEAD_DIM)
        grad_probs = jnp.einsum("qhd,khd->hqk", grad_heads, value_heads, preferred_element_type=f32)
        grad_scores = (probs * (grad_probs - delta[..., None])).astype(bf16)
        return (probs, grad_scores)

    def retrace(block_step, running):
        grad_query, grad_keys, grad_values = running
        offset = block_step * window
        key_piece = lax.dynamic_slice_in_dim(key_all, offset, window, 0)
        value_piece = lax.dynamic_slice_in_dim(value_all, offset, window, 0)
        probs, grad_scores = score_grads(key_piece, value_piece, offset, window)
        key_heads = key_piece.reshape(window, head_count, HEAD_DIM)
        grad_query = grad_query + jnp.einsum(
            "hqk,khd->qhd", grad_scores, key_heads, preferred_element_type=f32
        )
        piece_keys = (
            jnp.einsum("hqk,qhd->khd", grad_scores, query_heads, preferred_element_type=f32)
            * score_scale
        )
        piece_values = jnp.einsum(
            "hqk,qhd->khd", probs.astype(bf16), grad_heads, preferred_element_type=f32
        )
        grad_keys = lax.dynamic_update_slice_in_dim(
            grad_keys, piece_keys.reshape(window, model_width), offset, 0
        )
        grad_values = lax.dynamic_update_slice_in_dim(
            grad_values, piece_values.reshape(window, model_width), offset, 0
        )
        return (grad_query, grad_keys, grad_values)

    start_back = (
        jnp.zeros((row_count, head_count, HEAD_DIM), f32),
        jnp.zeros((length, model_width), f32),
        jnp.zeros((length, model_width), f32),
    )
    grad_query, grad_keys, grad_values = lax.fori_loop(0, needed, retrace, start_back)
    own_keys, own_values = (
        lax.psum_scatter(
            grad_keys.astype(jnp.bfloat16), "shard", scatter_dimension=0, tiled=True
        ).astype(jnp.float32),
        lax.psum_scatter(
            grad_values.astype(jnp.bfloat16), "shard", scatter_dimension=0, tiled=True
        ).astype(jnp.float32),
    )
    grad_q_turned = rotate(grad_query.reshape(row_count, model_width) * score_scale, -positions)
    grad_k_turned = rotate(own_keys, -positions)
    grad_joint = jnp.concatenate([grad_q_turned, grad_k_turned, own_values], axis=1).astype(bf16)
    grad_qkv_w = jnp.einsum("td,tf->df", normed_low, grad_joint, preferred_element_type=f32)
    joint_sums = jnp.sum(grad_joint.astype(f32), axis=0)
    grad_qk_b = joint_sums[: 2 * model_width]
    grad_value_b = joint_sums[2 * model_width :]
    grad_normed = jnp.einsum("tf,df->td", grad_joint, w_qkv, preferred_element_type=f32)
    grad_in_norm, grad_gain_one, grad_shift_one = norm_back(grad_normed)
    grad_block = grad_middle + grad_in_norm
    (
        own_qkv_w,
        own_out_w,
        own_in_w,
        own_down_w,
        own_qk_b,
        own_value_b,
        own_out_b,
        own_in_b,
        own_down_b,
        own_gain_one,
        own_shift_one,
        own_gain_two,
        own_shift_two,
    ) = (
        lax.psum_scatter(
            grad_qkv_w.astype(jnp.bfloat16), "shard", scatter_dimension=0, tiled=True
        ).astype(jnp.float32),
        lax.psum_scatter(
            grad_out_w.astype(jnp.bfloat16), "shard", scatter_dimension=0, tiled=True
        ).astype(jnp.float32),
        lax.psum_scatter(
            grad_in_w.astype(jnp.bfloat16), "shard", scatter_dimension=0, tiled=True
        ).astype(jnp.float32),
        lax.psum_scatter(
            grad_down_w.astype(jnp.bfloat16), "shard", scatter_dimension=0, tiled=True
        ).astype(jnp.float32),
        lax.psum_scatter(
            grad_qk_b.astype(jnp.bfloat16), "shard", scatter_dimension=0, tiled=True
        ).astype(jnp.float32),
        lax.psum_scatter(
            grad_value_b.astype(jnp.bfloat16), "shard", scatter_dimension=0, tiled=True
        ).astype(jnp.float32),
        lax.psum_scatter(
            grad_out_b.astype(jnp.bfloat16), "shard", scatter_dimension=0, tiled=True
        ).astype(jnp.float32),
        lax.psum_scatter(
            grad_in_b.astype(jnp.bfloat16), "shard", scatter_dimension=0, tiled=True
        ).astype(jnp.float32),
        lax.psum_scatter(
            grad_down_b.astype(jnp.bfloat16), "shard", scatter_dimension=0, tiled=True
        ).astype(jnp.float32),
        lax.psum_scatter(
            grad_gain_one.astype(jnp.bfloat16), "shard", scatter_dimension=0, tiled=True
        ).astype(jnp.float32),
        lax.psum_scatter(
            grad_shift_one.astype(jnp.bfloat16), "shard", scatter_dimension=0, tiled=True
        ).astype(jnp.float32),
        lax.psum_scatter(
            grad_gain_two.astype(jnp.bfloat16), "shard", scatter_dimension=0, tiled=True
        ).astype(jnp.float32),
        lax.psum_scatter(
            grad_shift_two.astype(jnp.bfloat16), "shard", scatter_dimension=0, tiled=True
        ).astype(jnp.float32),
    )
    (
        sum_qkv_w,
        sum_out_w,
        sum_in_w,
        sum_down_w,
        sum_qk_b,
        sum_value_b,
        sum_out_b,
        sum_in_b,
        sum_down_b,
        sum_gain_one,
        sum_shift_one,
        sum_gain_two,
        sum_shift_two,
    ) = (
        lax.psum(own_qkv_w.astype(jnp.bfloat16), "rep").astype(jnp.float32),
        lax.psum(own_out_w.astype(jnp.bfloat16), "rep").astype(jnp.float32),
        lax.psum(own_in_w.astype(jnp.bfloat16), "rep").astype(jnp.float32),
        lax.psum(own_down_w.astype(jnp.bfloat16), "rep").astype(jnp.float32),
        lax.psum(own_qk_b.astype(jnp.bfloat16), "rep").astype(jnp.float32),
        lax.psum(own_value_b.astype(jnp.bfloat16), "rep").astype(jnp.float32),
        lax.psum(own_out_b.astype(jnp.bfloat16), "rep").astype(jnp.float32),
        lax.psum(own_in_b.astype(jnp.bfloat16), "rep").astype(jnp.float32),
        lax.psum(own_down_b.astype(jnp.bfloat16), "rep").astype(jnp.float32),
        lax.psum(own_gain_one.astype(jnp.bfloat16), "rep").astype(jnp.float32),
        lax.psum(own_shift_one.astype(jnp.bfloat16), "rep").astype(jnp.float32),
        lax.psum(own_gain_two.astype(jnp.bfloat16), "rep").astype(jnp.float32),
        lax.psum(own_shift_two.astype(jnp.bfloat16), "rep").astype(jnp.float32),
    )
    return (
        layer_out,
        grad_block,
        grad_earlier,
        sum_qkv_w,
        sum_out_w,
        sum_in_w,
        sum_down_w,
        sum_qk_b,
        sum_value_b,
        sum_out_b,
        sum_in_b,
        sum_down_b,
        sum_gain_one,
        sum_shift_one,
        sum_gain_two,
        sum_shift_two,
        grad_depth,
    )


F32 = jnp.float32
BF16 = jnp.bfloat16
CHUNK = 2 * BLOCK
VMEM_LIMIT = 56 * 1024 * 1024


def cost(flops, moved, exps=0):
    return pl.CostEstimate(flops=flops, bytes_accessed=moved, transcendentals=exps)


def contract(left, right, left_dim, right_dim):
    return lax.dot_general(
        left, right, (((left_dim,), (right_dim,)), ((), ())), preferred_element_type=F32
    )


def qkv_kernel(x_ref, weight_ref, bias_ref, gain_ref, shift_ref, cos_ref, sin_ref, *refs):
    plain_ref, qt_ref, kt_ref, vt_ref, kv_ref = refs[-5:]
    x = x_ref[...].astype(F32)
    center = x - jnp.mean(x, axis=-1, keepdims=True)
    spread = jnp.mean(center * center, axis=-1, keepdims=True)
    plain = center * lax.rsqrt(spread + EPSILON)
    plain_ref[...] = plain.astype(BF16)
    low = (plain * gain_ref[...] + shift_ref[...]).astype(BF16)
    width = qt_ref.shape[0]
    half = HEAD_DIM // 2
    joint = contract(weight_ref[...], low, 1, 1) + bias_ref[...]
    cosine = cos_ref[...]
    sine = sin_ref[...]
    for head in range(width // HEAD_DIM):
        base = head * HEAD_DIM
        for part in range(2):
            start = part * width + base
            former = joint[start : start + half]
            latter = joint[start + half : start + HEAD_DIM]
            turned = jnp.concatenate(
                [former * cosine - latter * sine, former * sine + latter * cosine], axis=0
            )
            if part == 0:
                qt_ref[base : base + HEAD_DIM, :] = (turned * HEAD_DIM ** (-0.5)).astype(BF16)
            else:
                kt_ref[base : base + HEAD_DIM, :] = turned.astype(BF16)
                key = turned
        start = 2 * width + base
        value = joint[start : start + HEAD_DIM]
        vt_ref[base : base + HEAD_DIM, :] = value.astype(BF16)
        kv_ref[head] = jnp.transpose(jnp.concatenate([key, value], axis=0)).astype(BF16)


def project(tokens, weight_t, bias, gain, shift, cosine, sine, first, count, held):
    length, model_width = tokens.shape
    columns = weight_t.shape[0]
    width = columns // 3
    heads = width // HEAD_DIM
    half = HEAD_DIM // 2
    tile = CHUNK
    fixed = lambda i: (0, 0)
    down = lambda i: (first + i, 0)
    across = lambda i: (0, first + i)
    inputs = [tokens, weight_t, bias, gain, shift, cosine, sine]
    return pl.pallas_call(
        qkv_kernel,
        name="project",
        cost_estimate=cost(2 * count * tile * model_width * columns, 12 * count * tile * model_width),
        grid=(count,),
        in_specs=[
            pl.BlockSpec((tile, model_width), down),
            pl.BlockSpec((columns, model_width), fixed),
            pl.BlockSpec((columns, 1), fixed),
            pl.BlockSpec((1, model_width), fixed),
            pl.BlockSpec((1, model_width), fixed),
            pl.BlockSpec((half, tile), across),
            pl.BlockSpec((half, tile), across),
        ]
        + [pl.BlockSpec(memory_space=pl.ANY)] * len(held),
        out_specs=[
            pl.BlockSpec((tile, model_width), down),
            pl.BlockSpec((width, tile), across),
            pl.BlockSpec((width, tile), across),
            pl.BlockSpec((width, tile), across),
            pl.BlockSpec((heads, tile, 2 * HEAD_DIM), lambda i: (0, first + i, 0)),
        ],
        out_shape=[
            jax.ShapeDtypeStruct((length, model_width), BF16),
            jax.ShapeDtypeStruct((width, length), BF16),
            jax.ShapeDtypeStruct((width, length), BF16),
            jax.ShapeDtypeStruct((width, length), BF16),
            jax.ShapeDtypeStruct((heads, length, 2 * HEAD_DIM), BF16),
        ],
        input_output_aliases={len(inputs) + i: i for i in range(len(held))},
        compiler_params=pltpu.CompilerParams(vmem_limit_bytes=VMEM_LIMIT),
    )(*inputs, *held)


def average_kernel(weights_ref, earlier_ref, cotangent_ref, grad_ref, mix_ref, sums_ref):
    @pl.when(pl.program_id(0) == 0)
    def _():
        sums_ref[...] = jnp.zeros_like(sums_ref)

    cotangent = cotangent_ref[...]
    rows, columns = cotangent.shape
    mix = jnp.zeros_like(cotangent)
    for level in range(earlier_ref.shape[0]):
        value = earlier_ref[level].astype(F32)
        weight = weights_ref[level]
        mix = mix + weight * value
        grad_ref[level] = weight * cotangent
        sums_ref[level] += jnp.sum((value * cotangent).reshape(rows // 8, 8, columns), axis=0)
    mix_ref[...] = mix


def average(depth_weights, earlier, cotangent):
    levels, row_count, model_width = earlier.shape
    tile = row_count // 4
    return pl.pallas_call(
        average_kernel,
        name="average",
        cost_estimate=cost(6 * earlier.size, 6 * earlier.size + 8 * cotangent.size),
        grid_spec=pltpu.PrefetchScalarGridSpec(
            num_scalar_prefetch=1,
            grid=(4,),
            in_specs=[
                pl.BlockSpec((levels, tile, model_width), lambda i, w: (0, i, 0)),
                pl.BlockSpec((tile, model_width), lambda i, w: (i, 0)),
            ],
            out_specs=[
                pl.BlockSpec((levels, tile, model_width), lambda i, w: (0, i, 0)),
                pl.BlockSpec((tile, model_width), lambda i, w: (i, 0)),
                pl.BlockSpec((levels, 8, model_width), lambda i, w: (0, 0, 0)),
            ],
        ),
        out_shape=[
            jax.ShapeDtypeStruct(earlier.shape, F32),
            jax.ShapeDtypeStruct(cotangent.shape, F32),
            jax.ShapeDtypeStruct((levels, 8, model_width), F32),
        ],
        compiler_params=pltpu.CompilerParams(vmem_limit_bytes=VMEM_LIMIT),
    )(depth_weights, earlier, cotangent)


def last_mask(odd, rows):
    row = lax.broadcasted_iota(jnp.int32, (rows, BLOCK), 0)
    return row < rows - BLOCK * (1 - odd)


def over_chunks(pair, absorb, state):
    state = lax.fori_loop(0, pair // 2, lambda i, s: absorb(2 * i, 2 * CHUNK, s, False), state)
    return lax.cond(
        pair % 2 == 0,
        lambda s: absorb(pair, CHUNK, s, True),
        lambda s: absorb(pair - 1, 2 * CHUNK, s, True),
        state,
    )


def attend_kernel(core_ref, qt_ref, kv_ref, vt_ref, low_ref, full_ref, stat_ref, scores_ref):
    pair = pl.program_id(0)
    odd = core_ref[0] ^ (pair & 1)
    heads = qt_ref.shape[0] // HEAD_DIM
    blank = jnp.zeros((HEAD_DIM, BLOCK), BF16)
    queries = [
        jnp.concatenate([qt_ref[h * HEAD_DIM : (h + 1) * HEAD_DIM, :], blank], axis=0)
        for h in range(heads)
    ]
    fold = lambda value: value.reshape(value.shape[0] // 8, 8, BLOCK)

    def score(step, size, state, masked):
        keys = pl.ds(pl.multiple_of(step * CHUNK, CHUNK), size)
        fresh = []
        for h in range(heads):
            scores = contract(kv_ref[h, keys, :], queries[h], 1, 0)
            if masked:
                scores = jnp.where(last_mask(odd, size), scores, NEG)
            scores_ref[h, keys, :] = scores
            fresh.append(jnp.maximum(state[h], jnp.max(fold(scores), axis=0)))
        return fresh

    def mix(step, size, state, masked):
        keys = pl.ds(pl.multiple_of(step * CHUNK, CHUNK), size)
        fresh = []
        for h in range(heads):
            total, summed = state[h]
            weights = jnp.exp(scores_ref[h, keys, :] - highest[h])
            values = vt_ref[h * HEAD_DIM : (h + 1) * HEAD_DIM, keys]
            fresh.append(
                (
                    total + jnp.sum(fold(weights), axis=0),
                    summed + contract(values, weights.astype(BF16), 1, 0),
                )
            )
        return fresh

    state = [jnp.full((8, BLOCK), NEG, F32) for _ in range(heads)]
    state = over_chunks(pair, score, state)
    highest = [jnp.max(value, axis=0, keepdims=True) for value in state]
    state = [
        (jnp.zeros((8, BLOCK), F32), jnp.zeros((HEAD_DIM, BLOCK), F32)) for _ in range(heads)
    ]
    state = over_chunks(pair, mix, state)
    for h in range(heads):
        total, summed = state[h]
        total = jnp.sum(total, axis=0, keepdims=True)
        attended = summed / total
        full_ref[0, h * HEAD_DIM : (h + 1) * HEAD_DIM, :] = attended
        low_ref[0, h * HEAD_DIM : (h + 1) * HEAD_DIM, :] = attended.astype(BF16)
        stat_ref[0, h : h + 1, :] = highest[h] + jnp.log(total)


def attend(core, qt, kv, vt):
    width, length = qt.shape
    pairs = length // CHUNK
    own = lambda j, core: (0, 2 * j + (core[0] ^ (j & 1)))
    slot = lambda j, core: (j, 0, 0)
    return pl.pallas_call(
        attend_kernel,
        name="attend",
        cost_estimate=cost(
            2 * 2 * BLOCK * BLOCK * BLOCK * 2 * sum(range(1, pairs + 1)) * (width // HEAD_DIM),
            4 * kv.size + 8 * pairs * width * BLOCK,
            CHUNK * BLOCK * sum(range(1, pairs + 1)) * (width // HEAD_DIM),
        ),
        grid_spec=pltpu.PrefetchScalarGridSpec(
            num_scalar_prefetch=1,
            grid=(pairs,),
            in_specs=[
                pl.BlockSpec((width, BLOCK), own),
                pl.BlockSpec(kv.shape, lambda j, core: (0, 0, 0)),
                pl.BlockSpec(vt.shape, lambda j, core: (0, 0)),
            ],
            out_specs=[
                pl.BlockSpec((1, width, BLOCK), slot),
                pl.BlockSpec((1, width, BLOCK), slot),
                pl.BlockSpec((1, 8, BLOCK), slot),
            ],
            scratch_shapes=[pltpu.VMEM((width // HEAD_DIM, length, BLOCK), F32)],
        ),
        out_shape=[
            jax.ShapeDtypeStruct((pairs, width, BLOCK), BF16),
            jax.ShapeDtypeStruct((pairs, width, BLOCK), F32),
            jax.ShapeDtypeStruct((pairs, 8, BLOCK), F32),
        ],
        compiler_params=pltpu.CompilerParams(vmem_limit_bytes=VMEM_LIMIT),
    )(core, qt, kv, vt)


def retrace_kernel(
    core_ref, qt_ref, grad_ref, full_ref, stat_ref, cos_ref, sin_ref, kv_ref, kt_ref,
    weight_ref, joint_ref, normed_ref, dkv_ref,
):
    step_id = pl.program_id(0)
    pair = pl.num_programs(0) - 1 - step_id
    odd = core_ref[0] ^ (pair & 1)
    width = qt_ref.shape[0]
    heads = width // HEAD_DIM
    half = HEAD_DIM // 2

    @pl.when(step_id == 0)
    def _():
        dkv_ref[...] = jnp.zeros_like(dkv_ref)

    blank = jnp.zeros((HEAD_DIM, BLOCK), BF16)
    lefts, rights, deltas, norms = [], [], [], []
    for h in range(heads):
        rows = slice(h * HEAD_DIM, (h + 1) * HEAD_DIM)
        query = qt_ref[rows, :]
        grad = grad_ref[0, rows, :]
        lefts.append(
            jnp.concatenate(
                [
                    jnp.concatenate([query, blank], axis=1),
                    jnp.concatenate([blank, grad], axis=1),
                ],
                axis=0,
            )
        )
        rights.append(
            jnp.concatenate(
                [
                    jnp.concatenate([blank, query], axis=1),
                    jnp.concatenate([grad, blank], axis=1),
                ],
                axis=0,
            )
        )
        deltas.append(jnp.sum(grad.astype(F32) * full_ref[0, rows, :], axis=0, keepdims=True))
        norms.append(stat_ref[0, h : h + 1, :])

    def absorb(step, state, masked):
        keys = pl.ds(pl.multiple_of(step * CHUNK, CHUNK), CHUNK)
        fresh = []
        for h in range(heads):
            both = contract(kv_ref[h, keys, :], lefts[h], 1, 0)
            probs = jnp.exp(both[:, :BLOCK] - norms[h])
            if masked:
                probs = jnp.where(last_mask(odd, CHUNK), probs, 0.0)
            grad_scores = (probs * (both[:, BLOCK:] - deltas[h])).astype(BF16)
            joined = jnp.concatenate([probs.astype(BF16), grad_scores], axis=1)
            dkv_ref[h, keys, :] += contract(joined, rights[h], 1, 1)
            turned = kt_ref[h * HEAD_DIM : (h + 1) * HEAD_DIM, keys]
            fresh.append(state[h] + contract(turned, grad_scores, 1, 0))
        return fresh

    state = [jnp.zeros((HEAD_DIM, BLOCK), F32) for _ in range(heads)]
    state = lax.fori_loop(0, pair, lambda i, s: absorb(i, s, False), state)
    state = absorb(pair, state, True)
    offset = pl.multiple_of(pair * CHUNK, CHUNK)
    cosine = cos_ref[...]
    sine = sin_ref[...]
    column = lax.broadcasted_iota(jnp.int32, (HEAD_DIM, CHUNK), 1) // BLOCK

    for h in range(heads):
        base = h * HEAD_DIM
        doubled = jnp.concatenate([state[h], state[h]], axis=1) * HEAD_DIM ** (-0.5)
        doubled = jnp.where(column == odd, doubled, 0.0)
        turned_back = jnp.transpose(dkv_ref[h, pl.ds(offset, CHUNK), :])
        for part, value in ((0, doubled), (1, turned_back[:HEAD_DIM])):
            former = value[:half]
            latter = value[half:]
            turned = jnp.concatenate(
                [former * cosine + latter * sine, latter * cosine - former * sine], axis=0
            )
            start = part * width + base
            joint_ref[start : start + HEAD_DIM, :] = turned.astype(BF16)
        start = 2 * width + base
        joint_ref[start : start + HEAD_DIM, :] = turned_back[HEAD_DIM:].astype(BF16)
    normed_ref[...] = contract(joint_ref[...], weight_ref[...], 0, 0).astype(BF16)


def retrace(core, qt, grads, full, stats, cosine, sine, kv, kt, weight):
    width, length = qt.shape
    heads = width // HEAD_DIM
    half = HEAD_DIM // 2
    pairs = length // CHUNK
    back = lambda j: pairs - 1 - j
    own = lambda j, core: (0, 2 * back(j) + (core[0] ^ (back(j) & 1)))
    slot = lambda j, core: (back(j), 0, 0)
    across = lambda j, core: (0, back(j))
    return pl.pallas_call(
        retrace_kernel,
        name="retrace",
        cost_estimate=cost(
            5 * 2 * BLOCK * BLOCK * BLOCK * 2 * sum(range(1, pairs + 1)) * heads,
            3 * kv.size + 16 * pairs * width * BLOCK,
            CHUNK * BLOCK * sum(range(1, pairs + 1)) * heads,
        ),
        grid_spec=pltpu.PrefetchScalarGridSpec(
            num_scalar_prefetch=1,
            grid=(pairs,),
            in_specs=[
                pl.BlockSpec((width, BLOCK), own),
                pl.BlockSpec((1, width, BLOCK), slot),
                pl.BlockSpec((1, width, BLOCK), slot),
                pl.BlockSpec((1, 8, BLOCK), slot),
                pl.BlockSpec((half, CHUNK), across),
                pl.BlockSpec((half, CHUNK), across),
                pl.BlockSpec(kv.shape, lambda j, core: (0, 0, 0)),
                pl.BlockSpec(kt.shape, lambda j, core: (0, 0)),
                pl.BlockSpec(weight.shape, lambda j, core: (0, 0)),
            ],
            out_specs=[
                pl.BlockSpec((3 * width, CHUNK), across),
                pl.BlockSpec((CHUNK, weight.shape[1]), lambda j, core: (back(j), 0)),
            ],
            scratch_shapes=[pltpu.VMEM((heads, length, 2 * HEAD_DIM), F32)],
        ),
        out_shape=[
            jax.ShapeDtypeStruct((3 * width, length), BF16),
            jax.ShapeDtypeStruct((length, weight.shape[1]), BF16),
        ],
        compiler_params=pltpu.CompilerParams(vmem_limit_bytes=VMEM_LIMIT),
    )(core, qt, grads, full, stats, cosine, sine, kv, kt, weight)


def after(values, *earlier_values):
    values = tuple(values)
    return lax.optimization_barrier(values + tuple(earlier_values))[: len(values)]


def assemble_kernel(place_ref, *refs):
    down_ref, out_ref = refs[-2:]
    rep = place_ref[1]
    reps = (len(refs) - 2) // 2
    part = out_ref.shape[0]
    for side in range(2):
        @pl.when(pl.program_id(0) == side)
        def _():
            for k in range(reps):
                piece = refs[side * reps + k]
                rows = piece.shape[1]
                target = rep ^ k

                @pl.when(target < reps - 1)
                def _():
                    down_ref[pl.ds(pl.multiple_of(target * rows, rows), rows), :] = piece[0]

                @pl.when(target == reps - 1)
                def _():
                    out_ref[...] = piece[0, :part]


def assemble(place, mine, twin, part):
    owners, rows, columns = mine[0].shape
    reps = len(mine)
    groups = 2 * owners

    def held(side):
        def index(which, z, place):
            moving = (place[0] // 2 + owners - z) % owners
            fixed = (place[0] // 2 + owners - (owners - 1) * (1 - side)) % owners
            return (jnp.where(which == side, moving, fixed), 0, 0)

        return pl.BlockSpec((1, rows, columns), index)

    device = lambda which, z, place: 2 * z + (which ^ (place[0] % 2))
    target = lambda which, z, place: (device(which, z, place), 0)
    return pl.pallas_call(
        assemble_kernel,
        name="assemble",
        grid_spec=pltpu.PrefetchScalarGridSpec(
            num_scalar_prefetch=1,
            grid=(2, owners),
            in_specs=[held(0)] * reps + [held(1)] * reps,
            out_specs=[
                pl.BlockSpec(((reps - 1) * rows, columns), target),
                pl.BlockSpec((part, columns), target),
            ],
        ),
        out_shape=[
            jax.ShapeDtypeStruct((groups * (reps - 1) * rows, columns), BF16),
            jax.ShapeDtypeStruct((groups * part, columns), BF16),
        ],
        compiler_params=pltpu.CompilerParams(vmem_limit_bytes=VMEM_LIMIT),
    )(place, *mine, *twin)


def swap_core(value):
    groups = lax.axis_size("shard")
    return lax.ppermute(value, "shard", [(i, i ^ 1) for i in range(groups)])


def shift_owner(value, distance):
    groups = lax.axis_size("shard")
    step = 2 * distance
    return lax.ppermute(value, "shard", [(i, (i + step) % groups) for i in range(groups)])


def cross_rep(value, mask):
    return lax.ppermute(value, "rep", [(i, i ^ mask) for i in range(lax.axis_size("rep"))])


def pick(stacked, index, axis=0):
    return lax.dynamic_index_in_dim(stacked, index, axis, keepdims=False)


def add_low(*values):
    total = values[0].astype(F32)
    for value in values[1:]:
        total = total + value.astype(F32)
    return total.astype(BF16)


def fold_core(partial_sums, core):
    halves = partial_sums.reshape((-1, 2) + partial_sums.shape[1:])
    received = swap_core(pick(halves, 1 - core, 1))
    return add_low(pick(halves, core, 1), received)


def rep_parts(value):
    reps = lax.axis_size("rep")
    owners, rows, columns = value.shape
    return value.reshape(owners, reps, rows // reps, columns)


def send_rep(value):
    rep = lax.axis_index("rep")
    parts = rep_parts(value)
    return [cross_rep(pick(parts, rep ^ k, 1), k) for k in range(1, lax.axis_size("rep"))]


def pick_parts(value):
    rep = lax.axis_index("rep")
    parts = rep_parts(value)
    return [pick(parts, rep ^ k, 1) for k in range(lax.axis_size("rep"))]


def join_rep(value, received):
    return add_low(pick(rep_parts(value), lax.axis_index("rep"), 1), *received)


def unpack_kernel(rep_ref, *refs):
    reps = 4
    pieces = refs[: 3 * reps]
    in_ref, out_ref, qkv_ref, down_ref = refs[3 * reps : 3 * reps + 4]
    line_refs = refs[3 * reps + 4 :]
    hidden_width = in_ref.shape[1]
    model_width = out_ref.shape[1]
    columns = qkv_ref.shape[1] // 3
    owners = down_ref.shape[0] // in_ref.shape[0]
    width = columns // owners
    for k in range(reps):
        pair, joint, down = pieces[k::reps]
        rows = pair.shape[0]
        first = pl.multiple_of((rep_ref[0] ^ k) * rows, 8)
        own = pl.ds(first, rows)
        in_ref[own, :] = pair[:, :hidden_width].astype(F32)
        out_ref[own, :] = pair[:, hidden_width:].astype(F32)
        whole = joint[:, : 3 * columns].astype(F32)
        for part in range(3):
            qkv_ref[own, part * columns : (part + 1) * columns] = jnp.concatenate(
                [
                    whole[:, (3 * z + part) * width : (3 * z + part + 1) * width]
                    for z in range(owners)
                ],
                axis=1,
            )

        @pl.when(rep_ref[0] == k)
        def _():
            part = line_refs[0].shape[1] // 2
            lines = joint[:, 3 * columns :].astype(F32)
            row = 0
            for line_ref in line_refs:
                count = line_ref.shape[1] // part
                line_ref[...] = jnp.concatenate(
                    [lines[row + i : row + i + 1, :part] for i in range(count)], axis=1
                )
                row += count

        for z in range(owners):
            block = pl.ds(pl.multiple_of(owners * first + z * rows, 8), rows)
            down_ref[block, :] = down[:, z * model_width : (z + 1) * model_width].astype(F32)


def unpack(rep, pair, joint, down, widths, counts):
    hidden_width, model_width, columns = widths
    pieces = [*pair, *joint, *down]
    rows = len(pair) * pair[0].shape[0]
    owners = model_width * 3 // columns
    shapes = [
        (rows, hidden_width),
        (rows, model_width),
        (rows, 3 * model_width),
        (owners * rows, model_width),
    ] + [(1, count * rows) for count in counts]
    whole = pl.BlockSpec(memory_space=pltpu.VMEM)
    return pl.pallas_call(
        unpack_kernel,
        name="unpack",
        in_specs=[pl.BlockSpec(memory_space=pltpu.SMEM)] + [whole] * len(pieces),
        out_specs=[whole] * len(shapes),
        out_shape=[jax.ShapeDtypeStruct(shape, F32) for shape in shapes],
        compiler_params=pltpu.CompilerParams(vmem_limit_bytes=VMEM_LIMIT),
    )(rep, *pieces)


def split_depth(value):
    high = lax.reduce_precision(value, 8, 7)
    return jnp.concatenate([high, value - high]).astype(BF16)


def join_depth(value):
    value = value.astype(F32)
    half = value.shape[0] // 2
    return value[:half] + value[half:]


def add_ordered(values, index_of):
    stacked = jnp.stack(values)
    total = pick(stacked, index_of(0))
    for sender in range(1, len(values)):
        total = total + pick(stacked, index_of(sender))
    return total


def every_rep(value):
    return [value] + [cross_rep(value, k) for k in range(1, lax.axis_size("rep"))]


def exchange_owner(value, owner):
    owners = value.shape[0]
    received = [pick(value, owner)]
    for k in range(1, owners):
        received.append(shift_owner(pick(value, (owner + k) % owners), k))
    return received


def middle_kernel(
    core_ref, weights_ref, mixed_ref, x_ref, cotangent_ref, w_out_ref, b_out_ref, gain_ref,
    shift_ref, w_in_ref, b_in_ref, grad_ref,
    middle_ref, low_ref, active_ref, hidden_ref, total_ref, branch_ref, send_ref,
    sums_ref, hidden_sums_ref, plain_ref, scale_ref, back_ref,
):
    step = pl.program_id(0)
    core = core_ref[0]
    owners = mixed_ref.shape[0] // 2
    width = mixed_ref.shape[1]

    @pl.when(step == 0)
    def _():
        for half in range(2):
            rows = slice(half * BLOCK, (half + 1) * BLOCK)
            mixed = jnp.concatenate(
                [mixed_ref[2 * z + (core ^ half)] for z in range(owners)], axis=0
            )
            branch = contract(mixed, w_out_ref[...], 0, 0) + b_out_ref[...]
            middle = x_ref[rows, :].astype(F32) + branch
            middle_ref[rows, :] = middle
            center = middle - jnp.mean(middle, axis=-1, keepdims=True)
            scale = lax.rsqrt(jnp.mean(center * center, axis=-1, keepdims=True) + EPSILON)
            plain = center * scale
            scale_ref[rows, :] = jnp.broadcast_to(scale, (BLOCK, scale_ref.shape[1]))
            plain_ref[rows, :] = plain
            low_ref[rows, :] = (plain * gain_ref[...] + shift_ref[...]).astype(BF16)
        back_ref[...] = jnp.zeros_like(back_ref)

    hidden = contract(low_ref[...], w_in_ref[...], 1, 0) + b_in_ref[...]
    square = hidden * hidden
    bend = math.sqrt(2 / math.pi)
    turned = jnp.tanh(hidden * (bend + (bend * 0.044715) * square))
    share = 0.5 + 0.5 * turned
    active_ref[...] = (hidden * share).astype(BF16)
    slope = (0.5 * hidden) * (1.0 - turned * turned) * (bend + (3 * bend * 0.044715) * square)
    grad = (grad_ref[...].astype(F32) * (share + slope)).astype(BF16)
    hidden_ref[...] = grad
    hidden_sums_ref[...] = jnp.sum(grad.astype(F32), axis=0, keepdims=True)
    back_ref[...] += contract(grad, w_in_ref[...], 1, 1)

    @pl.when(step == pl.num_programs(0) - 1)
    def _():
        weight = weights_ref[4]
        sums = [jnp.zeros((1, back_ref.shape[1]), F32)] * 3
        for half in range(2):
            rows = slice(half * BLOCK, (half + 1) * BLOCK)
            back = back_ref[rows, :]
            plain = plain_ref[rows, :]
            scaled = back * gain_ref[...]
            total = weight * cotangent_ref[rows, :] + scale_ref[rows, :1] * (
                scaled
                - jnp.mean(scaled, axis=-1, keepdims=True)
                - plain * jnp.mean(scaled * plain, axis=-1, keepdims=True)
            )
            total_ref[rows, :] = total
            low = total.astype(BF16)
            branch_ref[rows, :] = low
            mixed = contract(w_out_ref[...], low, 1, 1).astype(BF16)
            for z in range(owners):
                send_ref[2 * z + (core ^ half)] = mixed[z * width : (z + 1) * width, :]
            for i, value in enumerate((low.astype(F32), back * plain, back)):
                sums[i] = sums[i] + jnp.sum(value, axis=0, keepdims=True)
        for i in range(3):
            sums_ref[i : i + 1, :] = sums[i]


def middle_part(
    core, depth_weights, mixed, x, cotangent, w_out, b_out, gain, shift, w_in, b_in, grad_active
):
    rows, model_width = x.shape
    hidden_width = w_in.shape[1]
    chunk = CHUNK
    whole = lambda value: pl.BlockSpec(value.shape, lambda j, *_: (0,) * value.ndim)
    across = pl.BlockSpec((rows, chunk), lambda j, *_: (0, j))
    line = pl.BlockSpec((1, chunk), lambda j, *_: (0, j))
    shapes = [
        jax.ShapeDtypeStruct((rows, model_width), F32),
        jax.ShapeDtypeStruct((rows, model_width), BF16),
        jax.ShapeDtypeStruct((rows, hidden_width), BF16),
        jax.ShapeDtypeStruct((rows, hidden_width), BF16),
        jax.ShapeDtypeStruct((rows, model_width), F32),
        jax.ShapeDtypeStruct((rows, model_width), BF16),
        jax.ShapeDtypeStruct(mixed.shape, BF16),
        jax.ShapeDtypeStruct((8, model_width), F32),
        jax.ShapeDtypeStruct((1, hidden_width), F32),
    ]
    out_specs = [whole(shape) for shape in shapes]
    out_specs[2] = out_specs[3] = across
    out_specs[8] = line
    return pl.pallas_call(
        middle_kernel,
        name="middle",
        cost_estimate=cost(
            4 * rows * model_width * (hidden_width + model_width),
            2 * w_in.size + 8 * grad_active.size,
            grad_active.size,
        ),
        grid_spec=pltpu.PrefetchScalarGridSpec(
            num_scalar_prefetch=2,
            grid=(hidden_width // chunk,),
            in_specs=[
                whole(mixed),
                whole(x),
                whole(cotangent),
                whole(w_out),
                whole(b_out),
                whole(gain),
                whole(shift),
                pl.BlockSpec((model_width, chunk), lambda j, *_: (0, j)),
                line,
                across,
            ],
            out_specs=out_specs,
            scratch_shapes=[
                pltpu.VMEM((rows, model_width), F32),
                pltpu.VMEM((rows, 128), F32),
                pltpu.VMEM((rows, model_width), F32),
            ],
        ),
        out_shape=shapes,
        compiler_params=pltpu.CompilerParams(vmem_limit_bytes=VMEM_LIMIT),
    )(
        core, depth_weights, mixed, x, cotangent, w_out, b_out, gain, shift, w_in, b_in,
        grad_active,
    )


def down_kernel(
    weights_ref, active_ref, down_grad_ref, w_down_ref, b_down_ref, middle_ref, mix_ref,
    cotangent_ref, down_ref, layer_ref, depth_ref, total_ref,
):
    step = pl.program_id(0)

    @pl.when(step == 0)
    def _():
        total_ref[...] = middle_ref[...] + b_down_ref[...]

    total_ref[...] += contract(active_ref[...], w_down_ref[...], 1, 0)
    down_ref[...] = contract(active_ref[...], down_grad_ref[...], 0, 0).astype(BF16)

    @pl.when(step == pl.num_programs(0) - 1)
    def _():
        result = total_ref[...]
        layer_ref[...] = weights_ref[4] * result + mix_ref[...]
        depth = (result * cotangent_ref[...]).reshape(-1, 8, result.shape[1])
        depth_ref[...] = jnp.sum(depth, axis=0)


def down_part(depth_weights, active, down_grad, w_down, b_down, middle, mix, cotangent):
    rows, model_width = middle.shape
    steps = active.shape[1] // model_width
    whole = lambda value: pl.BlockSpec(value.shape, lambda j, *_: (0,) * value.ndim)
    square = pl.BlockSpec((model_width, model_width), lambda j, *_: (j, 0))
    depth = jax.ShapeDtypeStruct((8, model_width), F32)
    return pl.pallas_call(
        down_kernel,
        name="down_part",
        grid_spec=pltpu.PrefetchScalarGridSpec(
            num_scalar_prefetch=1,
            grid=(steps,),
            in_specs=[
                pl.BlockSpec((rows, model_width), lambda j, *_: (0, j)),
                whole(down_grad), square, whole(b_down), whole(middle), whole(mix),
                whole(cotangent),
            ],
            out_specs=[square, whole(middle), whole(depth)],
            scratch_shapes=[pltpu.VMEM((rows, model_width), F32)],
        ),
        out_shape=[
            jax.ShapeDtypeStruct((steps * model_width, model_width), BF16),
            jax.ShapeDtypeStruct(middle.shape, F32),
            depth,
        ],
        compiler_params=pltpu.CompilerParams(vmem_limit_bytes=VMEM_LIMIT),
    )(depth_weights, active, down_grad, w_down, b_down, middle, mix, cotangent)


def pair_kernel(
    core_ref, low_ref, hidden_ref, mixed_ref, branch_ref,
    low_twin_ref, hidden_twin_ref, mixed_twin_ref, branch_twin_ref,
    own_ref, turned_ref, rows_ref,
):
    step = pl.program_id(0)
    core = core_ref[0]
    owners, part, width = own_ref.shape
    last = pl.num_programs(0) - 1

    @pl.when(step == 0)
    def _():
        for side, ref in ((0, low_ref), (1, low_twin_ref)):
            turned_ref[...] = jnp.transpose(ref[...].astype(F32)).astype(BF16)
            for z in range(owners):
                start = pl.multiple_of((2 * z + core) * part, part)
                rows_ref[side, z * part : (z + 1) * part, :] = turned_ref[pl.ds(start, part), :]

    @pl.when(step < last)
    def _():
        total = contract(rows_ref[0], hidden_ref[...], 1, 0)
        total = total + contract(rows_ref[1], hidden_twin_ref[...], 1, 0)
        own_ref[...] = total.astype(BF16).reshape(owners, part, width)

    @pl.when(step == last)
    def _():
        total = 0.0
        sides = ((core, mixed_ref, branch_ref), (1 - core, mixed_twin_ref, branch_twin_ref))
        for member, ref, grad_ref in sides:
            for half in range(2):
                mixed = jnp.concatenate(
                    [
                        ref[
                            2 * z + (member ^ half),
                            pl.ds(pl.multiple_of(core * part, part), part),
                            :,
                        ]
                        for z in range(owners)
                    ],
                    axis=0,
                )
                rows = slice(half * BLOCK, (half + 1) * BLOCK)
                total = total + contract(mixed, grad_ref[rows, :], 1, 0)
        own_ref[...] = total.astype(BF16).reshape(owners, part, width)


def pair_sums(core, own, twin):
    low, hidden, mixed, branch = own
    rows, model_width = low.shape
    owners = mixed.shape[0] // 2
    part = model_width // (2 * owners)
    steps = hidden.shape[1] // model_width
    whole = lambda value: pl.BlockSpec(value.shape, lambda j, core: (0,) * value.ndim)
    chunk = pl.BlockSpec((rows, model_width), lambda j, core: (0, jnp.minimum(j, steps - 1)))
    one_side = [whole(low), chunk, whole(mixed), whole(branch)]
    return pl.pallas_call(
        pair_kernel,
        name="pair_sums",
        grid_spec=pltpu.PrefetchScalarGridSpec(
            num_scalar_prefetch=1,
            grid=(steps + 1,),
            in_specs=one_side * 2,
            out_specs=pl.BlockSpec((owners, part, model_width), lambda j, core: (0, 0, j)),
            scratch_shapes=[
                pltpu.VMEM((model_width, rows), BF16),
                pltpu.VMEM((2, owners * part, rows), BF16),
            ],
        ),
        out_shape=jax.ShapeDtypeStruct((owners, part, (steps + 1) * model_width), BF16),
        compiler_params=pltpu.CompilerParams(vmem_limit_bytes=VMEM_LIMIT),
    )(core, *own, *twin)


def joint_kernel(
    core_ref, plain_ref, joint_ref, weight_ref, gain_ref, shift_ref,
    own_ref, other_ref, sums_ref, lines_ref, product_ref, full_ref,
):
    step = pl.program_id(0)
    core = core_ref[0]
    owners, part, columns = own_ref.shape
    joint = joint_ref[...]
    product = contract(joint, plain_ref[...], 1, 0)
    line = contract(jnp.ones((8, joint.shape[1]), BF16), joint, 1, 1)

    @pl.when(step == 0)
    def _():
        product_ref[...] = product
        lines_ref[...] = line

    @pl.when(step > 0)
    def _():
        product_ref[...] += product
        lines_ref[...] += line

    @pl.when(step == pl.num_programs(0) - 1)
    def _():
        total = product_ref[...]
        sums = jnp.transpose(lines_ref[...])[:, :1]
        weight = weight_ref[...].astype(F32)
        sums_ref[0:1, :] = jnp.sum(total * weight, axis=0, keepdims=True)
        sums_ref[1:2, :] = jnp.sum(sums * weight, axis=0, keepdims=True)
        full_ref[...] = jnp.transpose(gain_ref[...] * total + shift_ref[...] * sums).astype(BF16)
        for z in range(owners):
            for side, ref in ((0, own_ref), (1, other_ref)):
                start = pl.multiple_of((2 * z + (core ^ side)) * part, part)
                ref[z] = full_ref[pl.ds(start, part), :]


def joint_part(core, plain, joint_t, weight_t, gain, shift):
    length, model_width = plain.shape
    columns = joint_t.shape[0]
    owners = length // CHUNK // 2
    part = model_width // (2 * owners)
    whole = lambda value: pl.BlockSpec(value.shape, lambda j, core: (0,) * value.ndim)
    shapes = [
        jax.ShapeDtypeStruct((owners, part, columns), BF16),
        jax.ShapeDtypeStruct((owners, part, columns), BF16),
        jax.ShapeDtypeStruct((8, model_width), F32),
        jax.ShapeDtypeStruct((8, columns), F32),
    ]
    return pl.pallas_call(
        joint_kernel,
        name="joint_part",
        grid_spec=pltpu.PrefetchScalarGridSpec(
            num_scalar_prefetch=1,
            grid=(length // CHUNK,),
            in_specs=[
                pl.BlockSpec((CHUNK, model_width), lambda j, core: (j, 0)),
                pl.BlockSpec((columns, CHUNK), lambda j, core: (0, j)),
                whole(weight_t),
                whole(gain),
                whole(shift),
            ],
            out_specs=[whole(shape) for shape in shapes],
            scratch_shapes=[
                pltpu.VMEM((columns, model_width), F32),
                pltpu.VMEM((model_width, columns), BF16),
            ],
        ),
        out_shape=shapes,
        compiler_params=pltpu.CompilerParams(vmem_limit_bytes=VMEM_LIMIT),
    )(core, plain, joint_t, weight_t, gain, shift)


def head_split_device(
    block_in,
    earlier,
    cotangent,
    qkv_weight,
    out_weight,
    in_weight,
    down_weight,
    qk_bias,
    value_bias,
    out_bias,
    in_bias,
    down_bias,
    gain_one,
    shift_one,
    gain_two,
    shift_two,
    depth_weights,
):
    row_count, model_width = block_in.shape
    hidden_width = in_weight.shape[1]
    groups = lax.axis_size("shard")
    owners = groups // 2
    width = model_width // owners
    part = model_width // groups
    length = row_count * groups
    half = HEAD_DIM // 2
    member = lax.axis_index("shard")
    owner = member // 2
    core = member % 2

    pieces = qkv_weight.astype(BF16).reshape(part, 3, owners, width)
    pieces = jnp.transpose(pieces, (2, 0, 1, 3)).reshape(owners, part, 3 * width)
    vectors = (
        qk_bias, value_bias, gain_one, shift_one,
        out_bias, in_bias, down_bias, gain_two, shift_two,
    )
    late = lax.optimization_barrier(jnp.concatenate(vectors))
    early, late = late[: 5 * part], late[5 * part :]
    half_late = late.shape[0] // 2
    rows = [early, late[:half_late], late[half_late:]]
    rows = jnp.stack([jnp.pad(row, (0, 3 * width - row.shape[0])) for row in rows])
    early = jnp.pad(rows.astype(BF16), ((0, 5), (0, 0)))
    early = jnp.broadcast_to(early, (owners, 8, 3 * width))
    packets = exchange_owner(jnp.concatenate([pieces, early], axis=1), owner)
    packet = jnp.stack(packets)
    other_packet = swap_core(packet)

    tokens = lax.all_gather(block_in, "shard", axis=0, tiled=True)
    grad_earlier, mix, depth_sums = average(depth_weights, earlier, cotangent)

    by_core = jnp.stack([packet, other_packet])
    packet = jnp.stack(
        [
            lax.dynamic_slice(
                by_core,
                (core ^ (d % 2), (owner - d // 2) % owners, 0, 0),
                (1, 1, part + 8, 3 * width),
            )[0, 0]
            for d in range(groups)
        ]
    )
    w_own = packet[:, :part].reshape(model_width, 3 * width)
    early = packet[:, part].astype(F32)
    late = packet[:, part + 1 : part + 3, :half_late].astype(F32).reshape(groups, -1)
    b_qk = early[:, : 2 * part].reshape(2 * model_width)
    b_value = early[:, 2 * part : 3 * part].reshape(model_width)
    g_one = early[:, 3 * part : 4 * part].reshape(1, model_width)
    s_one = early[:, 4 * part : 5 * part].reshape(1, model_width)
    b_joint = jnp.concatenate([b_qk, b_value]).reshape(3, owners, width)
    b_own = lax.dynamic_index_in_dim(b_joint, owner, 1, keepdims=False).reshape(3 * width, 1)
    w_turned = jnp.transpose(w_own)

    freqs = 10000.0 ** (-jnp.arange(half, dtype=F32) / half)
    angles = freqs[:, None] * jnp.arange(length, dtype=jnp.int32).astype(F32)[None, :]
    cosine = jnp.cos(angles)
    sine = jnp.sin(angles)
    core_index = core.astype(jnp.int32).reshape(1)

    hidden_part = hidden_width // groups
    share = hidden_part // 3
    row = lambda first, size: late[:, first : first + size].reshape(1, groups * size)
    b_out = row(0, part)
    b_in = row(part, hidden_part)
    b_down = row(part + hidden_part, part)
    g_two = row(2 * part + hidden_part, part)
    s_two = row(3 * part + hidden_part, part)
    last = jnp.pad(out_weight.astype(BF16), ((0, share - part), (0, 0)))
    rep = lax.axis_index("rep")
    tail_packet = lax.dynamic_slice_in_dim(
        jnp.concatenate([down_weight.astype(BF16), last], axis=0), rep * share, share, 0
    )
    tokens, w_turned, b_own, cosine, sine, mix, tail_packet, in_packet = after(
        (tokens, w_turned, b_own, cosine, sine, mix, tail_packet, in_weight.astype(BF16)),
        grad_earlier,
        depth_sums,
    )
    tail_parts = [tail_packet] + [shift_owner(tail_packet, k) for k in range(1, owners)]
    states = project(tokens, w_turned, b_own, g_one, s_one, cosine, sine, 0, groups, ())
    plain_all, qt, kt, vt, kv, *tail_parts = lax.optimization_barrier((*states, *tail_parts))
    grad_result = depth_weights[4] * cotangent
    down_grad = grad_result.astype(BF16)
    tail_stack = jnp.stack(tail_parts)
    qt, tail_stack, in_packet, down_grad = lax.optimization_barrier(
        (qt, tail_stack, in_packet, down_grad)
    )
    w_in = lax.all_gather(in_packet, "shard", axis=0, tiled=True)
    tail_mine = every_rep(tail_stack)
    mixed_own, attended, stats = attend(core_index, qt, kv, vt)
    stats, *tail_mine = lax.optimization_barrier((stats, *tail_mine))
    mixed_two = lax.all_to_all(mixed_own, "shard", 0, 0)
    tail_other = [swap_core(value) for value in tail_mine]
    w_down, w_out = assemble(
        jnp.stack([member, rep]).astype(jnp.int32), tail_mine, tail_other, part
    )
    grad_active = contract(down_grad, w_down, 1, 1).astype(BF16)
    mixed_two, grad_active = lax.optimization_barrier((mixed_two, grad_active))

    inputs = block_in.astype(F32)
    (
        middle, normed_two_low, active, grad_hidden, grad_middle, branch_grad, grad_own,
        token_sums, grad_in_b,
    ) = middle_part(
        core_index, depth_weights, mixed_two, block_in, cotangent, w_out, b_out, g_two, s_two,
        w_in, b_in, grad_active,
    )
    grad_out_b, grad_gain_two, grad_shift_two = (token_sums[i] for i in range(3))
    grad_in_b = grad_in_b[0]
    grad_own = lax.all_to_all(grad_own, "shard", 0, 0)
    pair_own = (normed_two_low, grad_hidden, mixed_two, branch_grad)
    pair_twin = tuple(swap_core(value) for value in pair_own)
    grad_down_w, layer_out, last_depth = down_part(
        depth_weights, active, down_grad, w_down, b_down, middle, mix, cotangent
    )
    folded = pair_sums(core_index, pair_own, pair_twin)
    grad_down_b = jnp.sum(down_grad.astype(F32), axis=0)
    grad_own, folded, grad_down_w, last_depth = lax.optimization_barrier(
        (grad_own, folded, grad_down_w, last_depth)
    )
    depth = jnp.concatenate([depth_sums, last_depth[None]], axis=0).sum(axis=(1, 2))
    sent = send_rep(folded)
    down_sums = lax.psum_scatter(grad_down_w, "shard", scatter_dimension=0, tiled=True)
    joint_t, grad_normed = retrace(
        core_index, qt, grad_own, attended, stats, cosine, sine, kv, kt, w_turned
    )
    joint_t, grad_normed, folded, plain_all, depth, *sent = lax.optimization_barrier(
        (joint_t, grad_normed, folded, plain_all, depth, *sent)
    )
    grad_normed = lax.psum_scatter(
        grad_normed, "shard", scatter_dimension=0, tiled=True
    )
    folded = join_rep(folded, sent)

    own_sums, other_sums, first_sums, joint_sums = joint_part(
        core_index, plain_all, joint_t, w_turned, g_one, s_one
    )
    arrived = exchange_owner(folded, owner)
    own_sums, other_sums, first_sums, joint_sums, *arrived = lax.optimization_barrier(
        (own_sums, other_sums, first_sums, joint_sums, *arrived)
    )
    pair_sum = add_low(*arrived)
    grad_gain_one, grad_shift_one = first_sums[0], first_sums[1]
    joint_sums = joint_sums[0]

    spread_sums = lax.dynamic_update_slice(
        jnp.zeros((3, model_width), F32), joint_sums.reshape(3, width), (0, owner * width)
    ).reshape(3 * model_width)
    vectors = (
        spread_sums[: 2 * model_width],
        spread_sums[2 * model_width :],
        grad_out_b,
        grad_in_b,
        grad_down_b,
        grad_gain_one,
        grad_shift_one,
        grad_gain_two,
        grad_shift_two,
    )
    counts = [vector.shape[0] // model_width for vector in vectors]
    small = jnp.concatenate(
        [
            vector.reshape(groups, count, part).astype(BF16)
            for vector, count in zip(vectors, counts)
        ],
        axis=1,
    )
    small = jnp.pad(small, ((0, 0), (0, part - small.shape[1]), (0, 128 - part)))
    depth = split_depth(depth)
    mark = (part // 4 - 8, 3 * width)
    marked = jnp.zeros((4, part // 4, 128), BF16).at[:, mark[0], : depth.shape[0]].set(depth)
    small = small + marked.reshape(1, part, 128)
    small = small.reshape(owners, 2, part, 128)
    depth_of = lambda value: join_depth(
        value[mark[0], mark[1] : mark[1] + depth.shape[0]]
    )
    with_depth = lambda value, sums: value.at[
        :, mark[0], mark[1] : mark[1] + depth.shape[0]
    ].set(split_depth(sums))
    received = swap_core(
        jnp.concatenate([other_sums, pick(small, 1 - core, 1)], axis=2)
    )
    mixed_sums = add_low(
        jnp.concatenate([own_sums, pick(small, core, 1)], axis=2), received
    )
    depth_sum = join_depth(depth) + depth_of(received[0])
    down_parts = pick_parts(down_sums[None])
    down_rows = part // 4
    columns = 3 * width + 128
    sums_parts = [with_depth(value, depth_sum) for value in pick_parts(mixed_sums)]
    received = [
        cross_rep(
            jnp.concatenate([sums, down.reshape(owners, down_rows, model_width)], axis=2), k
        )
        for k, (sums, down) in enumerate(zip(sums_parts[1:], down_parts[1:]), 1)
    ]
    pair_sum, *received = lax.optimization_barrier((pair_sum, *received))
    pair_pieces = every_rep(pair_sum)
    mixed_sums = add_low(sums_parts[0], *[value[:, :, :columns] for value in received])
    depth_sum = add_ordered(
        [depth_of(value[0]) for value in (sums_parts[0], *received)], lambda k: rep ^ k
    )
    mixed_sums = with_depth(mixed_sums, depth_sum)
    down_sums = add_low(
        down_parts[0].reshape(owners, down_rows, model_width),
        *[value[:, :, columns:] for value in received],
    )
    down_pieces = every_rep(jnp.concatenate([down_sums[k] for k in range(owners)], axis=1))
    arrived = exchange_owner(mixed_sums, owner)
    arrived = lax.optimization_barrier((*arrived, *pair_pieces, *down_pieces))
    pair_pieces, down_pieces = arrived[owners : owners + 4], arrived[owners + 4 :]
    arrived = arrived[:owners]
    small = add_low(*[value[:, 3 * width :] for value in arrived])
    by_distance = jnp.stack([value[:, : 3 * width] for value in arrived])
    by_owner = [pick(by_distance, (owner - k) % owners) for k in range(owners)]
    joint_pieces = every_rep(jnp.concatenate([*by_owner, small], axis=1))
    depth_sums = [value[mark[0], mark[1] : mark[1] + depth.shape[0]] for value in arrived]
    grad_normed, *pieces = lax.optimization_barrier((grad_normed, *joint_pieces, *depth_sums))
    joint_pieces, depth_sums = pieces[:4], pieces[4:]
    grad_depth = add_ordered(
        [join_depth(value) for value in depth_sums], lambda k: (owner - k) % owners
    )
    sum_in, sum_out, sum_qkv, sum_down, *small_outs = unpack(
        lax.axis_index("rep").astype(jnp.int32).reshape(1),
        pair_pieces,
        joint_pieces,
        down_pieces,
        (hidden_width, model_width, 3 * width),
        counts,
    )
    small_outs = [value[0] for value in small_outs]
    grad_normed = grad_normed.astype(F32)
    center = inputs - jnp.mean(inputs, axis=-1, keepdims=True)
    scale = lax.rsqrt(jnp.mean(center * center, axis=-1, keepdims=True) + EPSILON)
    plain = center * scale
    scaled = grad_normed * g_one
    grad_block = grad_middle + scale * (
        scaled
        - jnp.mean(scaled, axis=-1, keepdims=True)
        - plain * jnp.mean(scaled * plain, axis=-1, keepdims=True)
    )

    return (
        layer_out,
        grad_block,
        grad_earlier,
        sum_qkv,
        sum_out,
        sum_in,
        sum_down,
        *small_outs,
        grad_depth,
    )


def per_device(*args):
    block_in = args[0]
    row_count, model_width = block_in.shape
    groups = lax.axis_size("shard")
    head_count = model_width // HEAD_DIM
    late_size = (4 * model_width + args[5].shape[1]) // groups
    if (
        groups == 8
        and lax.axis_size("rep") == 4
        and row_count == CHUNK
        and head_count % (groups // 2) == 0
        and head_count // (groups // 2) <= 8
        and late_size <= 12 * model_width // groups
        and args[5].shape[1] % (3 * groups) == 0
        and model_width // groups <= args[5].shape[1] // (3 * groups)
    ):
        return head_split_device(*args)
    return generic_device(*args)


def solution(mesh):
    placed = (
        P(("rep", "shard"), None),
        P(None, ("rep", "shard"), None),
        P(("rep", "shard"), None),
        P("shard", None),
        P("shard", None),
        P("shard", None),
        P("shard", None),
        P("shard"),
        P("shard"),
        P("shard"),
        P("shard"),
        P("shard"),
        P("shard"),
        P("shard"),
        P("shard"),
        P("shard"),
        P(),
    )
    return jax.shard_map(
        per_device,
        mesh=mesh,
        in_specs=placed,
        out_specs=(
            P(("rep", "shard"), None),
            P(("rep", "shard"), None),
            P(None, ("rep", "shard"), None),
            P("shard", None),
            P("shard", None),
            P("shard", None),
            P("shard", None),
            P("shard"),
            P("shard"),
            P("shard"),
            P("shard"),
            P("shard"),
            P("shard"),
            P("shard"),
            P("shard"),
            P("shard"),
            P(),
        ),
        check_vma=False,
    )
```

```python
from functools import partial
import math

import jax
import jax.numpy as jnp
from jax import lax
from jax.experimental import pallas as pl
from jax.experimental.pallas import tpu as pltpu
from jax.sharding import PartitionSpec as P

HEAD_DIM = 64
BLOCK = 256


NEG = -1e30
EPSILON = 1e-05


def layer_norm(inputs, gain, shift):
    center = inputs - jnp.mean(inputs, axis=-1, keepdims=True)
    spread = jnp.mean(center * center, axis=-1, keepdims=True)
    return center * lax.rsqrt(spread + EPSILON) * gain + shift


def rotate(inputs, positions):
    row_count = inputs.shape[0]
    split = inputs.reshape(row_count, -1, HEAD_DIM)
    half_dim = HEAD_DIM // 2
    freqs = 10000.0 ** (-jnp.arange(half_dim, dtype=jnp.float32) / half_dim)
    angles = positions.astype(jnp.float32)[:, None] * freqs[None, :]
    cosine = jnp.cos(angles)[:, None, :]
    sine = jnp.sin(angles)[:, None, :]
    former = split[..., :half_dim]
    latter = split[..., half_dim:]
    turned = jnp.concatenate(
        [former * cosine - latter * sine, former * sine + latter * cosine], axis=-1
    )
    return turned.reshape(row_count, -1)


def generic_device(
    block_in,
    earlier,
    cotangent,
    qkv_weight,
    out_weight,
    in_weight,
    down_weight,
    qk_bias,
    value_bias,
    out_bias,
    in_bias,
    down_bias,
    gain_one,
    shift_one,
    gain_two,
    shift_two,
    depth_weights,
):
    bf16 = jnp.bfloat16
    f32 = jnp.float32
    w_qkv, w_out, w_in, w_down, b_qk, b_value, b_out, b_in, b_down, g_one, s_one, g_two, s_two = (
        lax.all_gather(qkv_weight.astype(bf16), "shard", axis=0, tiled=True),
        lax.all_gather(out_weight.astype(bf16), "shard", axis=0, tiled=True),
        lax.all_gather(in_weight.astype(bf16), "shard", axis=0, tiled=True),
        lax.all_gather(down_weight.astype(bf16), "shard", axis=0, tiled=True),
        lax.all_gather(qk_bias.astype(bf16), "shard", axis=0, tiled=True),
        lax.all_gather(value_bias.astype(bf16), "shard", axis=0, tiled=True),
        lax.all_gather(out_bias.astype(bf16), "shard", axis=0, tiled=True),
        lax.all_gather(in_bias.astype(bf16), "shard", axis=0, tiled=True),
        lax.all_gather(down_bias.astype(bf16), "shard", axis=0, tiled=True),
        lax.all_gather(gain_one.astype(bf16), "shard", axis=0, tiled=True),
        lax.all_gather(shift_one.astype(bf16), "shard", axis=0, tiled=True),
        lax.all_gather(gain_two.astype(bf16), "shard", axis=0, tiled=True),
        lax.all_gather(shift_two.astype(bf16), "shard", axis=0, tiled=True),
    )
    row_count, model_width = block_in.shape
    head_count = model_width // HEAD_DIM
    groups = lax.axis_size("shard")
    length = row_count * groups
    window = min(512, length)
    member = lax.axis_index("shard")
    first_row = member * row_count
    last_end = first_row + row_count
    positions = first_row + jnp.arange(row_count, dtype=jnp.int32)
    query_block = positions // BLOCK
    score_scale = HEAD_DIM ** (-0.5)
    needed = (last_end + window - 1) // window
    inputs = block_in.astype(f32)
    normed, norm_back = jax.vjp(layer_norm, inputs, g_one.astype(f32), s_one.astype(f32))
    normed_low = normed.astype(bf16)
    joint_bias = jnp.concatenate([b_qk.astype(f32), b_value.astype(f32)])
    projected = jnp.dot(normed_low, w_qkv, preferred_element_type=f32) + joint_bias
    queries = rotate(projected[:, :model_width], positions).astype(bf16)
    key_rows = rotate(projected[:, model_width : 2 * model_width], positions).astype(bf16)
    values = projected[:, 2 * model_width :].astype(bf16)
    query_heads = queries.reshape(row_count, head_count, HEAD_DIM)

    def masked_scores(key_piece, key_start):
        piece_rows = key_piece.shape[0]
        key_heads = key_piece.reshape(piece_rows, head_count, HEAD_DIM)
        scores = (
            jnp.einsum("qhd,khd->hqk", query_heads, key_heads, preferred_element_type=f32)
            * score_scale
        )
        key_block = (key_start + jnp.arange(piece_rows, dtype=jnp.int32)) // BLOCK
        allowed = key_block[None, :] <= query_block[:, None]
        return (scores, allowed)

    def absorb(running, key_piece, value_piece, key_start):
        highest, denominator, summed = running
        scores, allowed = masked_scores(key_piece, key_start)
        scores = jnp.where(allowed[None], scores, NEG)
        new_high = jnp.maximum(highest, jnp.max(scores, axis=-1))
        rescale = jnp.exp(highest - new_high)
        weights = jnp.where(allowed[None], jnp.exp(scores - new_high[..., None]), 0.0)
        value_heads = value_piece.reshape(-1, head_count, HEAD_DIM)
        summed = summed * rescale[..., None] + jnp.einsum(
            "hqk,khd->hqd", weights.astype(bf16), value_heads, preferred_element_type=f32
        )
        return (new_high, denominator * rescale + jnp.sum(weights, axis=-1), summed)

    start_state = (
        jnp.full((head_count, row_count), NEG, f32),
        jnp.zeros((head_count, row_count), f32),
        jnp.zeros((head_count, row_count, HEAD_DIM), f32),
    )
    key_piece = lax.all_gather(key_rows, "shard", axis=0, tiled=True)
    value_piece = lax.all_gather(values, "shard", axis=0, tiled=True)
    piece_rows = key_piece.shape[0]
    sub_rows = math.gcd(piece_rows, window)
    usable = jnp.clip((last_end + sub_rows - 1) // sub_rows, 0, piece_rows // sub_rows)

    def advance(block_step, state_inner):
        offset = block_step * sub_rows
        return absorb(
            state_inner,
            lax.dynamic_slice_in_dim(key_piece, offset, sub_rows, 0),
            lax.dynamic_slice_in_dim(value_piece, offset, sub_rows, 0),
            offset,
        )

    highest, denominator, summed = lax.fori_loop(0, usable, advance, start_state)
    attended = summed / denominator[..., None]
    log_norm = highest + jnp.log(denominator)
    mixed = jnp.transpose(attended, (1, 0, 2)).reshape(row_count, model_width).astype(bf16)
    branch = jnp.dot(mixed, w_out, preferred_element_type=f32) + b_out.astype(f32)
    middle = inputs + branch
    normed_two, norm_two_back = jax.vjp(layer_norm, middle, g_two.astype(f32), s_two.astype(f32))
    normed_two_low = normed_two.astype(bf16)
    hidden = jnp.dot(normed_two_low, w_in, preferred_element_type=f32) + b_in.astype(f32)
    active_full, gelu_back = jax.vjp(partial(jax.nn.gelu, approximate=True), hidden)
    active = active_full.astype(bf16)
    result = middle + jnp.dot(active, w_down, preferred_element_type=f32) + b_down.astype(f32)
    stacked = earlier.astype(f32)
    layer_out = depth_weights[4] * result
    for level in range(4):
        layer_out = layer_out + depth_weights[level] * stacked[level]
    grad_earlier = depth_weights[:4][:, None, None] * cotangent[None]
    local_depth = jnp.concatenate(
        [jnp.sum(stacked * cotangent[None], axis=(1, 2)), jnp.sum(result * cotangent)[None]]
    )
    grad_depth = lax.psum(local_depth, ("rep", "shard"))
    grad_result = depth_weights[4] * cotangent
    down_grad = grad_result.astype(bf16)
    grad_down_w = jnp.einsum("tf,td->fd", active, down_grad, preferred_element_type=f32)
    grad_down_b = jnp.sum(down_grad.astype(f32), axis=0)
    grad_active = jnp.einsum("td,fd->tf", down_grad, w_down, preferred_element_type=f32)
    grad_hidden = gelu_back(grad_active)[0].astype(bf16)
    grad_in_w = jnp.einsum("td,tf->df", normed_two_low, grad_hidden, preferred_element_type=f32)
    grad_in_b = jnp.sum(grad_hidden.astype(f32), axis=0)
    grad_normed_two = jnp.einsum("tf,df->td", grad_hidden, w_in, preferred_element_type=f32)
    grad_mid_norm, grad_gain_two, grad_shift_two = norm_two_back(grad_normed_two)
    grad_middle = grad_result + grad_mid_norm
    branch_grad = grad_middle.astype(bf16)
    grad_out_w = jnp.einsum("td,te->de", mixed, branch_grad, preferred_element_type=f32)
    grad_out_b = jnp.sum(branch_grad.astype(f32), axis=0)
    grad_mixed = jnp.einsum("te,de->td", branch_grad, w_out, preferred_element_type=f32).astype(
        bf16
    )
    key_all, value_all = (
        lax.all_gather(key_rows, "shard", axis=0, tiled=True),
        lax.all_gather(values, "shard", axis=0, tiled=True),
    )
    grad_heads = grad_mixed.reshape(row_count, head_count, HEAD_DIM)
    delta = jnp.einsum("qhd,hqd->hq", grad_heads.astype(f32), attended)

    def score_grads(key_piece, value_piece, offset, piece_rows):
        scores, allowed = masked_scores(key_piece, offset)
        probs = jnp.where(allowed[None], jnp.exp(scores - log_norm[..., None]), 0.0)
        value_heads = value_piece.reshape(piece_rows, head_count, HEAD_DIM)
        grad_probs = jnp.einsum("qhd,khd->hqk", grad_heads, value_heads, preferred_element_type=f32)
        grad_scores = (probs * (grad_probs - delta[..., None])).astype(bf16)
        return (probs, grad_scores)

    def retrace(block_step, running):
        grad_query, grad_keys, grad_values = running
        offset = block_step * window
        key_piece = lax.dynamic_slice_in_dim(key_all, offset, window, 0)
        value_piece = lax.dynamic_slice_in_dim(value_all, offset, window, 0)
        probs, grad_scores = score_grads(key_piece, value_piece, offset, window)
        key_heads = key_piece.reshape(window, head_count, HEAD_DIM)
        grad_query = grad_query + jnp.einsum(
            "hqk,khd->qhd", grad_scores, key_heads, preferred_element_type=f32
        )
        piece_keys = (
            jnp.einsum("hqk,qhd->khd", grad_scores, query_heads, preferred_element_type=f32)
            * score_scale
        )
        piece_values = jnp.einsum(
            "hqk,qhd->khd", probs.astype(bf16), grad_heads, preferred_element_type=f32
        )
        grad_keys = lax.dynamic_update_slice_in_dim(
            grad_keys, piece_keys.reshape(window, model_width), offset, 0
        )
        grad_values = lax.dynamic_update_slice_in_dim(
            grad_values, piece_values.reshape(window, model_width), offset, 0
        )
        return (grad_query, grad_keys, grad_values)

    start_back = (
        jnp.zeros((row_count, head_count, HEAD_DIM), f32),
        jnp.zeros((length, model_width), f32),
        jnp.zeros((length, model_width), f32),
    )
    grad_query, grad_keys, grad_values = lax.fori_loop(0, needed, retrace, start_back)
    own_keys, own_values = (
        lax.psum_scatter(
            grad_keys.astype(jnp.bfloat16), "shard", scatter_dimension=0, tiled=True
        ).astype(jnp.float32),
        lax.psum_scatter(
            grad_values.astype(jnp.bfloat16), "shard", scatter_dimension=0, tiled=True
        ).astype(jnp.float32),
    )
    grad_q_turned = rotate(grad_query.reshape(row_count, model_width) * score_scale, -positions)
    grad_k_turned = rotate(own_keys, -positions)
    grad_joint = jnp.concatenate([grad_q_turned, grad_k_turned, own_values], axis=1).astype(bf16)
    grad_qkv_w = jnp.einsum("td,tf->df", normed_low, grad_joint, preferred_element_type=f32)
    joint_sums = jnp.sum(grad_joint.astype(f32), axis=0)
    grad_qk_b = joint_sums[: 2 * model_width]
    grad_value_b = joint_sums[2 * model_width :]
    grad_normed = jnp.einsum("tf,df->td", grad_joint, w_qkv, preferred_element_type=f32)
    grad_in_norm, grad_gain_one, grad_shift_one = norm_back(grad_normed)
    grad_block = grad_middle + grad_in_norm
    (
        own_qkv_w,
        own_out_w,
        own_in_w,
        own_down_w,
        own_qk_b,
        own_value_b,
        own_out_b,
        own_in_b,
        own_down_b,
        own_gain_one,
        own_shift_one,
        own_gain_two,
        own_shift_two,
    ) = (
        lax.psum_scatter(
            grad_qkv_w.astype(jnp.bfloat16), "shard", scatter_dimension=0, tiled=True
        ).astype(jnp.float32),
        lax.psum_scatter(
            grad_out_w.astype(jnp.bfloat16), "shard", scatter_dimension=0, tiled=True
        ).astype(jnp.float32),
        lax.psum_scatter(
            grad_in_w.astype(jnp.bfloat16), "shard", scatter_dimension=0, tiled=True
        ).astype(jnp.float32),
        lax.psum_scatter(
            grad_down_w.astype(jnp.bfloat16), "shard", scatter_dimension=0, tiled=True
        ).astype(jnp.float32),
        lax.psum_scatter(
            grad_qk_b.astype(jnp.bfloat16), "shard", scatter_dimension=0, tiled=True
        ).astype(jnp.float32),
        lax.psum_scatter(
            grad_value_b.astype(jnp.bfloat16), "shard", scatter_dimension=0, tiled=True
        ).astype(jnp.float32),
        lax.psum_scatter(
            grad_out_b.astype(jnp.bfloat16), "shard", scatter_dimension=0, tiled=True
        ).astype(jnp.float32),
        lax.psum_scatter(
            grad_in_b.astype(jnp.bfloat16), "shard", scatter_dimension=0, tiled=True
        ).astype(jnp.float32),
        lax.psum_scatter(
            grad_down_b.astype(jnp.bfloat16), "shard", scatter_dimension=0, tiled=True
        ).astype(jnp.float32),
        lax.psum_scatter(
            grad_gain_one.astype(jnp.bfloat16), "shard", scatter_dimension=0, tiled=True
        ).astype(jnp.float32),
        lax.psum_scatter(
            grad_shift_one.astype(jnp.bfloat16), "shard", scatter_dimension=0, tiled=True
        ).astype(jnp.float32),
        lax.psum_scatter(
            grad_gain_two.astype(jnp.bfloat16), "shard", scatter_dimension=0, tiled=True
        ).astype(jnp.float32),
        lax.psum_scatter(
            grad_shift_two.astype(jnp.bfloat16), "shard", scatter_dimension=0, tiled=True
        ).astype(jnp.float32),
    )
    (
        sum_qkv_w,
        sum_out_w,
        sum_in_w,
        sum_down_w,
        sum_qk_b,
        sum_value_b,
        sum_out_b,
        sum_in_b,
        sum_down_b,
        sum_gain_one,
        sum_shift_one,
        sum_gain_two,
        sum_shift_two,
    ) = (
        lax.psum(own_qkv_w.astype(jnp.bfloat16), "rep").astype(jnp.float32),
        lax.psum(own_out_w.astype(jnp.bfloat16), "rep").astype(jnp.float32),
        lax.psum(own_in_w.astype(jnp.bfloat16), "rep").astype(jnp.float32),
        lax.psum(own_down_w.astype(jnp.bfloat16), "rep").astype(jnp.float32),
        lax.psum(own_qk_b.astype(jnp.bfloat16), "rep").astype(jnp.float32),
        lax.psum(own_value_b.astype(jnp.bfloat16), "rep").astype(jnp.float32),
        lax.psum(own_out_b.astype(jnp.bfloat16), "rep").astype(jnp.float32),
        lax.psum(own_in_b.astype(jnp.bfloat16), "rep").astype(jnp.float32),
        lax.psum(own_down_b.astype(jnp.bfloat16), "rep").astype(jnp.float32),
        lax.psum(own_gain_one.astype(jnp.bfloat16), "rep").astype(jnp.float32),
        lax.psum(own_shift_one.astype(jnp.bfloat16), "rep").astype(jnp.float32),
        lax.psum(own_gain_two.astype(jnp.bfloat16), "rep").astype(jnp.float32),
        lax.psum(own_shift_two.astype(jnp.bfloat16), "rep").astype(jnp.float32),
    )
    return (
        layer_out,
        grad_block,
        grad_earlier,
        sum_qkv_w,
        sum_out_w,
        sum_in_w,
        sum_down_w,
        sum_qk_b,
        sum_value_b,
        sum_out_b,
        sum_in_b,
        sum_down_b,
        sum_gain_one,
        sum_shift_one,
        sum_gain_two,
        sum_shift_two,
        grad_depth,
    )


F32 = jnp.float32
BF16 = jnp.bfloat16
CHUNK = 2 * BLOCK
VMEM_LIMIT = 56 * 1024 * 1024


def cost(flops, moved, exps=0):
    return pl.CostEstimate(flops=flops, bytes_accessed=moved, transcendentals=exps)


def contract(left, right, left_dim, right_dim):
    return lax.dot_general(
        left, right, (((left_dim,), (right_dim,)), ((), ())), preferred_element_type=F32
    )


def qkv_kernel(x_ref, weight_ref, bias_ref, gain_ref, shift_ref, cos_ref, sin_ref, *refs):
    plain_ref, qt_ref, kt_ref, vt_ref, kv_ref = refs[-5:]
    x = x_ref[...].astype(F32)
    center = x - jnp.mean(x, axis=-1, keepdims=True)
    spread = jnp.mean(center * center, axis=-1, keepdims=True)
    plain = center * lax.rsqrt(spread + EPSILON)
    plain_ref[...] = plain.astype(BF16)
    low = (plain * gain_ref[...] + shift_ref[...]).astype(BF16)
    width = qt_ref.shape[0]
    half = HEAD_DIM // 2
    joint = contract(weight_ref[...], low, 1, 1) + bias_ref[...]
    cosine = cos_ref[...]
    sine = sin_ref[...]
    for head in range(width // HEAD_DIM):
        base = head * HEAD_DIM
        for part in range(2):
            start = part * width + base
            former = joint[start : start + half]
            latter = joint[start + half : start + HEAD_DIM]
            turned = jnp.concatenate(
                [former * cosine - latter * sine, former * sine + latter * cosine], axis=0
            )
            if part == 0:
                qt_ref[base : base + HEAD_DIM, :] = (turned * HEAD_DIM ** (-0.5)).astype(BF16)
            else:
                kt_ref[base : base + HEAD_DIM, :] = turned.astype(BF16)
                key = turned
        start = 2 * width + base
        value = joint[start : start + HEAD_DIM]
        vt_ref[base : base + HEAD_DIM, :] = value.astype(BF16)
        kv_ref[head] = jnp.transpose(jnp.concatenate([key, value], axis=0)).astype(BF16)


def project(tokens, weight_t, bias, gain, shift, cosine, sine, first, count, held):
    length, model_width = tokens.shape
    columns = weight_t.shape[0]
    width = columns // 3
    heads = width // HEAD_DIM
    half = HEAD_DIM // 2
    tile = CHUNK
    fixed = lambda i: (0, 0)
    down = lambda i: (first + i, 0)
    across = lambda i: (0, first + i)
    inputs = [tokens, weight_t, bias, gain, shift, cosine, sine]
    return pl.pallas_call(
        qkv_kernel,
        name="project",
        cost_estimate=cost(2 * count * tile * model_width * columns, 12 * count * tile * model_width),
        grid=(count,),
        in_specs=[
            pl.BlockSpec((tile, model_width), down),
            pl.BlockSpec((columns, model_width), fixed),
            pl.BlockSpec((columns, 1), fixed),
            pl.BlockSpec((1, model_width), fixed),
            pl.BlockSpec((1, model_width), fixed),
            pl.BlockSpec((half, tile), across),
            pl.BlockSpec((half, tile), across),
        ]
        + [pl.BlockSpec(memory_space=pl.ANY)] * len(held),
        out_specs=[
            pl.BlockSpec((tile, model_width), down),
            pl.BlockSpec((width, tile), across),
            pl.BlockSpec((width, tile), across),
            pl.BlockSpec((width, tile), across),
            pl.BlockSpec((heads, tile, 2 * HEAD_DIM), lambda i: (0, first + i, 0)),
        ],
        out_shape=[
            jax.ShapeDtypeStruct((length, model_width), BF16),
            jax.ShapeDtypeStruct((width, length), BF16),
            jax.ShapeDtypeStruct((width, length), BF16),
            jax.ShapeDtypeStruct((width, length), BF16),
            jax.ShapeDtypeStruct((heads, length, 2 * HEAD_DIM), BF16),
        ],
        input_output_aliases={len(inputs) + i: i for i in range(len(held))},
        compiler_params=pltpu.CompilerParams(vmem_limit_bytes=VMEM_LIMIT),
    )(*inputs, *held)


def average_kernel(weights_ref, earlier_ref, cotangent_ref, grad_ref, mix_ref, sums_ref):
    @pl.when(pl.program_id(0) == 0)
    def _():
        sums_ref[...] = jnp.zeros_like(sums_ref)

    cotangent = cotangent_ref[...]
    rows, columns = cotangent.shape
    mix = jnp.zeros_like(cotangent)
    for level in range(earlier_ref.shape[0]):
        value = earlier_ref[level].astype(F32)
        weight = weights_ref[level]
        mix = mix + weight * value
        grad_ref[level] = weight * cotangent
        sums_ref[level] += jnp.sum((value * cotangent).reshape(rows // 8, 8, columns), axis=0)
    mix_ref[...] = mix


def average(depth_weights, earlier, cotangent):
    levels, row_count, model_width = earlier.shape
    tile = row_count // 4
    return pl.pallas_call(
        average_kernel,
        name="average",
        cost_estimate=cost(6 * earlier.size, 6 * earlier.size + 8 * cotangent.size),
        grid_spec=pltpu.PrefetchScalarGridSpec(
            num_scalar_prefetch=1,
            grid=(4,),
            in_specs=[
                pl.BlockSpec((levels, tile, model_width), lambda i, w: (0, i, 0)),
                pl.BlockSpec((tile, model_width), lambda i, w: (i, 0)),
            ],
            out_specs=[
                pl.BlockSpec((levels, tile, model_width), lambda i, w: (0, i, 0)),
                pl.BlockSpec((tile, model_width), lambda i, w: (i, 0)),
                pl.BlockSpec((levels, 8, model_width), lambda i, w: (0, 0, 0)),
            ],
        ),
        out_shape=[
            jax.ShapeDtypeStruct(earlier.shape, F32),
            jax.ShapeDtypeStruct(cotangent.shape, F32),
            jax.ShapeDtypeStruct((levels, 8, model_width), F32),
        ],
        compiler_params=pltpu.CompilerParams(vmem_limit_bytes=VMEM_LIMIT),
    )(depth_weights, earlier, cotangent)


def last_mask(odd, rows):
    row = lax.broadcasted_iota(jnp.int32, (rows, BLOCK), 0)
    return row < rows - BLOCK * (1 - odd)


def over_chunks(pair, absorb, state):
    state = lax.fori_loop(0, pair // 2, lambda i, s: absorb(2 * i, 2 * CHUNK, s, False), state)
    return lax.cond(
        pair % 2 == 0,
        lambda s: absorb(pair, CHUNK, s, True),
        lambda s: absorb(pair - 1, 2 * CHUNK, s, True),
        state,
    )


def attend_kernel(core_ref, qt_ref, kv_ref, vt_ref, low_ref, full_ref, stat_ref, scores_ref):
    pair = pl.program_id(0)
    odd = core_ref[0] ^ (pair & 1)
    heads = qt_ref.shape[0] // HEAD_DIM
    blank = jnp.zeros((HEAD_DIM, BLOCK), BF16)
    queries = [
        jnp.concatenate([qt_ref[h * HEAD_DIM : (h + 1) * HEAD_DIM, :], blank], axis=0)
        for h in range(heads)
    ]
    fold = lambda value: value.reshape(value.shape[0] // 8, 8, BLOCK)

    def score(step, size, state, masked):
        keys = pl.ds(pl.multiple_of(step * CHUNK, CHUNK), size)
        fresh = []
        for h in range(heads):
            scores = contract(kv_ref[h, keys, :], queries[h], 1, 0)
            if masked:
                scores = jnp.where(last_mask(odd, size), scores, NEG)
            scores_ref[h, keys, :] = scores
            fresh.append(jnp.maximum(state[h], jnp.max(fold(scores), axis=0)))
        return fresh

    def mix(step, size, state, masked):
        keys = pl.ds(pl.multiple_of(step * CHUNK, CHUNK), size)
        fresh = []
        for h in range(heads):
            total, summed = state[h]
            weights = jnp.exp(scores_ref[h, keys, :] - highest[h])
            values = vt_ref[h * HEAD_DIM : (h + 1) * HEAD_DIM, keys]
            fresh.append(
                (
                    total + jnp.sum(fold(weights), axis=0),
                    summed + contract(values, weights.astype(BF16), 1, 0),
                )
            )
        return fresh

    state = [jnp.full((8, BLOCK), NEG, F32) for _ in range(heads)]
    state = over_chunks(pair, score, state)
    highest = [jnp.max(value, axis=0, keepdims=True) for value in state]
    state = [
        (jnp.zeros((8, BLOCK), F32), jnp.zeros((HEAD_DIM, BLOCK), F32)) for _ in range(heads)
    ]
    state = over_chunks(pair, mix, state)
    for h in range(heads):
        total, summed = state[h]
        total = jnp.sum(total, axis=0, keepdims=True)
        attended = summed / total
        full_ref[0, h * HEAD_DIM : (h + 1) * HEAD_DIM, :] = attended
        low_ref[0, h * HEAD_DIM : (h + 1) * HEAD_DIM, :] = attended.astype(BF16)
        stat_ref[0, h : h + 1, :] = highest[h] + jnp.log(total)


def attend(core, qt, kv, vt):
    width, length = qt.shape
    pairs = length // CHUNK
    own = lambda j, core: (0, 2 * j + (core[0] ^ (j & 1)))
    slot = lambda j, core: (j, 0, 0)
    return pl.pallas_call(
        attend_kernel,
        name="attend",
        cost_estimate=cost(
            2 * 2 * BLOCK * BLOCK * BLOCK * 2 * sum(range(1, pairs + 1)) * (width // HEAD_DIM),
            4 * kv.size + 8 * pairs * width * BLOCK,
            CHUNK * BLOCK * sum(range(1, pairs + 1)) * (width // HEAD_DIM),
        ),
        grid_spec=pltpu.PrefetchScalarGridSpec(
            num_scalar_prefetch=1,
            grid=(pairs,),
            in_specs=[
                pl.BlockSpec((width, BLOCK), own),
                pl.BlockSpec(kv.shape, lambda j, core: (0, 0, 0)),
                pl.BlockSpec(vt.shape, lambda j, core: (0, 0)),
            ],
            out_specs=[
                pl.BlockSpec((1, width, BLOCK), slot),
                pl.BlockSpec((1, width, BLOCK), slot),
                pl.BlockSpec((1, 8, BLOCK), slot),
            ],
            scratch_shapes=[pltpu.VMEM((width // HEAD_DIM, length, BLOCK), F32)],
        ),
        out_shape=[
            jax.ShapeDtypeStruct((pairs, width, BLOCK), BF16),
            jax.ShapeDtypeStruct((pairs, width, BLOCK), F32),
            jax.ShapeDtypeStruct((pairs, 8, BLOCK), F32),
        ],
        compiler_params=pltpu.CompilerParams(vmem_limit_bytes=VMEM_LIMIT),
    )(core, qt, kv, vt)


def retrace_kernel(
    core_ref, qt_ref, grad_ref, full_ref, stat_ref, cos_ref, sin_ref, kv_ref, kt_ref,
    weight_ref, joint_ref, normed_ref, dkv_ref,
):
    step_id = pl.program_id(0)
    pair = pl.num_programs(0) - 1 - step_id
    odd = core_ref[0] ^ (pair & 1)
    width = qt_ref.shape[0]
    heads = width // HEAD_DIM
    half = HEAD_DIM // 2

    @pl.when(step_id == 0)
    def _():
        dkv_ref[...] = jnp.zeros_like(dkv_ref)

    blank = jnp.zeros((HEAD_DIM, BLOCK), BF16)
    lefts, rights, deltas, norms = [], [], [], []
    for h in range(heads):
        rows = slice(h * HEAD_DIM, (h + 1) * HEAD_DIM)
        query = qt_ref[rows, :]
        grad = grad_ref[0, rows, :]
        lefts.append(
            jnp.concatenate(
                [
                    jnp.concatenate([query, blank], axis=1),
                    jnp.concatenate([blank, grad], axis=1),
                ],
                axis=0,
            )
        )
        rights.append(
            jnp.concatenate(
                [
                    jnp.concatenate([blank, query], axis=1),
                    jnp.concatenate([grad, blank], axis=1),
                ],
                axis=0,
            )
        )
        deltas.append(jnp.sum(grad.astype(F32) * full_ref[0, rows, :], axis=0, keepdims=True))
        norms.append(stat_ref[0, h : h + 1, :])

    def absorb(step, state, masked):
        keys = pl.ds(pl.multiple_of(step * CHUNK, CHUNK), CHUNK)
        fresh = []
        for h in range(heads):
            both = contract(kv_ref[h, keys, :], lefts[h], 1, 0)
            probs = jnp.exp(both[:, :BLOCK] - norms[h])
            if masked:
                probs = jnp.where(last_mask(odd, CHUNK), probs, 0.0)
            grad_scores = (probs * (both[:, BLOCK:] - deltas[h])).astype(BF16)
            joined = jnp.concatenate([probs.astype(BF16), grad_scores], axis=1)
            dkv_ref[h, keys, :] += contract(joined, rights[h], 1, 1)
            turned = kt_ref[h * HEAD_DIM : (h + 1) * HEAD_DIM, keys]
            fresh.append(state[h] + contract(turned, grad_scores, 1, 0))
        return fresh

    state = [jnp.zeros((HEAD_DIM, BLOCK), F32) for _ in range(heads)]
    state = lax.fori_loop(0, pair, lambda i, s: absorb(i, s, False), state)
    state = absorb(pair, state, True)
    offset = pl.multiple_of(pair * CHUNK, CHUNK)
    cosine = cos_ref[...]
    sine = sin_ref[...]
    column = lax.broadcasted_iota(jnp.int32, (HEAD_DIM, CHUNK), 1) // BLOCK

    for h in range(heads):
        base = h * HEAD_DIM
        doubled = jnp.concatenate([state[h], state[h]], axis=1) * HEAD_DIM ** (-0.5)
        doubled = jnp.where(column == odd, doubled, 0.0)
        turned_back = jnp.transpose(dkv_ref[h, pl.ds(offset, CHUNK), :])
        for part, value in ((0, doubled), (1, turned_back[:HEAD_DIM])):
            former = value[:half]
            latter = value[half:]
            turned = jnp.concatenate(
                [former * cosine + latter * sine, latter * cosine - former * sine], axis=0
            )
            start = part * width + base
            joint_ref[start : start + HEAD_DIM, :] = turned.astype(BF16)
        start = 2 * width + base
        joint_ref[start : start + HEAD_DIM, :] = turned_back[HEAD_DIM:].astype(BF16)
    normed_ref[...] = contract(joint_ref[...], weight_ref[...], 0, 0).astype(BF16)


def retrace(core, qt, grads, full, stats, cosine, sine, kv, kt, weight):
    width, length = qt.shape
    heads = width // HEAD_DIM
    half = HEAD_DIM // 2
    pairs = length // CHUNK
    back = lambda j: pairs - 1 - j
    own = lambda j, core: (0, 2 * back(j) + (core[0] ^ (back(j) & 1)))
    slot = lambda j, core: (back(j), 0, 0)
    across = lambda j, core: (0, back(j))
    return pl.pallas_call(
        retrace_kernel,
        name="retrace",
        cost_estimate=cost(
            5 * 2 * BLOCK * BLOCK * BLOCK * 2 * sum(range(1, pairs + 1)) * heads,
            3 * kv.size + 16 * pairs * width * BLOCK,
            CHUNK * BLOCK * sum(range(1, pairs + 1)) * heads,
        ),
        grid_spec=pltpu.PrefetchScalarGridSpec(
            num_scalar_prefetch=1,
            grid=(pairs,),
            in_specs=[
                pl.BlockSpec((width, BLOCK), own),
                pl.BlockSpec((1, width, BLOCK), slot),
                pl.BlockSpec((1, width, BLOCK), slot),
                pl.BlockSpec((1, 8, BLOCK), slot),
                pl.BlockSpec((half, CHUNK), across),
                pl.BlockSpec((half, CHUNK), across),
                pl.BlockSpec(kv.shape, lambda j, core: (0, 0, 0)),
                pl.BlockSpec(kt.shape, lambda j, core: (0, 0)),
                pl.BlockSpec(weight.shape, lambda j, core: (0, 0)),
            ],
            out_specs=[
                pl.BlockSpec((3 * width, CHUNK), across),
                pl.BlockSpec((CHUNK, weight.shape[1]), lambda j, core: (back(j), 0)),
            ],
            scratch_shapes=[pltpu.VMEM((heads, length, 2 * HEAD_DIM), F32)],
        ),
        out_shape=[
            jax.ShapeDtypeStruct((3 * width, length), BF16),
            jax.ShapeDtypeStruct((length, weight.shape[1]), BF16),
        ],
        compiler_params=pltpu.CompilerParams(vmem_limit_bytes=VMEM_LIMIT),
    )(core, qt, grads, full, stats, cosine, sine, kv, kt, weight)


def after(values, *earlier_values):
    values = tuple(values)
    return lax.optimization_barrier(values + tuple(earlier_values))[: len(values)]


def assemble_kernel(place_ref, *refs):
    down_ref, out_ref = refs[-2:]
    rep = place_ref[1]
    reps = (len(refs) - 2) // 2
    part = out_ref.shape[0]
    for side in range(2):
        @pl.when(pl.program_id(0) == side)
        def _():
            for k in range(reps):
                piece = refs[side * reps + k]
                rows = piece.shape[1]
                target = rep ^ k

                @pl.when(target < reps - 1)
                def _():
                    down_ref[pl.ds(pl.multiple_of(target * rows, rows), rows), :] = piece[0]

                @pl.when(target == reps - 1)
                def _():
                    out_ref[...] = piece[0, :part]


def assemble(place, mine, twin, part):
    owners, rows, columns = mine[0].shape
    reps = len(mine)
    groups = 2 * owners

    def held(side):
        def index(which, z, place):
            moving = (place[0] // 2 + owners - z) % owners
            fixed = (place[0] // 2 + owners - (owners - 1) * (1 - side)) % owners
            return (jnp.where(which == side, moving, fixed), 0, 0)

        return pl.BlockSpec((1, rows, columns), index)

    device = lambda which, z, place: 2 * z + (which ^ (place[0] % 2))
    target = lambda which, z, place: (device(which, z, place), 0)
    return pl.pallas_call(
        assemble_kernel,
        name="assemble",
        grid_spec=pltpu.PrefetchScalarGridSpec(
            num_scalar_prefetch=1,
            grid=(2, owners),
            in_specs=[held(0)] * reps + [held(1)] * reps,
            out_specs=[
                pl.BlockSpec(((reps - 1) * rows, columns), target),
                pl.BlockSpec((part, columns), target),
            ],
        ),
        out_shape=[
            jax.ShapeDtypeStruct((groups * (reps - 1) * rows, columns), BF16),
            jax.ShapeDtypeStruct((groups * part, columns), BF16),
        ],
        compiler_params=pltpu.CompilerParams(vmem_limit_bytes=VMEM_LIMIT),
    )(place, *mine, *twin)


def swap_core(value):
    groups = lax.axis_size("shard")
    return lax.ppermute(value, "shard", [(i, i ^ 1) for i in range(groups)])


def shift_owner(value, distance):
    groups = lax.axis_size("shard")
    step = 2 * distance
    return lax.ppermute(value, "shard", [(i, (i + step) % groups) for i in range(groups)])


def cross_rep(value, mask):
    return lax.ppermute(value, "rep", [(i, i ^ mask) for i in range(lax.axis_size("rep"))])


def pick(stacked, index, axis=0):
    return lax.dynamic_index_in_dim(stacked, index, axis, keepdims=False)


def add_low(*values):
    total = values[0].astype(F32)
    for value in values[1:]:
        total = total + value.astype(F32)
    return total.astype(BF16)


def fold_core(partial_sums, core):
    halves = partial_sums.reshape((-1, 2) + partial_sums.shape[1:])
    received = swap_core(pick(halves, 1 - core, 1))
    return add_low(pick(halves, core, 1), received)


def rep_parts(value):
    reps = lax.axis_size("rep")
    owners, rows, columns = value.shape
    return value.reshape(owners, reps, rows // reps, columns)


def send_rep(value):
    rep = lax.axis_index("rep")
    parts = rep_parts(value)
    return [cross_rep(pick(parts, rep ^ k, 1), k) for k in range(1, lax.axis_size("rep"))]


def pick_parts(value):
    rep = lax.axis_index("rep")
    parts = rep_parts(value)
    return [pick(parts, rep ^ k, 1) for k in range(lax.axis_size("rep"))]


def join_rep(value, received):
    return add_low(pick(rep_parts(value), lax.axis_index("rep"), 1), *received)


def unpack_kernel(rep_ref, *refs):
    reps = 4
    pieces = refs[: 3 * reps]
    in_ref, out_ref, qkv_ref, down_ref = refs[3 * reps : 3 * reps + 4]
    line_refs = refs[3 * reps + 4 :]
    hidden_width = in_ref.shape[1]
    model_width = out_ref.shape[1]
    columns = qkv_ref.shape[1] // 3
    owners = down_ref.shape[0] // in_ref.shape[0]
    width = columns // owners
    for k in range(reps):
        pair, joint, down = pieces[k::reps]
        rows = pair.shape[0]
        first = pl.multiple_of((rep_ref[0] ^ k) * rows, 8)
        own = pl.ds(first, rows)
        in_ref[own, :] = pair[:, :hidden_width].astype(F32)
        out_ref[own, :] = pair[:, hidden_width:].astype(F32)
        whole = joint[:, : 3 * columns].astype(F32)
        for part in range(3):
            qkv_ref[own, part * columns : (part + 1) * columns] = jnp.concatenate(
                [
                    whole[:, (3 * z + part) * width : (3 * z + part + 1) * width]
                    for z in range(owners)
                ],
                axis=1,
            )

        @pl.when(rep_ref[0] == k)
        def _():
            part = line_refs[0].shape[1] // 2
            lines = joint[:, 3 * columns :].astype(F32)
            row = 0
            for line_ref in line_refs:
                count = line_ref.shape[1] // part
                line_ref[...] = jnp.concatenate(
                    [lines[row + i : row + i + 1, :part] for i in range(count)], axis=1
                )
                row += count

        for z in range(owners):
            block = pl.ds(pl.multiple_of(owners * first + z * rows, 8), rows)
            down_ref[block, :] = down[:, z * model_width : (z + 1) * model_width].astype(F32)


def unpack(rep, pair, joint, down, widths, counts):
    hidden_width, model_width, columns = widths
    pieces = [*pair, *joint, *down]
    rows = len(pair) * pair[0].shape[0]
    owners = model_width * 3 // columns
    shapes = [
        (rows, hidden_width),
        (rows, model_width),
        (rows, 3 * model_width),
        (owners * rows, model_width),
    ] + [(1, count * rows) for count in counts]
    whole = pl.BlockSpec(memory_space=pltpu.VMEM)
    return pl.pallas_call(
        unpack_kernel,
        name="unpack",
        in_specs=[pl.BlockSpec(memory_space=pltpu.SMEM)] + [whole] * len(pieces),
        out_specs=[whole] * len(shapes),
        out_shape=[jax.ShapeDtypeStruct(shape, F32) for shape in shapes],
        compiler_params=pltpu.CompilerParams(vmem_limit_bytes=VMEM_LIMIT),
    )(rep, *pieces)


def split_depth(value):
    high = lax.reduce_precision(value, 8, 7)
    return jnp.concatenate([high, value - high]).astype(BF16)


def join_depth(value):
    value = value.astype(F32)
    half = value.shape[0] // 2
    return value[:half] + value[half:]


def add_ordered(values, index_of):
    stacked = jnp.stack(values)
    total = pick(stacked, index_of(0))
    for sender in range(1, len(values)):
        total = total + pick(stacked, index_of(sender))
    return total


def every_rep(value):
    return [value] + [cross_rep(value, k) for k in range(1, lax.axis_size("rep"))]


def exchange_owner(value, owner):
    owners = value.shape[0]
    received = [pick(value, owner)]
    for k in range(1, owners):
        received.append(shift_owner(pick(value, (owner + k) % owners), k))
    return received


def middle_kernel(
    core_ref, weights_ref, mixed_ref, x_ref, cotangent_ref, w_out_ref, b_out_ref, gain_ref,
    shift_ref, w_in_ref, b_in_ref, grad_ref,
    middle_ref, low_ref, active_ref, hidden_ref, total_ref, branch_ref, send_ref,
    sums_ref, hidden_sums_ref, plain_ref, scale_ref, back_ref,
):
    step = pl.program_id(0)
    core = core_ref[0]
    owners = mixed_ref.shape[0] // 2
    width = mixed_ref.shape[1]

    @pl.when(step == 0)
    def _():
        for half in range(2):
            rows = slice(half * BLOCK, (half + 1) * BLOCK)
            mixed = jnp.concatenate(
                [mixed_ref[2 * z + (core ^ half)] for z in range(owners)], axis=0
            )
            branch = contract(mixed, w_out_ref[...], 0, 0) + b_out_ref[...]
            middle = x_ref[rows, :].astype(F32) + branch
            middle_ref[rows, :] = middle
            center = middle - jnp.mean(middle, axis=-1, keepdims=True)
            scale = lax.rsqrt(jnp.mean(center * center, axis=-1, keepdims=True) + EPSILON)
            plain = center * scale
            scale_ref[rows, :] = jnp.broadcast_to(scale, (BLOCK, scale_ref.shape[1]))
            plain_ref[rows, :] = plain
            low_ref[rows, :] = (plain * gain_ref[...] + shift_ref[...]).astype(BF16)
        back_ref[...] = jnp.zeros_like(back_ref)

    hidden = contract(low_ref[...], w_in_ref[...], 1, 0) + b_in_ref[...]
    square = hidden * hidden
    bend = math.sqrt(2 / math.pi)
    turned = jnp.tanh(hidden * (bend + (bend * 0.044715) * square))
    share = 0.5 + 0.5 * turned
    active_ref[...] = (hidden * share).astype(BF16)
    slope = (0.5 * hidden) * (1.0 - turned * turned) * (bend + (3 * bend * 0.044715) * square)
    grad = (grad_ref[...].astype(F32) * (share + slope)).astype(BF16)
    hidden_ref[...] = grad
    hidden_sums_ref[...] = jnp.sum(grad.astype(F32), axis=0, keepdims=True)
    back_ref[...] += contract(grad, w_in_ref[...], 1, 1)

    @pl.when(step == pl.num_programs(0) - 1)
    def _():
        weight = weights_ref[4]
        sums = [jnp.zeros((1, back_ref.shape[1]), F32)] * 3
        for half in range(2):
            rows = slice(half * BLOCK, (half + 1) * BLOCK)
            back = back_ref[rows, :]
            plain = plain_ref[rows, :]
            scaled = back * gain_ref[...]
            total = weight * cotangent_ref[rows, :] + scale_ref[rows, :1] * (
                scaled
                - jnp.mean(scaled, axis=-1, keepdims=True)
                - plain * jnp.mean(scaled * plain, axis=-1, keepdims=True)
            )
            total_ref[rows, :] = total
            low = total.astype(BF16)
            branch_ref[rows, :] = low
            mixed = contract(w_out_ref[...], low, 1, 1).astype(BF16)
            for z in range(owners):
                send_ref[2 * z + (core ^ half)] = mixed[z * width : (z + 1) * width, :]
            for i, value in enumerate((low.astype(F32), back * plain, back)):
                sums[i] = sums[i] + jnp.sum(value, axis=0, keepdims=True)
        for i in range(3):
            sums_ref[i : i + 1, :] = sums[i]


def middle_part(
    core, depth_weights, mixed, x, cotangent, w_out, b_out, gain, shift, w_in, b_in, grad_active
):
    rows, model_width = x.shape
    hidden_width = w_in.shape[1]
    chunk = CHUNK
    whole = lambda value: pl.BlockSpec(value.shape, lambda j, *_: (0,) * value.ndim)
    across = pl.BlockSpec((rows, chunk), lambda j, *_: (0, j))
    line = pl.BlockSpec((1, chunk), lambda j, *_: (0, j))
    shapes = [
        jax.ShapeDtypeStruct((rows, model_width), F32),
        jax.ShapeDtypeStruct((rows, model_width), BF16),
        jax.ShapeDtypeStruct((rows, hidden_width), BF16),
        jax.ShapeDtypeStruct((rows, hidden_width), BF16),
        jax.ShapeDtypeStruct((rows, model_width), F32),
        jax.ShapeDtypeStruct((rows, model_width), BF16),
        jax.ShapeDtypeStruct(mixed.shape, BF16),
        jax.ShapeDtypeStruct((8, model_width), F32),
        jax.ShapeDtypeStruct((1, hidden_width), F32),
    ]
    out_specs = [whole(shape) for shape in shapes]
    out_specs[2] = out_specs[3] = across
    out_specs[8] = line
    return pl.pallas_call(
        middle_kernel,
        name="middle",
        cost_estimate=cost(
            4 * rows * model_width * (hidden_width + model_width),
            2 * w_in.size + 8 * grad_active.size,
            grad_active.size,
        ),
        grid_spec=pltpu.PrefetchScalarGridSpec(
            num_scalar_prefetch=2,
            grid=(hidden_width // chunk,),
            in_specs=[
                whole(mixed),
                whole(x),
                whole(cotangent),
                whole(w_out),
                whole(b_out),
                whole(gain),
                whole(shift),
                pl.BlockSpec((model_width, chunk), lambda j, *_: (0, j)),
                line,
                across,
            ],
            out_specs=out_specs,
            scratch_shapes=[
                pltpu.VMEM((rows, model_width), F32),
                pltpu.VMEM((rows, 128), F32),
                pltpu.VMEM((rows, model_width), F32),
            ],
        ),
        out_shape=shapes,
        compiler_params=pltpu.CompilerParams(vmem_limit_bytes=VMEM_LIMIT),
    )(
        core, depth_weights, mixed, x, cotangent, w_out, b_out, gain, shift, w_in, b_in,
        grad_active,
    )


def down_kernel(active_ref, down_grad_ref, down_ref):
    down_ref[...] = contract(active_ref[...], down_grad_ref[...], 0, 0).astype(BF16)


def down_part(active, down_grad):
    rows, model_width = down_grad.shape
    steps = active.shape[1] // model_width
    return pl.pallas_call(
        down_kernel,
        name="down_part",
        grid=(steps,),
        in_specs=[
            pl.BlockSpec((rows, model_width), lambda j: (0, j)),
            pl.BlockSpec((rows, model_width), lambda j: (0, 0)),
        ],
        out_specs=pl.BlockSpec((model_width, model_width), lambda j: (j, 0)),
        out_shape=jax.ShapeDtypeStruct((steps * model_width, model_width), BF16),
        compiler_params=pltpu.CompilerParams(vmem_limit_bytes=VMEM_LIMIT),
    )(active, down_grad)


def result_kernel(
    weights_ref, active_ref, w_down_ref, b_down_ref, middle_ref, mix_ref, cotangent_ref,
    layer_ref, depth_ref, total_ref,
):
    step = pl.program_id(0)

    @pl.when(step == 0)
    def _():
        total_ref[...] = middle_ref[...] + b_down_ref[...]

    total_ref[...] += contract(active_ref[...], w_down_ref[...], 1, 0)

    @pl.when(step == pl.num_programs(0) - 1)
    def _():
        result = total_ref[...]
        layer_ref[...] = weights_ref[4] * result + mix_ref[...]
        depth = (result * cotangent_ref[...]).reshape(-1, 8, result.shape[1])
        depth_ref[...] = jnp.sum(depth, axis=0)


def result_part(depth_weights, active, w_down, b_down, middle, mix, cotangent):
    rows, model_width = middle.shape
    steps = active.shape[1] // model_width
    whole = lambda value: pl.BlockSpec(value.shape, lambda j, *_: (0,) * value.ndim)
    depth = jax.ShapeDtypeStruct((8, model_width), F32)
    return pl.pallas_call(
        result_kernel,
        name="result_part",
        grid_spec=pltpu.PrefetchScalarGridSpec(
            num_scalar_prefetch=1,
            grid=(steps,),
            in_specs=[
                pl.BlockSpec((rows, model_width), lambda j, *_: (0, j)),
                pl.BlockSpec((model_width, model_width), lambda j, *_: (j, 0)),
                whole(b_down), whole(middle), whole(mix), whole(cotangent),
            ],
            out_specs=[whole(middle), whole(depth)],
            scratch_shapes=[pltpu.VMEM((rows, model_width), F32)],
        ),
        out_shape=[jax.ShapeDtypeStruct(middle.shape, F32), depth],
        compiler_params=pltpu.CompilerParams(vmem_limit_bytes=VMEM_LIMIT),
    )(depth_weights, active, w_down, b_down, middle, mix, cotangent)


def pair_kernel(
    core_ref, low_ref, hidden_ref, mixed_ref, branch_ref,
    low_twin_ref, hidden_twin_ref, mixed_twin_ref, branch_twin_ref,
    own_ref, turned_ref, rows_ref,
):
    step = pl.program_id(0)
    core = core_ref[0]
    owners, part, width = own_ref.shape
    last = pl.num_programs(0) - 1

    @pl.when(step == 0)
    def _():
        for side, ref in ((0, low_ref), (1, low_twin_ref)):
            turned_ref[...] = jnp.transpose(ref[...].astype(F32)).astype(BF16)
            for z in range(owners):
                start = pl.multiple_of((2 * z + core) * part, part)
                rows_ref[side, z * part : (z + 1) * part, :] = turned_ref[pl.ds(start, part), :]

    @pl.when(step < last)
    def _():
        total = contract(rows_ref[0], hidden_ref[...], 1, 0)
        total = total + contract(rows_ref[1], hidden_twin_ref[...], 1, 0)
        own_ref[...] = total.astype(BF16).reshape(owners, part, width)

    @pl.when(step == last)
    def _():
        total = 0.0
        sides = ((core, mixed_ref, branch_ref), (1 - core, mixed_twin_ref, branch_twin_ref))
        for member, ref, grad_ref in sides:
            for half in range(2):
                mixed = jnp.concatenate(
                    [
                        ref[
                            2 * z + (member ^ half),
                            pl.ds(pl.multiple_of(core * part, part), part),
                            :,
                        ]
                        for z in range(owners)
                    ],
                    axis=0,
                )
                rows = slice(half * BLOCK, (half + 1) * BLOCK)
                total = total + contract(mixed, grad_ref[rows, :], 1, 0)
        own_ref[...] = total.astype(BF16).reshape(owners, part, width)


def pair_sums(core, own, twin):
    low, hidden, mixed, branch = own
    rows, model_width = low.shape
    owners = mixed.shape[0] // 2
    part = model_width // (2 * owners)
    steps = hidden.shape[1] // model_width
    whole = lambda value: pl.BlockSpec(value.shape, lambda j, core: (0,) * value.ndim)
    chunk = pl.BlockSpec((rows, model_width), lambda j, core: (0, jnp.minimum(j, steps - 1)))
    one_side = [whole(low), chunk, whole(mixed), whole(branch)]
    return pl.pallas_call(
        pair_kernel,
        name="pair_sums",
        grid_spec=pltpu.PrefetchScalarGridSpec(
            num_scalar_prefetch=1,
            grid=(steps + 1,),
            in_specs=one_side * 2,
            out_specs=pl.BlockSpec((owners, part, model_width), lambda j, core: (0, 0, j)),
            scratch_shapes=[
                pltpu.VMEM((model_width, rows), BF16),
                pltpu.VMEM((2, owners * part, rows), BF16),
            ],
        ),
        out_shape=jax.ShapeDtypeStruct((owners, part, (steps + 1) * model_width), BF16),
        compiler_params=pltpu.CompilerParams(vmem_limit_bytes=VMEM_LIMIT),
    )(core, *own, *twin)


def joint_kernel(
    core_ref, plain_ref, joint_ref, weight_ref, gain_ref, shift_ref,
    own_ref, other_ref, sums_ref, lines_ref, product_ref, full_ref,
):
    step = pl.program_id(0)
    core = core_ref[0]
    owners, part, columns = own_ref.shape
    joint = joint_ref[...]
    product = contract(joint, plain_ref[...], 1, 0)
    line = contract(jnp.ones((8, joint.shape[1]), BF16), joint, 1, 1)

    @pl.when(step == 0)
    def _():
        product_ref[...] = product
        lines_ref[...] = line

    @pl.when(step > 0)
    def _():
        product_ref[...] += product
        lines_ref[...] += line

    @pl.when(step == pl.num_programs(0) - 1)
    def _():
        total = product_ref[...]
        sums = jnp.transpose(lines_ref[...])[:, :1]
        weight = weight_ref[...].astype(F32)
        sums_ref[0:1, :] = jnp.sum(total * weight, axis=0, keepdims=True)
        sums_ref[1:2, :] = jnp.sum(sums * weight, axis=0, keepdims=True)
        full_ref[...] = jnp.transpose(gain_ref[...] * total + shift_ref[...] * sums).astype(BF16)
        for z in range(owners):
            for side, ref in ((0, own_ref), (1, other_ref)):
                start = pl.multiple_of((2 * z + (core ^ side)) * part, part)
                ref[z] = full_ref[pl.ds(start, part), :]


def joint_part(core, plain, joint_t, weight_t, gain, shift):
    length, model_width = plain.shape
    columns = joint_t.shape[0]
    owners = length // CHUNK // 2
    part = model_width // (2 * owners)
    whole = lambda value: pl.BlockSpec(value.shape, lambda j, core: (0,) * value.ndim)
    shapes = [
        jax.ShapeDtypeStruct((owners, part, columns), BF16),
        jax.ShapeDtypeStruct((owners, part, columns), BF16),
        jax.ShapeDtypeStruct((8, model_width), F32),
        jax.ShapeDtypeStruct((8, columns), F32),
    ]
    return pl.pallas_call(
        joint_kernel,
        name="joint_part",
        grid_spec=pltpu.PrefetchScalarGridSpec(
            num_scalar_prefetch=1,
            grid=(length // CHUNK,),
            in_specs=[
                pl.BlockSpec((CHUNK, model_width), lambda j, core: (j, 0)),
                pl.BlockSpec((columns, CHUNK), lambda j, core: (0, j)),
                whole(weight_t),
                whole(gain),
                whole(shift),
            ],
            out_specs=[whole(shape) for shape in shapes],
            scratch_shapes=[
                pltpu.VMEM((columns, model_width), F32),
                pltpu.VMEM((model_width, columns), BF16),
            ],
        ),
        out_shape=shapes,
        compiler_params=pltpu.CompilerParams(vmem_limit_bytes=VMEM_LIMIT),
    )(core, plain, joint_t, weight_t, gain, shift)


def head_split_device(
    block_in,
    earlier,
    cotangent,
    qkv_weight,
    out_weight,
    in_weight,
    down_weight,
    qk_bias,
    value_bias,
    out_bias,
    in_bias,
    down_bias,
    gain_one,
    shift_one,
    gain_two,
    shift_two,
    depth_weights,
):
    row_count, model_width = block_in.shape
    hidden_width = in_weight.shape[1]
    groups = lax.axis_size("shard")
    owners = groups // 2
    width = model_width // owners
    part = model_width // groups
    length = row_count * groups
    half = HEAD_DIM // 2
    member = lax.axis_index("shard")
    owner = member // 2
    core = member % 2

    pieces = qkv_weight.astype(BF16).reshape(part, 3, owners, width)
    pieces = jnp.transpose(pieces, (2, 0, 1, 3)).reshape(owners, part, 3 * width)
    vectors = (
        qk_bias, value_bias, gain_one, shift_one,
        out_bias, in_bias, down_bias, gain_two, shift_two,
    )
    late = lax.optimization_barrier(jnp.concatenate(vectors))
    early, late = late[: 5 * part], late[5 * part :]
    half_late = late.shape[0] // 2
    rows = [early, late[:half_late], late[half_late:]]
    rows = jnp.stack([jnp.pad(row, (0, 3 * width - row.shape[0])) for row in rows])
    early = jnp.pad(rows.astype(BF16), ((0, 5), (0, 0)))
    early = jnp.broadcast_to(early, (owners, 8, 3 * width))
    packets = exchange_owner(jnp.concatenate([pieces, early], axis=1), owner)
    packet = jnp.stack(packets)
    other_packet = swap_core(packet)

    tokens = lax.all_gather(block_in, "shard", axis=0, tiled=True)
    grad_earlier, mix, depth_sums = average(depth_weights, earlier, cotangent)

    by_core = jnp.stack([packet, other_packet])
    packet = jnp.stack(
        [
            lax.dynamic_slice(
                by_core,
                (core ^ (d % 2), (owner - d // 2) % owners, 0, 0),
                (1, 1, part + 8, 3 * width),
            )[0, 0]
            for d in range(groups)
        ]
    )
    w_own = packet[:, :part].reshape(model_width, 3 * width)
    early = packet[:, part].astype(F32)
    late = packet[:, part + 1 : part + 3, :half_late].astype(F32).reshape(groups, -1)
    b_qk = early[:, : 2 * part].reshape(2 * model_width)
    b_value = early[:, 2 * part : 3 * part].reshape(model_width)
    g_one = early[:, 3 * part : 4 * part].reshape(1, model_width)
    s_one = early[:, 4 * part : 5 * part].reshape(1, model_width)
    b_joint = jnp.concatenate([b_qk, b_value]).reshape(3, owners, width)
    b_own = lax.dynamic_index_in_dim(b_joint, owner, 1, keepdims=False).reshape(3 * width, 1)
    w_turned = jnp.transpose(w_own)

    freqs = 10000.0 ** (-jnp.arange(half, dtype=F32) / half)
    angles = freqs[:, None] * jnp.arange(length, dtype=jnp.int32).astype(F32)[None, :]
    cosine = jnp.cos(angles)
    sine = jnp.sin(angles)
    core_index = core.astype(jnp.int32).reshape(1)

    hidden_part = hidden_width // groups
    share = hidden_part // 3
    row = lambda first, size: late[:, first : first + size].reshape(1, groups * size)
    b_out = row(0, part)
    b_in = row(part, hidden_part)
    b_down = row(part + hidden_part, part)
    g_two = row(2 * part + hidden_part, part)
    s_two = row(3 * part + hidden_part, part)
    last = jnp.pad(out_weight.astype(BF16), ((0, share - part), (0, 0)))
    rep = lax.axis_index("rep")
    tail_packet = lax.dynamic_slice_in_dim(
        jnp.concatenate([down_weight.astype(BF16), last], axis=0), rep * share, share, 0
    )
    tokens, w_turned, b_own, cosine, sine, mix, tail_packet, in_packet = after(
        (tokens, w_turned, b_own, cosine, sine, mix, tail_packet, in_weight.astype(BF16)),
        grad_earlier,
        depth_sums,
    )
    tail_parts = [tail_packet] + [shift_owner(tail_packet, k) for k in range(1, owners)]
    states = project(tokens, w_turned, b_own, g_one, s_one, cosine, sine, 0, groups, ())
    plain_all, qt, kt, vt, kv, *tail_parts = lax.optimization_barrier((*states, *tail_parts))
    grad_result = depth_weights[4] * cotangent
    down_grad = grad_result.astype(BF16)
    tail_stack = jnp.stack(tail_parts)
    qt, tail_stack, in_packet, down_grad = lax.optimization_barrier(
        (qt, tail_stack, in_packet, down_grad)
    )
    w_in = lax.all_gather(in_packet, "shard", axis=0, tiled=True)
    tail_mine = every_rep(tail_stack)
    mixed_own, attended, stats = attend(core_index, qt, kv, vt)
    stats, *tail_mine = lax.optimization_barrier((stats, *tail_mine))
    mixed_two = lax.all_to_all(mixed_own, "shard", 0, 0)
    tail_other = [swap_core(value) for value in tail_mine]
    w_down, w_out = assemble(
        jnp.stack([member, rep]).astype(jnp.int32), tail_mine, tail_other, part
    )
    grad_active = contract(down_grad, w_down, 1, 1).astype(BF16)
    mixed_two, grad_active = lax.optimization_barrier((mixed_two, grad_active))

    inputs = block_in.astype(F32)
    (
        middle, normed_two_low, active, grad_hidden, grad_middle, branch_grad, grad_own,
        token_sums, grad_in_b,
    ) = middle_part(
        core_index, depth_weights, mixed_two, block_in, cotangent, w_out, b_out, g_two, s_two,
        w_in, b_in, grad_active,
    )
    grad_out_b, grad_gain_two, grad_shift_two = (token_sums[i] for i in range(3))
    grad_in_b = grad_in_b[0]
    grad_own = lax.all_to_all(grad_own, "shard", 0, 0)
    pair_own = (normed_two_low, grad_hidden, mixed_two, branch_grad)
    pair_twin = tuple(swap_core(value) for value in pair_own)
    grad_down_w = down_part(active, down_grad)
    folded = pair_sums(core_index, pair_own, pair_twin)
    grad_down_b = jnp.sum(down_grad.astype(F32), axis=0)
    grad_own, folded, grad_down_w = lax.optimization_barrier((grad_own, folded, grad_down_w))
    sent = send_rep(folded)
    down_sums = lax.psum_scatter(grad_down_w, "shard", scatter_dimension=0, tiled=True)
    joint_t, grad_normed = retrace(
        core_index, qt, grad_own, attended, stats, cosine, sine, kv, kt, w_turned
    )
    joint_t, grad_normed, folded, plain_all, active, *sent = lax.optimization_barrier(
        (joint_t, grad_normed, folded, plain_all, active, *sent)
    )
    grad_normed = lax.psum_scatter(
        grad_normed, "shard", scatter_dimension=0, tiled=True
    )
    folded = join_rep(folded, sent)

    own_sums, other_sums, first_sums, joint_sums = joint_part(
        core_index, plain_all, joint_t, w_turned, g_one, s_one
    )
    arrived = exchange_owner(folded, owner)
    layer_out, last_depth = result_part(
        depth_weights, active, w_down, b_down, middle, mix, cotangent
    )
    own_sums, other_sums, first_sums, joint_sums, last_depth, *arrived = (
        lax.optimization_barrier(
            (own_sums, other_sums, first_sums, joint_sums, last_depth, *arrived)
        )
    )
    pair_sum = add_low(*arrived)
    grad_gain_one, grad_shift_one = first_sums[0], first_sums[1]
    joint_sums = joint_sums[0]

    spread_sums = lax.dynamic_update_slice(
        jnp.zeros((3, model_width), F32), joint_sums.reshape(3, width), (0, owner * width)
    ).reshape(3 * model_width)
    vectors = (
        spread_sums[: 2 * model_width],
        spread_sums[2 * model_width :],
        grad_out_b,
        grad_in_b,
        grad_down_b,
        grad_gain_one,
        grad_shift_one,
        grad_gain_two,
        grad_shift_two,
    )
    counts = [vector.shape[0] // model_width for vector in vectors]
    small = jnp.concatenate(
        [
            vector.reshape(groups, count, part).astype(BF16)
            for vector, count in zip(vectors, counts)
        ],
        axis=1,
    )
    small = jnp.pad(small, ((0, 0), (0, part - small.shape[1]), (0, 128 - part)))
    mark = (part // 4 - 8, 3 * width)
    small = small.reshape(owners, 2, part, 128)
    depth_count = 2 * depth_weights.shape[0]
    depth_row = lambda value: value[mark[0], mark[1] : mark[1] + depth_count]
    with_depth = lambda value, sums: value.at[
        :, mark[0], mark[1] : mark[1] + depth_count
    ].set(split_depth(sums))
    received = swap_core(
        jnp.concatenate([other_sums, pick(small, 1 - core, 1)], axis=2)
    )
    mixed_sums = add_low(
        jnp.concatenate([own_sums, pick(small, core, 1)], axis=2), received
    )
    depth_sum = jnp.concatenate([depth_sums, last_depth[None]], axis=0).sum(axis=(1, 2))
    down_parts = pick_parts(down_sums[None])
    down_rows = part // 4
    columns = 3 * width + 128
    sums_parts = [with_depth(value, depth_sum) for value in pick_parts(mixed_sums)]
    received = [
        cross_rep(
            jnp.concatenate([sums, down.reshape(owners, down_rows, model_width)], axis=2), k
        )
        for k, (sums, down) in enumerate(zip(sums_parts[1:], down_parts[1:]), 1)
    ]
    pair_sum, *received = lax.optimization_barrier((pair_sum, *received))
    pair_pieces = every_rep(pair_sum)
    mixed_sums = add_low(sums_parts[0], *[value[:, :, :columns] for value in received])
    depth_sum = add_ordered(
        [join_depth(depth_row(value[0])) for value in (sums_parts[0], *received)], lambda k: rep ^ k
    )
    mixed_sums = with_depth(mixed_sums, depth_sum)
    down_sums = add_low(
        down_parts[0].reshape(owners, down_rows, model_width),
        *[value[:, :, columns:] for value in received],
    )
    down_pieces = every_rep(jnp.concatenate([down_sums[k] for k in range(owners)], axis=1))
    arrived = exchange_owner(mixed_sums, owner)
    arrived = lax.optimization_barrier((*arrived, *pair_pieces, *down_pieces))
    pair_pieces, down_pieces = arrived[owners : owners + 4], arrived[owners + 4 :]
    arrived = arrived[:owners]
    small = add_low(*[value[:, 3 * width :] for value in arrived])
    by_distance = jnp.stack([value[:, : 3 * width] for value in arrived])
    by_owner = [pick(by_distance, (owner - k) % owners) for k in range(owners)]
    joint_pieces = every_rep(jnp.concatenate([*by_owner, small], axis=1))
    depth_sums = [depth_row(value) for value in arrived]
    grad_normed, *pieces = lax.optimization_barrier((grad_normed, *joint_pieces, *depth_sums))
    joint_pieces, depth_sums = pieces[:4], pieces[4:]
    grad_depth = add_ordered(
        [join_depth(value) for value in depth_sums], lambda k: (owner - k) % owners
    )
    grad_depth = grad_depth + swap_core(grad_depth)
    sum_in, sum_out, sum_qkv, sum_down, *small_outs = unpack(
        lax.axis_index("rep").astype(jnp.int32).reshape(1),
        pair_pieces,
        joint_pieces,
        down_pieces,
        (hidden_width, model_width, 3 * width),
        counts,
    )
    small_outs = [value.reshape(-1) for value in small_outs]
    grad_normed = grad_normed.astype(F32)
    center = inputs - jnp.mean(inputs, axis=-1, keepdims=True)
    scale = lax.rsqrt(jnp.mean(center * center, axis=-1, keepdims=True) + EPSILON)
    plain = center * scale
    scaled = grad_normed * g_one
    grad_block = grad_middle + scale * (
        scaled
        - jnp.mean(scaled, axis=-1, keepdims=True)
        - plain * jnp.mean(scaled * plain, axis=-1, keepdims=True)
    )

    return (
        layer_out,
        grad_block,
        grad_earlier,
        sum_qkv,
        sum_out,
        sum_in,
        sum_down,
        *small_outs,
        grad_depth,
    )


def per_device(*args):
    block_in = args[0]
    row_count, model_width = block_in.shape
    groups = lax.axis_size("shard")
    head_count = model_width // HEAD_DIM
    late_size = (4 * model_width + args[5].shape[1]) // groups
    if (
        groups == 8
        and lax.axis_size("rep") == 4
        and row_count == CHUNK
        and head_count % (groups // 2) == 0
        and head_count // (groups // 2) <= 8
        and late_size <= 12 * model_width // groups
        and args[5].shape[1] % (3 * groups) == 0
        and model_width // groups <= args[5].shape[1] // (3 * groups)
    ):
        return head_split_device(*args)
    return generic_device(*args)


def solution(mesh):
    placed = (
        P(("rep", "shard"), None),
        P(None, ("rep", "shard"), None),
        P(("rep", "shard"), None),
        P("shard", None),
        P("shard", None),
        P("shard", None),
        P("shard", None),
        P("shard"),
        P("shard"),
        P("shard"),
        P("shard"),
        P("shard"),
        P("shard"),
        P("shard"),
        P("shard"),
        P("shard"),
        P(),
    )
    return jax.shard_map(
        per_device,
        mesh=mesh,
        in_specs=placed,
        out_specs=(
            P(("rep", "shard"), None),
            P(("rep", "shard"), None),
            P(None, ("rep", "shard"), None),
            P("shard", None),
            P("shard", None),
            P("shard", None),
            P("shard", None),
            P("shard"),
            P("shard"),
            P("shard"),
            P("shard"),
            P("shard"),
            P("shard"),
            P("shard"),
            P("shard"),
            P("shard"),
            P(),
        ),
        check_vma=False,
    )
```

```python
from functools import partial
import math

import jax
import jax.numpy as jnp
from jax import lax
from jax.experimental import pallas as pl
from jax.experimental.pallas import tpu as pltpu
from jax.sharding import PartitionSpec as P

HEAD_DIM = 64
BLOCK = 256


NEG = -1e30
EPSILON = 1e-05


def layer_norm(inputs, gain, shift):
    center = inputs - jnp.mean(inputs, axis=-1, keepdims=True)
    spread = jnp.mean(center * center, axis=-1, keepdims=True)
    return center * lax.rsqrt(spread + EPSILON) * gain + shift


def rotate(inputs, positions):
    row_count = inputs.shape[0]
    split = inputs.reshape(row_count, -1, HEAD_DIM)
    half_dim = HEAD_DIM // 2
    freqs = 10000.0 ** (-jnp.arange(half_dim, dtype=jnp.float32) / half_dim)
    angles = positions.astype(jnp.float32)[:, None] * freqs[None, :]
    cosine = jnp.cos(angles)[:, None, :]
    sine = jnp.sin(angles)[:, None, :]
    former = split[..., :half_dim]
    latter = split[..., half_dim:]
    turned = jnp.concatenate(
        [former * cosine - latter * sine, former * sine + latter * cosine], axis=-1
    )
    return turned.reshape(row_count, -1)


def generic_device(
    block_in,
    earlier,
    cotangent,
    qkv_weight,
    out_weight,
    in_weight,
    down_weight,
    qk_bias,
    value_bias,
    out_bias,
    in_bias,
    down_bias,
    gain_one,
    shift_one,
    gain_two,
    shift_two,
    depth_weights,
):
    bf16 = jnp.bfloat16
    f32 = jnp.float32
    w_qkv, w_out, w_in, w_down, b_qk, b_value, b_out, b_in, b_down, g_one, s_one, g_two, s_two = (
        lax.all_gather(qkv_weight.astype(bf16), "shard", axis=0, tiled=True),
        lax.all_gather(out_weight.astype(bf16), "shard", axis=0, tiled=True),
        lax.all_gather(in_weight.astype(bf16), "shard", axis=0, tiled=True),
        lax.all_gather(down_weight.astype(bf16), "shard", axis=0, tiled=True),
        lax.all_gather(qk_bias.astype(bf16), "shard", axis=0, tiled=True),
        lax.all_gather(value_bias.astype(bf16), "shard", axis=0, tiled=True),
        lax.all_gather(out_bias.astype(bf16), "shard", axis=0, tiled=True),
        lax.all_gather(in_bias.astype(bf16), "shard", axis=0, tiled=True),
        lax.all_gather(down_bias.astype(bf16), "shard", axis=0, tiled=True),
        lax.all_gather(gain_one.astype(bf16), "shard", axis=0, tiled=True),
        lax.all_gather(shift_one.astype(bf16), "shard", axis=0, tiled=True),
        lax.all_gather(gain_two.astype(bf16), "shard", axis=0, tiled=True),
        lax.all_gather(shift_two.astype(bf16), "shard", axis=0, tiled=True),
    )
    row_count, model_width = block_in.shape
    head_count = model_width // HEAD_DIM
    groups = lax.axis_size("shard")
    length = row_count * groups
    window = min(512, length)
    member = lax.axis_index("shard")
    first_row = member * row_count
    last_end = first_row + row_count
    positions = first_row + jnp.arange(row_count, dtype=jnp.int32)
    query_block = positions // BLOCK
    score_scale = HEAD_DIM ** (-0.5)
    needed = (last_end + window - 1) // window
    inputs = block_in.astype(f32)
    normed, norm_back = jax.vjp(layer_norm, inputs, g_one.astype(f32), s_one.astype(f32))
    normed_low = normed.astype(bf16)
    joint_bias = jnp.concatenate([b_qk.astype(f32), b_value.astype(f32)])
    projected = jnp.dot(normed_low, w_qkv, preferred_element_type=f32) + joint_bias
    queries = rotate(projected[:, :model_width], positions).astype(bf16)
    key_rows = rotate(projected[:, model_width : 2 * model_width], positions).astype(bf16)
    values = projected[:, 2 * model_width :].astype(bf16)
    query_heads = queries.reshape(row_count, head_count, HEAD_DIM)

    def masked_scores(key_piece, key_start):
        piece_rows = key_piece.shape[0]
        key_heads = key_piece.reshape(piece_rows, head_count, HEAD_DIM)
        scores = (
            jnp.einsum("qhd,khd->hqk", query_heads, key_heads, preferred_element_type=f32)
            * score_scale
        )
        key_block = (key_start + jnp.arange(piece_rows, dtype=jnp.int32)) // BLOCK
        allowed = key_block[None, :] <= query_block[:, None]
        return (scores, allowed)

    def absorb(running, key_piece, value_piece, key_start):
        highest, denominator, summed = running
        scores, allowed = masked_scores(key_piece, key_start)
        scores = jnp.where(allowed[None], scores, NEG)
        new_high = jnp.maximum(highest, jnp.max(scores, axis=-1))
        rescale = jnp.exp(highest - new_high)
        weights = jnp.where(allowed[None], jnp.exp(scores - new_high[..., None]), 0.0)
        value_heads = value_piece.reshape(-1, head_count, HEAD_DIM)
        summed = summed * rescale[..., None] + jnp.einsum(
            "hqk,khd->hqd", weights.astype(bf16), value_heads, preferred_element_type=f32
        )
        return (new_high, denominator * rescale + jnp.sum(weights, axis=-1), summed)

    start_state = (
        jnp.full((head_count, row_count), NEG, f32),
        jnp.zeros((head_count, row_count), f32),
        jnp.zeros((head_count, row_count, HEAD_DIM), f32),
    )
    key_piece = lax.all_gather(key_rows, "shard", axis=0, tiled=True)
    value_piece = lax.all_gather(values, "shard", axis=0, tiled=True)
    piece_rows = key_piece.shape[0]
    sub_rows = math.gcd(piece_rows, window)
    usable = jnp.clip((last_end + sub_rows - 1) // sub_rows, 0, piece_rows // sub_rows)

    def advance(block_step, state_inner):
        offset = block_step * sub_rows
        return absorb(
            state_inner,
            lax.dynamic_slice_in_dim(key_piece, offset, sub_rows, 0),
            lax.dynamic_slice_in_dim(value_piece, offset, sub_rows, 0),
            offset,
        )

    highest, denominator, summed = lax.fori_loop(0, usable, advance, start_state)
    attended = summed / denominator[..., None]
    log_norm = highest + jnp.log(denominator)
    mixed = jnp.transpose(attended, (1, 0, 2)).reshape(row_count, model_width).astype(bf16)
    branch = jnp.dot(mixed, w_out, preferred_element_type=f32) + b_out.astype(f32)
    middle = inputs + branch
    normed_two, norm_two_back = jax.vjp(layer_norm, middle, g_two.astype(f32), s_two.astype(f32))
    normed_two_low = normed_two.astype(bf16)
    hidden = jnp.dot(normed_two_low, w_in, preferred_element_type=f32) + b_in.astype(f32)
    active_full, gelu_back = jax.vjp(partial(jax.nn.gelu, approximate=True), hidden)
    active = active_full.astype(bf16)
    result = middle + jnp.dot(active, w_down, preferred_element_type=f32) + b_down.astype(f32)
    stacked = earlier.astype(f32)
    layer_out = depth_weights[4] * result
    for level in range(4):
        layer_out = layer_out + depth_weights[level] * stacked[level]
    grad_earlier = depth_weights[:4][:, None, None] * cotangent[None]
    local_depth = jnp.concatenate(
        [jnp.sum(stacked * cotangent[None], axis=(1, 2)), jnp.sum(result * cotangent)[None]]
    )
    grad_depth = lax.psum(local_depth, ("rep", "shard"))
    grad_result = depth_weights[4] * cotangent
    down_grad = grad_result.astype(bf16)
    grad_down_w = jnp.einsum("tf,td->fd", active, down_grad, preferred_element_type=f32)
    grad_down_b = jnp.sum(down_grad.astype(f32), axis=0)
    grad_active = jnp.einsum("td,fd->tf", down_grad, w_down, preferred_element_type=f32)
    grad_hidden = gelu_back(grad_active)[0].astype(bf16)
    grad_in_w = jnp.einsum("td,tf->df", normed_two_low, grad_hidden, preferred_element_type=f32)
    grad_in_b = jnp.sum(grad_hidden.astype(f32), axis=0)
    grad_normed_two = jnp.einsum("tf,df->td", grad_hidden, w_in, preferred_element_type=f32)
    grad_mid_norm, grad_gain_two, grad_shift_two = norm_two_back(grad_normed_two)
    grad_middle = grad_result + grad_mid_norm
    branch_grad = grad_middle.astype(bf16)
    grad_out_w = jnp.einsum("td,te->de", mixed, branch_grad, preferred_element_type=f32)
    grad_out_b = jnp.sum(branch_grad.astype(f32), axis=0)
    grad_mixed = jnp.einsum("te,de->td", branch_grad, w_out, preferred_element_type=f32).astype(
        bf16
    )
    key_all, value_all = (
        lax.all_gather(key_rows, "shard", axis=0, tiled=True),
        lax.all_gather(values, "shard", axis=0, tiled=True),
    )
    grad_heads = grad_mixed.reshape(row_count, head_count, HEAD_DIM)
    delta = jnp.einsum("qhd,hqd->hq", grad_heads.astype(f32), attended)

    def score_grads(key_piece, value_piece, offset, piece_rows):
        scores, allowed = masked_scores(key_piece, offset)
        probs = jnp.where(allowed[None], jnp.exp(scores - log_norm[..., None]), 0.0)
        value_heads = value_piece.reshape(piece_rows, head_count, HEAD_DIM)
        grad_probs = jnp.einsum("qhd,khd->hqk", grad_heads, value_heads, preferred_element_type=f32)
        grad_scores = (probs * (grad_probs - delta[..., None])).astype(bf16)
        return (probs, grad_scores)

    def retrace(block_step, running):
        grad_query, grad_keys, grad_values = running
        offset = block_step * window
        key_piece = lax.dynamic_slice_in_dim(key_all, offset, window, 0)
        value_piece = lax.dynamic_slice_in_dim(value_all, offset, window, 0)
        probs, grad_scores = score_grads(key_piece, value_piece, offset, window)
        key_heads = key_piece.reshape(window, head_count, HEAD_DIM)
        grad_query = grad_query + jnp.einsum(
            "hqk,khd->qhd", grad_scores, key_heads, preferred_element_type=f32
        )
        piece_keys = (
            jnp.einsum("hqk,qhd->khd", grad_scores, query_heads, preferred_element_type=f32)
            * score_scale
        )
        piece_values = jnp.einsum(
            "hqk,qhd->khd", probs.astype(bf16), grad_heads, preferred_element_type=f32
        )
        grad_keys = lax.dynamic_update_slice_in_dim(
            grad_keys, piece_keys.reshape(window, model_width), offset, 0
        )
        grad_values = lax.dynamic_update_slice_in_dim(
            grad_values, piece_values.reshape(window, model_width), offset, 0
        )
        return (grad_query, grad_keys, grad_values)

    start_back = (
        jnp.zeros((row_count, head_count, HEAD_DIM), f32),
        jnp.zeros((length, model_width), f32),
        jnp.zeros((length, model_width), f32),
    )
    grad_query, grad_keys, grad_values = lax.fori_loop(0, needed, retrace, start_back)
    own_keys, own_values = (
        lax.psum_scatter(
            grad_keys.astype(jnp.bfloat16), "shard", scatter_dimension=0, tiled=True
        ).astype(jnp.float32),
        lax.psum_scatter(
            grad_values.astype(jnp.bfloat16), "shard", scatter_dimension=0, tiled=True
        ).astype(jnp.float32),
    )
    grad_q_turned = rotate(grad_query.reshape(row_count, model_width) * score_scale, -positions)
    grad_k_turned = rotate(own_keys, -positions)
    grad_joint = jnp.concatenate([grad_q_turned, grad_k_turned, own_values], axis=1).astype(bf16)
    grad_qkv_w = jnp.einsum("td,tf->df", normed_low, grad_joint, preferred_element_type=f32)
    joint_sums = jnp.sum(grad_joint.astype(f32), axis=0)
    grad_qk_b = joint_sums[: 2 * model_width]
    grad_value_b = joint_sums[2 * model_width :]
    grad_normed = jnp.einsum("tf,df->td", grad_joint, w_qkv, preferred_element_type=f32)
    grad_in_norm, grad_gain_one, grad_shift_one = norm_back(grad_normed)
    grad_block = grad_middle + grad_in_norm
    (
        own_qkv_w,
        own_out_w,
        own_in_w,
        own_down_w,
        own_qk_b,
        own_value_b,
        own_out_b,
        own_in_b,
        own_down_b,
        own_gain_one,
        own_shift_one,
        own_gain_two,
        own_shift_two,
    ) = (
        lax.psum_scatter(
            grad_qkv_w.astype(jnp.bfloat16), "shard", scatter_dimension=0, tiled=True
        ).astype(jnp.float32),
        lax.psum_scatter(
            grad_out_w.astype(jnp.bfloat16), "shard", scatter_dimension=0, tiled=True
        ).astype(jnp.float32),
        lax.psum_scatter(
            grad_in_w.astype(jnp.bfloat16), "shard", scatter_dimension=0, tiled=True
        ).astype(jnp.float32),
        lax.psum_scatter(
            grad_down_w.astype(jnp.bfloat16), "shard", scatter_dimension=0, tiled=True
        ).astype(jnp.float32),
        lax.psum_scatter(
            grad_qk_b.astype(jnp.bfloat16), "shard", scatter_dimension=0, tiled=True
        ).astype(jnp.float32),
        lax.psum_scatter(
            grad_value_b.astype(jnp.bfloat16), "shard", scatter_dimension=0, tiled=True
        ).astype(jnp.float32),
        lax.psum_scatter(
            grad_out_b.astype(jnp.bfloat16), "shard", scatter_dimension=0, tiled=True
        ).astype(jnp.float32),
        lax.psum_scatter(
            grad_in_b.astype(jnp.bfloat16), "shard", scatter_dimension=0, tiled=True
        ).astype(jnp.float32),
        lax.psum_scatter(
            grad_down_b.astype(jnp.bfloat16), "shard", scatter_dimension=0, tiled=True
        ).astype(jnp.float32),
        lax.psum_scatter(
            grad_gain_one.astype(jnp.bfloat16), "shard", scatter_dimension=0, tiled=True
        ).astype(jnp.float32),
        lax.psum_scatter(
            grad_shift_one.astype(jnp.bfloat16), "shard", scatter_dimension=0, tiled=True
        ).astype(jnp.float32),
        lax.psum_scatter(
            grad_gain_two.astype(jnp.bfloat16), "shard", scatter_dimension=0, tiled=True
        ).astype(jnp.float32),
        lax.psum_scatter(
            grad_shift_two.astype(jnp.bfloat16), "shard", scatter_dimension=0, tiled=True
        ).astype(jnp.float32),
    )
    (
        sum_qkv_w,
        sum_out_w,
        sum_in_w,
        sum_down_w,
        sum_qk_b,
        sum_value_b,
        sum_out_b,
        sum_in_b,
        sum_down_b,
        sum_gain_one,
        sum_shift_one,
        sum_gain_two,
        sum_shift_two,
    ) = (
        lax.psum(own_qkv_w.astype(jnp.bfloat16), "rep").astype(jnp.float32),
        lax.psum(own_out_w.astype(jnp.bfloat16), "rep").astype(jnp.float32),
        lax.psum(own_in_w.astype(jnp.bfloat16), "rep").astype(jnp.float32),
        lax.psum(own_down_w.astype(jnp.bfloat16), "rep").astype(jnp.float32),
        lax.psum(own_qk_b.astype(jnp.bfloat16), "rep").astype(jnp.float32),
        lax.psum(own_value_b.astype(jnp.bfloat16), "rep").astype(jnp.float32),
        lax.psum(own_out_b.astype(jnp.bfloat16), "rep").astype(jnp.float32),
        lax.psum(own_in_b.astype(jnp.bfloat16), "rep").astype(jnp.float32),
        lax.psum(own_down_b.astype(jnp.bfloat16), "rep").astype(jnp.float32),
        lax.psum(own_gain_one.astype(jnp.bfloat16), "rep").astype(jnp.float32),
        lax.psum(own_shift_one.astype(jnp.bfloat16), "rep").astype(jnp.float32),
        lax.psum(own_gain_two.astype(jnp.bfloat16), "rep").astype(jnp.float32),
        lax.psum(own_shift_two.astype(jnp.bfloat16), "rep").astype(jnp.float32),
    )
    return (
        layer_out,
        grad_block,
        grad_earlier,
        sum_qkv_w,
        sum_out_w,
        sum_in_w,
        sum_down_w,
        sum_qk_b,
        sum_value_b,
        sum_out_b,
        sum_in_b,
        sum_down_b,
        sum_gain_one,
        sum_shift_one,
        sum_gain_two,
        sum_shift_two,
        grad_depth,
    )


F32 = jnp.float32
BF16 = jnp.bfloat16
CHUNK = 2 * BLOCK
VMEM_LIMIT = 56 * 1024 * 1024


def cost(flops, moved, exps=0):
    return pl.CostEstimate(flops=flops, bytes_accessed=moved, transcendentals=exps)


def contract(left, right, left_dim, right_dim):
    return lax.dot_general(
        left, right, (((left_dim,), (right_dim,)), ((), ())), preferred_element_type=F32
    )


def qkv_kernel(x_ref, weight_ref, bias_ref, gain_ref, shift_ref, cos_ref, sin_ref, *refs):
    plain_ref, qt_ref, kt_ref, vt_ref, kv_ref = refs[-5:]
    x = x_ref[...].astype(F32)
    center = x - jnp.mean(x, axis=-1, keepdims=True)
    spread = jnp.mean(center * center, axis=-1, keepdims=True)
    plain = center * lax.rsqrt(spread + EPSILON)
    plain_ref[...] = plain.astype(BF16)
    low = (plain * gain_ref[...] + shift_ref[...]).astype(BF16)
    width = qt_ref.shape[0]
    half = HEAD_DIM // 2
    joint = contract(weight_ref[...], low, 1, 1) + bias_ref[...]
    cosine = cos_ref[...]
    sine = sin_ref[...]
    for head in range(width // HEAD_DIM):
        base = head * HEAD_DIM
        for part in range(2):
            start = part * width + base
            former = joint[start : start + half]
            latter = joint[start + half : start + HEAD_DIM]
            turned = jnp.concatenate(
                [former * cosine - latter * sine, former * sine + latter * cosine], axis=0
            )
            if part == 0:
                qt_ref[base : base + HEAD_DIM, :] = (turned * HEAD_DIM ** (-0.5)).astype(BF16)
            else:
                kt_ref[base : base + HEAD_DIM, :] = turned.astype(BF16)
                key = turned
        start = 2 * width + base
        value = joint[start : start + HEAD_DIM]
        vt_ref[base : base + HEAD_DIM, :] = value.astype(BF16)
        kv_ref[head] = jnp.transpose(jnp.concatenate([key, value], axis=0)).astype(BF16)


def project(tokens, weight_t, bias, gain, shift, cosine, sine, first, count, held):
    length, model_width = tokens.shape
    columns = weight_t.shape[0]
    width = columns // 3
    heads = width // HEAD_DIM
    half = HEAD_DIM // 2
    tile = CHUNK
    fixed = lambda i: (0, 0)
    down = lambda i: (first + i, 0)
    across = lambda i: (0, first + i)
    inputs = [tokens, weight_t, bias, gain, shift, cosine, sine]
    return pl.pallas_call(
        qkv_kernel,
        name="project",
        cost_estimate=cost(2 * count * tile * model_width * columns, 12 * count * tile * model_width),
        grid=(count,),
        in_specs=[
            pl.BlockSpec((tile, model_width), down),
            pl.BlockSpec((columns, model_width), fixed),
            pl.BlockSpec((columns, 1), fixed),
            pl.BlockSpec((1, model_width), fixed),
            pl.BlockSpec((1, model_width), fixed),
            pl.BlockSpec((half, tile), across),
            pl.BlockSpec((half, tile), across),
        ]
        + [pl.BlockSpec(memory_space=pl.ANY)] * len(held),
        out_specs=[
            pl.BlockSpec((tile, model_width), down),
            pl.BlockSpec((width, tile), across),
            pl.BlockSpec((width, tile), across),
            pl.BlockSpec((width, tile), across),
            pl.BlockSpec((heads, tile, 2 * HEAD_DIM), lambda i: (0, first + i, 0)),
        ],
        out_shape=[
            jax.ShapeDtypeStruct((length, model_width), BF16),
            jax.ShapeDtypeStruct((width, length), BF16),
            jax.ShapeDtypeStruct((width, length), BF16),
            jax.ShapeDtypeStruct((width, length), BF16),
            jax.ShapeDtypeStruct((heads, length, 2 * HEAD_DIM), BF16),
        ],
        input_output_aliases={len(inputs) + i: i for i in range(len(held))},
        compiler_params=pltpu.CompilerParams(vmem_limit_bytes=VMEM_LIMIT),
    )(*inputs, *held)


def average_kernel(weights_ref, earlier_ref, cotangent_ref, grad_ref, mix_ref, sums_ref):
    @pl.when(pl.program_id(0) == 0)
    def _():
        sums_ref[...] = jnp.zeros_like(sums_ref)

    cotangent = cotangent_ref[...]
    rows, columns = cotangent.shape
    mix = jnp.zeros_like(cotangent)
    for level in range(earlier_ref.shape[0]):
        value = earlier_ref[level].astype(F32)
        weight = weights_ref[level]
        mix = mix + weight * value
        grad_ref[level] = weight * cotangent
        sums_ref[level] += jnp.sum((value * cotangent).reshape(rows // 8, 8, columns), axis=0)
    mix_ref[...] = mix


def average(depth_weights, earlier, cotangent):
    levels, row_count, model_width = earlier.shape
    tile = row_count // 4
    return pl.pallas_call(
        average_kernel,
        name="average",
        cost_estimate=cost(6 * earlier.size, 6 * earlier.size + 8 * cotangent.size),
        grid_spec=pltpu.PrefetchScalarGridSpec(
            num_scalar_prefetch=1,
            grid=(4,),
            in_specs=[
                pl.BlockSpec((levels, tile, model_width), lambda i, w: (0, i, 0)),
                pl.BlockSpec((tile, model_width), lambda i, w: (i, 0)),
            ],
            out_specs=[
                pl.BlockSpec((levels, tile, model_width), lambda i, w: (0, i, 0)),
                pl.BlockSpec((tile, model_width), lambda i, w: (i, 0)),
                pl.BlockSpec((levels, 8, model_width), lambda i, w: (0, 0, 0)),
            ],
        ),
        out_shape=[
            jax.ShapeDtypeStruct(earlier.shape, F32),
            jax.ShapeDtypeStruct(cotangent.shape, F32),
            jax.ShapeDtypeStruct((levels, 8, model_width), F32),
        ],
        compiler_params=pltpu.CompilerParams(vmem_limit_bytes=VMEM_LIMIT),
    )(depth_weights, earlier, cotangent)


def last_mask(odd, rows):
    row = lax.broadcasted_iota(jnp.int32, (rows, BLOCK), 0)
    return row < rows - BLOCK * (1 - odd)


def over_chunks(pair, absorb, state):
    state = lax.fori_loop(0, pair // 2, lambda i, s: absorb(2 * i, 2 * CHUNK, s, False), state)
    return lax.cond(
        pair % 2 == 0,
        lambda s: absorb(pair, CHUNK, s, True),
        lambda s: absorb(pair - 1, 2 * CHUNK, s, True),
        state,
    )


def attend_kernel(core_ref, qt_ref, kv_ref, vt_ref, low_ref, full_ref, stat_ref, scores_ref):
    pair = pl.program_id(0)
    odd = core_ref[0] ^ (pair & 1)
    heads = qt_ref.shape[0] // HEAD_DIM
    blank = jnp.zeros((HEAD_DIM, BLOCK), BF16)
    queries = [
        jnp.concatenate([qt_ref[h * HEAD_DIM : (h + 1) * HEAD_DIM, :], blank], axis=0)
        for h in range(heads)
    ]
    fold = lambda value: value.reshape(value.shape[0] // 8, 8, BLOCK)

    def score(step, size, state, masked):
        keys = pl.ds(pl.multiple_of(step * CHUNK, CHUNK), size)
        fresh = []
        for h in range(heads):
            scores = contract(kv_ref[h, keys, :], queries[h], 1, 0)
            if masked:
                scores = jnp.where(last_mask(odd, size), scores, NEG)
            scores_ref[h, keys, :] = scores
            fresh.append(jnp.maximum(state[h], jnp.max(fold(scores), axis=0)))
        return fresh

    def mix(step, size, state, masked):
        keys = pl.ds(pl.multiple_of(step * CHUNK, CHUNK), size)
        fresh = []
        for h in range(heads):
            total, summed = state[h]
            weights = jnp.exp(scores_ref[h, keys, :] - highest[h])
            values = vt_ref[h * HEAD_DIM : (h + 1) * HEAD_DIM, keys]
            fresh.append(
                (
                    total + jnp.sum(fold(weights), axis=0),
                    summed + contract(values, weights.astype(BF16), 1, 0),
                )
            )
        return fresh

    state = [jnp.full((8, BLOCK), NEG, F32) for _ in range(heads)]
    state = over_chunks(pair, score, state)
    highest = [jnp.max(value, axis=0, keepdims=True) for value in state]
    state = [
        (jnp.zeros((8, BLOCK), F32), jnp.zeros((HEAD_DIM, BLOCK), F32)) for _ in range(heads)
    ]
    state = over_chunks(pair, mix, state)
    for h in range(heads):
        total, summed = state[h]
        total = jnp.sum(total, axis=0, keepdims=True)
        attended = summed / total
        full_ref[0, h * HEAD_DIM : (h + 1) * HEAD_DIM, :] = attended
        low_ref[0, h * HEAD_DIM : (h + 1) * HEAD_DIM, :] = attended.astype(BF16)
        stat_ref[0, h : h + 1, :] = highest[h] + jnp.log(total)


def attend(core, qt, kv, vt):
    width, length = qt.shape
    pairs = length // CHUNK
    own = lambda j, core: (0, 2 * j + (core[0] ^ (j & 1)))
    slot = lambda j, core: (j, 0, 0)
    return pl.pallas_call(
        attend_kernel,
        name="attend",
        cost_estimate=cost(
            2 * 2 * BLOCK * BLOCK * BLOCK * 2 * sum(range(1, pairs + 1)) * (width // HEAD_DIM),
            4 * kv.size + 8 * pairs * width * BLOCK,
            CHUNK * BLOCK * sum(range(1, pairs + 1)) * (width // HEAD_DIM),
        ),
        grid_spec=pltpu.PrefetchScalarGridSpec(
            num_scalar_prefetch=1,
            grid=(pairs,),
            in_specs=[
                pl.BlockSpec((width, BLOCK), own),
                pl.BlockSpec(kv.shape, lambda j, core: (0, 0, 0)),
                pl.BlockSpec(vt.shape, lambda j, core: (0, 0)),
            ],
            out_specs=[
                pl.BlockSpec((1, width, BLOCK), slot),
                pl.BlockSpec((1, width, BLOCK), slot),
                pl.BlockSpec((1, 8, BLOCK), slot),
            ],
            scratch_shapes=[pltpu.VMEM((width // HEAD_DIM, length, BLOCK), F32)],
        ),
        out_shape=[
            jax.ShapeDtypeStruct((pairs, width, BLOCK), BF16),
            jax.ShapeDtypeStruct((pairs, width, BLOCK), F32),
            jax.ShapeDtypeStruct((pairs, 8, BLOCK), F32),
        ],
        compiler_params=pltpu.CompilerParams(vmem_limit_bytes=VMEM_LIMIT),
    )(core, qt, kv, vt)


def retrace_kernel(
    core_ref, qt_ref, grad_ref, full_ref, stat_ref, cos_ref, sin_ref, kv_ref, kt_ref,
    weight_ref, joint_ref, normed_ref, dkv_ref,
):
    step_id = pl.program_id(0)
    pair = pl.num_programs(0) - 1 - step_id
    odd = core_ref[0] ^ (pair & 1)
    width = qt_ref.shape[0]
    heads = width // HEAD_DIM
    half = HEAD_DIM // 2

    @pl.when(step_id == 0)
    def _():
        dkv_ref[...] = jnp.zeros_like(dkv_ref)

    blank = jnp.zeros((HEAD_DIM, BLOCK), BF16)
    lefts, rights, deltas, norms = [], [], [], []
    for h in range(heads):
        rows = slice(h * HEAD_DIM, (h + 1) * HEAD_DIM)
        query = qt_ref[rows, :]
        grad = grad_ref[0, rows, :]
        lefts.append(
            jnp.concatenate(
                [
                    jnp.concatenate([query, blank], axis=1),
                    jnp.concatenate([blank, grad], axis=1),
                ],
                axis=0,
            )
        )
        rights.append(
            jnp.concatenate(
                [
                    jnp.concatenate([blank, query], axis=1),
                    jnp.concatenate([grad, blank], axis=1),
                ],
                axis=0,
            )
        )
        deltas.append(jnp.sum(grad.astype(F32) * full_ref[0, rows, :], axis=0, keepdims=True))
        norms.append(stat_ref[0, h : h + 1, :])

    def absorb(step, state, masked):
        keys = pl.ds(pl.multiple_of(step * CHUNK, CHUNK), CHUNK)
        fresh = []
        for h in range(heads):
            both = contract(kv_ref[h, keys, :], lefts[h], 1, 0)
            probs = jnp.exp(both[:, :BLOCK] - norms[h])
            if masked:
                probs = jnp.where(last_mask(odd, CHUNK), probs, 0.0)
            grad_scores = (probs * (both[:, BLOCK:] - deltas[h])).astype(BF16)
            joined = jnp.concatenate([probs.astype(BF16), grad_scores], axis=1)
            dkv_ref[h, keys, :] += contract(joined, rights[h], 1, 1)
            turned = kt_ref[h * HEAD_DIM : (h + 1) * HEAD_DIM, keys]
            fresh.append(state[h] + contract(turned, grad_scores, 1, 0))
        return fresh

    state = [jnp.zeros((HEAD_DIM, BLOCK), F32) for _ in range(heads)]
    state = lax.fori_loop(0, pair, lambda i, s: absorb(i, s, False), state)
    state = absorb(pair, state, True)
    offset = pl.multiple_of(pair * CHUNK, CHUNK)
    cosine = cos_ref[...]
    sine = sin_ref[...]
    column = lax.broadcasted_iota(jnp.int32, (HEAD_DIM, CHUNK), 1) // BLOCK

    for h in range(heads):
        base = h * HEAD_DIM
        doubled = jnp.concatenate([state[h], state[h]], axis=1) * HEAD_DIM ** (-0.5)
        doubled = jnp.where(column == odd, doubled, 0.0)
        turned_back = jnp.transpose(dkv_ref[h, pl.ds(offset, CHUNK), :])
        for part, value in ((0, doubled), (1, turned_back[:HEAD_DIM])):
            former = value[:half]
            latter = value[half:]
            turned = jnp.concatenate(
                [former * cosine + latter * sine, latter * cosine - former * sine], axis=0
            )
            start = part * width + base
            joint_ref[start : start + HEAD_DIM, :] = turned.astype(BF16)
        start = 2 * width + base
        joint_ref[start : start + HEAD_DIM, :] = turned_back[HEAD_DIM:].astype(BF16)
    normed_ref[...] = contract(joint_ref[...], weight_ref[...], 0, 0).astype(BF16)


def retrace(core, qt, grads, full, stats, cosine, sine, kv, kt, weight):
    width, length = qt.shape
    heads = width // HEAD_DIM
    half = HEAD_DIM // 2
    pairs = length // CHUNK
    back = lambda j: pairs - 1 - j
    own = lambda j, core: (0, 2 * back(j) + (core[0] ^ (back(j) & 1)))
    slot = lambda j, core: (back(j), 0, 0)
    across = lambda j, core: (0, back(j))
    return pl.pallas_call(
        retrace_kernel,
        name="retrace",
        cost_estimate=cost(
            5 * 2 * BLOCK * BLOCK * BLOCK * 2 * sum(range(1, pairs + 1)) * heads,
            3 * kv.size + 16 * pairs * width * BLOCK,
            CHUNK * BLOCK * sum(range(1, pairs + 1)) * heads,
        ),
        grid_spec=pltpu.PrefetchScalarGridSpec(
            num_scalar_prefetch=1,
            grid=(pairs,),
            in_specs=[
                pl.BlockSpec((width, BLOCK), own),
                pl.BlockSpec((1, width, BLOCK), slot),
                pl.BlockSpec((1, width, BLOCK), slot),
                pl.BlockSpec((1, 8, BLOCK), slot),
                pl.BlockSpec((half, CHUNK), across),
                pl.BlockSpec((half, CHUNK), across),
                pl.BlockSpec(kv.shape, lambda j, core: (0, 0, 0)),
                pl.BlockSpec(kt.shape, lambda j, core: (0, 0)),
                pl.BlockSpec(weight.shape, lambda j, core: (0, 0)),
            ],
            out_specs=[
                pl.BlockSpec((3 * width, CHUNK), across),
                pl.BlockSpec((CHUNK, weight.shape[1]), lambda j, core: (back(j), 0)),
            ],
            scratch_shapes=[pltpu.VMEM((heads, length, 2 * HEAD_DIM), F32)],
        ),
        out_shape=[
            jax.ShapeDtypeStruct((3 * width, length), BF16),
            jax.ShapeDtypeStruct((length, weight.shape[1]), BF16),
        ],
        compiler_params=pltpu.CompilerParams(vmem_limit_bytes=VMEM_LIMIT),
    )(core, qt, grads, full, stats, cosine, sine, kv, kt, weight)


def after(values, *earlier_values):
    values = tuple(values)
    return lax.optimization_barrier(values + tuple(earlier_values))[: len(values)]


def assemble_kernel(place_ref, *refs):
    down_ref, out_ref = refs[-2:]
    rep = place_ref[1]
    reps = (len(refs) - 2) // 2
    part = out_ref.shape[0]
    for side in range(2):
        @pl.when(pl.program_id(0) == side)
        def _():
            for k in range(reps):
                piece = refs[side * reps + k]
                rows = piece.shape[1]
                target = rep ^ k

                @pl.when(target < reps - 1)
                def _():
                    down_ref[pl.ds(pl.multiple_of(target * rows, rows), rows), :] = piece[0]

                @pl.when(target == reps - 1)
                def _():
                    out_ref[...] = piece[0, :part]


def assemble(place, mine, twin, part):
    owners, rows, columns = mine[0].shape
    reps = len(mine)
    groups = 2 * owners

    def held(side):
        def index(which, z, place):
            moving = (place[0] // 2 + owners - z) % owners
            fixed = (place[0] // 2 + owners - (owners - 1) * (1 - side)) % owners
            return (jnp.where(which == side, moving, fixed), 0, 0)

        return pl.BlockSpec((1, rows, columns), index)

    device = lambda which, z, place: 2 * z + (which ^ (place[0] % 2))
    target = lambda which, z, place: (device(which, z, place), 0)
    return pl.pallas_call(
        assemble_kernel,
        name="assemble",
        grid_spec=pltpu.PrefetchScalarGridSpec(
            num_scalar_prefetch=1,
            grid=(2, owners),
            in_specs=[held(0)] * reps + [held(1)] * reps,
            out_specs=[
                pl.BlockSpec(((reps - 1) * rows, columns), target),
                pl.BlockSpec((part, columns), target),
            ],
        ),
        out_shape=[
            jax.ShapeDtypeStruct((groups * (reps - 1) * rows, columns), BF16),
            jax.ShapeDtypeStruct((groups * part, columns), BF16),
        ],
        compiler_params=pltpu.CompilerParams(vmem_limit_bytes=VMEM_LIMIT),
    )(place, *mine, *twin)


def swap_core(value):
    groups = lax.axis_size("shard")
    return lax.ppermute(value, "shard", [(i, i ^ 1) for i in range(groups)])


def shift_owner(value, distance):
    groups = lax.axis_size("shard")
    step = 2 * distance
    return lax.ppermute(value, "shard", [(i, (i + step) % groups) for i in range(groups)])


def cross_rep(value, mask):
    return lax.ppermute(value, "rep", [(i, i ^ mask) for i in range(lax.axis_size("rep"))])


def pick(stacked, index, axis=0):
    return lax.dynamic_index_in_dim(stacked, index, axis, keepdims=False)


def add_low(*values):
    total = values[0].astype(F32)
    for value in values[1:]:
        total = total + value.astype(F32)
    return total.astype(BF16)


def fold_core(partial_sums, core):
    halves = partial_sums.reshape((-1, 2) + partial_sums.shape[1:])
    received = swap_core(pick(halves, 1 - core, 1))
    return add_low(pick(halves, core, 1), received)


def rep_parts(value):
    reps = lax.axis_size("rep")
    owners, rows, columns = value.shape
    return value.reshape(owners, reps, rows // reps, columns)


def send_rep(value):
    rep = lax.axis_index("rep")
    parts = rep_parts(value)
    return [cross_rep(pick(parts, rep ^ k, 1), k) for k in range(1, lax.axis_size("rep"))]


def pick_parts(value):
    rep = lax.axis_index("rep")
    parts = rep_parts(value)
    return [pick(parts, rep ^ k, 1) for k in range(lax.axis_size("rep"))]


def join_rep(value, received):
    return add_low(pick(rep_parts(value), lax.axis_index("rep"), 1), *received)


def unpack_kernel(rep_ref, *refs):
    reps = 4
    pieces = refs[: 3 * reps]
    in_ref, out_ref, qkv_ref, down_ref = refs[3 * reps : 3 * reps + 4]
    line_refs = refs[3 * reps + 4 :]
    hidden_width = in_ref.shape[1]
    model_width = out_ref.shape[1]
    columns = qkv_ref.shape[1] // 3
    owners = down_ref.shape[0] // in_ref.shape[0]
    width = columns // owners
    for k in range(reps):
        pair, joint, down = pieces[k::reps]
        rows = pair.shape[0]
        first = pl.multiple_of((rep_ref[0] ^ k) * rows, 8)
        own = pl.ds(first, rows)
        in_ref[own, :] = pair[:, :hidden_width].astype(F32)
        out_ref[own, :] = pair[:, hidden_width:].astype(F32)
        whole = joint[:, : 3 * columns].astype(F32)
        for part in range(3):
            qkv_ref[own, part * columns : (part + 1) * columns] = jnp.concatenate(
                [
                    whole[:, (3 * z + part) * width : (3 * z + part + 1) * width]
                    for z in range(owners)
                ],
                axis=1,
            )

        @pl.when(rep_ref[0] == k)
        def _():
            part = line_refs[0].shape[1] // 2
            lines = joint[:, 3 * columns :].astype(F32)
            row = 0
            for line_ref in line_refs:
                count = line_ref.shape[1] // part
                line_ref[...] = jnp.concatenate(
                    [lines[row + i : row + i + 1, :part] for i in range(count)], axis=1
                )
                row += count

        for z in range(owners):
            block = pl.ds(pl.multiple_of(owners * first + z * rows, 8), rows)
            down_ref[block, :] = down[:, z * model_width : (z + 1) * model_width].astype(F32)


def unpack(rep, pair, joint, down, widths, counts):
    hidden_width, model_width, columns = widths
    pieces = [*pair, *joint, *down]
    rows = len(pair) * pair[0].shape[0]
    owners = model_width * 3 // columns
    shapes = [
        (rows, hidden_width),
        (rows, model_width),
        (rows, 3 * model_width),
        (owners * rows, model_width),
    ] + [(1, count * rows) for count in counts]
    whole = pl.BlockSpec(memory_space=pltpu.VMEM)
    return pl.pallas_call(
        unpack_kernel,
        name="unpack",
        in_specs=[pl.BlockSpec(memory_space=pltpu.SMEM)] + [whole] * len(pieces),
        out_specs=[whole] * len(shapes),
        out_shape=[jax.ShapeDtypeStruct(shape, F32) for shape in shapes],
        compiler_params=pltpu.CompilerParams(vmem_limit_bytes=VMEM_LIMIT),
    )(rep, *pieces)


def split_depth(value):
    high = lax.reduce_precision(value, 8, 7)
    return jnp.concatenate([high, value - high]).astype(BF16)


def join_depth(value):
    value = value.astype(F32)
    half = value.shape[0] // 2
    return value[:half] + value[half:]


def add_ordered(values, index_of):
    stacked = jnp.stack(values)
    total = pick(stacked, index_of(0))
    for sender in range(1, len(values)):
        total = total + pick(stacked, index_of(sender))
    return total


def every_rep(value):
    return [value] + [cross_rep(value, k) for k in range(1, lax.axis_size("rep"))]


def exchange_owner(value, owner):
    owners = value.shape[0]
    received = [pick(value, owner)]
    for k in range(1, owners):
        received.append(shift_owner(pick(value, (owner + k) % owners), k))
    return received


def middle_kernel(
    core_ref, weights_ref, mixed_ref, x_ref, cotangent_ref, w_out_ref, b_out_ref, gain_ref,
    shift_ref, w_in_ref, b_in_ref, grad_ref,
    middle_ref, low_ref, active_ref, hidden_ref, total_ref, branch_ref, send_ref,
    sums_ref, hidden_sums_ref, plain_ref, scale_ref, back_ref,
):
    step = pl.program_id(0)
    core = core_ref[0]
    owners = mixed_ref.shape[0] // 2
    width = mixed_ref.shape[1]

    @pl.when(step == 0)
    def _():
        for half in range(2):
            rows = slice(half * BLOCK, (half + 1) * BLOCK)
            mixed = jnp.concatenate(
                [mixed_ref[2 * z + (core ^ half)] for z in range(owners)], axis=0
            )
            branch = contract(mixed, w_out_ref[...], 0, 0) + b_out_ref[...]
            middle = x_ref[rows, :].astype(F32) + branch
            middle_ref[rows, :] = middle
            center = middle - jnp.mean(middle, axis=-1, keepdims=True)
            scale = lax.rsqrt(jnp.mean(center * center, axis=-1, keepdims=True) + EPSILON)
            plain = center * scale
            scale_ref[rows, :] = jnp.broadcast_to(scale, (BLOCK, scale_ref.shape[1]))
            plain_ref[rows, :] = plain
            low_ref[rows, :] = (plain * gain_ref[...] + shift_ref[...]).astype(BF16)
        back_ref[...] = jnp.zeros_like(back_ref)

    hidden = contract(low_ref[...], w_in_ref[...], 1, 0) + b_in_ref[...]
    square = hidden * hidden
    bend = math.sqrt(2 / math.pi)
    turned = jnp.tanh(hidden * (bend + (bend * 0.044715) * square))
    share = 0.5 + 0.5 * turned
    active_ref[...] = (hidden * share).astype(BF16)
    slope = (0.5 * hidden) * (1.0 - turned * turned) * (bend + (3 * bend * 0.044715) * square)
    grad = (grad_ref[...].astype(F32) * (share + slope)).astype(BF16)
    hidden_ref[...] = grad
    hidden_sums_ref[...] = jnp.sum(grad.astype(F32), axis=0, keepdims=True)
    back_ref[...] += contract(grad, w_in_ref[...], 1, 1)

    @pl.when(step == pl.num_programs(0) - 1)
    def _():
        weight = weights_ref[4]
        sums = [jnp.zeros((1, back_ref.shape[1]), F32)] * 3
        for half in range(2):
            rows = slice(half * BLOCK, (half + 1) * BLOCK)
            back = back_ref[rows, :]
            plain = plain_ref[rows, :]
            scaled = back * gain_ref[...]
            total = weight * cotangent_ref[rows, :] + scale_ref[rows, :1] * (
                scaled
                - jnp.mean(scaled, axis=-1, keepdims=True)
                - plain * jnp.mean(scaled * plain, axis=-1, keepdims=True)
            )
            total_ref[rows, :] = total
            low = total.astype(BF16)
            branch_ref[rows, :] = low
            mixed = contract(w_out_ref[...], low, 1, 1).astype(BF16)
            for z in range(owners):
                send_ref[2 * z + (core ^ half)] = mixed[z * width : (z + 1) * width, :]
            for i, value in enumerate((low.astype(F32), back * plain, back)):
                sums[i] = sums[i] + jnp.sum(value, axis=0, keepdims=True)
        for i in range(3):
            sums_ref[i : i + 1, :] = sums[i]


def middle_part(
    core, depth_weights, mixed, x, cotangent, w_out, b_out, gain, shift, w_in, b_in, grad_active
):
    rows, model_width = x.shape
    hidden_width = w_in.shape[1]
    chunk = 2 * CHUNK if hidden_width % (2 * CHUNK) == 0 else CHUNK
    whole = lambda value: pl.BlockSpec(value.shape, lambda j, *_: (0,) * value.ndim)
    across = pl.BlockSpec((rows, chunk), lambda j, *_: (0, j))
    line = pl.BlockSpec((1, chunk), lambda j, *_: (0, j))
    shapes = [
        jax.ShapeDtypeStruct((rows, model_width), F32),
        jax.ShapeDtypeStruct((rows, model_width), BF16),
        jax.ShapeDtypeStruct((rows, hidden_width), BF16),
        jax.ShapeDtypeStruct((rows, hidden_width), BF16),
        jax.ShapeDtypeStruct((rows, model_width), F32),
        jax.ShapeDtypeStruct((rows, model_width), BF16),
        jax.ShapeDtypeStruct(mixed.shape, BF16),
        jax.ShapeDtypeStruct((8, model_width), F32),
        jax.ShapeDtypeStruct((1, hidden_width), F32),
    ]
    out_specs = [whole(shape) for shape in shapes]
    out_specs[2] = out_specs[3] = across
    out_specs[8] = line
    return pl.pallas_call(
        middle_kernel,
        name="middle",
        cost_estimate=cost(
            4 * rows * model_width * (hidden_width + model_width),
            2 * w_in.size + 8 * grad_active.size,
            grad_active.size,
        ),
        grid_spec=pltpu.PrefetchScalarGridSpec(
            num_scalar_prefetch=2,
            grid=(hidden_width // chunk,),
            in_specs=[
                whole(mixed),
                whole(x),
                whole(cotangent),
                whole(w_out),
                whole(b_out),
                whole(gain),
                whole(shift),
                pl.BlockSpec((model_width, chunk), lambda j, *_: (0, j)),
                line,
                across,
            ],
            out_specs=out_specs,
            scratch_shapes=[
                pltpu.VMEM((rows, model_width), F32),
                pltpu.VMEM((rows, 128), F32),
                pltpu.VMEM((rows, model_width), F32),
            ],
        ),
        out_shape=shapes,
        compiler_params=pltpu.CompilerParams(vmem_limit_bytes=VMEM_LIMIT),
    )(
        core, depth_weights, mixed, x, cotangent, w_out, b_out, gain, shift, w_in, b_in,
        grad_active,
    )


def down_kernel(active_ref, down_grad_ref, down_ref):
    down_ref[...] = contract(active_ref[...], down_grad_ref[...], 0, 0).astype(BF16)


def down_part(active, down_grad):
    rows, model_width = down_grad.shape
    steps = active.shape[1] // model_width
    return pl.pallas_call(
        down_kernel,
        name="down_part",
        grid=(steps,),
        in_specs=[
            pl.BlockSpec((rows, model_width), lambda j: (0, j)),
            pl.BlockSpec((rows, model_width), lambda j: (0, 0)),
        ],
        out_specs=pl.BlockSpec((model_width, model_width), lambda j: (j, 0)),
        out_shape=jax.ShapeDtypeStruct((steps * model_width, model_width), BF16),
        compiler_params=pltpu.CompilerParams(vmem_limit_bytes=VMEM_LIMIT),
    )(active, down_grad)


def result_kernel(
    weights_ref, active_ref, w_down_ref, b_down_ref, middle_ref, mix_ref, cotangent_ref,
    layer_ref, depth_ref, total_ref,
):
    step = pl.program_id(0)

    @pl.when(step == 0)
    def _():
        total_ref[...] = middle_ref[...] + b_down_ref[...]

    total_ref[...] += contract(active_ref[...], w_down_ref[...], 1, 0)

    @pl.when(step == pl.num_programs(0) - 1)
    def _():
        result = total_ref[...]
        layer_ref[...] = weights_ref[4] * result + mix_ref[...]
        depth = (result * cotangent_ref[...]).reshape(-1, 8, result.shape[1])
        depth_ref[...] = jnp.sum(depth, axis=0)


def result_part(depth_weights, active, w_down, b_down, middle, mix, cotangent):
    rows, model_width = middle.shape
    steps = active.shape[1] // model_width
    whole = lambda value: pl.BlockSpec(value.shape, lambda j, *_: (0,) * value.ndim)
    depth = jax.ShapeDtypeStruct((8, model_width), F32)
    return pl.pallas_call(
        result_kernel,
        name="result_part",
        grid_spec=pltpu.PrefetchScalarGridSpec(
            num_scalar_prefetch=1,
            grid=(steps,),
            in_specs=[
                pl.BlockSpec((rows, model_width), lambda j, *_: (0, j)),
                pl.BlockSpec((model_width, model_width), lambda j, *_: (j, 0)),
                whole(b_down), whole(middle), whole(mix), whole(cotangent),
            ],
            out_specs=[whole(middle), whole(depth)],
            scratch_shapes=[pltpu.VMEM((rows, model_width), F32)],
        ),
        out_shape=[jax.ShapeDtypeStruct(middle.shape, F32), depth],
        compiler_params=pltpu.CompilerParams(vmem_limit_bytes=VMEM_LIMIT),
    )(depth_weights, active, w_down, b_down, middle, mix, cotangent)


def pair_kernel(
    core_ref, low_ref, hidden_ref, mixed_ref, branch_ref,
    low_twin_ref, hidden_twin_ref, mixed_twin_ref, branch_twin_ref,
    own_ref, turned_ref, rows_ref,
):
    step = pl.program_id(0)
    core = core_ref[0]
    owners, part, width = own_ref.shape
    last = pl.num_programs(0) - 1

    @pl.when(step == 0)
    def _():
        for side, ref in ((0, low_ref), (1, low_twin_ref)):
            turned_ref[...] = jnp.transpose(ref[...].astype(F32)).astype(BF16)
            for z in range(owners):
                start = pl.multiple_of((2 * z + core) * part, part)
                rows_ref[side, z * part : (z + 1) * part, :] = turned_ref[pl.ds(start, part), :]

    @pl.when(step < last)
    def _():
        total = contract(rows_ref[0], hidden_ref[...], 1, 0)
        total = total + contract(rows_ref[1], hidden_twin_ref[...], 1, 0)
        own_ref[...] = total.astype(BF16).reshape(owners, part, width)

    @pl.when(step == last)
    def _():
        total = 0.0
        sides = ((core, mixed_ref, branch_ref), (1 - core, mixed_twin_ref, branch_twin_ref))
        for member, ref, grad_ref in sides:
            for half in range(2):
                mixed = jnp.concatenate(
                    [
                        ref[
                            2 * z + (member ^ half),
                            pl.ds(pl.multiple_of(core * part, part), part),
                            :,
                        ]
                        for z in range(owners)
                    ],
                    axis=0,
                )
                rows = slice(half * BLOCK, (half + 1) * BLOCK)
                total = total + contract(mixed, grad_ref[rows, :], 1, 0)
        own_ref[...] = total.astype(BF16).reshape(owners, part, width)


def pair_sums(core, own, twin):
    low, hidden, mixed, branch = own
    rows, model_width = low.shape
    owners = mixed.shape[0] // 2
    part = model_width // (2 * owners)
    steps = hidden.shape[1] // model_width
    whole = lambda value: pl.BlockSpec(value.shape, lambda j, core: (0,) * value.ndim)
    chunk = pl.BlockSpec((rows, model_width), lambda j, core: (0, jnp.minimum(j, steps - 1)))
    one_side = [whole(low), chunk, whole(mixed), whole(branch)]
    return pl.pallas_call(
        pair_kernel,
        name="pair_sums",
        grid_spec=pltpu.PrefetchScalarGridSpec(
            num_scalar_prefetch=1,
            grid=(steps + 1,),
            in_specs=one_side * 2,
            out_specs=pl.BlockSpec((owners, part, model_width), lambda j, core: (0, 0, j)),
            scratch_shapes=[
                pltpu.VMEM((model_width, rows), BF16),
                pltpu.VMEM((2, owners * part, rows), BF16),
            ],
        ),
        out_shape=jax.ShapeDtypeStruct((owners, part, (steps + 1) * model_width), BF16),
        compiler_params=pltpu.CompilerParams(vmem_limit_bytes=VMEM_LIMIT),
    )(core, *own, *twin)


def joint_kernel(
    core_ref, plain_ref, joint_ref, weight_ref, gain_ref, shift_ref,
    own_ref, other_ref, sums_ref, lines_ref, product_ref, full_ref,
):
    step = pl.program_id(0)
    core = core_ref[0]
    owners, part, columns = own_ref.shape
    joint = joint_ref[...]
    product = contract(joint, plain_ref[...], 1, 0)
    line = contract(jnp.ones((8, joint.shape[1]), BF16), joint, 1, 1)

    @pl.when(step == 0)
    def _():
        product_ref[...] = product
        lines_ref[...] = line

    @pl.when(step > 0)
    def _():
        product_ref[...] += product
        lines_ref[...] += line

    @pl.when(step == pl.num_programs(0) - 1)
    def _():
        total = product_ref[...]
        sums = jnp.transpose(lines_ref[...])[:, :1]
        weight = weight_ref[...].astype(F32)
        sums_ref[0:1, :] = jnp.sum(total * weight, axis=0, keepdims=True)
        sums_ref[1:2, :] = jnp.sum(sums * weight, axis=0, keepdims=True)
        full_ref[...] = jnp.transpose(gain_ref[...] * total + shift_ref[...] * sums).astype(BF16)
        for z in range(owners):
            for side, ref in ((0, own_ref), (1, other_ref)):
                start = pl.multiple_of((2 * z + (core ^ side)) * part, part)
                ref[z] = full_ref[pl.ds(start, part), :]


def joint_part(core, plain, joint_t, weight_t, gain, shift):
    length, model_width = plain.shape
    columns = joint_t.shape[0]
    owners = length // CHUNK // 2
    part = model_width // (2 * owners)
    tile = 2 * CHUNK
    whole = lambda value: pl.BlockSpec(value.shape, lambda j, core: (0,) * value.ndim)
    shapes = [
        jax.ShapeDtypeStruct((owners, part, columns), BF16),
        jax.ShapeDtypeStruct((owners, part, columns), BF16),
        jax.ShapeDtypeStruct((8, model_width), F32),
        jax.ShapeDtypeStruct((8, columns), F32),
    ]
    return pl.pallas_call(
        joint_kernel,
        name="joint_part",
        grid_spec=pltpu.PrefetchScalarGridSpec(
            num_scalar_prefetch=1,
            grid=(length // tile,),
            in_specs=[
                pl.BlockSpec((tile, model_width), lambda j, core: (j, 0)),
                pl.BlockSpec((columns, tile), lambda j, core: (0, j)),
                whole(weight_t),
                whole(gain),
                whole(shift),
            ],
            out_specs=[whole(shape) for shape in shapes],
            scratch_shapes=[
                pltpu.VMEM((columns, model_width), F32),
                pltpu.VMEM((model_width, columns), BF16),
            ],
        ),
        out_shape=shapes,
        compiler_params=pltpu.CompilerParams(vmem_limit_bytes=VMEM_LIMIT),
    )(core, plain, joint_t, weight_t, gain, shift)


def head_split_device(
    block_in,
    earlier,
    cotangent,
    qkv_weight,
    out_weight,
    in_weight,
    down_weight,
    qk_bias,
    value_bias,
    out_bias,
    in_bias,
    down_bias,
    gain_one,
    shift_one,
    gain_two,
    shift_two,
    depth_weights,
):
    row_count, model_width = block_in.shape
    hidden_width = in_weight.shape[1]
    groups = lax.axis_size("shard")
    owners = groups // 2
    width = model_width // owners
    part = model_width // groups
    length = row_count * groups
    half = HEAD_DIM // 2
    member = lax.axis_index("shard")
    owner = member // 2
    core = member % 2

    pieces = qkv_weight.astype(BF16).reshape(part, 3, owners, width)
    pieces = jnp.transpose(pieces, (2, 0, 1, 3)).reshape(owners, part, 3 * width)
    vectors = (
        qk_bias, value_bias, gain_one, shift_one,
        out_bias, in_bias, down_bias, gain_two, shift_two,
    )
    late = lax.optimization_barrier(jnp.concatenate(vectors))
    early, late = late[: 5 * part], late[5 * part :]
    half_late = late.shape[0] // 2
    rows = [early, late[:half_late], late[half_late:]]
    rows = jnp.stack([jnp.pad(row, (0, 3 * width - row.shape[0])) for row in rows])
    early = jnp.pad(rows.astype(BF16), ((0, 5), (0, 0)))
    early = jnp.broadcast_to(early, (owners, 8, 3 * width))
    packets = exchange_owner(jnp.concatenate([pieces, early], axis=1), owner)
    packet = jnp.stack(packets)
    other_packet = swap_core(packet)

    tokens = lax.all_gather(block_in, "shard", axis=0, tiled=True)
    grad_earlier, mix, depth_sums = average(depth_weights, earlier, cotangent)

    by_core = jnp.stack([packet, other_packet])
    packet = jnp.stack(
        [
            lax.dynamic_slice(
                by_core,
                (core ^ (d % 2), (owner - d // 2) % owners, 0, 0),
                (1, 1, part + 8, 3 * width),
            )[0, 0]
            for d in range(groups)
        ]
    )
    w_own = packet[:, :part].reshape(model_width, 3 * width)
    early = packet[:, part].astype(F32)
    late = packet[:, part + 1 : part + 3, :half_late].astype(F32).reshape(groups, -1)
    b_qk = early[:, : 2 * part].reshape(2 * model_width)
    b_value = early[:, 2 * part : 3 * part].reshape(model_width)
    g_one = early[:, 3 * part : 4 * part].reshape(1, model_width)
    s_one = early[:, 4 * part : 5 * part].reshape(1, model_width)
    b_joint = jnp.concatenate([b_qk, b_value]).reshape(3, owners, width)
    b_own = lax.dynamic_index_in_dim(b_joint, owner, 1, keepdims=False).reshape(3 * width, 1)
    w_turned = jnp.transpose(w_own)

    freqs = 10000.0 ** (-jnp.arange(half, dtype=F32) / half)
    angles = freqs[:, None] * jnp.arange(length, dtype=jnp.int32).astype(F32)[None, :]
    cosine = jnp.cos(angles)
    sine = jnp.sin(angles)
    core_index = core.astype(jnp.int32).reshape(1)

    hidden_part = hidden_width // groups
    share = hidden_part // 3
    row = lambda first, size: late[:, first : first + size].reshape(1, groups * size)
    b_out = row(0, part)
    b_in = row(part, hidden_part)
    b_down = row(part + hidden_part, part)
    g_two = row(2 * part + hidden_part, part)
    s_two = row(3 * part + hidden_part, part)
    last = jnp.pad(out_weight.astype(BF16), ((0, share - part), (0, 0)))
    rep = lax.axis_index("rep")
    tail_packet = lax.dynamic_slice_in_dim(
        jnp.concatenate([down_weight.astype(BF16), last], axis=0), rep * share, share, 0
    )
    tokens, w_turned, b_own, cosine, sine, mix, tail_packet, in_packet = after(
        (tokens, w_turned, b_own, cosine, sine, mix, tail_packet, in_weight.astype(BF16)),
        grad_earlier,
        depth_sums,
    )
    tail_parts = [tail_packet] + [shift_owner(tail_packet, k) for k in range(1, owners)]
    states = project(tokens, w_turned, b_own, g_one, s_one, cosine, sine, 0, groups, ())
    plain_all, qt, kt, vt, kv, *tail_parts = lax.optimization_barrier((*states, *tail_parts))
    grad_result = depth_weights[4] * cotangent
    down_grad = grad_result.astype(BF16)
    tail_stack = jnp.stack(tail_parts)
    qt, tail_stack, in_packet, down_grad = lax.optimization_barrier(
        (qt, tail_stack, in_packet, down_grad)
    )
    w_in = lax.all_gather(in_packet, "shard", axis=0, tiled=True)
    tail_mine = every_rep(tail_stack)
    mixed_own, attended, stats = attend(core_index, qt, kv, vt)
    stats, *tail_mine = lax.optimization_barrier((stats, *tail_mine))
    mixed_two = lax.all_to_all(mixed_own, "shard", 0, 0)
    tail_other = [swap_core(value) for value in tail_mine]
    w_down, w_out = assemble(
        jnp.stack([member, rep]).astype(jnp.int32), tail_mine, tail_other, part
    )
    grad_active = contract(down_grad, w_down, 1, 1).astype(BF16)
    mixed_two, grad_active = lax.optimization_barrier((mixed_two, grad_active))

    inputs = block_in.astype(F32)
    (
        middle, normed_two_low, active, grad_hidden, grad_middle, branch_grad, grad_own,
        token_sums, grad_in_b,
    ) = middle_part(
        core_index, depth_weights, mixed_two, block_in, cotangent, w_out, b_out, g_two, s_two,
        w_in, b_in, grad_active,
    )
    grad_out_b, grad_gain_two, grad_shift_two = (token_sums[i] for i in range(3))
    grad_in_b = grad_in_b[0]
    grad_own = lax.all_to_all(grad_own, "shard", 0, 0)
    pair_own = (normed_two_low, grad_hidden, mixed_two, branch_grad)
    pair_twin = tuple(swap_core(value) for value in pair_own)
    grad_down_w = down_part(active, down_grad)
    folded = pair_sums(core_index, pair_own, pair_twin)
    grad_down_b = jnp.sum(down_grad.astype(F32), axis=0)
    grad_own, folded, grad_down_w = lax.optimization_barrier((grad_own, folded, grad_down_w))
    sent = send_rep(folded)
    down_sums = lax.psum_scatter(grad_down_w, "shard", scatter_dimension=0, tiled=True)
    joint_t, grad_normed = retrace(
        core_index, qt, grad_own, attended, stats, cosine, sine, kv, kt, w_turned
    )
    joint_t, grad_normed, folded, plain_all, active, *sent = lax.optimization_barrier(
        (joint_t, grad_normed, folded, plain_all, active, *sent)
    )
    grad_normed = lax.psum_scatter(
        grad_normed, "shard", scatter_dimension=0, tiled=True
    )
    folded = join_rep(folded, sent)

    own_sums, other_sums, first_sums, joint_sums = joint_part(
        core_index, plain_all, joint_t, w_turned, g_one, s_one
    )
    arrived = exchange_owner(folded, owner)
    layer_out, last_depth = result_part(
        depth_weights, active, w_down, b_down, middle, mix, cotangent
    )
    own_sums, other_sums, first_sums, joint_sums, last_depth, *arrived = (
        lax.optimization_barrier(
            (own_sums, other_sums, first_sums, joint_sums, last_depth, *arrived)
        )
    )
    pair_sum = add_low(*arrived)
    grad_gain_one, grad_shift_one = first_sums[0], first_sums[1]
    joint_sums = joint_sums[0]

    spread_sums = lax.dynamic_update_slice(
        jnp.zeros((3, model_width), F32), joint_sums.reshape(3, width), (0, owner * width)
    ).reshape(3 * model_width)
    vectors = (
        spread_sums[: 2 * model_width],
        spread_sums[2 * model_width :],
        grad_out_b,
        grad_in_b,
        grad_down_b,
        grad_gain_one,
        grad_shift_one,
        grad_gain_two,
        grad_shift_two,
    )
    counts = [vector.shape[0] // model_width for vector in vectors]
    small = jnp.concatenate(
        [
            vector.reshape(groups, count, part).astype(BF16)
            for vector, count in zip(vectors, counts)
        ],
        axis=1,
    )
    small = jnp.pad(small, ((0, 0), (0, part - small.shape[1]), (0, 128 - part)))
    mark = (part // 4 - 8, 3 * width)
    small = small.reshape(owners, 2, part, 128)
    depth_count = 2 * depth_weights.shape[0]
    depth_row = lambda value: value[mark[0], mark[1] : mark[1] + depth_count]
    with_depth = lambda value, sums: value.at[
        :, mark[0], mark[1] : mark[1] + depth_count
    ].set(split_depth(sums))
    received = swap_core(
        jnp.concatenate([other_sums, pick(small, 1 - core, 1)], axis=2)
    )
    mixed_sums = add_low(
        jnp.concatenate([own_sums, pick(small, core, 1)], axis=2), received
    )
    depth_sum = jnp.concatenate([depth_sums, last_depth[None]], axis=0).sum(axis=(1, 2))
    depth_sum = depth_sum + swap_core(depth_sum)
    down_parts = pick_parts(down_sums[None])
    down_rows = part // 4
    columns = 3 * width + 128
    sums_parts = [with_depth(value, depth_sum) for value in pick_parts(mixed_sums)]
    received = [
        cross_rep(
            jnp.concatenate([sums, down.reshape(owners, down_rows, model_width)], axis=2), k
        )
        for k, (sums, down) in enumerate(zip(sums_parts[1:], down_parts[1:]), 1)
    ]
    pair_sum, *received = lax.optimization_barrier((pair_sum, *received))
    pair_pieces = every_rep(pair_sum)
    mixed_sums = add_low(sums_parts[0], *[value[:, :, :columns] for value in received])
    depth_sum = add_ordered(
        [join_depth(depth_row(value[0])) for value in (sums_parts[0], *received)], lambda k: rep ^ k
    )
    mixed_sums = with_depth(mixed_sums, depth_sum)
    down_sums = add_low(
        down_parts[0].reshape(owners, down_rows, model_width),
        *[value[:, :, columns:] for value in received],
    )
    down_pieces = every_rep(jnp.concatenate([down_sums[k] for k in range(owners)], axis=1))
    arrived = exchange_owner(mixed_sums, owner)
    small = add_low(*[value[:, 3 * width :] for value in arrived])
    by_distance = jnp.stack([value[:, : 3 * width] for value in arrived])
    by_owner = [pick(by_distance, (owner - k) % owners) for k in range(owners)]
    joint_pieces = every_rep(jnp.concatenate([*by_owner, small], axis=1))
    depth_sums = [depth_row(value) for value in arrived]
    pieces = lax.optimization_barrier(
        (*joint_pieces, *pair_pieces, *down_pieces, *depth_sums)
    )
    joint_pieces, pair_pieces = pieces[:4], pieces[4:8]
    down_pieces, depth_sums = pieces[8:12], pieces[12:]
    grad_depth = add_ordered(
        [join_depth(value) for value in depth_sums], lambda k: (owner - k) % owners
    )
    sum_in, sum_out, sum_qkv, sum_down, *small_outs = unpack(
        lax.axis_index("rep").astype(jnp.int32).reshape(1),
        pair_pieces,
        joint_pieces,
        down_pieces,
        (hidden_width, model_width, 3 * width),
        counts,
    )
    small_outs = [value.reshape(-1) for value in small_outs]
    finished = (sum_in, sum_out, sum_qkv, sum_down, grad_depth, *small_outs)
    grad_normed, sum_in, sum_out, sum_qkv, sum_down, grad_depth, *small_outs = (
        lax.optimization_barrier((grad_normed, *finished))
    )
    grad_normed = grad_normed.astype(F32)
    center = inputs - jnp.mean(inputs, axis=-1, keepdims=True)
    scale = lax.rsqrt(jnp.mean(center * center, axis=-1, keepdims=True) + EPSILON)
    plain = center * scale
    scaled = grad_normed * g_one
    grad_block = grad_middle + scale * (
        scaled
        - jnp.mean(scaled, axis=-1, keepdims=True)
        - plain * jnp.mean(scaled * plain, axis=-1, keepdims=True)
    )

    return (
        layer_out,
        grad_block,
        grad_earlier,
        sum_qkv,
        sum_out,
        sum_in,
        sum_down,
        *small_outs,
        grad_depth,
    )


def per_device(*args):
    block_in = args[0]
    row_count, model_width = block_in.shape
    groups = lax.axis_size("shard")
    head_count = model_width // HEAD_DIM
    late_size = (4 * model_width + args[5].shape[1]) // groups
    if (
        groups == 8
        and lax.axis_size("rep") == 4
        and row_count == CHUNK
        and head_count % (groups // 2) == 0
        and head_count // (groups // 2) <= 8
        and late_size <= 12 * model_width // groups
        and args[5].shape[1] % (3 * groups) == 0
        and model_width // groups <= args[5].shape[1] // (3 * groups)
    ):
        return head_split_device(*args)
    return generic_device(*args)


def solution(mesh):
    placed = (
        P(("rep", "shard"), None),
        P(None, ("rep", "shard"), None),
        P(("rep", "shard"), None),
        P("shard", None),
        P("shard", None),
        P("shard", None),
        P("shard", None),
        P("shard"),
        P("shard"),
        P("shard"),
        P("shard"),
        P("shard"),
        P("shard"),
        P("shard"),
        P("shard"),
        P("shard"),
        P(),
    )
    return jax.shard_map(
        per_device,
        mesh=mesh,
        in_specs=placed,
        out_specs=(
            P(("rep", "shard"), None),
            P(("rep", "shard"), None),
            P(None, ("rep", "shard"), None),
            P("shard", None),
            P("shard", None),
            P("shard", None),
            P("shard", None),
            P("shard"),
            P("shard"),
            P("shard"),
            P("shard"),
            P("shard"),
            P("shard"),
            P("shard"),
            P("shard"),
            P("shard"),
            P(),
        ),
        check_vma=False,
    )
```

```python
from functools import partial
import math

import jax
import jax.numpy as jnp
from jax import lax
from jax.experimental import pallas as pl
from jax.experimental.pallas import tpu as pltpu
from jax.sharding import PartitionSpec as P

HEAD_DIM = 64
BLOCK = 256


NEG = -1e30
EPSILON = 1e-05


def layer_norm(inputs, gain, shift):
    center = inputs - jnp.mean(inputs, axis=-1, keepdims=True)
    spread = jnp.mean(center * center, axis=-1, keepdims=True)
    return center * lax.rsqrt(spread + EPSILON) * gain + shift


def rotate(inputs, positions):
    row_count = inputs.shape[0]
    split = inputs.reshape(row_count, -1, HEAD_DIM)
    half_dim = HEAD_DIM // 2
    freqs = 10000.0 ** (-jnp.arange(half_dim, dtype=jnp.float32) / half_dim)
    angles = positions.astype(jnp.float32)[:, None] * freqs[None, :]
    cosine = jnp.cos(angles)[:, None, :]
    sine = jnp.sin(angles)[:, None, :]
    former = split[..., :half_dim]
    latter = split[..., half_dim:]
    turned = jnp.concatenate(
        [former * cosine - latter * sine, former * sine + latter * cosine], axis=-1
    )
    return turned.reshape(row_count, -1)


def generic_device(
    block_in,
    earlier,
    cotangent,
    qkv_weight,
    out_weight,
    in_weight,
    down_weight,
    qk_bias,
    value_bias,
    out_bias,
    in_bias,
    down_bias,
    gain_one,
    shift_one,
    gain_two,
    shift_two,
    depth_weights,
):
    bf16 = jnp.bfloat16
    f32 = jnp.float32
    w_qkv, w_out, w_in, w_down, b_qk, b_value, b_out, b_in, b_down, g_one, s_one, g_two, s_two = (
        lax.all_gather(qkv_weight.astype(bf16), "shard", axis=0, tiled=True),
        lax.all_gather(out_weight.astype(bf16), "shard", axis=0, tiled=True),
        lax.all_gather(in_weight.astype(bf16), "shard", axis=0, tiled=True),
        lax.all_gather(down_weight.astype(bf16), "shard", axis=0, tiled=True),
        lax.all_gather(qk_bias.astype(bf16), "shard", axis=0, tiled=True),
        lax.all_gather(value_bias.astype(bf16), "shard", axis=0, tiled=True),
        lax.all_gather(out_bias.astype(bf16), "shard", axis=0, tiled=True),
        lax.all_gather(in_bias.astype(bf16), "shard", axis=0, tiled=True),
        lax.all_gather(down_bias.astype(bf16), "shard", axis=0, tiled=True),
        lax.all_gather(gain_one.astype(bf16), "shard", axis=0, tiled=True),
        lax.all_gather(shift_one.astype(bf16), "shard", axis=0, tiled=True),
        lax.all_gather(gain_two.astype(bf16), "shard", axis=0, tiled=True),
        lax.all_gather(shift_two.astype(bf16), "shard", axis=0, tiled=True),
    )
    row_count, model_width = block_in.shape
    head_count = model_width // HEAD_DIM
    groups = lax.axis_size("shard")
    length = row_count * groups
    window = min(512, length)
    member = lax.axis_index("shard")
    first_row = member * row_count
    last_end = first_row + row_count
    positions = first_row + jnp.arange(row_count, dtype=jnp.int32)
    query_block = positions // BLOCK
    score_scale = HEAD_DIM ** (-0.5)
    needed = (last_end + window - 1) // window
    inputs = block_in.astype(f32)
    normed, norm_back = jax.vjp(layer_norm, inputs, g_one.astype(f32), s_one.astype(f32))
    normed_low = normed.astype(bf16)
    joint_bias = jnp.concatenate([b_qk.astype(f32), b_value.astype(f32)])
    projected = jnp.dot(normed_low, w_qkv, preferred_element_type=f32) + joint_bias
    queries = rotate(projected[:, :model_width], positions).astype(bf16)
    key_rows = rotate(projected[:, model_width : 2 * model_width], positions).astype(bf16)
    values = projected[:, 2 * model_width :].astype(bf16)
    query_heads = queries.reshape(row_count, head_count, HEAD_DIM)

    def masked_scores(key_piece, key_start):
        piece_rows = key_piece.shape[0]
        key_heads = key_piece.reshape(piece_rows, head_count, HEAD_DIM)
        scores = (
            jnp.einsum("qhd,khd->hqk", query_heads, key_heads, preferred_element_type=f32)
            * score_scale
        )
        key_block = (key_start + jnp.arange(piece_rows, dtype=jnp.int32)) // BLOCK
        allowed = key_block[None, :] <= query_block[:, None]
        return (scores, allowed)

    def absorb(running, key_piece, value_piece, key_start):
        highest, denominator, summed = running
        scores, allowed = masked_scores(key_piece, key_start)
        scores = jnp.where(allowed[None], scores, NEG)
        new_high = jnp.maximum(highest, jnp.max(scores, axis=-1))
        rescale = jnp.exp(highest - new_high)
        weights = jnp.where(allowed[None], jnp.exp(scores - new_high[..., None]), 0.0)
        value_heads = value_piece.reshape(-1, head_count, HEAD_DIM)
        summed = summed * rescale[..., None] + jnp.einsum(
            "hqk,khd->hqd", weights.astype(bf16), value_heads, preferred_element_type=f32
        )
        return (new_high, denominator * rescale + jnp.sum(weights, axis=-1), summed)

    start_state = (
        jnp.full((head_count, row_count), NEG, f32),
        jnp.zeros((head_count, row_count), f32),
        jnp.zeros((head_count, row_count, HEAD_DIM), f32),
    )
    key_piece = lax.all_gather(key_rows, "shard", axis=0, tiled=True)
    value_piece = lax.all_gather(values, "shard", axis=0, tiled=True)
    piece_rows = key_piece.shape[0]
    sub_rows = math.gcd(piece_rows, window)
    usable = jnp.clip((last_end + sub_rows - 1) // sub_rows, 0, piece_rows // sub_rows)

    def advance(block_step, state_inner):
        offset = block_step * sub_rows
        return absorb(
            state_inner,
            lax.dynamic_slice_in_dim(key_piece, offset, sub_rows, 0),
            lax.dynamic_slice_in_dim(value_piece, offset, sub_rows, 0),
            offset,
        )

    highest, denominator, summed = lax.fori_loop(0, usable, advance, start_state)
    attended = summed / denominator[..., None]
    log_norm = highest + jnp.log(denominator)
    mixed = jnp.transpose(attended, (1, 0, 2)).reshape(row_count, model_width).astype(bf16)
    branch = jnp.dot(mixed, w_out, preferred_element_type=f32) + b_out.astype(f32)
    middle = inputs + branch
    normed_two, norm_two_back = jax.vjp(layer_norm, middle, g_two.astype(f32), s_two.astype(f32))
    normed_two_low = normed_two.astype(bf16)
    hidden = jnp.dot(normed_two_low, w_in, preferred_element_type=f32) + b_in.astype(f32)
    active_full, gelu_back = jax.vjp(partial(jax.nn.gelu, approximate=True), hidden)
    active = active_full.astype(bf16)
    result = middle + jnp.dot(active, w_down, preferred_element_type=f32) + b_down.astype(f32)
    stacked = earlier.astype(f32)
    layer_out = depth_weights[4] * result
    for level in range(4):
        layer_out = layer_out + depth_weights[level] * stacked[level]
    grad_earlier = depth_weights[:4][:, None, None] * cotangent[None]
    local_depth = jnp.concatenate(
        [jnp.sum(stacked * cotangent[None], axis=(1, 2)), jnp.sum(result * cotangent)[None]]
    )
    grad_depth = lax.psum(local_depth, ("rep", "shard"))
    grad_result = depth_weights[4] * cotangent
    down_grad = grad_result.astype(bf16)
    grad_down_w = jnp.einsum("tf,td->fd", active, down_grad, preferred_element_type=f32)
    grad_down_b = jnp.sum(down_grad.astype(f32), axis=0)
    grad_active = jnp.einsum("td,fd->tf", down_grad, w_down, preferred_element_type=f32)
    grad_hidden = gelu_back(grad_active)[0].astype(bf16)
    grad_in_w = jnp.einsum("td,tf->df", normed_two_low, grad_hidden, preferred_element_type=f32)
    grad_in_b = jnp.sum(grad_hidden.astype(f32), axis=0)
    grad_normed_two = jnp.einsum("tf,df->td", grad_hidden, w_in, preferred_element_type=f32)
    grad_mid_norm, grad_gain_two, grad_shift_two = norm_two_back(grad_normed_two)
    grad_middle = grad_result + grad_mid_norm
    branch_grad = grad_middle.astype(bf16)
    grad_out_w = jnp.einsum("td,te->de", mixed, branch_grad, preferred_element_type=f32)
    grad_out_b = jnp.sum(branch_grad.astype(f32), axis=0)
    grad_mixed = jnp.einsum("te,de->td", branch_grad, w_out, preferred_element_type=f32).astype(
        bf16
    )
    key_all, value_all = (
        lax.all_gather(key_rows, "shard", axis=0, tiled=True),
        lax.all_gather(values, "shard", axis=0, tiled=True),
    )
    grad_heads = grad_mixed.reshape(row_count, head_count, HEAD_DIM)
    delta = jnp.einsum("qhd,hqd->hq", grad_heads.astype(f32), attended)

    def score_grads(key_piece, value_piece, offset, piece_rows):
        scores, allowed = masked_scores(key_piece, offset)
        probs = jnp.where(allowed[None], jnp.exp(scores - log_norm[..., None]), 0.0)
        value_heads = value_piece.reshape(piece_rows, head_count, HEAD_DIM)
        grad_probs = jnp.einsum("qhd,khd->hqk", grad_heads, value_heads, preferred_element_type=f32)
        grad_scores = (probs * (grad_probs - delta[..., None])).astype(bf16)
        return (probs, grad_scores)

    def retrace(block_step, running):
        grad_query, grad_keys, grad_values = running
        offset = block_step * window
        key_piece = lax.dynamic_slice_in_dim(key_all, offset, window, 0)
        value_piece = lax.dynamic_slice_in_dim(value_all, offset, window, 0)
        probs, grad_scores = score_grads(key_piece, value_piece, offset, window)
        key_heads = key_piece.reshape(window, head_count, HEAD_DIM)
        grad_query = grad_query + jnp.einsum(
            "hqk,khd->qhd", grad_scores, key_heads, preferred_element_type=f32
        )
        piece_keys = (
            jnp.einsum("hqk,qhd->khd", grad_scores, query_heads, preferred_element_type=f32)
            * score_scale
        )
        piece_values = jnp.einsum(
            "hqk,qhd->khd", probs.astype(bf16), grad_heads, preferred_element_type=f32
        )
        grad_keys = lax.dynamic_update_slice_in_dim(
            grad_keys, piece_keys.reshape(window, model_width), offset, 0
        )
        grad_values = lax.dynamic_update_slice_in_dim(
            grad_values, piece_values.reshape(window, model_width), offset, 0
        )
        return (grad_query, grad_keys, grad_values)

    start_back = (
        jnp.zeros((row_count, head_count, HEAD_DIM), f32),
        jnp.zeros((length, model_width), f32),
        jnp.zeros((length, model_width), f32),
    )
    grad_query, grad_keys, grad_values = lax.fori_loop(0, needed, retrace, start_back)
    own_keys, own_values = (
        lax.psum_scatter(
            grad_keys.astype(jnp.bfloat16), "shard", scatter_dimension=0, tiled=True
        ).astype(jnp.float32),
        lax.psum_scatter(
            grad_values.astype(jnp.bfloat16), "shard", scatter_dimension=0, tiled=True
        ).astype(jnp.float32),
    )
    grad_q_turned = rotate(grad_query.reshape(row_count, model_width) * score_scale, -positions)
    grad_k_turned = rotate(own_keys, -positions)
    grad_joint = jnp.concatenate([grad_q_turned, grad_k_turned, own_values], axis=1).astype(bf16)
    grad_qkv_w = jnp.einsum("td,tf->df", normed_low, grad_joint, preferred_element_type=f32)
    joint_sums = jnp.sum(grad_joint.astype(f32), axis=0)
    grad_qk_b = joint_sums[: 2 * model_width]
    grad_value_b = joint_sums[2 * model_width :]
    grad_normed = jnp.einsum("tf,df->td", grad_joint, w_qkv, preferred_element_type=f32)
    grad_in_norm, grad_gain_one, grad_shift_one = norm_back(grad_normed)
    grad_block = grad_middle + grad_in_norm
    (
        own_qkv_w,
        own_out_w,
        own_in_w,
        own_down_w,
        own_qk_b,
        own_value_b,
        own_out_b,
        own_in_b,
        own_down_b,
        own_gain_one,
        own_shift_one,
        own_gain_two,
        own_shift_two,
    ) = (
        lax.psum_scatter(
            grad_qkv_w.astype(jnp.bfloat16), "shard", scatter_dimension=0, tiled=True
        ).astype(jnp.float32),
        lax.psum_scatter(
            grad_out_w.astype(jnp.bfloat16), "shard", scatter_dimension=0, tiled=True
        ).astype(jnp.float32),
        lax.psum_scatter(
            grad_in_w.astype(jnp.bfloat16), "shard", scatter_dimension=0, tiled=True
        ).astype(jnp.float32),
        lax.psum_scatter(
            grad_down_w.astype(jnp.bfloat16), "shard", scatter_dimension=0, tiled=True
        ).astype(jnp.float32),
        lax.psum_scatter(
            grad_qk_b.astype(jnp.bfloat16), "shard", scatter_dimension=0, tiled=True
        ).astype(jnp.float32),
        lax.psum_scatter(
            grad_value_b.astype(jnp.bfloat16), "shard", scatter_dimension=0, tiled=True
        ).astype(jnp.float32),
        lax.psum_scatter(
            grad_out_b.astype(jnp.bfloat16), "shard", scatter_dimension=0, tiled=True
        ).astype(jnp.float32),
        lax.psum_scatter(
            grad_in_b.astype(jnp.bfloat16), "shard", scatter_dimension=0, tiled=True
        ).astype(jnp.float32),
        lax.psum_scatter(
            grad_down_b.astype(jnp.bfloat16), "shard", scatter_dimension=0, tiled=True
        ).astype(jnp.float32),
        lax.psum_scatter(
            grad_gain_one.astype(jnp.bfloat16), "shard", scatter_dimension=0, tiled=True
        ).astype(jnp.float32),
        lax.psum_scatter(
            grad_shift_one.astype(jnp.bfloat16), "shard", scatter_dimension=0, tiled=True
        ).astype(jnp.float32),
        lax.psum_scatter(
            grad_gain_two.astype(jnp.bfloat16), "shard", scatter_dimension=0, tiled=True
        ).astype(jnp.float32),
        lax.psum_scatter(
            grad_shift_two.astype(jnp.bfloat16), "shard", scatter_dimension=0, tiled=True
        ).astype(jnp.float32),
    )
    (
        sum_qkv_w,
        sum_out_w,
        sum_in_w,
        sum_down_w,
        sum_qk_b,
        sum_value_b,
        sum_out_b,
        sum_in_b,
        sum_down_b,
        sum_gain_one,
        sum_shift_one,
        sum_gain_two,
        sum_shift_two,
    ) = (
        lax.psum(own_qkv_w.astype(jnp.bfloat16), "rep").astype(jnp.float32),
        lax.psum(own_out_w.astype(jnp.bfloat16), "rep").astype(jnp.float32),
        lax.psum(own_in_w.astype(jnp.bfloat16), "rep").astype(jnp.float32),
        lax.psum(own_down_w.astype(jnp.bfloat16), "rep").astype(jnp.float32),
        lax.psum(own_qk_b.astype(jnp.bfloat16), "rep").astype(jnp.float32),
        lax.psum(own_value_b.astype(jnp.bfloat16), "rep").astype(jnp.float32),
        lax.psum(own_out_b.astype(jnp.bfloat16), "rep").astype(jnp.float32),
        lax.psum(own_in_b.astype(jnp.bfloat16), "rep").astype(jnp.float32),
        lax.psum(own_down_b.astype(jnp.bfloat16), "rep").astype(jnp.float32),
        lax.psum(own_gain_one.astype(jnp.bfloat16), "rep").astype(jnp.float32),
        lax.psum(own_shift_one.astype(jnp.bfloat16), "rep").astype(jnp.float32),
        lax.psum(own_gain_two.astype(jnp.bfloat16), "rep").astype(jnp.float32),
        lax.psum(own_shift_two.astype(jnp.bfloat16), "rep").astype(jnp.float32),
    )
    return (
        layer_out,
        grad_block,
        grad_earlier,
        sum_qkv_w,
        sum_out_w,
        sum_in_w,
        sum_down_w,
        sum_qk_b,
        sum_value_b,
        sum_out_b,
        sum_in_b,
        sum_down_b,
        sum_gain_one,
        sum_shift_one,
        sum_gain_two,
        sum_shift_two,
        grad_depth,
    )


F32 = jnp.float32
BF16 = jnp.bfloat16
CHUNK = 2 * BLOCK
VMEM_LIMIT = 56 * 1024 * 1024


def cost(flops, moved, exps=0):
    return pl.CostEstimate(flops=flops, bytes_accessed=moved, transcendentals=exps)


def contract(left, right, left_dim, right_dim):
    return lax.dot_general(
        left, right, (((left_dim,), (right_dim,)), ((), ())), preferred_element_type=F32
    )


def qkv_kernel(x_ref, weight_ref, bias_ref, gain_ref, shift_ref, cos_ref, sin_ref, *refs):
    plain_ref, qt_ref, kt_ref, vt_ref, kv_ref = refs[-5:]
    x = x_ref[...].astype(F32)
    center = x - jnp.mean(x, axis=-1, keepdims=True)
    spread = jnp.mean(center * center, axis=-1, keepdims=True)
    plain = center * lax.rsqrt(spread + EPSILON)
    plain_ref[...] = plain.astype(BF16)
    low = (plain * gain_ref[...] + shift_ref[...]).astype(BF16)
    width = qt_ref.shape[0]
    half = HEAD_DIM // 2
    joint = contract(weight_ref[...], low, 1, 1) + bias_ref[...]
    cosine = cos_ref[...]
    sine = sin_ref[...]
    for head in range(width // HEAD_DIM):
        base = head * HEAD_DIM
        for part in range(2):
            start = part * width + base
            former = joint[start : start + half]
            latter = joint[start + half : start + HEAD_DIM]
            turned = jnp.concatenate(
                [former * cosine - latter * sine, former * sine + latter * cosine], axis=0
            )
            if part == 0:
                qt_ref[base : base + HEAD_DIM, :] = (turned * HEAD_DIM ** (-0.5)).astype(BF16)
            else:
                kt_ref[base : base + HEAD_DIM, :] = turned.astype(BF16)
                key = turned
        start = 2 * width + base
        value = joint[start : start + HEAD_DIM]
        vt_ref[base : base + HEAD_DIM, :] = value.astype(BF16)
        kv_ref[head] = jnp.transpose(jnp.concatenate([key, value], axis=0).astype(BF16))


def project(tokens, weight_t, bias, gain, shift, cosine, sine, first, count, held):
    length, model_width = tokens.shape
    columns = weight_t.shape[0]
    width = columns // 3
    heads = width // HEAD_DIM
    half = HEAD_DIM // 2
    tile = CHUNK
    fixed = lambda i: (0, 0)
    down = lambda i: (first + i, 0)
    across = lambda i: (0, first + i)
    inputs = [tokens, weight_t, bias, gain, shift, cosine, sine]
    return pl.pallas_call(
        qkv_kernel,
        name="project",
        cost_estimate=cost(2 * count * tile * model_width * columns, 12 * count * tile * model_width),
        grid=(count,),
        in_specs=[
            pl.BlockSpec((tile, model_width), down),
            pl.BlockSpec((columns, model_width), fixed),
            pl.BlockSpec((columns, 1), fixed),
            pl.BlockSpec((1, model_width), fixed),
            pl.BlockSpec((1, model_width), fixed),
            pl.BlockSpec((half, tile), across),
            pl.BlockSpec((half, tile), across),
        ]
        + [pl.BlockSpec(memory_space=pl.ANY)] * len(held),
        out_specs=[
            pl.BlockSpec((tile, model_width), down),
            pl.BlockSpec((width, tile), across),
            pl.BlockSpec((width, tile), across),
            pl.BlockSpec((width, tile), across),
            pl.BlockSpec((heads, tile, 2 * HEAD_DIM), lambda i: (0, first + i, 0)),
        ],
        out_shape=[
            jax.ShapeDtypeStruct((length, model_width), BF16),
            jax.ShapeDtypeStruct((width, length), BF16),
            jax.ShapeDtypeStruct((width, length), BF16),
            jax.ShapeDtypeStruct((width, length), BF16),
            jax.ShapeDtypeStruct((heads, length, 2 * HEAD_DIM), BF16),
        ],
        input_output_aliases={len(inputs) + i: i for i in range(len(held))},
        compiler_params=pltpu.CompilerParams(vmem_limit_bytes=VMEM_LIMIT),
    )(*inputs, *held)


def average_kernel(weights_ref, earlier_ref, cotangent_ref, grad_ref, mix_ref, sums_ref):
    @pl.when(pl.program_id(0) == 0)
    def _():
        sums_ref[...] = jnp.zeros_like(sums_ref)

    cotangent = cotangent_ref[...]
    rows, columns = cotangent.shape
    mix = jnp.zeros_like(cotangent)
    for level in range(earlier_ref.shape[0]):
        value = earlier_ref[level].astype(F32)
        weight = weights_ref[level]
        mix = mix + weight * value
        grad_ref[level] = weight * cotangent
        sums_ref[level] += jnp.sum((value * cotangent).reshape(rows // 8, 8, columns), axis=0)
    mix_ref[...] = mix


def average(depth_weights, earlier, cotangent):
    levels, row_count, model_width = earlier.shape
    tile = row_count // 4
    return pl.pallas_call(
        average_kernel,
        name="average",
        cost_estimate=cost(6 * earlier.size, 6 * earlier.size + 8 * cotangent.size),
        grid_spec=pltpu.PrefetchScalarGridSpec(
            num_scalar_prefetch=1,
            grid=(4,),
            in_specs=[
                pl.BlockSpec((levels, tile, model_width), lambda i, w: (0, i, 0)),
                pl.BlockSpec((tile, model_width), lambda i, w: (i, 0)),
            ],
            out_specs=[
                pl.BlockSpec((levels, tile, model_width), lambda i, w: (0, i, 0)),
                pl.BlockSpec((tile, model_width), lambda i, w: (i, 0)),
                pl.BlockSpec((levels, 8, model_width), lambda i, w: (0, 0, 0)),
            ],
        ),
        out_shape=[
            jax.ShapeDtypeStruct(earlier.shape, F32),
            jax.ShapeDtypeStruct(cotangent.shape, F32),
            jax.ShapeDtypeStruct((levels, 8, model_width), F32),
        ],
        compiler_params=pltpu.CompilerParams(vmem_limit_bytes=VMEM_LIMIT),
    )(depth_weights, earlier, cotangent)


def last_mask(odd, rows):
    row = lax.broadcasted_iota(jnp.int32, (rows, BLOCK), 0)
    return row < rows - BLOCK * (1 - odd)


def over_chunks(pair, absorb, state):
    state = lax.fori_loop(0, pair // 2, lambda i, s: absorb(2 * i, 2 * CHUNK, s, False), state)
    return lax.cond(
        pair % 2 == 0,
        lambda s: absorb(pair, CHUNK, s, True),
        lambda s: absorb(pair - 1, 2 * CHUNK, s, True),
        state,
    )


def attend_kernel(core_ref, qt_ref, kv_ref, vt_ref, low_ref, full_ref, stat_ref, scores_ref):
    pair = pl.program_id(0)
    odd = core_ref[0] ^ (pair & 1)
    heads = qt_ref.shape[0] // HEAD_DIM
    blank = jnp.zeros((HEAD_DIM, BLOCK), BF16)
    queries = [
        jnp.concatenate([qt_ref[h * HEAD_DIM : (h + 1) * HEAD_DIM, :], blank], axis=0)
        for h in range(heads)
    ]
    fold = lambda value: value.reshape(value.shape[0] // 8, 8, BLOCK)

    def score(step, size, state, masked):
        keys = pl.ds(pl.multiple_of(step * CHUNK, CHUNK), size)
        fresh = []
        for h in range(heads):
            scores = contract(kv_ref[h, keys, :], queries[h], 1, 0)
            if masked:
                scores = jnp.where(last_mask(odd, size), scores, NEG)
            scores_ref[h, keys, :] = scores
            fresh.append(jnp.maximum(state[h], jnp.max(fold(scores), axis=0)))
        return fresh

    def mix(step, size, state, masked):
        keys = pl.ds(pl.multiple_of(step * CHUNK, CHUNK), size)
        fresh = []
        for h in range(heads):
            total, summed = state[h]
            weights = jnp.exp(scores_ref[h, keys, :] - highest[h])
            values = vt_ref[h * HEAD_DIM : (h + 1) * HEAD_DIM, keys]
            fresh.append(
                (
                    total + jnp.sum(fold(weights), axis=0),
                    summed + contract(values, weights.astype(BF16), 1, 0),
                )
            )
        return fresh

    state = [jnp.full((8, BLOCK), NEG, F32) for _ in range(heads)]
    state = over_chunks(pair, score, state)
    highest = [jnp.max(value, axis=0, keepdims=True) for value in state]
    state = [
        (jnp.zeros((8, BLOCK), F32), jnp.zeros((HEAD_DIM, BLOCK), F32)) for _ in range(heads)
    ]
    state = over_chunks(pair, mix, state)
    for h in range(heads):
        total, summed = state[h]
        total = jnp.sum(total, axis=0, keepdims=True)
        attended = summed / total
        full_ref[0, h * HEAD_DIM : (h + 1) * HEAD_DIM, :] = attended
        low_ref[0, h * HEAD_DIM : (h + 1) * HEAD_DIM, :] = attended.astype(BF16)
        stat_ref[0, h : h + 1, :] = highest[h] + jnp.log(total)


def attend(core, qt, kv, vt):
    width, length = qt.shape
    pairs = length // CHUNK
    own = lambda j, core: (0, 2 * j + (core[0] ^ (j & 1)))
    slot = lambda j, core: (j, 0, 0)
    return pl.pallas_call(
        attend_kernel,
        name="attend",
        cost_estimate=cost(
            2 * 2 * BLOCK * BLOCK * BLOCK * 2 * sum(range(1, pairs + 1)) * (width // HEAD_DIM),
            4 * kv.size + 8 * pairs * width * BLOCK,
            CHUNK * BLOCK * sum(range(1, pairs + 1)) * (width // HEAD_DIM),
        ),
        grid_spec=pltpu.PrefetchScalarGridSpec(
            num_scalar_prefetch=1,
            grid=(pairs,),
            in_specs=[
                pl.BlockSpec((width, BLOCK), own),
                pl.BlockSpec(kv.shape, lambda j, core: (0, 0, 0)),
                pl.BlockSpec(vt.shape, lambda j, core: (0, 0)),
            ],
            out_specs=[
                pl.BlockSpec((1, width, BLOCK), slot),
                pl.BlockSpec((1, width, BLOCK), slot),
                pl.BlockSpec((1, 8, BLOCK), slot),
            ],
            scratch_shapes=[pltpu.VMEM((width // HEAD_DIM, length, BLOCK), F32)],
        ),
        out_shape=[
            jax.ShapeDtypeStruct((pairs, width, BLOCK), BF16),
            jax.ShapeDtypeStruct((pairs, width, BLOCK), F32),
            jax.ShapeDtypeStruct((pairs, 8, BLOCK), F32),
        ],
        compiler_params=pltpu.CompilerParams(vmem_limit_bytes=VMEM_LIMIT),
    )(core, qt, kv, vt)


def retrace_kernel(
    core_ref, qt_ref, grad_ref, full_ref, stat_ref, cos_ref, sin_ref, kv_ref, kt_ref,
    weight_ref, joint_ref, normed_ref, dkv_ref,
):
    step_id = pl.program_id(0)
    pair = pl.num_programs(0) - 1 - step_id
    odd = core_ref[0] ^ (pair & 1)
    width = qt_ref.shape[0]
    heads = width // HEAD_DIM
    half = HEAD_DIM // 2

    @pl.when(step_id == 0)
    def _():
        dkv_ref[...] = jnp.zeros_like(dkv_ref)

    blank = jnp.zeros((HEAD_DIM, BLOCK), BF16)
    lefts, rights, deltas, norms = [], [], [], []
    for h in range(heads):
        rows = slice(h * HEAD_DIM, (h + 1) * HEAD_DIM)
        query = qt_ref[rows, :]
        grad = grad_ref[0, rows, :]
        lefts.append(
            jnp.concatenate(
                [
                    jnp.concatenate([query, blank], axis=1),
                    jnp.concatenate([blank, grad], axis=1),
                ],
                axis=0,
            )
        )
        rights.append(
            jnp.concatenate(
                [
                    jnp.concatenate([blank, query], axis=1),
                    jnp.concatenate([grad, blank], axis=1),
                ],
                axis=0,
            )
        )
        deltas.append(jnp.sum(grad.astype(F32) * full_ref[0, rows, :], axis=0, keepdims=True))
        norms.append(stat_ref[0, h : h + 1, :])

    def absorb(step, state, masked):
        keys = pl.ds(pl.multiple_of(step * CHUNK, CHUNK), CHUNK)
        fresh = []
        for h in range(heads):
            both = contract(kv_ref[h, keys, :], lefts[h], 1, 0)
            probs = jnp.exp(both[:, :BLOCK] - norms[h])
            if masked:
                probs = jnp.where(last_mask(odd, CHUNK), probs, 0.0)
            grad_scores = (probs * (both[:, BLOCK:] - deltas[h])).astype(BF16)
            joined = jnp.concatenate([probs.astype(BF16), grad_scores], axis=1)
            dkv_ref[h, keys, :] += contract(joined, rights[h], 1, 1)
            turned = kt_ref[h * HEAD_DIM : (h + 1) * HEAD_DIM, keys]
            fresh.append(state[h] + contract(turned, grad_scores, 1, 0))
        return fresh

    state = [jnp.zeros((HEAD_DIM, BLOCK), F32) for _ in range(heads)]
    state = lax.fori_loop(0, pair, lambda i, s: absorb(i, s, False), state)
    state = absorb(pair, state, True)
    offset = pl.multiple_of(pair * CHUNK, CHUNK)
    cosine = cos_ref[...]
    sine = sin_ref[...]
    column = lax.broadcasted_iota(jnp.int32, (HEAD_DIM, CHUNK), 1) // BLOCK

    for h in range(heads):
        base = h * HEAD_DIM
        doubled = jnp.concatenate([state[h], state[h]], axis=1) * HEAD_DIM ** (-0.5)
        doubled = jnp.where(column == odd, doubled, 0.0)
        turned_back = jnp.transpose(dkv_ref[h, pl.ds(offset, CHUNK), :])
        for part, value in ((0, doubled), (1, turned_back[:HEAD_DIM])):
            former = value[:half]
            latter = value[half:]
            turned = jnp.concatenate(
                [former * cosine + latter * sine, latter * cosine - former * sine], axis=0
            )
            start = part * width + base
            joint_ref[start : start + HEAD_DIM, :] = turned.astype(BF16)
        start = 2 * width + base
        joint_ref[start : start + HEAD_DIM, :] = turned_back[HEAD_DIM:].astype(BF16)
    normed_ref[...] = contract(joint_ref[...], weight_ref[...], 0, 0).astype(BF16)


def retrace(core, qt, grads, full, stats, cosine, sine, kv, kt, weight):
    width, length = qt.shape
    heads = width // HEAD_DIM
    half = HEAD_DIM // 2
    pairs = length // CHUNK
    back = lambda j: pairs - 1 - j
    own = lambda j, core: (0, 2 * back(j) + (core[0] ^ (back(j) & 1)))
    slot = lambda j, core: (back(j), 0, 0)
    across = lambda j, core: (0, back(j))
    return pl.pallas_call(
        retrace_kernel,
        name="retrace",
        cost_estimate=cost(
            5 * 2 * BLOCK * BLOCK * BLOCK * 2 * sum(range(1, pairs + 1)) * heads,
            3 * kv.size + 16 * pairs * width * BLOCK,
            CHUNK * BLOCK * sum(range(1, pairs + 1)) * heads,
        ),
        grid_spec=pltpu.PrefetchScalarGridSpec(
            num_scalar_prefetch=1,
            grid=(pairs,),
            in_specs=[
                pl.BlockSpec((width, BLOCK), own),
                pl.BlockSpec((1, width, BLOCK), slot),
                pl.BlockSpec((1, width, BLOCK), slot),
                pl.BlockSpec((1, 8, BLOCK), slot),
                pl.BlockSpec((half, CHUNK), across),
                pl.BlockSpec((half, CHUNK), across),
                pl.BlockSpec(kv.shape, lambda j, core: (0, 0, 0)),
                pl.BlockSpec(kt.shape, lambda j, core: (0, 0)),
                pl.BlockSpec(weight.shape, lambda j, core: (0, 0)),
            ],
            out_specs=[
                pl.BlockSpec((3 * width, CHUNK), across),
                pl.BlockSpec((CHUNK, weight.shape[1]), lambda j, core: (back(j), 0)),
            ],
            scratch_shapes=[pltpu.VMEM((heads, length, 2 * HEAD_DIM), F32)],
        ),
        out_shape=[
            jax.ShapeDtypeStruct((3 * width, length), BF16),
            jax.ShapeDtypeStruct((length, weight.shape[1]), BF16),
        ],
        compiler_params=pltpu.CompilerParams(vmem_limit_bytes=VMEM_LIMIT),
    )(core, qt, grads, full, stats, cosine, sine, kv, kt, weight)


def after(values, *earlier_values):
    values = tuple(values)
    return lax.optimization_barrier(values + tuple(earlier_values))[: len(values)]


def assemble_kernel(place_ref, *refs):
    down_ref, out_ref = refs[-2:]
    rep = place_ref[1]
    reps = (len(refs) - 2) // 2
    part = out_ref.shape[0]
    for side in range(2):
        @pl.when(pl.program_id(0) == side)
        def _():
            for k in range(reps):
                piece = refs[side * reps + k]
                rows = piece.shape[1]
                target = rep ^ k

                @pl.when(target < reps - 1)
                def _():
                    down_ref[pl.ds(pl.multiple_of(target * rows, rows), rows), :] = piece[0]

                @pl.when(target == reps - 1)
                def _():
                    out_ref[...] = piece[0, :part]


def assemble(place, mine, twin, part):
    owners, rows, columns = mine[0].shape
    reps = len(mine)
    groups = 2 * owners

    def held(side):
        def index(which, z, place):
            moving = (place[0] // 2 + owners - z) % owners
            fixed = (place[0] // 2 + owners - (owners - 1) * (1 - side)) % owners
            return (jnp.where(which == side, moving, fixed), 0, 0)

        return pl.BlockSpec((1, rows, columns), index)

    device = lambda which, z, place: 2 * z + (which ^ (place[0] % 2))
    target = lambda which, z, place: (device(which, z, place), 0)
    return pl.pallas_call(
        assemble_kernel,
        name="assemble",
        grid_spec=pltpu.PrefetchScalarGridSpec(
            num_scalar_prefetch=1,
            grid=(2, owners),
            in_specs=[held(0)] * reps + [held(1)] * reps,
            out_specs=[
                pl.BlockSpec(((reps - 1) * rows, columns), target),
                pl.BlockSpec((part, columns), target),
            ],
        ),
        out_shape=[
            jax.ShapeDtypeStruct((groups * (reps - 1) * rows, columns), BF16),
            jax.ShapeDtypeStruct((groups * part, columns), BF16),
        ],
        compiler_params=pltpu.CompilerParams(vmem_limit_bytes=VMEM_LIMIT),
    )(place, *mine, *twin)


def swap_core(value):
    groups = lax.axis_size("shard")
    return lax.ppermute(value, "shard", [(i, i ^ 1) for i in range(groups)])


def shift_owner(value, distance):
    groups = lax.axis_size("shard")
    step = 2 * distance
    return lax.ppermute(value, "shard", [(i, (i + step) % groups) for i in range(groups)])


def cross_rep(value, mask):
    return lax.ppermute(value, "rep", [(i, i ^ mask) for i in range(lax.axis_size("rep"))])


def pick(stacked, index, axis=0):
    return lax.dynamic_index_in_dim(stacked, index, axis, keepdims=False)


def add_low(*values):
    total = values[0].astype(F32)
    for value in values[1:]:
        total = total + value.astype(F32)
    return total.astype(BF16)


def fold_core(partial_sums, core):
    halves = partial_sums.reshape((-1, 2) + partial_sums.shape[1:])
    received = swap_core(pick(halves, 1 - core, 1))
    return add_low(pick(halves, core, 1), received)


def rep_parts(value):
    reps = lax.axis_size("rep")
    owners, rows, columns = value.shape
    return value.reshape(owners, reps, rows // reps, columns)


def send_rep(value):
    rep = lax.axis_index("rep")
    parts = rep_parts(value)
    return [cross_rep(pick(parts, rep ^ k, 1), k) for k in range(1, lax.axis_size("rep"))]


def pick_parts(value):
    rep = lax.axis_index("rep")
    parts = rep_parts(value)
    return [pick(parts, rep ^ k, 1) for k in range(lax.axis_size("rep"))]


def join_rep(value, received):
    return add_low(pick(rep_parts(value), lax.axis_index("rep"), 1), *received)


def unpack_kernel(rep_ref, *refs):
    reps = 4
    pieces = refs[: 3 * reps]
    in_ref, out_ref, qkv_ref, down_ref = refs[3 * reps : 3 * reps + 4]
    line_refs = refs[3 * reps + 4 :]
    hidden_width = in_ref.shape[1]
    model_width = out_ref.shape[1]
    columns = qkv_ref.shape[1] // 3
    owners = down_ref.shape[0] // in_ref.shape[0]
    width = columns // owners
    for k in range(reps):
        pair, joint, down = pieces[k::reps]
        rows = pair.shape[0]
        first = pl.multiple_of((rep_ref[0] ^ k) * rows, 8)
        own = pl.ds(first, rows)
        in_ref[own, :] = pair[:, :hidden_width].astype(F32)
        out_ref[own, :] = pair[:, hidden_width:].astype(F32)
        whole = joint[:, : 3 * columns].astype(F32)
        for part in range(3):
            qkv_ref[own, part * columns : (part + 1) * columns] = jnp.concatenate(
                [
                    whole[:, (3 * z + part) * width : (3 * z + part + 1) * width]
                    for z in range(owners)
                ],
                axis=1,
            )

        @pl.when(rep_ref[0] == k)
        def _():
            part = line_refs[0].shape[1] // 2
            lines = joint[:, 3 * columns :].astype(F32)
            row = 0
            for line_ref in line_refs:
                count = line_ref.shape[1] // part
                line_ref[...] = jnp.concatenate(
                    [lines[row + i : row + i + 1, :part] for i in range(count)], axis=1
                )
                row += count

        for z in range(owners):
            block = pl.ds(pl.multiple_of(owners * first + z * rows, 8), rows)
            down_ref[block, :] = down[:, z * model_width : (z + 1) * model_width].astype(F32)


def unpack(rep, pair, joint, down, widths, counts):
    hidden_width, model_width, columns = widths
    pieces = [*pair, *joint, *down]
    rows = len(pair) * pair[0].shape[0]
    owners = model_width * 3 // columns
    shapes = [
        (rows, hidden_width),
        (rows, model_width),
        (rows, 3 * model_width),
        (owners * rows, model_width),
    ] + [(1, count * rows) for count in counts]
    whole = pl.BlockSpec(memory_space=pltpu.VMEM)
    return pl.pallas_call(
        unpack_kernel,
        name="unpack",
        in_specs=[pl.BlockSpec(memory_space=pltpu.SMEM)] + [whole] * len(pieces),
        out_specs=[whole] * len(shapes),
        out_shape=[jax.ShapeDtypeStruct(shape, F32) for shape in shapes],
        compiler_params=pltpu.CompilerParams(vmem_limit_bytes=VMEM_LIMIT),
    )(rep, *pieces)


def split_depth(value):
    high = lax.reduce_precision(value, 8, 7)
    return jnp.concatenate([high, value - high]).astype(BF16)


def join_depth(value):
    value = value.astype(F32)
    half = value.shape[0] // 2
    return value[:half] + value[half:]


def add_ordered(values, index_of):
    stacked = jnp.stack(values)
    total = pick(stacked, index_of(0))
    for sender in range(1, len(values)):
        total = total + pick(stacked, index_of(sender))
    return total


def every_rep(value):
    return [value] + [cross_rep(value, k) for k in range(1, lax.axis_size("rep"))]


def exchange_owner(value, owner):
    owners = value.shape[0]
    received = [pick(value, owner)]
    for k in range(1, owners):
        received.append(shift_owner(pick(value, (owner + k) % owners), k))
    return received


def middle_kernel(
    core_ref, weights_ref, mixed_ref, x_ref, cotangent_ref, w_out_ref, b_out_ref, gain_ref,
    shift_ref, w_in_ref, b_in_ref, grad_ref,
    middle_ref, low_ref, active_ref, hidden_ref, total_ref, branch_ref, send_ref,
    sums_ref, hidden_sums_ref, plain_ref, scale_ref, back_ref,
):
    step = pl.program_id(0)
    core = core_ref[0]
    owners = mixed_ref.shape[0] // 2
    width = mixed_ref.shape[1]

    @pl.when(step == 0)
    def _():
        for half in range(2):
            rows = slice(half * BLOCK, (half + 1) * BLOCK)
            mixed = jnp.concatenate(
                [mixed_ref[2 * z + (core ^ half)] for z in range(owners)], axis=0
            )
            branch = contract(mixed, w_out_ref[...], 0, 0) + b_out_ref[...]
            middle = x_ref[rows, :].astype(F32) + branch
            middle_ref[rows, :] = middle
            center = middle - jnp.mean(middle, axis=-1, keepdims=True)
            scale = lax.rsqrt(jnp.mean(center * center, axis=-1, keepdims=True) + EPSILON)
            plain = center * scale
            scale_ref[rows, :] = jnp.broadcast_to(scale, (BLOCK, scale_ref.shape[1]))
            plain_ref[rows, :] = plain
            low_ref[rows, :] = (plain * gain_ref[...] + shift_ref[...]).astype(BF16)
        back_ref[...] = jnp.zeros_like(back_ref)

    hidden = contract(low_ref[...], w_in_ref[...], 1, 0) + b_in_ref[...]
    square = hidden * hidden
    bend = math.sqrt(2 / math.pi)
    turned = jnp.tanh(hidden * (bend + (bend * 0.044715) * square))
    share = 0.5 + 0.5 * turned
    active_ref[...] = (hidden * share).astype(BF16)
    slope = (0.5 * hidden) * (1.0 - turned * turned) * (bend + (3 * bend * 0.044715) * square)
    grad = (grad_ref[...].astype(F32) * (share + slope)).astype(BF16)
    hidden_ref[...] = grad
    hidden_sums_ref[...] = jnp.sum(grad.astype(F32), axis=0, keepdims=True)
    back_ref[...] += contract(grad, w_in_ref[...], 1, 1)

    @pl.when(step == pl.num_programs(0) - 1)
    def _():
        weight = weights_ref[4]
        sums = [jnp.zeros((1, back_ref.shape[1]), F32)] * 3
        for half in range(2):
            rows = slice(half * BLOCK, (half + 1) * BLOCK)
            back = back_ref[rows, :]
            plain = plain_ref[rows, :]
            scaled = back * gain_ref[...]
            total = weight * cotangent_ref[rows, :] + scale_ref[rows, :1] * (
                scaled
                - jnp.mean(scaled, axis=-1, keepdims=True)
                - plain * jnp.mean(scaled * plain, axis=-1, keepdims=True)
            )
            total_ref[rows, :] = total
            low = total.astype(BF16)
            branch_ref[rows, :] = low
            mixed = contract(w_out_ref[...], low, 1, 1).astype(BF16)
            for z in range(owners):
                send_ref[2 * z + (core ^ half)] = mixed[z * width : (z + 1) * width, :]
            for i, value in enumerate((low.astype(F32), back * plain, back)):
                sums[i] = sums[i] + jnp.sum(value, axis=0, keepdims=True)
        for i in range(3):
            sums_ref[i : i + 1, :] = sums[i]


def middle_part(
    core, depth_weights, mixed, x, cotangent, w_out, b_out, gain, shift, w_in, b_in, grad_active
):
    rows, model_width = x.shape
    hidden_width = w_in.shape[1]
    chunk = 2 * CHUNK if hidden_width % (2 * CHUNK) == 0 else CHUNK
    whole = lambda value: pl.BlockSpec(value.shape, lambda j, *_: (0,) * value.ndim)
    across = pl.BlockSpec((rows, chunk), lambda j, *_: (0, j))
    line = pl.BlockSpec((1, chunk), lambda j, *_: (0, j))
    shapes = [
        jax.ShapeDtypeStruct((rows, model_width), F32),
        jax.ShapeDtypeStruct((rows, model_width), BF16),
        jax.ShapeDtypeStruct((rows, hidden_width), BF16),
        jax.ShapeDtypeStruct((rows, hidden_width), BF16),
        jax.ShapeDtypeStruct((rows, model_width), F32),
        jax.ShapeDtypeStruct((rows, model_width), BF16),
        jax.ShapeDtypeStruct(mixed.shape, BF16),
        jax.ShapeDtypeStruct((8, model_width), F32),
        jax.ShapeDtypeStruct((1, hidden_width), F32),
    ]
    out_specs = [whole(shape) for shape in shapes]
    out_specs[2] = out_specs[3] = across
    out_specs[8] = line
    return pl.pallas_call(
        middle_kernel,
        name="middle",
        cost_estimate=cost(
            4 * rows * model_width * (hidden_width + model_width),
            2 * w_in.size + 8 * grad_active.size,
            grad_active.size,
        ),
        grid_spec=pltpu.PrefetchScalarGridSpec(
            num_scalar_prefetch=2,
            grid=(hidden_width // chunk,),
            in_specs=[
                whole(mixed),
                whole(x),
                whole(cotangent),
                whole(w_out),
                whole(b_out),
                whole(gain),
                whole(shift),
                pl.BlockSpec((model_width, chunk), lambda j, *_: (0, j)),
                line,
                across,
            ],
            out_specs=out_specs,
            scratch_shapes=[
                pltpu.VMEM((rows, model_width), F32),
                pltpu.VMEM((rows, 128), F32),
                pltpu.VMEM((rows, model_width), F32),
            ],
        ),
        out_shape=shapes,
        compiler_params=pltpu.CompilerParams(vmem_limit_bytes=VMEM_LIMIT),
    )(
        core, depth_weights, mixed, x, cotangent, w_out, b_out, gain, shift, w_in, b_in,
        grad_active,
    )


def down_kernel(active_ref, down_grad_ref, down_ref):
    down_ref[...] = contract(active_ref[...], down_grad_ref[...], 0, 0).astype(BF16)


def down_part(active, down_grad):
    rows, model_width = down_grad.shape
    steps = active.shape[1] // model_width
    return pl.pallas_call(
        down_kernel,
        name="down_part",
        grid=(steps,),
        in_specs=[
            pl.BlockSpec((rows, model_width), lambda j: (0, j)),
            pl.BlockSpec((rows, model_width), lambda j: (0, 0)),
        ],
        out_specs=pl.BlockSpec((model_width, model_width), lambda j: (j, 0)),
        out_shape=jax.ShapeDtypeStruct((steps * model_width, model_width), BF16),
        compiler_params=pltpu.CompilerParams(vmem_limit_bytes=VMEM_LIMIT),
    )(active, down_grad)


def result_kernel(
    weights_ref, active_ref, w_down_ref, b_down_ref, middle_ref, mix_ref, cotangent_ref,
    layer_ref, depth_ref, total_ref,
):
    step = pl.program_id(0)

    @pl.when(step == 0)
    def _():
        total_ref[...] = middle_ref[...] + b_down_ref[...]

    total_ref[...] += contract(active_ref[...], w_down_ref[...], 1, 0)

    @pl.when(step == pl.num_programs(0) - 1)
    def _():
        result = total_ref[...]
        layer_ref[...] = weights_ref[4] * result + mix_ref[...]
        depth = (result * cotangent_ref[...]).reshape(-1, 8, result.shape[1])
        depth_ref[...] = jnp.sum(depth, axis=0)


def result_part(depth_weights, active, w_down, b_down, middle, mix, cotangent):
    rows, model_width = middle.shape
    steps = active.shape[1] // model_width
    whole = lambda value: pl.BlockSpec(value.shape, lambda j, *_: (0,) * value.ndim)
    depth = jax.ShapeDtypeStruct((8, model_width), F32)
    return pl.pallas_call(
        result_kernel,
        name="result_part",
        grid_spec=pltpu.PrefetchScalarGridSpec(
            num_scalar_prefetch=1,
            grid=(steps,),
            in_specs=[
                pl.BlockSpec((rows, model_width), lambda j, *_: (0, j)),
                pl.BlockSpec((model_width, model_width), lambda j, *_: (j, 0)),
                whole(b_down), whole(middle), whole(mix), whole(cotangent),
            ],
            out_specs=[whole(middle), whole(depth)],
            scratch_shapes=[pltpu.VMEM((rows, model_width), F32)],
        ),
        out_shape=[jax.ShapeDtypeStruct(middle.shape, F32), depth],
        compiler_params=pltpu.CompilerParams(vmem_limit_bytes=VMEM_LIMIT),
    )(depth_weights, active, w_down, b_down, middle, mix, cotangent)


def pair_kernel(
    core_ref, low_ref, hidden_ref, mixed_ref, branch_ref,
    low_twin_ref, hidden_twin_ref, mixed_twin_ref, branch_twin_ref,
    own_ref, turned_ref, rows_ref,
):
    step = pl.program_id(0)
    core = core_ref[0]
    owners, part, width = own_ref.shape
    last = pl.num_programs(0) - 1

    @pl.when(step == 0)
    def _():
        for side, ref in ((0, low_ref), (1, low_twin_ref)):
            turned_ref[...] = jnp.transpose(ref[...])
            for z in range(owners):
                start = pl.multiple_of((2 * z + core) * part, part)
                rows_ref[side, z * part : (z + 1) * part, :] = turned_ref[pl.ds(start, part), :]

    @pl.when(step < last)
    def _():
        total = contract(rows_ref[0], hidden_ref[...], 1, 0)
        total = total + contract(rows_ref[1], hidden_twin_ref[...], 1, 0)
        own_ref[...] = total.astype(BF16).reshape(owners, part, width)

    @pl.when(step == last)
    def _():
        total = 0.0
        sides = ((core, mixed_ref, branch_ref), (1 - core, mixed_twin_ref, branch_twin_ref))
        for member, ref, grad_ref in sides:
            for half in range(2):
                mixed = jnp.concatenate(
                    [
                        ref[
                            2 * z + (member ^ half),
                            pl.ds(pl.multiple_of(core * part, part), part),
                            :,
                        ]
                        for z in range(owners)
                    ],
                    axis=0,
                )
                rows = slice(half * BLOCK, (half + 1) * BLOCK)
                total = total + contract(mixed, grad_ref[rows, :], 1, 0)
        own_ref[...] = total.astype(BF16).reshape(owners, part, width)


def pair_sums(core, own, twin):
    low, hidden, mixed, branch = own
    rows, model_width = low.shape
    owners = mixed.shape[0] // 2
    part = model_width // (2 * owners)
    steps = hidden.shape[1] // model_width
    whole = lambda value: pl.BlockSpec(value.shape, lambda j, core: (0,) * value.ndim)
    chunk = pl.BlockSpec((rows, model_width), lambda j, core: (0, jnp.minimum(j, steps - 1)))
    one_side = [whole(low), chunk, whole(mixed), whole(branch)]
    return pl.pallas_call(
        pair_kernel,
        name="pair_sums",
        grid_spec=pltpu.PrefetchScalarGridSpec(
            num_scalar_prefetch=1,
            grid=(steps + 1,),
            in_specs=one_side * 2,
            out_specs=pl.BlockSpec((owners, part, model_width), lambda j, core: (0, 0, j)),
            scratch_shapes=[
                pltpu.VMEM((model_width, rows), BF16),
                pltpu.VMEM((2, owners * part, rows), BF16),
            ],
        ),
        out_shape=jax.ShapeDtypeStruct((owners, part, (steps + 1) * model_width), BF16),
        compiler_params=pltpu.CompilerParams(vmem_limit_bytes=VMEM_LIMIT),
    )(core, *own, *twin)


def joint_kernel(
    core_ref, plain_ref, joint_ref, weight_ref, gain_ref, shift_ref,
    own_ref, other_ref, sums_ref, lines_ref, product_ref, full_ref,
):
    step = pl.program_id(0)
    core = core_ref[0]
    owners, part, columns = own_ref.shape
    joint = joint_ref[...]
    product = contract(joint, plain_ref[...], 1, 0)
    line = contract(jnp.ones((8, joint.shape[1]), BF16), joint, 1, 1)

    @pl.when(step == 0)
    def _():
        product_ref[...] = product
        lines_ref[...] = line

    @pl.when(step > 0)
    def _():
        product_ref[...] += product
        lines_ref[...] += line

    @pl.when(step == pl.num_programs(0) - 1)
    def _():
        total = product_ref[...]
        sums = jnp.transpose(lines_ref[...])[:, :1]
        weight = weight_ref[...].astype(F32)
        sums_ref[0:1, :] = jnp.sum(total * weight, axis=0, keepdims=True)
        sums_ref[1:2, :] = jnp.sum(sums * weight, axis=0, keepdims=True)
        full_ref[...] = jnp.transpose(gain_ref[...] * total + shift_ref[...] * sums).astype(BF16)
        for z in range(owners):
            for side, ref in ((0, own_ref), (1, other_ref)):
                start = pl.multiple_of((2 * z + (core ^ side)) * part, part)
                ref[z] = full_ref[pl.ds(start, part), :]


def joint_part(core, plain, joint_t, weight_t, gain, shift):
    length, model_width = plain.shape
    columns = joint_t.shape[0]
    owners = length // CHUNK // 2
    part = model_width // (2 * owners)
    tile = 2 * CHUNK
    whole = lambda value: pl.BlockSpec(value.shape, lambda j, core: (0,) * value.ndim)
    shapes = [
        jax.ShapeDtypeStruct((owners, part, columns), BF16),
        jax.ShapeDtypeStruct((owners, part, columns), BF16),
        jax.ShapeDtypeStruct((8, model_width), F32),
        jax.ShapeDtypeStruct((8, columns), F32),
    ]
    return pl.pallas_call(
        joint_kernel,
        name="joint_part",
        grid_spec=pltpu.PrefetchScalarGridSpec(
            num_scalar_prefetch=1,
            grid=(length // tile,),
            in_specs=[
                pl.BlockSpec((tile, model_width), lambda j, core: (j, 0)),
                pl.BlockSpec((columns, tile), lambda j, core: (0, j)),
                whole(weight_t),
                whole(gain),
                whole(shift),
            ],
            out_specs=[whole(shape) for shape in shapes],
            scratch_shapes=[
                pltpu.VMEM((columns, model_width), F32),
                pltpu.VMEM((model_width, columns), BF16),
            ],
        ),
        out_shape=shapes,
        compiler_params=pltpu.CompilerParams(vmem_limit_bytes=VMEM_LIMIT),
    )(core, plain, joint_t, weight_t, gain, shift)


def head_split_device(
    block_in,
    earlier,
    cotangent,
    qkv_weight,
    out_weight,
    in_weight,
    down_weight,
    qk_bias,
    value_bias,
    out_bias,
    in_bias,
    down_bias,
    gain_one,
    shift_one,
    gain_two,
    shift_two,
    depth_weights,
):
    row_count, model_width = block_in.shape
    hidden_width = in_weight.shape[1]
    groups = lax.axis_size("shard")
    owners = groups // 2
    width = model_width // owners
    part = model_width // groups
    length = row_count * groups
    half = HEAD_DIM // 2
    member = lax.axis_index("shard")
    owner = member // 2
    core = member % 2

    pieces = qkv_weight.astype(BF16).reshape(part, 3, owners, width)
    pieces = jnp.transpose(pieces, (2, 0, 1, 3)).reshape(owners, part, 3 * width)
    vectors = (
        qk_bias, value_bias, gain_one, shift_one,
        out_bias, in_bias, down_bias, gain_two, shift_two,
    )
    late = lax.optimization_barrier(jnp.concatenate(vectors))
    early, late = late[: 5 * part], late[5 * part :]
    half_late = late.shape[0] // 2
    rows = [early, late[:half_late], late[half_late:]]
    rows = jnp.stack([jnp.pad(row, (0, 3 * width - row.shape[0])) for row in rows])
    early = jnp.pad(rows.astype(BF16), ((0, 5), (0, 0)))
    early = jnp.broadcast_to(early, (owners, 8, 3 * width))
    packets = exchange_owner(jnp.concatenate([pieces, early], axis=1), owner)
    packet = jnp.stack(packets)
    other_packet = swap_core(packet)

    tokens = lax.all_gather(block_in, "shard", axis=0, tiled=True)
    grad_earlier, mix, depth_sums = average(depth_weights, earlier, cotangent)

    by_core = jnp.stack([packet, other_packet])
    packet = jnp.stack(
        [
            lax.dynamic_slice(
                by_core,
                (core ^ (d % 2), (owner - d // 2) % owners, 0, 0),
                (1, 1, part + 8, 3 * width),
            )[0, 0]
            for d in range(groups)
        ]
    )
    w_own = packet[:, :part].reshape(model_width, 3 * width)
    early = packet[:, part].astype(F32)
    late = packet[:, part + 1 : part + 3, :half_late].astype(F32).reshape(groups, -1)
    b_qk = early[:, : 2 * part].reshape(2 * model_width)
    b_value = early[:, 2 * part : 3 * part].reshape(model_width)
    g_one = early[:, 3 * part : 4 * part].reshape(1, model_width)
    s_one = early[:, 4 * part : 5 * part].reshape(1, model_width)
    b_joint = jnp.concatenate([b_qk, b_value]).reshape(3, owners, width)
    b_own = lax.dynamic_index_in_dim(b_joint, owner, 1, keepdims=False).reshape(3 * width, 1)
    w_turned = jnp.transpose(w_own)

    freqs = 10000.0 ** (-jnp.arange(half, dtype=F32) / half)
    angles = freqs[:, None] * jnp.arange(length, dtype=jnp.int32).astype(F32)[None, :]
    cosine = jnp.cos(angles)
    sine = jnp.sin(angles)
    core_index = core.astype(jnp.int32).reshape(1)

    hidden_part = hidden_width // groups
    share = hidden_part // 3
    row = lambda first, size: late[:, first : first + size].reshape(1, groups * size)
    b_out = row(0, part)
    b_in = row(part, hidden_part)
    b_down = row(part + hidden_part, part)
    g_two = row(2 * part + hidden_part, part)
    s_two = row(3 * part + hidden_part, part)
    last = jnp.pad(out_weight.astype(BF16), ((0, share - part), (0, 0)))
    rep = lax.axis_index("rep")
    tail_packet = lax.dynamic_slice_in_dim(
        jnp.concatenate([down_weight.astype(BF16), last], axis=0), rep * share, share, 0
    )
    tokens, w_turned, b_own, cosine, sine, mix, tail_packet, in_packet = after(
        (tokens, w_turned, b_own, cosine, sine, mix, tail_packet, in_weight.astype(BF16)),
        grad_earlier,
        depth_sums,
    )
    tail_parts = [tail_packet] + [shift_owner(tail_packet, k) for k in range(1, owners)]
    states = project(tokens, w_turned, b_own, g_one, s_one, cosine, sine, 0, groups, ())
    plain_all, qt, kt, vt, kv, *tail_parts = lax.optimization_barrier((*states, *tail_parts))
    grad_result = depth_weights[4] * cotangent
    down_grad = grad_result.astype(BF16)
    tail_stack = jnp.stack(tail_parts)
    qt, tail_stack, in_packet, down_grad = lax.optimization_barrier(
        (qt, tail_stack, in_packet, down_grad)
    )
    w_in = lax.all_gather(in_packet, "shard", axis=0, tiled=True)
    tail_mine = every_rep(tail_stack)
    mixed_own, attended, stats = attend(core_index, qt, kv, vt)
    stats, *tail_mine = lax.optimization_barrier((stats, *tail_mine))
    mixed_two = lax.all_to_all(mixed_own, "shard", 0, 0)
    tail_other = [swap_core(value) for value in tail_mine]
    w_down, w_out = assemble(
        jnp.stack([member, rep]).astype(jnp.int32), tail_mine, tail_other, part
    )
    grad_active = contract(down_grad, w_down, 1, 1).astype(BF16)
    mixed_two, grad_active = lax.optimization_barrier((mixed_two, grad_active))

    inputs = block_in.astype(F32)
    (
        middle, normed_two_low, active, grad_hidden, grad_middle, branch_grad, grad_own,
        token_sums, grad_in_b,
    ) = middle_part(
        core_index, depth_weights, mixed_two, block_in, cotangent, w_out, b_out, g_two, s_two,
        w_in, b_in, grad_active,
    )
    grad_out_b, grad_gain_two, grad_shift_two = (token_sums[i] for i in range(3))
    grad_in_b = grad_in_b[0]
    grad_own = lax.all_to_all(grad_own, "shard", 0, 0)
    pair_own = (normed_two_low, grad_hidden, mixed_two, branch_grad)
    pair_twin = tuple(swap_core(value) for value in pair_own)
    grad_down_w = down_part(active, down_grad)
    folded = pair_sums(core_index, pair_own, pair_twin)
    grad_down_b = jnp.sum(down_grad.astype(F32), axis=0)
    grad_own, folded, grad_down_w = lax.optimization_barrier((grad_own, folded, grad_down_w))
    sent = send_rep(folded)
    down_sums = lax.psum_scatter(grad_down_w, "shard", scatter_dimension=0, tiled=True)
    joint_t, grad_normed = retrace(
        core_index, qt, grad_own, attended, stats, cosine, sine, kv, kt, w_turned
    )
    joint_t, grad_normed, folded, plain_all, active, *sent = lax.optimization_barrier(
        (joint_t, grad_normed, folded, plain_all, active, *sent)
    )
    grad_normed = lax.psum_scatter(
        grad_normed, "shard", scatter_dimension=0, tiled=True
    )
    folded = join_rep(folded, sent)

    own_sums, other_sums, first_sums, joint_sums = joint_part(
        core_index, plain_all, joint_t, w_turned, g_one, s_one
    )
    arrived = exchange_owner(folded, owner)
    layer_out, last_depth = result_part(
        depth_weights, active, w_down, b_down, middle, mix, cotangent
    )
    own_sums, other_sums, first_sums, joint_sums, last_depth, *arrived = (
        lax.optimization_barrier(
            (own_sums, other_sums, first_sums, joint_sums, last_depth, *arrived)
        )
    )
    pair_sum = add_low(*arrived)
    grad_gain_one, grad_shift_one = first_sums[0], first_sums[1]
    joint_sums = joint_sums[0]

    spread_sums = lax.dynamic_update_slice(
        jnp.zeros((3, model_width), F32), joint_sums.reshape(3, width), (0, owner * width)
    ).reshape(3 * model_width)
    vectors = (
        spread_sums[: 2 * model_width],
        spread_sums[2 * model_width :],
        grad_out_b,
        grad_in_b,
        grad_down_b,
        grad_gain_one,
        grad_shift_one,
        grad_gain_two,
        grad_shift_two,
    )
    counts = [vector.shape[0] // model_width for vector in vectors]
    small = jnp.concatenate(
        [
            vector.reshape(groups, count, part).astype(BF16)
            for vector, count in zip(vectors, counts)
        ],
        axis=1,
    )
    small = jnp.pad(small, ((0, 0), (0, part - small.shape[1]), (0, 128 - part)))
    mark = (part // 4 - 8, 3 * width)
    small = small.reshape(owners, 2, part, 128)
    depth_count = 2 * depth_weights.shape[0]
    depth_row = lambda value: value[mark[0], mark[1] : mark[1] + depth_count]
    with_depth = lambda value, sums: value.at[
        :, mark[0], mark[1] : mark[1] + depth_count
    ].set(split_depth(sums))
    received = swap_core(
        jnp.concatenate([other_sums, pick(small, 1 - core, 1)], axis=2)
    )
    mixed_sums = add_low(
        jnp.concatenate([own_sums, pick(small, core, 1)], axis=2), received
    )
    depth_sum = jnp.concatenate([depth_sums, last_depth[None]], axis=0).sum(axis=(1, 2))
    depth_sum = depth_sum + swap_core(depth_sum)
    down_parts = pick_parts(down_sums[None])
    down_rows = part // 4
    columns = 3 * width + 128
    sums_parts = [with_depth(value, depth_sum) for value in pick_parts(mixed_sums)]
    received = [
        cross_rep(
            jnp.concatenate([sums, down.reshape(owners, down_rows, model_width)], axis=2), k
        )
        for k, (sums, down) in enumerate(zip(sums_parts[1:], down_parts[1:]), 1)
    ]
    pair_sum, *received = lax.optimization_barrier((pair_sum, *received))
    pair_pieces = every_rep(pair_sum)
    mixed_sums = add_low(sums_parts[0], *[value[:, :, :columns] for value in received])
    depth_sum = add_ordered(
        [join_depth(depth_row(value[0])) for value in (sums_parts[0], *received)], lambda k: rep ^ k
    )
    mixed_sums = with_depth(mixed_sums, depth_sum)
    down_sums = add_low(
        down_parts[0].reshape(owners, down_rows, model_width),
        *[value[:, :, columns:] for value in received],
    )
    down_pieces = every_rep(jnp.concatenate([down_sums[k] for k in range(owners)], axis=1))
    arrived = exchange_owner(mixed_sums, owner)
    small = add_low(*[value[:, 3 * width :] for value in arrived])
    by_distance = jnp.stack([value[:, : 3 * width] for value in arrived])
    by_owner = [pick(by_distance, (owner - k) % owners) for k in range(owners)]
    joint_pieces = every_rep(jnp.concatenate([*by_owner, small], axis=1))
    depth_sums = [depth_row(value) for value in arrived]
    pieces = lax.optimization_barrier(
        (*joint_pieces, *pair_pieces, *down_pieces, *depth_sums)
    )
    joint_pieces, pair_pieces = pieces[:4], pieces[4:8]
    down_pieces, depth_sums = pieces[8:12], pieces[12:]
    grad_depth = add_ordered(
        [join_depth(value) for value in depth_sums], lambda k: (owner - k) % owners
    )
    sum_in, sum_out, sum_qkv, sum_down, *small_outs = unpack(
        lax.axis_index("rep").astype(jnp.int32).reshape(1),
        pair_pieces,
        joint_pieces,
        down_pieces,
        (hidden_width, model_width, 3 * width),
        counts,
    )
    small_outs = [value.reshape(-1) for value in small_outs]
    finished = (sum_in, sum_out, sum_qkv, sum_down, grad_depth, *small_outs)
    grad_normed, sum_in, sum_out, sum_qkv, sum_down, grad_depth, *small_outs = (
        lax.optimization_barrier((grad_normed, *finished))
    )
    grad_normed = grad_normed.astype(F32)
    center = inputs - jnp.mean(inputs, axis=-1, keepdims=True)
    scale = lax.rsqrt(jnp.mean(center * center, axis=-1, keepdims=True) + EPSILON)
    plain = center * scale
    scaled = grad_normed * g_one
    grad_block = grad_middle + scale * (
        scaled
        - jnp.mean(scaled, axis=-1, keepdims=True)
        - plain * jnp.mean(scaled * plain, axis=-1, keepdims=True)
    )

    return (
        layer_out,
        grad_block,
        grad_earlier,
        sum_qkv,
        sum_out,
        sum_in,
        sum_down,
        *small_outs,
        grad_depth,
    )


def per_device(*args):
    block_in = args[0]
    row_count, model_width = block_in.shape
    groups = lax.axis_size("shard")
    head_count = model_width // HEAD_DIM
    late_size = (4 * model_width + args[5].shape[1]) // groups
    if (
        groups == 8
        and lax.axis_size("rep") == 4
        and row_count == CHUNK
        and head_count % (groups // 2) == 0
        and head_count // (groups // 2) <= 8
        and late_size <= 12 * model_width // groups
        and args[5].shape[1] % (3 * groups) == 0
        and model_width // groups <= args[5].shape[1] // (3 * groups)
    ):
        return head_split_device(*args)
    return generic_device(*args)


def solution(mesh):
    placed = (
        P(("rep", "shard"), None),
        P(None, ("rep", "shard"), None),
        P(("rep", "shard"), None),
        P("shard", None),
        P("shard", None),
        P("shard", None),
        P("shard", None),
        P("shard"),
        P("shard"),
        P("shard"),
        P("shard"),
        P("shard"),
        P("shard"),
        P("shard"),
        P("shard"),
        P("shard"),
        P(),
    )
    return jax.shard_map(
        per_device,
        mesh=mesh,
        in_specs=placed,
        out_specs=(
            P(("rep", "shard"), None),
            P(("rep", "shard"), None),
            P(None, ("rep", "shard"), None),
            P("shard", None),
            P("shard", None),
            P("shard", None),
            P("shard", None),
            P("shard"),
            P("shard"),
            P("shard"),
            P("shard"),
            P("shard"),
            P("shard"),
            P("shard"),
            P("shard"),
            P("shard"),
            P(),
        ),
        check_vma=False,
    )
```
